32 devices in a mesh: dp: 4 (over z), row: 2 (over core), col: 4 (over y, x).
Axes of the slice: x: 2, y: 2, z: 4, core: 2. Of those that a mesh axis runs over, the one named last changes fastest.
Arguments:
- hidden_in: bfloat16 [4096, 2048], P(('dp', 'row', 'col')), may hold values from -6 to 6
- cotangent: bfloat16 [4096, 2048], P(('dp', 'row', 'col')), may hold values from -6 to 6
- norm_attn: float32 [2048], replicated, may hold values from 0.5 to 1.5
- w_query: bfloat16 [2048, 2048], P('col', 'row'), may hold values from -0.125 to 0.125
- w_key: bfloat16 [2048, 2048], P('col', 'row'), may hold values from -0.125 to 0.125
- w_value: bfloat16 [2048, 2048], P('col', 'row'), may hold values from -0.125 to 0.125
- query_gain: float32 [2048], replicated, may hold values from 0.5 to 1.5
- key_gain: float32 [2048], replicated, may hold values from 0.5 to 1.5
- w_out: bfloat16 [2048, 2048], P('row', 'col'), may hold values from -1 to 1
- norm_moe: float32 [2048], replicated, may hold values from 0.5 to 1.5
- w_router: bfloat16 [2048, 16], replicated, may hold values from -0.09375 to 0.09375
- w_gate: bfloat16 [16, 2048, 1024], P(('dp', 'col'), None, 'row'), may hold values from -0.125 to 0.125
- w_up: bfloat16 [16, 2048, 1024], P(('dp', 'col'), None, 'row'), may hold values from -0.125 to 0.125
- w_down: bfloat16 [16, 1024, 2048], P(('dp', 'col'), 'row'), may hold values from -2 to 2
- routes: int32 [4096, 8], P(('dp', 'row', 'col')), may hold values from 0 to 15, all different within a row; in each aligned block of 128 rows (0 to 127, 128 to 255, ...) at most 128 rows name the same one
Outputs:
- block_out: bfloat16 [4096, 2048], P(('dp', 'row', 'col'))
- grad_input: float32 [4096, 2048], P(('dp', 'row', 'col'))
- grad_norm_attn: float32 [2048], replicated
- grad_query: float32 [2048, 2048], P('col', 'row')
- grad_key: float32 [2048, 2048], P('col', 'row')
- grad_value: float32 [2048, 2048], P('col', 'row')
- grad_query_gain: float32 [2048], replicated
- grad_key_gain: float32 [2048], replicated
- grad_out_proj: float32 [2048, 2048], P('row', 'col')
- grad_norm_moe: float32 [2048], replicated
- grad_router: float32 [2048, 16], replicated
- grad_gate: float32 [16, 2048, 1024], P(('dp', 'col'), None, 'row')
- grad_up: float32 [16, 2048, 1024], P(('dp', 'col'), None, 'row')
- grad_down: float32 [16, 1024, 2048], P(('dp', 'col'), 'row')
The draws below stay inside these ranges and needn't reach their ends.
Inputs may be any that keep to these rules, and one draw needn't show every extreme that they name: `routes`: each row names 8 different experts. Among the 128 rows of one device no expert is named more than 128 times, and in some devices' rows one expert is named exactly 128 times.
All inputs are finite; a program needn't handle non-finite values.
Results may differ from the reference program's by a relative error of at most 0.019.
Values may be sent and summed in bfloat16 or wider, within the bound.
A program may use at most 320 MiB of HBM per device.

```python
import math
import jax
import jax.numpy as jnp
import numpy as np
from jax import lax

D = 2048
HEADS = 16
HEAD_DIM = 128
FFE = 1024
TOPK = 8
SEQ_LEN = 1024
TOK_DEV = 128
TOKENS = 4096
EXPERTS = 16
CAP = 128


def block_levels(own_key, dims, cuts, least, largest):
    loudness, own = 1.0, jax.random.fold_in(own_key, 6)
    for position, blocks in cuts:
        steps = jnp.exp(jax.random.uniform(jax.random.fold_in(own, position), (blocks,), jnp.float32, least / len(cuts), largest / len(cuts)))
        loudness = loudness * jnp.repeat(steps, dims[position] // blocks).reshape([-1 if axis == position else 1 for axis in range(len(dims))])
    return loudness


def shared_out(key, own, number, rows, number_of, top, limit, lean):
    order = jax.random.permutation(key, number_of)
    heavy_load, common = load_shares(number_of, rows * top, limit, lean, True), load_shares(number_of, rows * top, limit, lean, False)
    places = jnp.arange(number_of)

    def named(sizes, offset_by):
        used = int((sizes > 0).sum())
        fixed = max(1, used // 4)
        passed = fixed + (places - fixed + offset_by * (used - fixed)) % max(1, number_of - fixed)
        return jnp.zeros((number_of,), jnp.int32).at[order[jnp.where(places < fixed, places, passed)]].set(jnp.asarray(sizes, jnp.int32))

    sizes = jnp.where(number % 4 == 0, named(heavy_load, number // 4), named(common, number - number // 4 - 1))
    mixed = jax.random.permutation(jax.random.fold_in(own, 3), number_of)
    giver, sink = mixed[0:number_of // 2 * 2:2], mixed[1:number_of // 2 * 2:2]
    margin = jnp.minimum(sizes[giver] - 1, limit - sizes[sink]) // 2
    margin = jnp.where((giver == order[0]) | (sink == order[0]) | (sizes[sink] == 0), 0, jnp.maximum(margin, 0))
    passed = jax.random.randint(jax.random.fold_in(own, 4), (number_of // 2,), 0, 1 << 20) % (margin + 1)
    sizes = sizes.at[giver].add(-passed).at[sink].add(passed)
    items = jnp.searchsorted(jnp.cumsum(sizes), jnp.arange(rows * top), side="right").astype(jnp.int32)
    table = items.reshape(top, rows).T
    table = table[jax.random.permutation(jax.random.fold_in(own, 1), rows)]
    offset_by = jax.random.randint(jax.random.fold_in(own, 2), (rows, 1), 0, top)
    return jnp.take_along_axis(table, (jnp.arange(top)[None, :] + offset_by) % top, axis=1)


def load_shares(amount, total, reach, lean, full):
    loads = [(1 << 20) // math.isqrt(rank ** lean) + 1 for rank in range(1, amount + 1)]
    largest = reach if full else min(reach, max(-(-total // amount), total * loads[0] // sum(loads)))
    least = 1 if total - largest >= amount - 1 else 0
    given, rest = [largest] + [least] * (amount - 1), total - largest - least * (amount - 1)
    while rest > 0:
        free = [i for i in range(1, amount) if given[i] < largest] or [i for i in range(1, amount) if given[i] < reach]
        whole, budget = sum([loads[i] for i in free]), rest
        for i in free:
            more = min(reach - given[i], max(1, budget * loads[i] // whole), rest)
            given[i] = given[i] + more
            rest = rest - more
    return np.array(given)


def centred(own_key, extent, spread, limit, shards=(), kind=jnp.bfloat16):
    values = jax.random.normal(own_key, extent, jnp.float32) * spread
    if len(shards) > 0:
        values = block_levels(own_key, extent, shards, -0.22, 0.18) * values
    return jnp.clip(values, min=-limit, max=limit).astype(kind)


def setup_inputs(seed: int = 0) -> dict:
    seeds = jax.random.split(jax.random.key(seed), 16)
    hidden_in = centred(seeds[0], (TOKENS, D), 1.0, 6.0, ((0, 32),))
    cotangent = centred(seeds[1], (TOKENS, D), 1.0, 6.0, ((0, 32),))
    norm_attn = jnp.clip(1.0 + 0.1 * jax.random.normal(seeds[2], (D,), jnp.float32), 0.5, 1.5)
    w_query = centred(seeds[3], (D, D), D ** -0.5, 0.125, ((0, 4), (1, 2)))
    w_key = centred(seeds[4], (D, D), D ** -0.5, 0.125, ((0, 4), (1, 2)))
    w_value = centred(seeds[5], (D, D), D ** -0.5, 0.125, ((0, 4), (1, 2)))
    query_gain = jnp.clip(1.0 + 0.1 * jax.random.normal(seeds[6], (D,), jnp.float32), 0.5, 1.5)
    key_gain = jnp.clip(1.0 + 0.1 * jax.random.normal(seeds[7], (D,), jnp.float32), 0.5, 1.5)
    w_out = centred(seeds[8], (D, D), (D * 16 // SEQ_LEN) ** -0.5, 1.0, ((0, 2), (1, 4)))
    norm_moe = jnp.clip(1.0 + 0.1 * jax.random.normal(seeds[9], (D,), jnp.float32), 0.5, 1.5)
    w_router = centred(seeds[10], (D, EXPERTS), (2 * D) ** -0.5, 0.09375)
    w_gate = centred(seeds[11], (EXPERTS, D, FFE), D ** -0.5, 0.125, ((0, 16), (2, 2)))
    w_up = centred(seeds[12], (EXPERTS, D, FFE), D ** -0.5, 0.125, ((0, 16), (2, 2)))
    w_down = centred(seeds[13], (EXPERTS, FFE, D), (max(FFE // 128, 1)) ** -0.5, 2.0, ((0, 16), (1, 2)))
    routes_keys = jax.random.split(jax.random.fold_in(seeds[14], 1), TOKENS // TOK_DEV)
    routes_turns = jax.random.permutation(jax.random.fold_in(seeds[14], 3), TOKENS // TOK_DEV)
    routes = jax.vmap(lambda own, number: shared_out(jax.random.fold_in(seeds[14], 2), own, number, TOK_DEV, EXPERTS, TOPK, CAP, 2))(routes_keys, routes_turns).reshape((TOKENS, TOPK))
    return {"hidden_in": hidden_in, "cotangent": cotangent, "norm_attn": norm_attn, "w_query": w_query, "w_key": w_key, "w_value": w_value, "query_gain": query_gain, "key_gain": key_gain, "w_out": w_out, "norm_moe": norm_moe, "w_router": w_router, "w_gate": w_gate, "w_up": w_up, "w_down": w_down, "routes": routes}


@jax.custom_vjp
def low(v):
    return lax.optimization_barrier(v.astype(jnp.bfloat16)).astype(jnp.float32)

@jax.custom_vjp
def low_back(v):
    return v

def low_keep(v):
    return (low(v), None)

def low_pass(kept, grad):
    return (grad,)

def back_keep(v):
    return (v, None)

def back_low(kept, grad):
    return (low(grad),)
low.defvjp(low_keep, low_pass)
low_back.defvjp(back_keep, back_low)
EPSILON = 1e-05
THETA = 10000.0
MASKED = -1e+30
HIGHEST = lax.Precision.HIGHEST

def product(left, right):
    return jnp.dot(left, right, precision=HIGHEST, preferred_element_type=jnp.float32)

def rms_apply(values, gain_row):
    return values * lax.rsqrt(lax.optimization_barrier(jnp.mean(values * values, axis=-1, keepdims=True)) + EPSILON) * gain_row

def turn_tables():
    positions = jnp.arange(SEQ_LEN, dtype=jnp.float32)
    inverse = THETA ** (-jnp.arange(0, HEAD_DIM, 2, dtype=jnp.float32) / HEAD_DIM)
    angles = positions[:, None] * inverse[None, :]
    angles = jnp.concatenate([angles, angles], axis=-1)
    return (jnp.cos(angles)[:, None, :], jnp.sin(angles)[:, None, :])

def rotate(values, cosine, sine_table):
    middle = HEAD_DIM // 2
    turned = jnp.concatenate([-values[..., middle:], values[..., :middle]], axis=-1)
    return values * cosine + turned * sine_table

def attend_one(pieces):
    queries, key_rows, value_rows = pieces
    scores = jnp.einsum('qhd,khd->hqk', queries, key_rows, precision=HIGHEST)
    scores = low_back(scores)
    causal = jnp.arange(SEQ_LEN)[:, None] >= jnp.arange(SEQ_LEN)[None, :]
    scores = jnp.where(causal[None], scores, MASKED)
    highest = lax.optimization_barrier(jnp.max(scores, axis=-1, keepdims=True))
    weights = jnp.exp(scores - highest)
    weights = weights / lax.optimization_barrier(jnp.sum(weights, axis=-1, keepdims=True))
    return jnp.einsum('hqk,khd->qhd', low(weights), value_rows, precision=HIGHEST)

def make_forward(routes):
    chosen = lax.optimization_barrier(jnp.sum((routes[:, :, None] == jnp.arange(EXPERTS)[None, None, :]).astype(jnp.float32), axis=1))

    def forward(inputs, norm_attn, w_query, w_key, w_value, query_gain, key_gain, w_out, norm_moe, w_router, w_gate, w_up, w_down):
        normal_x = low(rms_apply(inputs, norm_attn))
        query_raw = low_back(product(normal_x, w_query))
        key_raw = low_back(product(normal_x, w_key))
        value_rows = low(low_back(product(normal_x, w_value)))
        cosine, sine_table = turn_tables()
        shaped = (TOKENS // SEQ_LEN, SEQ_LEN, HEADS, HEAD_DIM)
        queries = low(rotate(rms_apply(query_raw, query_gain).reshape(shaped), cosine, sine_table) * HEAD_DIM ** (-0.5))
        key_rows = low(rotate(rms_apply(key_raw, key_gain).reshape(shaped), cosine, sine_table))
        mixed_heads = lax.map(jax.checkpoint(attend_one), (queries, key_rows, value_rows.reshape(shaped)))
        mixed_heads = low(low_back(mixed_heads.reshape(TOKENS, D)))
        state_rows = inputs + low_back(product(mixed_heads, w_out))
        normal_h = low(rms_apply(state_rows, norm_moe))
        logits = low_back(product(normal_h, w_router))
        shifted = jnp.exp(logits - lax.optimization_barrier(jnp.max(logits, axis=-1, keepdims=True)))
        probabilities = shifted / lax.optimization_barrier(jnp.sum(shifted, axis=-1, keepdims=True))
        shares = probabilities * chosen

        def expert_one(running, pieces):
            gate_weight, up_weight, down_weight, column = pieces
            entry_rows = low_back(normal_h)
            gate_rows = low_back(product(entry_rows, gate_weight))
            up_rows = low_back(product(entry_rows, up_weight))
            active = low(gate_rows * jax.nn.sigmoid(gate_rows) * up_rows)
            result = low_back(low(product(active, down_weight)))
            return (running + column[:, None] * result, None)
        mixture, unused = lax.scan(jax.checkpoint(expert_one), jnp.zeros((TOKENS, D), jnp.float32), (w_gate, w_up, w_down, shares.T))
        return state_rows + mixture
    return forward

def reference(hidden_in, cotangent, norm_attn, w_query, w_key, w_value, query_gain, key_gain, w_out, norm_moe, w_router, w_gate, w_up, w_down, routes):
    forward = make_forward(routes)
    block_out, pullback = jax.vjp(forward, hidden_in.astype(jnp.float32), norm_attn, w_query.astype(jnp.float32), w_key.astype(jnp.float32), w_value.astype(jnp.float32), query_gain, key_gain, w_out.astype(jnp.float32), norm_moe, w_router.astype(jnp.float32), w_gate.astype(jnp.float32), w_up.astype(jnp.float32), w_down.astype(jnp.float32))
    gradients = pullback(cotangent.astype(jnp.float32))
    return (block_out.astype(jnp.bfloat16), gradients[0], gradients[1], gradients[2], gradients[3], gradients[4], gradients[5], gradients[6], gradients[7], gradients[8], gradients[9], gradients[10], gradients[11], gradients[12])
```

```python
import functools

import jax
import jax.numpy as jnp
from jax import lax
from jax.experimental import pallas as pl
from jax.experimental.pallas import tpu as pltpu
from jax.sharding import PartitionSpec as P

MESH = pl.DeviceIdType.MESH
ANYSPEC = pl.BlockSpec(memory_space=pl.ANY)

def place():
    return lax.axis_index("dp"), lax.axis_index("row"), lax.axis_index("col")

def greet(peers):
    barrier = pltpu.get_barrier_semaphore()
    for peer in peers:
        pl.semaphore_signal(barrier, inc=1, device_id=peer, device_id_type=MESH)
    pl.semaphore_wait(barrier, len(peers))

def gather_kernel(planes, parts, count, *refs):
    ins, outs = refs[:count], refs[count:2 * count]
    own_sem, send_sem, recv_sem = refs[2 * count:]
    z, r, c = place()
    first, second, diag = c ^ (1 + r), c ^ (2 - r), c ^ 3
    partner = (z, 1 - r, c)
    to_first, to_second = (z, r, first), (z, r, second)
    greet([to_first, to_second, partner] + [(z ^ k, r, c) for k in range(1, planes)])
    pieces = []
    for a in range(count):
        cut = parts if a == 0 else 1
        pieces += [(a, p, ins[a].shape[0], ins[a].shape[0] // cut) for p in range(cut)]

    def number(zz, rr, cc):
        return ((zz if planes > 1 else 0) * 2 + rr) * 4 + cc

    def place_of(i, which):
        a, p, depth, cut = pieces[i]
        return outs[a].at[pl.ds(pl.multiple_of(which * depth + p * cut, cut), cut)]

    sent = [[] for _ in pieces]

    def send(i, which, target, own=False):
        a, p, depth, cut = pieces[i]
        spot = place_of(i, which)
        copy = pltpu.make_async_remote_copy(
            src_ref=ins[a].at[pl.ds(p * cut, cut)] if own else spot, dst_ref=spot,
            send_sem=send_sem.at[i, len(sent[i])], recv_sem=recv_sem.at[i, which],
            device_id=target, device_id_type=MESH)
        copy.start()
        sent[i].append(copy)

    def await_block(i, which):
        spot = place_of(i, which)
        pltpu.make_async_remote_copy(
            src_ref=spot, dst_ref=spot, send_sem=send_sem.at[i, 0], recv_sem=recv_sem.at[i, which],
            device_id=partner, device_id_type=MESH).wait_recv()

    mine = number(z, r, c)
    keeps = []
    every = range(len(pieces))
    for i in every:
        for target in [to_first, to_second] + [(z ^ k, r, c) for k in range(1, planes)] + [partner]:
            send(i, mine, target, True)
    for a in range(count):
        keep = pltpu.make_async_copy(ins[a], outs[a].at[pl.ds(pl.multiple_of(mine * ins[a].shape[0], ins[a].shape[0]), ins[a].shape[0])], own_sem.at[a])
        keep.start()
        keeps.append(keep)

    def forward(which, targets):
        for i in every:
            await_block(i, which)
            for target in targets:
                send(i, which, target)

    for step in range(planes + 2):
        if 0 < step < planes:
            forward(number(z ^ step, r, c), [to_first, to_second, partner])
        if 0 <= step - 1 < planes:
            forward(number(z ^ (step - 1), r, first), [to_second, partner])
            forward(number(z ^ (step - 1), r, second), [partner])
        if 0 <= step - 2 < planes:
            forward(number(z ^ (step - 2), r, diag), [partner])
    for k in range(planes):
        for j in range(4):
            for i in every:
                await_block(i, number(z ^ k, 1 - r, c ^ j))
    for keep in keeps:
        keep.wait()
    for copies in sent:
        for copy in copies:
            copy.wait_send()

def gather(arrays, planes, collective_id, parts=1):
    count = len(arrays)
    blocks = planes * 8
    sends = (3 + planes - 1) + (planes - 1) * 3 + planes * 4
    pieces = count - 1 + parts
    return pl.pallas_call(
        functools.partial(gather_kernel, planes, parts, count),
        out_shape=[jax.ShapeDtypeStruct((blocks * a.shape[0],) + a.shape[1:], a.dtype) for a in arrays],
        in_specs=[ANYSPEC] * count, out_specs=[ANYSPEC] * count,
        scratch_shapes=[pltpu.SemaphoreType.DMA((count,)), pltpu.SemaphoreType.DMA((pieces, sends)), pltpu.SemaphoreType.DMA((pieces, blocks))],
        compiler_params=pltpu.CompilerParams(collective_id=collective_id, has_side_effects=True),
    )(*arrays)

def reduce_kernel(planes, count, *refs):
    parts, outs = refs[:count], refs[count:2 * count]
    held, fromp, relay, near, far = (refs[(2 + i) * count:(3 + i) * count] for i in range(5))
    load_sem, pair_send, pair_recv, send_sem, relay_recv, near_recv, far_recv = refs[7 * count:]
    z, r, c = place()
    first, second, diag = c ^ (1 + r), c ^ (2 - r), c ^ 3
    partner = (z, 1 - r, c)
    to_first, to_second = (z, r, first), (z, r, second)
    greet([to_first, to_second, partner] + [(z ^ k, r, c) for k in range(1, planes)])
    depth = outs[0].shape[0]
    every = range(count)

    def rows(a, zz, rr, cc):
        which = ((zz if planes > 1 else 0) * 2 + rr) * 4 + cc
        return parts[a].at[pl.ds(pl.multiple_of(which * depth, depth), depth)]

    columns, partner_columns = [c, first, second, diag], [c, second, first, diag]
    loads, pairs = {}, {}
    for k in reversed(range(planes)):
        for j in (3, 2, 1, 0):
            for a in every:
                load = pltpu.make_async_copy(rows(a, z ^ k, r, columns[j]), held[a].at[k, j], load_sem.at[a, k, j])
                load.start()
                pair = pltpu.make_async_remote_copy(
                    src_ref=rows(a, z ^ k, 1 - r, partner_columns[j]), dst_ref=fromp[a].at[k, j],
                    send_sem=pair_send.at[a, k, j], recv_sem=pair_recv.at[a, k, j], device_id=partner, device_id_type=MESH)
                pair.start()
                loads[a, k, j], pairs[a, k, j] = load, pair
    step_rows = 32

    def add(target, sources):
        def body(i, _):
            at = pl.ds(pl.multiple_of(i * step_rows, step_rows), step_rows)
            total = sources[0][at].astype(jnp.float32)
            for source in sources[1:]:
                total = total + source[at].astype(jnp.float32)
            target[at] = total.astype(target.dtype)
            return 0
        lax.fori_loop(0, depth // step_rows, body, 0)

    sent = [[] for _ in every]

    def send(a, source, target, recv, device):
        copy = pltpu.make_async_remote_copy(
            src_ref=source, dst_ref=target, send_sem=send_sem.at[a, len(sent[a])], recv_sem=recv,
            device_id=device, device_id_type=MESH)
        copy.start()
        sent[a].append(copy)

    def await_in(a, target, recv):
        pltpu.make_async_remote_copy(
            src_ref=target, dst_ref=target, send_sem=send_sem.at[a, 0], recv_sem=recv,
            device_id=partner, device_id_type=MESH).wait_recv()

    def ready(a, k, j):
        loads[a, k, j].wait()
        pairs[a, k, j].wait_recv()

    def to_relay(k):
        for j in (3, 2):
            for a in every:
                ready(a, k, j)
                mine = held[a].at[k, j]
                add(mine, [mine, fromp[a].at[k, j]])
                if j == 3:
                    send(a, mine, relay[a].at[k], relay_recv.at[a, k], to_second)
                else:
                    send(a, mine, near[a].at[k, 1], near_recv.at[a, k, 1], to_second)

    def pass_on(k):
        for a in every:
            ready(a, k, 1)
            await_in(a, relay[a].at[k], relay_recv.at[a, k])
            mine = held[a].at[k, 1]
            add(mine, [mine, fromp[a].at[k, 1], relay[a].at[k]])
            send(a, mine, near[a].at[k, 0], near_recv.at[a, k, 0], to_first)

    def collect(k):
        for a in every:
            ready(a, k, 0)
            await_in(a, near[a].at[k, 0], near_recv.at[a, k, 0])
            await_in(a, near[a].at[k, 1], near_recv.at[a, k, 1])
            mine = held[a].at[k, 0]
            terms = [mine, fromp[a].at[k, 0], near[a].at[k, 0], near[a].at[k, 1]]
            if k > 0:
                add(mine, terms)
                send(a, mine, far[a].at[k - 1], far_recv.at[a, k - 1], (z ^ k, r, c))
            else:
                for i in range(planes - 1):
                    await_in(a, far[a].at[i], far_recv.at[a, i])
                add(outs[a], terms + [far[a].at[i] for i in range(planes - 1)])

    order = list(reversed(range(planes)))
    for step in range(planes + 2):
        if step < planes:
            to_relay(order[step])
        if 0 <= step - 1 < planes:
            pass_on(order[step - 1])
        if 0 <= step - 2 < planes:
            collect(order[step - 2])
    for copies in sent:
        for copy in copies:
            copy.wait_send()
    for pair in pairs.values():
        pair.wait_send()


def reduce_scatter(partials, planes, collective_id):
    count, blocks = len(partials), planes * 8
    shapes = [((p.shape[0] // blocks, p.shape[1]), p.dtype) for p in partials]
    sends, far = planes * 4 - 1, max(planes - 1, 1)
    scratch = [pltpu.VMEM(lead + shape, kind) for lead in ((planes, 4), (planes, 4), (planes,), (planes, 2), (far,)) for shape, kind in shapes]
    dma = pltpu.SemaphoreType.DMA
    return pl.pallas_call(
        functools.partial(reduce_kernel, planes, count),
        out_shape=[jax.ShapeDtypeStruct(shape, jnp.float32) for shape, _ in shapes],
        in_specs=[ANYSPEC] * count, out_specs=[pl.BlockSpec(memory_space=pltpu.VMEM)] * count,
        scratch_shapes=scratch + [
            dma((count, planes, 4)), dma((count, planes, 4)), dma((count, planes, 4)), dma((count, sends)),
            dma((count, planes)), dma((count, planes, 2)), dma((count, far))],
        compiler_params=pltpu.CompilerParams(collective_id=collective_id, has_side_effects=True, vmem_limit_bytes=48 * 2**20),
    )(*partials)


def exchange_kernel(wq_ref, wk_ref, wv_ref, wo_ref, proj_ref, out_ref, own_sem, send_sem, recv_sem):
    z, r, c = place()
    width = proj_ref.shape[1] // 3
    depth = wq_ref.shape[0]
    out_rows, out_width = out_ref.shape[0], wo_ref.shape[1]
    greet([(z, r, c ^ j) for j in range(1, 4)])

    def source(a, target):
        if a < 3:
            return (wq_ref, wk_ref, wv_ref)[a].at[:, pl.ds(pl.multiple_of(target * width, width), width)]
        return wo_ref.at[pl.ds(pl.multiple_of(target * out_rows, out_rows), out_rows), :]

    def spot(a, origin):
        if a < 3:
            return proj_ref.at[pl.ds(pl.multiple_of(origin * depth, depth), depth), pl.ds(a * width, width)]
        return out_ref.at[:, pl.ds(pl.multiple_of(origin * out_width, out_width), out_width)]

    waits = []
    for a in range(4):
        keep = pltpu.make_async_copy(source(a, c), spot(a, c), own_sem.at[a])
        keep.start()
        waits.append(keep.wait)
        for j in range(1, 4):
            copy = pltpu.make_async_remote_copy(
                src_ref=source(a, c ^ j), dst_ref=spot(a, c), send_sem=send_sem.at[a, j - 1],
                recv_sem=recv_sem.at[a, j - 1], device_id=(z, r, c ^ j), device_id_type=MESH)
            copy.start()
            waits.append(copy.wait_send)
    for a in range(4):
        for j in range(1, 4):
            arrived = spot(a, c ^ j)
            pltpu.make_async_remote_copy(
                src_ref=arrived, dst_ref=arrived, send_sem=send_sem.at[a, j - 1], recv_sem=recv_sem.at[a, j - 1],
                device_id=(z, r, c ^ j), device_id_type=MESH).wait_recv()
    for wait in waits:
        wait()


def exchange_weights(w_query, w_key, w_value, w_out, collective_id):
    depth, half = w_query.shape
    kind = w_query.dtype
    width, out_rows, out_width = half // 4, w_out.shape[0] // 4, w_out.shape[1] * 4
    return pl.pallas_call(
        exchange_kernel,
        out_shape=[jax.ShapeDtypeStruct((depth * 4, 3 * width), kind), jax.ShapeDtypeStruct((out_rows, out_width), kind)],
        in_specs=[ANYSPEC] * 4, out_specs=[ANYSPEC] * 2,
        scratch_shapes=[pltpu.SemaphoreType.DMA((4,)), pltpu.SemaphoreType.DMA((4, 3)), pltpu.SemaphoreType.DMA((4, 3))],
        compiler_params=pltpu.CompilerParams(collective_id=collective_id, has_side_effects=True),
    )(w_query, w_key, w_value, w_out)


def total_kernel(value_ref, out_ref, slots, send_sem, recv_sem):
    z, r, c = place()
    peers = [(z, r ^ (j >> 2), c ^ (j & 3)) for j in range(1, 8)]
    greet(peers)
    copies = []
    for j, peer in enumerate(peers):
        copy = pltpu.make_async_remote_copy(
            src_ref=value_ref, dst_ref=slots.at[j], send_sem=send_sem.at[j], recv_sem=recv_sem.at[j],
            device_id=peer, device_id_type=MESH)
        copy.start()
        copies.append(copy)
    for copy in copies:
        copy.wait()
    here = r * 4 + c
    total = jnp.zeros(value_ref.shape, jnp.float32)
    for who in range(8):
        which = here ^ who
        term = jnp.where(which == 0, value_ref[...], slots[jnp.maximum(which - 1, 0)])
        total = total + term
    out_ref[...] = total


def group_total(value, collective_id):
    return pl.pallas_call(
        total_kernel,
        out_shape=jax.ShapeDtypeStruct(value.shape, jnp.float32),
        in_specs=[pl.BlockSpec(memory_space=pltpu.VMEM)], out_specs=pl.BlockSpec(memory_space=pltpu.VMEM),
        scratch_shapes=[pltpu.VMEM((7,) + value.shape, jnp.float32), pltpu.SemaphoreType.DMA((7,)), pltpu.SemaphoreType.DMA((7,))],
        compiler_params=pltpu.CompilerParams(collective_id=collective_id, has_side_effects=True),
    )(value)


HEAD_DIM = 128
SEQ_LEN = 1024
EPSILON = 1e-05
THETA = 10000.0
MASKED = -1e30
GROUP = ("row", "col")
EVERYONE = ("dp", "row", "col")


def on_links():
    return lax.axis_size("dp") == 4 and lax.axis_size("col") == 4 and lax.axis_size("row") == 2


def gather_tokens(arrays, everyone, collective_id, parts):
    if on_links():
        return gather(arrays, 4 if everyone else 1, collective_id, parts)
    axes = EVERYONE if everyone else GROUP
    return [lax.all_gather(a, axes, axis=0, tiled=True) for a in arrays]


def scatter_sums(arrays, everyone, collective_id):
    if on_links():
        return reduce_scatter(arrays, 4 if everyone else 1, collective_id)
    axes = EVERYONE if everyone else GROUP
    return [lax.psum_scatter(a, axes, scatter_dimension=0, tiled=True).astype(jnp.float32) for a in arrays]


def to_heads(w_query, w_key, w_value, w_out):
    if on_links():
        return exchange_weights(w_query, w_key, w_value, w_out, 1)
    pieces = [lax.all_to_all(w, "col", split_axis=1, concat_axis=0, tiled=True) for w in (w_query, w_key, w_value)]
    return jnp.concatenate(pieces, axis=1), lax.all_to_all(w_out, "col", split_axis=0, concat_axis=1, tiled=True)


def sum_over_heads(first_part, second_part, collective_id):
    if on_links():
        stacked = jnp.concatenate([first_part, second_part]).reshape(-1, 128)
        total = group_total(stacked, collective_id).reshape(2, -1)
        return total[0], total[1]
    return lax.psum((first_part, second_part), GROUP)


def inverse_rms(values):
    return lax.rsqrt(jnp.mean(values * values, axis=-1, keepdims=True) + EPSILON)


def norm_backward(values, inv_scale, gain_row, upstream):
    weighted = gain_row * upstream
    inner_sum = jnp.sum(weighted * values, axis=-1, keepdims=True)
    grad_values = inv_scale * weighted - values * inv_scale**3 * inner_sum / values.shape[-1]
    return (grad_values, jnp.sum(upstream * values * inv_scale, axis=0))


def contract(left, right):
    return jnp.dot(left, right, preferred_element_type=jnp.float32)


def contract_rows(left, right):
    return lax.dot_general(
        left, right, (((0,), (0,)), ((), ())), preferred_element_type=jnp.float32
    )


def contract_cols(left, right):
    return lax.dot_general(
        left, right, (((1,), (1,)), ((), ())), preferred_element_type=jnp.float32
    )


def turn_tables(total_rows, seq_length, head_width):
    positions = (jnp.arange(total_rows) % seq_length).astype(jnp.float32)
    inverse = THETA ** (-jnp.arange(0, head_width, 2, dtype=jnp.float32) / head_width)
    angles = positions[:, None] * inverse[None, :]
    angles = jnp.concatenate([angles, angles], axis=-1)
    return (jnp.cos(angles)[:, None, :], jnp.sin(angles)[:, None, :])


def rotate(values, cosine, sine_table):
    middle = values.shape[-1] // 2
    turned = jnp.concatenate([-values[..., middle:], values[..., :middle]], axis=-1)
    return values * cosine + turned * sine_table


def unrotate(upstream, cosine, sine_table):
    middle = upstream.shape[-1] // 2
    turned_part = upstream * sine_table
    return upstream * cosine + jnp.concatenate(
        [turned_part[..., middle:], -turned_part[..., :middle]], axis=-1
    )


def attend_forward(queries, key_rows, value_rows):
    length = queries.shape[0]
    block_rows = min(512, length)
    outputs = []
    sums_log = []
    for first_row in range(0, length, block_rows):
        finish = first_row + block_rows
        scores = jnp.einsum(
            "qhd,khd->hqk",
            queries[first_row:finish],
            key_rows[:finish],
            preferred_element_type=jnp.float32,
        )
        causal = (first_row + jnp.arange(block_rows))[:, None] >= jnp.arange(finish)[None, :]
        scores = jnp.where(causal[None], scores, MASKED)
        highest = jnp.max(scores, axis=-1, keepdims=True)
        weights = jnp.exp(scores - highest)
        totals = jnp.sum(weights, axis=-1, keepdims=True)
        weights = (weights / totals).astype(jnp.bfloat16)
        outputs.append(
            jnp.einsum(
                "hqk,khd->qhd", weights, value_rows[:finish], preferred_element_type=jnp.float32
            )
        )
        sums_log.append((highest + jnp.log(totals))[..., 0])
    return (jnp.concatenate(outputs, axis=0), jnp.concatenate(sums_log, axis=1))


def attend_backward(queries, key_rows, value_rows, grad_out, sums_log):
    length = queries.shape[0]
    block_rows = min(512, length)
    grad_queries = []
    grad_keys = jnp.zeros(key_rows.shape, jnp.float32)
    grad_values = jnp.zeros(value_rows.shape, jnp.float32)
    for first_row in range(0, length, block_rows):
        finish = first_row + block_rows
        scores = jnp.einsum(
            "qhd,khd->hqk",
            queries[first_row:finish],
            key_rows[:finish],
            preferred_element_type=jnp.float32,
        )
        causal = (first_row + jnp.arange(block_rows))[:, None] >= jnp.arange(finish)[None, :]
        scores = jnp.where(causal[None], scores, MASKED)
        weights = jnp.exp(scores - sums_log[:, first_row:finish, None])
        grad_weights = jnp.einsum(
            "qhd,khd->hqk",
            grad_out[first_row:finish],
            value_rows[:finish],
            preferred_element_type=jnp.float32,
        )
        centre = jnp.sum(weights * grad_weights, axis=-1, keepdims=True)
        grad_scores = (weights * (grad_weights - centre)).astype(jnp.bfloat16)
        grad_queries.append(
            jnp.einsum(
                "hqk,khd->qhd", grad_scores, key_rows[:finish], preferred_element_type=jnp.float32
            )
        )
        grad_keys = grad_keys.at[:finish].add(
            jnp.einsum(
                "hqk,qhd->khd",
                grad_scores,
                queries[first_row:finish],
                preferred_element_type=jnp.float32,
            )
        )
        grad_values = grad_values.at[:finish].add(
            jnp.einsum(
                "hqk,qhd->khd",
                weights.astype(jnp.bfloat16),
                grad_out[first_row:finish],
                preferred_element_type=jnp.float32,
            )
        )
    return (jnp.concatenate(grad_queries, axis=0), grad_keys, grad_values)


def by_sequence(step, pieces, sequences):
    if sequences == 1:
        return tuple(out[None] for out in step(*[p[0] for p in pieces]))
    return lax.map(lambda each: step(*each), tuple(pieces))


def expert_rows(normal_h, side, cotangent, gate_use, up_use, down_use, expert_count):
    (all_cotangent,) = gather_tokens([cotangent], True, 3, 2)
    rows_h, rows_side = gather_tokens([normal_h, side], True, 6, 2)
    expert = lax.axis_index("dp") * lax.axis_size("col") + lax.axis_index("col")
    lane = jnp.arange(side.shape[1])
    own_share = jnp.sum(
        jnp.where((lane == expert) | (lane == expert + expert_count), rows_side.astype(jnp.float32), 0.0),
        axis=1,
        keepdims=True,
    )
    back_rows = contract_cols(all_cotangent, down_use)
    gate_rows = contract(rows_h, gate_use)
    up_rows = contract(rows_h, up_use)
    sigmoid_gate = jax.nn.sigmoid(gate_rows)
    silu_gate = gate_rows * sigmoid_gate
    active = silu_gate * up_rows
    route_grad = jnp.sum(active * back_rows, axis=1, keepdims=True)
    active_share = (own_share * active).astype(jnp.bfloat16)
    grad_active = own_share * back_rows
    grad_gate_rows = (
        grad_active * up_rows * sigmoid_gate * (1.0 + gate_rows * (1.0 - sigmoid_gate))
    ).astype(jnp.bfloat16)
    grad_up_rows = (grad_active * silu_gate).astype(jnp.bfloat16)
    entry_part = (contract_cols(grad_gate_rows, gate_use) + contract_cols(grad_up_rows, up_use)).astype(jnp.bfloat16)
    grad_side = jnp.where(jnp.arange(128 if expert_count <= 128 else expert_count)[None, :] == expert, route_grad, 0.0).astype(jnp.bfloat16)
    entry_rows, grad_probs_all = scatter_sums([entry_part, grad_side], True, 7)
    out_part = contract(active_share, down_use).astype(jnp.bfloat16)
    (mixture,) = scatter_sums([out_part], True, 8)
    grad_down_w = contract_rows(active_share, all_cotangent)
    grad_gate_w = contract_rows(rows_h, grad_gate_rows)
    grad_up_w = contract_rows(rows_h, grad_up_rows)
    return entry_rows, grad_probs_all, mixture, grad_gate_w, grad_up_w, grad_down_w


def per_device(
    hidden_in,
    cotangent,
    norm_attn,
    w_query,
    w_key,
    w_value,
    query_gain,
    key_gain,
    w_out,
    norm_moe,
    w_router,
    w_gate,
    w_up,
    w_down,
    routes,
):
    inputs = hidden_in.astype(jnp.float32)
    upstream = cotangent.astype(jnp.float32)
    token_count, top_count = routes.shape
    model_width = inputs.shape[1]
    expert_count = w_router.shape[1]

    inv_input = inverse_rms(inputs)
    normal_x = (inputs * inv_input * norm_attn).astype(jnp.bfloat16)
    w_proj, w_out_own = to_heads(w_query, w_key, w_value, w_out)
    (gathered_x,) = gather_tokens([normal_x], False, 2, 2)
    group_tokens = gathered_x.shape[0]
    raw = contract(gathered_x, w_proj)
    local_width = w_proj.shape[1] // 3
    query_raw = raw[:, :local_width]
    key_raw = raw[:, local_width : 2 * local_width]
    value_heads = raw[:, 2 * local_width :].astype(jnp.bfloat16)
    head_count = local_width // HEAD_DIM
    query_square, key_square = sum_over_heads(
        jnp.sum(query_raw * query_raw, axis=-1), jnp.sum(key_raw * key_raw, axis=-1), 4
    )
    inv_query = lax.rsqrt(query_square / model_width + EPSILON)[:, None]
    inv_key = lax.rsqrt(key_square / model_width + EPSILON)[:, None]
    offset = (lax.axis_index("row") * lax.axis_size("col") + lax.axis_index("col")) * local_width
    gain_query = lax.dynamic_slice_in_dim(query_gain, offset, local_width)
    gain_key = lax.dynamic_slice_in_dim(key_gain, offset, local_width)
    cosine, sine_table = turn_tables(group_tokens, SEQ_LEN, HEAD_DIM)
    head_shape = (group_tokens, head_count, HEAD_DIM)
    sequences = group_tokens // SEQ_LEN
    seq_shape = (sequences, SEQ_LEN, head_count, HEAD_DIM)
    query_heads = (
        rotate((query_raw * inv_query * gain_query).reshape(head_shape), cosine, sine_table)
        * HEAD_DIM ** (-0.5)
    ).astype(jnp.bfloat16)
    key_heads = rotate(
        (key_raw * inv_key * gain_key).reshape(head_shape), cosine, sine_table
    ).astype(jnp.bfloat16)
    query_seq = query_heads.reshape(seq_shape)
    key_seq = key_heads.reshape(seq_shape)
    value_seq = value_heads.reshape(seq_shape)
    mixed, sums_log = by_sequence(attend_forward, (query_seq, key_seq, value_seq), sequences)
    mixed_heads = mixed.reshape(group_tokens, local_width).astype(jnp.bfloat16)
    attn_part = contract(mixed_heads, w_out_own).astype(jnp.bfloat16)
    (attn_rows,) = scatter_sums([attn_part], False, 5)
    state_rows = inputs + attn_rows

    inv_state = inverse_rms(state_rows)
    normal_h = (state_rows * inv_state * norm_moe).astype(jnp.bfloat16)
    logits = contract(normal_h, w_router)
    shifted = jnp.exp(logits - jnp.max(logits, axis=-1, keepdims=True))
    probabilities = shifted / jnp.sum(shifted, axis=-1, keepdims=True)
    selected = jnp.sum(
        (routes[:, :, None] == jnp.arange(expert_count)[None, None, :]).astype(jnp.float32), axis=1
    )
    shares = probabilities * selected
    share_high = shares.astype(jnp.bfloat16)
    share_low = (shares - share_high.astype(jnp.float32)).astype(jnp.bfloat16)
    side_width = max(2 * expert_count, 128)
    side = jnp.concatenate(
        [
            share_high,
            share_low,
            jnp.zeros((token_count, side_width - 2 * expert_count), jnp.bfloat16),
        ],
        axis=1,
    )

    chunks = max(1, lax.axis_size(EVERYONE) // 32)
    if chunks == 1:
        entry_rows, grad_probs_all, mixture, *expert_grads = expert_rows(
            normal_h, side, cotangent, w_gate[0], w_up[0], w_down[0], expert_count
        )
    else:

        def piece_step(sums, piece):
            entry, probs, mixed_rows, *grads = expert_rows(*piece, w_gate[0], w_up[0], w_down[0], expert_count)
            return [s + g for s, g in zip(sums, grads)], (entry, probs, mixed_rows)

        cut = [a.reshape((chunks, token_count // chunks) + a.shape[1:]) for a in (normal_h, side, cotangent)]
        empty = [jnp.zeros(w.shape[1:], jnp.float32) for w in (w_gate, w_up, w_down)]
        expert_grads, rows = lax.scan(piece_step, empty, cut)
        entry_rows, grad_probs_all, mixture = [r.reshape((token_count,) + r.shape[2:]) for r in rows]
    grad_gate_w, grad_up_w, grad_down_w = expert_grads
    block_out = (state_rows + mixture).astype(jnp.bfloat16)

    grad_probs = selected * grad_probs_all[:, :expert_count]
    grad_logits = (
        probabilities * (grad_probs - jnp.sum(probabilities * grad_probs, axis=-1, keepdims=True))
    ).astype(jnp.bfloat16)
    grad_normal_h = entry_rows + contract_cols(grad_logits, w_router)
    grad_router_part = contract_rows(normal_h, grad_logits)
    grad_state_part, grad_moe_part = norm_backward(state_rows, inv_state, norm_moe, grad_normal_h)
    grad_state = upstream + grad_state_part
    grad_attn = grad_state.astype(jnp.bfloat16)
    (grad_gathered,) = gather_tokens([grad_attn], False, 9, 2)
    grad_out_own = contract_rows(mixed_heads, grad_gathered).astype(jnp.bfloat16)
    grad_mixed = contract_cols(grad_gathered, w_out_own).astype(jnp.bfloat16)
    grad_query_seq, grad_key_seq, grad_value_seq = by_sequence(
        attend_backward,
        (query_seq, key_seq, value_seq, grad_mixed.reshape(seq_shape), sums_log),
        sequences,
    )
    grad_normal_q = unrotate(
        grad_query_seq.reshape(head_shape) * HEAD_DIM ** (-0.5), cosine, sine_table
    ).reshape(group_tokens, local_width)
    grad_normal_k = unrotate(grad_key_seq.reshape(head_shape), cosine, sine_table).reshape(
        group_tokens, local_width
    )
    weighted_q = gain_query * grad_normal_q
    weighted_k = gain_key * grad_normal_k
    inner_q, inner_k = sum_over_heads(
        jnp.sum(weighted_q * query_raw, axis=-1), jnp.sum(weighted_k * key_raw, axis=-1), 10
    )
    grad_query_raw = (
        inv_query * weighted_q - query_raw * inv_query**3 * inner_q[:, None] / model_width
    )
    grad_key_raw = inv_key * weighted_k - key_raw * inv_key**3 * inner_k[:, None] / model_width
    grad_qgain_part = jnp.sum(grad_normal_q * query_raw * inv_query, axis=0)
    grad_kgain_part = jnp.sum(grad_normal_k * key_raw * inv_key, axis=0)
    grad_raw = jnp.concatenate(
        [grad_query_raw, grad_key_raw, grad_value_seq.reshape(group_tokens, local_width)], axis=1
    ).astype(jnp.bfloat16)
    grad_x_part = contract_cols(grad_raw, w_proj).astype(jnp.bfloat16)
    (grad_normal_x,) = scatter_sums([grad_x_part], False, 11)
    grad_proj_own = contract_rows(gathered_x, grad_raw).astype(jnp.bfloat16)
    grad_input_part, grad_attn_gain = norm_backward(inputs, inv_input, norm_attn, grad_normal_x)
    grad_input = grad_state + grad_input_part
    grad_query, grad_key, grad_value, grad_out_proj = weight_sums(grad_proj_own, grad_out_own)
    full_width = query_gain.shape[0]
    padded_qgain = lax.dynamic_update_slice_in_dim(
        jnp.zeros((full_width,), jnp.float32), grad_qgain_part, offset, 0
    )
    padded_kgain = lax.dynamic_update_slice_in_dim(
        jnp.zeros((full_width,), jnp.float32), grad_kgain_part, offset, 0
    )
    grad_norm_attn, grad_query_gain, grad_key_gain, grad_norm_moe, grad_router = lax.psum(
        (grad_attn_gain, padded_qgain, padded_kgain, grad_moe_part, grad_router_part),
        ("dp", "row", "col"),
    )
    return (
        block_out,
        grad_input,
        grad_norm_attn,
        grad_query,
        grad_key,
        grad_value,
        grad_query_gain,
        grad_key_gain,
        grad_out_proj,
        grad_norm_moe,
        grad_router,
        grad_gate_w[None],
        grad_up_w[None],
        grad_down_w[None],
    )


def weight_sums(grad_proj_own, grad_out_own):
    width = grad_proj_own.shape[1] // 3
    blocks = [
        lax.all_to_all(grad_proj_own[:, a * width : (a + 1) * width], "col", split_axis=0, concat_axis=1, tiled=True)
        for a in range(3)
    ]
    out_block = lax.all_to_all(grad_out_own, "col", split_axis=1, concat_axis=0, tiled=True)
    return [total.astype(jnp.float32) for total in lax.psum((*blocks, out_block), "dp")]


def solution(mesh):
    placed = (
        P(("dp", "row", "col"), None),
        P(("dp", "row", "col"), None),
        P(),
        P("col", "row"),
        P("col", "row"),
        P("col", "row"),
        P(),
        P(),
        P("row", "col"),
        P(),
        P(),
        P(("dp", "col"), None, "row"),
        P(("dp", "col"), None, "row"),
        P(("dp", "col"), "row", None),
        P(("dp", "row", "col"), None),
    )
    return jax.shard_map(
        per_device,
        mesh=mesh,
        in_specs=placed,
        out_specs=(
            P(("dp", "row", "col"), None),
            P(("dp", "row", "col"), None),
            P(),
            P("col", "row"),
            P("col", "row"),
            P("col", "row"),
            P(),
            P(),
            P("row", "col"),
            P(),
            P(),
            P(("dp", "col"), None, "row"),
            P(("dp", "col"), None, "row"),
            P(("dp", "col"), "row", None),
        ),
        check_vma=False,
    )
```

```python
import functools

import jax
import jax.numpy as jnp
from jax import lax
from jax.experimental import pallas as pl
from jax.experimental.pallas import tpu as pltpu
from jax.sharding import PartitionSpec as P

MESH = pl.DeviceIdType.MESH
ANYSPEC = pl.BlockSpec(memory_space=pl.ANY)

def place():
    return lax.axis_index("dp"), lax.axis_index("row"), lax.axis_index("col")

def greet(peers):
    barrier = pltpu.get_barrier_semaphore()
    for peer in peers:
        pl.semaphore_signal(barrier, inc=1, device_id=peer, device_id_type=MESH)
    pl.semaphore_wait(barrier, len(peers))

def gather_kernel(planes, parts, count, *refs):
    ins, outs = refs[:count], refs[count:2 * count]
    own_sem, send_sem, recv_sem = refs[2 * count:]
    z, r, c = place()
    first, second, diag = c ^ (1 + r), c ^ (2 - r), c ^ 3
    partner = (z, 1 - r, c)
    to_first, to_second = (z, r, first), (z, r, second)
    greet([to_first, to_second, partner] + [(z ^ k, r, c) for k in range(1, planes)])
    pieces = []
    for a in range(count):
        cut = parts if a == 0 else 1
        pieces += [(a, p, ins[a].shape[0], ins[a].shape[0] // cut) for p in range(cut)]

    def number(zz, rr, cc):
        return ((zz if planes > 1 else 0) * 2 + rr) * 4 + cc

    def place_of(i, which):
        a, p, depth, cut = pieces[i]
        return outs[a].at[pl.ds(pl.multiple_of(which * depth + p * cut, cut), cut)]

    sent = [[] for _ in pieces]

    def send(i, which, target, own=False):
        a, p, depth, cut = pieces[i]
        spot = place_of(i, which)
        copy = pltpu.make_async_remote_copy(
            src_ref=ins[a].at[pl.ds(p * cut, cut)] if own else spot, dst_ref=spot,
            send_sem=send_sem.at[i, len(sent[i])], recv_sem=recv_sem.at[i, which],
            device_id=target, device_id_type=MESH)
        copy.start()
        sent[i].append(copy)

    def await_block(i, which):
        spot = place_of(i, which)
        pltpu.make_async_remote_copy(
            src_ref=spot, dst_ref=spot, send_sem=send_sem.at[i, 0], recv_sem=recv_sem.at[i, which],
            device_id=partner, device_id_type=MESH).wait_recv()

    mine = number(z, r, c)
    keeps = []
    every = range(len(pieces))
    for i in every:
        for target in [to_first, to_second] + [(z ^ k, r, c) for k in range(1, planes)] + [partner]:
            send(i, mine, target, True)
    for a in range(count):
        keep = pltpu.make_async_copy(ins[a], outs[a].at[pl.ds(pl.multiple_of(mine * ins[a].shape[0], ins[a].shape[0]), ins[a].shape[0])], own_sem.at[a])
        keep.start()
        keeps.append(keep)

    def forward(which, targets):
        for i in every:
            await_block(i, which)
            for target in targets:
                send(i, which, target)

    for step in range(planes + 2):
        if 0 < step < planes:
            forward(number(z ^ step, r, c), [to_first, to_second, partner])
        if 0 <= step - 1 < planes:
            forward(number(z ^ (step - 1), r, first), [to_second, partner])
            forward(number(z ^ (step - 1), r, second), [partner])
        if 0 <= step - 2 < planes:
            forward(number(z ^ (step - 2), r, diag), [partner])
    for k in range(planes):
        for j in range(4):
            for i in every:
                await_block(i, number(z ^ k, 1 - r, c ^ j))
    for keep in keeps:
        keep.wait()
    for copies in sent:
        for copy in copies:
            copy.wait_send()

def gather(arrays, planes, collective_id, parts=1):
    count = len(arrays)
    blocks = planes * 8
    sends = (3 + planes - 1) + (planes - 1) * 3 + planes * 4
    pieces = count - 1 + parts
    return pl.pallas_call(
        functools.partial(gather_kernel, planes, parts, count),
        out_shape=[jax.ShapeDtypeStruct((blocks * a.shape[0],) + a.shape[1:], a.dtype) for a in arrays],
        in_specs=[ANYSPEC] * count, out_specs=[ANYSPEC] * count,
        scratch_shapes=[pltpu.SemaphoreType.DMA((count,)), pltpu.SemaphoreType.DMA((pieces, sends)), pltpu.SemaphoreType.DMA((pieces, blocks))],
        compiler_params=pltpu.CompilerParams(collective_id=collective_id, has_side_effects=True),
    )(*arrays)

def reduce_steps(planes, parts, outs, buffers, semaphores, filler):
    held, fromp, relay, near, far = buffers
    load_sem, pair_send, pair_recv, send_sem, relay_recv, near_recv, far_recv = semaphores
    z, r, c = place()
    first, second, diag = c ^ (1 + r), c ^ (2 - r), c ^ 3
    partner = (z, 1 - r, c)
    to_first, to_second = (z, r, first), (z, r, second)
    greet([to_first, to_second, partner] + [(z ^ k, r, c) for k in range(1, planes)])
    depth = outs[0].shape[0]
    every = range(len(parts))

    def rows(a, k, rr, cc):
        which = (((z ^ k) if planes > 1 else 0) * 2 + rr) * 4 + cc
        return parts[a].at[pl.ds(pl.multiple_of(which * depth, depth), depth)]

    columns, partner_columns = [c, first, second, diag], [c, second, first, diag]

    def remote(source, target, send, recv, device):
        return pltpu.make_async_remote_copy(
            src_ref=source, dst_ref=target, send_sem=send, recv_sem=recv, device_id=device, device_id_type=MESH)

    def load(a, k, j):
        return pltpu.make_async_copy(rows(a, k, r, columns[j]), held[a].at[k, j], load_sem.at[a, k, j])

    def pair(a, k, j):
        return remote(rows(a, k, 1 - r, partner_columns[j]), fromp[a].at[k, j], pair_send.at[a, k, j], pair_recv.at[a, k, j], partner)

    def begin(i, _):
        k = planes - 1 - i
        for j in (3, 2, 1, 0):
            for a in every:
                load(a, k, j).start()
                pair(a, k, j).start()
        return 0

    lax.fori_loop(0, planes, begin, 0)
    step_rows = min(32, depth)

    def add(target, sources):
        def body(i, _):
            at = pl.ds(pl.multiple_of(i * step_rows, step_rows), step_rows)
            total = sources[0][at].astype(jnp.float32)
            for source in sources[1:]:
                total = total + source[at].astype(jnp.float32)
            target[at] = total.astype(target.dtype)
            return 0
        lax.fori_loop(0, depth // step_rows, body, 0)

    def ready(a, k, j):
        load(a, k, j).wait()
        pair(a, k, j).wait_recv()

    def to_diag(a, k):
        return remote(held[a].at[k, 3], relay[a].at[k], send_sem.at[a, k, 0], relay_recv.at[a, k], to_second)

    def to_near(a, k, which):
        source, device = (held[a].at[k, 2], to_second) if which else (held[a].at[k, 1], to_first)
        return remote(source, near[a].at[k, which], send_sem.at[a, k, 1 + which], near_recv.at[a, k, which], device)

    def to_far(a, k):
        slot = jnp.maximum(k - 1, 0)
        return remote(held[a].at[k, 0], far[a].at[slot], send_sem.at[a, k, 3], far_recv.at[a, slot], (z ^ k, r, c))

    def to_relay(k):
        for a in every:
            ready(a, k, 3)
            add(held[a].at[k, 3], [held[a].at[k, 3], fromp[a].at[k, 3]])
            to_diag(a, k).start()
        for a in every:
            ready(a, k, 2)
            add(held[a].at[k, 2], [held[a].at[k, 2], fromp[a].at[k, 2]])
            to_near(a, k, 1).start()

    def pass_on(k):
        for a in every:
            ready(a, k, 1)
            to_diag(a, k).wait_recv()
            add(held[a].at[k, 1], [held[a].at[k, 1], fromp[a].at[k, 1], relay[a].at[k]])
            to_near(a, k, 0).start()

    def collect(k):
        for a in every:
            ready(a, k, 0)
            to_near(a, k, 0).wait_recv()
            to_near(a, k, 1).wait_recv()
            terms = [held[a].at[k, 0], fromp[a].at[k, 0], near[a].at[k, 0], near[a].at[k, 1]]

            @pl.when(k > 0)
            def _():
                add(held[a].at[k, 0], terms)
                to_far(a, k).start()

            @pl.when(k == 0)
            def _():
                for i in range(1, planes):
                    to_far(a, i).wait_recv()
                add(outs[a], terms + [far[a].at[i] for i in range(planes - 1)])

    def step_body(step, _):
        @pl.when(step < planes)
        def _():
            to_relay(planes - 1 - step)

        @pl.when(jnp.logical_and(step >= 1, step < planes + 1))
        def _():
            pass_on(planes - step)

        @pl.when(step >= 2)
        def _():
            collect(planes + 1 - step)
        if filler is not None:
            filler(step)
        return 0

    lax.fori_loop(0, planes + 2, step_body, 0)

    def drain(k, _):
        for a in every:
            for j in range(4):
                pair(a, k, j).wait_send()
            to_diag(a, k).wait_send()
            to_near(a, k, 0).wait_send()
            to_near(a, k, 1).wait_send()

            @pl.when(k > 0)
            def _():
                to_far(a, k).wait_send()
        return 0

    lax.fori_loop(0, planes, drain, 0)


def reduce_scratch(partials, planes):
    shapes = [((p.shape[0] // (planes * 8), p.shape[1]), p.dtype) for p in partials]
    count, far = len(partials), max(planes - 1, 1)
    dma = pltpu.SemaphoreType.DMA
    buffers = [pltpu.VMEM(lead + shape, kind) for lead in ((planes, 4), (planes, 4), (planes,), (planes, 2), (far,)) for shape, kind in shapes]
    return shapes, buffers, [
        dma((count, planes, 4)), dma((count, planes, 4)), dma((count, planes, 4)), dma((count, planes, 4)),
        dma((count, planes)), dma((count, planes, 2)), dma((count, far))]


def reduce_kernel(planes, count, *refs):
    buffers = [refs[(2 + i) * count:(3 + i) * count] for i in range(5)]
    reduce_steps(planes, refs[:count], refs[count:2 * count], buffers, refs[7 * count:], None)


def reduce_scatter(partials, planes, collective_id):
    count = len(partials)
    shapes, buffers, semaphores = reduce_scratch(partials, planes)
    return pl.pallas_call(
        functools.partial(reduce_kernel, planes, count),
        out_shape=[jax.ShapeDtypeStruct(shape, jnp.float32) for shape, _ in shapes],
        in_specs=[ANYSPEC] * count, out_specs=[pl.BlockSpec(memory_space=pltpu.VMEM)] * count,
        scratch_shapes=buffers + semaphores,
        compiler_params=pltpu.CompilerParams(collective_id=collective_id, has_side_effects=True, vmem_limit_bytes=48 * 2**20),
    )(*partials)


def exchange_kernel(wq_ref, wk_ref, wv_ref, wo_ref, proj_ref, out_ref, own_sem, send_sem, recv_sem):
    z, r, c = place()
    width = proj_ref.shape[1] // 3
    depth = wq_ref.shape[0]
    out_rows, out_width = out_ref.shape[0], wo_ref.shape[1]
    greet([(z, r, c ^ j) for j in range(1, 4)])

    def source(a, target):
        if a < 3:
            return (wq_ref, wk_ref, wv_ref)[a].at[:, pl.ds(pl.multiple_of(target * width, width), width)]
        return wo_ref.at[pl.ds(pl.multiple_of(target * out_rows, out_rows), out_rows), :]

    def spot(a, origin):
        if a < 3:
            return proj_ref.at[pl.ds(pl.multiple_of(origin * depth, depth), depth), pl.ds(a * width, width)]
        return out_ref.at[:, pl.ds(pl.multiple_of(origin * out_width, out_width), out_width)]

    waits = []
    for a in range(4):
        keep = pltpu.make_async_copy(source(a, c), spot(a, c), own_sem.at[a])
        keep.start()
        waits.append(keep.wait)
        for j in range(1, 4):
            copy = pltpu.make_async_remote_copy(
                src_ref=source(a, c ^ j), dst_ref=spot(a, c), send_sem=send_sem.at[a, j - 1],
                recv_sem=recv_sem.at[a, j - 1], device_id=(z, r, c ^ j), device_id_type=MESH)
            copy.start()
            waits.append(copy.wait_send)
    for a in range(4):
        for j in range(1, 4):
            arrived = spot(a, c ^ j)
            pltpu.make_async_remote_copy(
                src_ref=arrived, dst_ref=arrived, send_sem=send_sem.at[a, j - 1], recv_sem=recv_sem.at[a, j - 1],
                device_id=(z, r, c ^ j), device_id_type=MESH).wait_recv()
    for wait in waits:
        wait()


def exchange_weights(w_query, w_key, w_value, w_out, collective_id):
    depth, half = w_query.shape
    kind = w_query.dtype
    width, out_rows, out_width = half // 4, w_out.shape[0] // 4, w_out.shape[1] * 4
    return pl.pallas_call(
        exchange_kernel,
        out_shape=[jax.ShapeDtypeStruct((depth * 4, 3 * width), kind), jax.ShapeDtypeStruct((out_rows, out_width), kind)],
        in_specs=[ANYSPEC] * 4, out_specs=[ANYSPEC] * 2,
        scratch_shapes=[pltpu.SemaphoreType.DMA((4,)), pltpu.SemaphoreType.DMA((4, 3)), pltpu.SemaphoreType.DMA((4, 3))],
        compiler_params=pltpu.CompilerParams(collective_id=collective_id, has_side_effects=True),
    )(w_query, w_key, w_value, w_out)


def total_kernel(value_ref, out_ref, slots, send_sem, recv_sem):
    z, r, c = place()
    peers = [(z, r ^ (j >> 2), c ^ (j & 3)) for j in range(1, 8)]
    greet(peers)
    copies = []
    for j, peer in enumerate(peers):
        copy = pltpu.make_async_remote_copy(
            src_ref=value_ref, dst_ref=slots.at[j], send_sem=send_sem.at[j], recv_sem=recv_sem.at[j],
            device_id=peer, device_id_type=MESH)
        copy.start()
        copies.append(copy)
    for copy in copies:
        copy.wait()
    here = r * 4 + c
    total = jnp.zeros(value_ref.shape, jnp.float32)
    for who in range(8):
        which = here ^ who
        term = jnp.where(which == 0, value_ref[...], slots[jnp.maximum(which - 1, 0)])
        total = total + term
    out_ref[...] = total


def group_total(value, collective_id):
    return pl.pallas_call(
        total_kernel,
        out_shape=jax.ShapeDtypeStruct(value.shape, jnp.float32),
        in_specs=[pl.BlockSpec(memory_space=pltpu.VMEM)], out_specs=pl.BlockSpec(memory_space=pltpu.VMEM),
        scratch_shapes=[pltpu.VMEM((7,) + value.shape, jnp.float32), pltpu.SemaphoreType.DMA((7,)), pltpu.SemaphoreType.DMA((7,))],
        compiler_params=pltpu.CompilerParams(collective_id=collective_id, has_side_effects=True),
    )(value)


def finish_kernel(planes, proj_ref, outp_ref, small_ref, proj_out, outp_out, small_out, proj_own, outp_own, proj_in, outp_in,
                  slices, far_slices, own_sem, swap_send, swap_recv, down_send, down_recv, up_send, up_recv,
                  slice_send, slice_recv, far_send, far_recv, whole_send, whole_recv):
    z, r, c = place()
    here = r * 4 + c
    group = [(z, r ^ (j >> 2), c ^ (j & 3)) for j in range(1, 8)]
    greet(group + [(z ^ k, r, c) for k in range(1, planes)])
    width = proj_ref.shape[1] // 3
    depth, out_width = proj_ref.shape[0] // 4, outp_ref.shape[1] // 4
    out_rows, step = outp_ref.shape[0], proj_ref.shape[0] // 16
    chunks = 16

    def remote(source, target, send, recv, device):
        return pltpu.make_async_remote_copy(
            src_ref=source, dst_ref=target, send_sem=send, recv_sem=recv, device_id=device, device_id_type=MESH)

    def piece(i, target):
        if i < 12:
            a, m = i // 4, i % 4
            return proj_ref.at[pl.ds(pl.multiple_of(target * depth + m * step, step), step), pl.ds(a * width, width)]
        return outp_ref.at[:, pl.ds(pl.multiple_of(target * out_width, out_width), out_width)]

    def spot(i, origin):
        a, m = i // 4, i % 4
        return proj_own.at[a, pl.ds(m * step, step), pl.ds(pl.multiple_of(origin * width, width), width)]

    def rows(proj, outp, i):
        if i < 12:
            return proj.at[i // 4, pl.ds((i % 4) * step, step), :]
        return outp.at[pl.ds((i - 12) * out_rows, out_rows), :]

    small_copies = []
    for j in range(1, 8):
        copy = remote(small_ref.at[here ^ j], slices.at[here], slice_send.at[j], slice_recv.at[here], group[j - 1])
        copy.start()
        small_copies.append(copy)

    order = [0, 1, 2, 3, 12, 13, 4, 5, 6, 7, 14, 15, 8, 9, 10, 11]
    swaps = []
    for i in order:
        if i < 12:
            keep = pltpu.make_async_copy(piece(i, c), spot(i, c), own_sem.at[i])
            keep.start()
            for j in range(1, 4):
                copy = remote(piece(i, c ^ j), spot(i, c), swap_send.at[i, j - 1], swap_recv.at[i, j - 1], (z, r, c ^ j))
                copy.start()
                swaps.append(copy)
        else:
            @pl.when(c == i - 12)
            def _():
                pltpu.make_async_copy(piece(i, c), rows(proj_own, outp_own, i), own_sem.at[i]).start()
                for j in range(1, 4):
                    remote(piece(i, c ^ j), rows(proj_own, outp_own, i), swap_send.at[i, j - 1], swap_recv.at[i, 0], (z, r, c ^ j)).start()

    def local_ready(i):
        target = rows(proj_own, outp_own, i)
        if i < 12:
            pltpu.make_async_copy(piece(i, c), spot(i, c), own_sem.at[i]).wait()
            for j in range(1, 4):
                arrived = spot(i, c ^ j)
                remote(arrived, arrived, swap_send.at[i, j - 1], swap_recv.at[i, j - 1], (z, r, c ^ j)).wait_recv()
        else:
            @pl.when(c == i - 12)
            def _():
                pltpu.make_async_copy(piece(i, c), target, own_sem.at[i]).wait()

            @pl.when(c != i - 12)
            def _():
                remote(target, target, swap_send.at[i, 0], swap_recv.at[i, 0], (z, r, c ^ 1)).wait_recv()

    def combine(target, first, second, count):
        def body(s, _):
            at = pl.ds(pl.multiple_of(s * 32, 32), 32)
            total = first[at].astype(jnp.float32) + second[at].astype(jnp.float32)
            target[at] = total.astype(target.dtype)
            return 0
        lax.fori_loop(0, count // 32, body, 0)

    def seat(i):
        root_low = i % 2 == 0
        spot_from_root = z if root_low else planes - 1 - z
        up = (jnp.minimum(z + 1, planes - 1) if root_low else jnp.maximum(z - 1, 0), r, c)
        down = (jnp.maximum(z - 1, 0) if root_low else jnp.minimum(z + 1, planes - 1), r, c)
        return spot_from_root, up, down

    def count_of(i):
        return step if i < 12 else out_rows

    def to_root(i, p):
        _, up, down = seat(i)
        own, arriving, result = rows(proj_own, outp_own, i), rows(proj_in, outp_in, i), rows(proj_out, outp_out, i)
        local_ready(i)
        if p < planes - 1:
            remote(arriving, arriving, down_send.at[i], down_recv.at[i], up).wait_recv()
        if p == 0:
            combine(result, own, arriving, count_of(i))
            remote(result, result, up_send.at[i], up_recv.at[i], up).start()
        else:
            if p < planes - 1:
                combine(own, own, arriving, count_of(i))
            remote(own, arriving, down_send.at[i], down_recv.at[i], down).start()

    def from_root(i, p):
        _, up, down = seat(i)
        result = rows(proj_out, outp_out, i)
        remote(result, result, up_send.at[i], up_recv.at[i], down).wait_recv()
        if p < planes - 1:
            remote(result, result, up_send.at[i], up_recv.at[i], up).start()

    def small_group():
        for j in range(1, 8):
            arrived = slices.at[here ^ j]
            remote(arrived, arrived, slice_send.at[0], slice_recv.at[here ^ j], group[j - 1]).wait_recv()
        slices[here] = small_ref[here]
        total = slices[0]
        for j in range(1, 8):
            total = total + slices[j]
        far_slices[z] = total
        for k in range(1, planes):
            copy = remote(far_slices.at[z], far_slices.at[z], far_send.at[k - 1], far_recv.at[z], (z ^ k, r, c))
            copy.start()
            small_copies.append(copy)

    def small_far():
        for k in range(1, planes):
            arrived = far_slices.at[z ^ k]
            remote(arrived, arrived, far_send.at[k - 1], far_recv.at[z ^ k], (z ^ k, r, c)).wait_recv()
        total = far_slices[0]
        for k in range(1, planes):
            total = total + far_slices[k]
        small_out[here] = total
        for j in range(1, 8):
            copy = remote(small_out.at[here], small_out.at[here], whole_send.at[j], whole_recv.at[here], group[j - 1])
            copy.start()
            small_copies.append(copy)

    lag = 2
    hops = 2 * planes - 1
    for s in range(chunks + (hops - 1) * lag):
        for h in range(hops):
            if 0 <= s - h * lag < chunks:
                i = order[s - h * lag]
                p = planes - 1 - h if h < planes else h - planes + 1

                @pl.when(seat(i)[0] == p)
                def _(i=i, p=p, h=h):
                    if h < planes:
                        to_root(i, p)
                    else:
                        from_root(i, p)
        if s == 2:
            small_group()
        if s == 12:
            small_far()
    for j in range(1, 8):
        arrived = small_out.at[here ^ j]
        remote(arrived, arrived, whole_send.at[0], whole_recv.at[here ^ j], group[j - 1]).wait_recv()
    for copy in small_copies + swaps:
        copy.wait_send()
    for i in range(12, 16):
        @pl.when(c == i - 12)
        def _():
            for j in range(1, 4):
                remote(piece(i, c ^ j), rows(proj_own, outp_own, i), swap_send.at[i, j - 1], swap_recv.at[i, 0], (z, r, c ^ j)).wait_send()
    for i in range(chunks):
        p, up, down = seat(i)
        own, arriving, result = rows(proj_own, outp_own, i), rows(proj_in, outp_in, i), rows(proj_out, outp_out, i)

        @pl.when(p > 0)
        def _():
            remote(own, arriving, down_send.at[i], down_recv.at[i], down).wait_send()

        @pl.when(p < planes - 1)
        def _():
            remote(result, result, up_send.at[i], up_recv.at[i], up).wait_send()


def finish(grad_proj_own, grad_out_own, small, planes, collective_id):
    depth, width = grad_proj_own.shape[0] // 4, grad_proj_own.shape[1] // 3
    out_rows, out_width = grad_out_own.shape[0], grad_out_own.shape[1] // 4
    kind = grad_proj_own.dtype
    proj, outp = (3, depth, 4 * width), (4 * out_rows, out_width)
    vmem = pl.BlockSpec(memory_space=pltpu.VMEM)
    dma = pltpu.SemaphoreType.DMA
    return pl.pallas_call(
        functools.partial(finish_kernel, planes),
        out_shape=[jax.ShapeDtypeStruct(proj, kind), jax.ShapeDtypeStruct(outp, kind), jax.ShapeDtypeStruct(small.shape, small.dtype)],
        in_specs=[ANYSPEC, ANYSPEC, vmem], out_specs=[vmem, vmem, vmem],
        scratch_shapes=[
            pltpu.VMEM(proj, kind), pltpu.VMEM(outp, kind), pltpu.VMEM(proj, kind), pltpu.VMEM(outp, kind),
            pltpu.VMEM(small.shape, jnp.float32), pltpu.VMEM((planes,) + small.shape[1:], jnp.float32),
            dma((16,)), dma((16, 3)), dma((16, 3)), dma((16,)), dma((16,)), dma((16,)), dma((16,)),
            dma((8,)), dma((8,)), dma((planes,)), dma((planes,)), dma((8,)), dma((8,))],
        compiler_params=pltpu.CompilerParams(collective_id=collective_id, has_side_effects=True, vmem_limit_bytes=40 * 2**20),
    )(grad_proj_own, grad_out_own, small)


def expert_kernel(planes, experts, own_h, own_side, cot, w_gate, w_up, w_down,
                  all_h, all_side, entry_out, route_out, active_out, grad_gate_out, grad_up_out,
                  gate_use, up_use, down_use, rows_h, rows_c, rows_side, back_rows,
                  gate_rows, up_rows, active_rows, grad_gate, grad_up, entry_stage, route_stage,
                  weight_sem, own_sem, send_sem, recv_sem, cot_sem, load_sem, store_sem):
    z, r, c = place()
    first, second, diag = c ^ (1 + r), c ^ (2 - r), c ^ 3
    partner = (z, 1 - r, c)
    to_first, to_second = (z, r, first), (z, r, second)
    count = own_h.shape[0]
    group = 4 * count
    expert = z * 4 + c
    half = count // 2
    pieces = [(own_h, all_h, 0, half), (own_h, all_h, half, half), (own_side, all_side, 0, count)]

    weights = [(w_gate, gate_use), (w_up, up_use), (w_down, down_use)]
    for i, (source, target) in enumerate(weights):
        pltpu.make_async_copy(source, target, weight_sem.at[i]).start()

    def number(zz, rr, cc):
        return (zz * 2 + rr) * 4 + cc

    def spot(i, which):
        _, target, start, size = pieces[i]
        return target.at[pl.ds(pl.multiple_of(which * count + start, size), size)]

    def copy_of(i, source, which, k, slot, device):
        return pltpu.make_async_remote_copy(
            src_ref=source, dst_ref=spot(i, which), send_sem=send_sem.at[i, k, slot], recv_sem=recv_sem.at[i, which],
            device_id=device, device_id_type=MESH)

    def own_piece(i):
        source, _, start, size = pieces[i]
        return source.at[pl.ds(start, size)]

    def await_block(i, which):
        copy_of(i, spot(i, which), which, 0, 0, partner).wait_recv()

    def forward(which, k, targets):
        for i in range(3):
            await_block(i, which)
            for slot, device in targets:
                copy_of(i, spot(i, which), which, k, slot, device).start()

    greet([to_first, to_second, partner] + [(z ^ k, r, c) for k in range(1, planes)])
    mine = number(z, r, c)
    for i in range(3):
        for slot, device in ((0, to_first), (1, to_second)):
            copy_of(i, own_piece(i), mine, 0, slot, device).start()
        for k in range(1, planes):
            copy_of(i, own_piece(i), mine, k, 7, (z ^ k, r, c)).start()
        copy_of(i, own_piece(i), mine, 0, 2, partner).start()
    keeps = [pltpu.make_async_copy(own_piece(i), spot(i, mine), own_sem.at[i]) for i in range(3)]
    for keep in keeps:
        keep.start()

    def base_of(k, rr):
        return pl.multiple_of(number(z ^ k, rr, 0) * count, group)

    def dot(left, right):
        return jnp.dot(left, right, preferred_element_type=jnp.float32)

    def dot_turned(left, right):
        return lax.dot_general(left, right, (((1,), (1,)), ((), ())), preferred_element_type=jnp.float32)

    def cot_copy(g):
        rr = jnp.where(g % 2 == 0, r, 1 - r)
        return pltpu.make_async_copy(cot.at[pl.ds(base_of(g // 2, rr), group)], rows_c.at[g % 2], cot_sem.at[g % 2])

    cot_copy(0).start()
    for i, (source, target) in enumerate(weights):
        pltpu.make_async_copy(source, target, weight_sem.at[i]).wait()

    def back_body(g, _):
        @pl.when(g + 1 < 2 * planes)
        def _():
            cot_copy(g + 1).start()

        cot_copy(g).wait()
        back_rows[g] = dot_turned(rows_c[g % 2], down_use[...])
        return 0

    lax.fori_loop(0, 2 * planes, back_body, 0)
    for keep in keeps:
        keep.wait()

    def stores(k, rr, slot):
        at = pl.ds(base_of(k, rr), group)
        return [
            pltpu.make_async_copy(source.at[slot], target.at[at], store_sem.at[slot, i])
            for i, (source, target) in enumerate((
                (entry_stage, entry_out), (route_stage, route_out), (active_rows, active_out),
                (grad_gate, grad_gate_out), (grad_up, grad_up_out)))]

    def compute(k, rr, slot):
        at = pl.ds(base_of(k, rr), group)
        loads = [pltpu.make_async_copy(all_h.at[at], rows_h, load_sem.at[0]),
                 pltpu.make_async_copy(all_side.at[at], rows_side, load_sem.at[1])]
        for load in loads:
            load.start()
        for load in loads:
            load.wait()
        gate_rows[...] = dot(rows_h[...], gate_use[...])
        up_rows[...] = dot(rows_h[...], up_use[...])

        @pl.when(k > 0)
        def _():
            for store in stores(k, rr, slot):
                store.wait()

        part = 64
        lane = lax.broadcasted_iota(jnp.int32, (part, rows_side.shape[1]), 1)

        @pl.loop(0, group // part)
        def _(t):
            at = pl.ds(pl.multiple_of(t * part, part), part)
            mask = (lane == expert) | (lane == expert + experts)
            share = jnp.sum(jnp.where(mask, rows_side[at, :].astype(jnp.float32), 0.0), axis=1, keepdims=True)
            gate, up, back = gate_rows[at, :], up_rows[at, :], back_rows[2 * k + slot, at, :]
            squash = jax.nn.sigmoid(gate)
            silu = gate * squash
            active = silu * up
            route = jnp.sum(active * back, axis=1, keepdims=True)
            route_stage[slot, at, :] = jnp.where(lane == expert, route, 0.0).astype(jnp.bfloat16)
            active_rows[slot, at, :] = (share * active).astype(jnp.bfloat16)
            grad_active = share * back
            grad_gate[slot, at, :] = (grad_active * up * squash * (1.0 + gate * (1.0 - squash))).astype(jnp.bfloat16)
            grad_up[slot, at, :] = (grad_active * silu).astype(jnp.bfloat16)

        entry = dot_turned(grad_gate[slot], gate_use[...]) + dot_turned(grad_up[slot], up_use[...])
        entry_stage[slot] = entry.astype(jnp.bfloat16)
        for store in stores(k, rr, slot):
            store.start()

    def step_body(step, _):
        @pl.when(jnp.logical_and(step > 0, step < planes))
        def _():
            forward(number(z ^ step, r, c), step, ((0, to_first), (1, to_second), (2, partner)))

        @pl.when(jnp.logical_and(step >= 1, step < planes + 1))
        def _():
            k = step - 1
            forward(number(z ^ k, r, first), k, ((3, to_second), (4, partner)))
            forward(number(z ^ k, r, second), k, ((5, partner),))

        @pl.when(jnp.logical_and(step >= 2, step < planes + 2))
        def _():
            k = step - 2
            forward(number(z ^ k, r, diag), k, ((6, partner),))
            compute(k, r, 0)

        @pl.when(jnp.logical_and(step >= 3, step < planes + 3))
        def _():
            k = step - 3
            for j in range(4):
                for i in range(3):
                    await_block(i, number(z ^ k, 1 - r, c ^ j))
            compute(k, 1 - r, 1)
        return 0

    lax.fori_loop(0, planes + 3, step_body, 0)
    for slot, rr in ((0, r), (1, 1 - r)):
        for store in stores(planes - 1, rr, slot):
            store.wait()

    def drain(k, _):
        for i in range(3):
            for slot in range(7):
                copy_of(i, spot(i, mine), mine, k, slot, partner).wait_send()

            @pl.when(k > 0)
            def _():
                copy_of(i, spot(i, mine), mine, k, 7, partner).wait_send()
        return 0

    lax.fori_loop(0, planes, drain, 0)


def expert_rows_on_links(normal_h, side, all_cotangent, w_gate, w_up, w_down, experts, collective_id):
    planes = lax.axis_size("dp")
    count, width = normal_h.shape
    hidden = w_gate.shape[1]
    total, group, low, wide = planes * 8 * count, 4 * count, jnp.bfloat16, jnp.float32
    sides = side.shape[1]
    vmem, dma = pltpu.VMEM, pltpu.SemaphoreType.DMA
    outs = [jax.ShapeDtypeStruct((total, n), low) for n in (width, sides, width, sides, hidden, hidden, hidden)]
    return pl.pallas_call(
        functools.partial(expert_kernel, planes, experts),
        out_shape=outs, in_specs=[ANYSPEC] * 6, out_specs=[ANYSPEC] * 7,
        scratch_shapes=[
            vmem((width, hidden), low), vmem((width, hidden), low), vmem((hidden, width), low),
            vmem((group, width), low), vmem((2, group, width), low), vmem((group, sides), low), vmem((2 * planes, group, hidden), wide),
            vmem((group, hidden), wide), vmem((group, hidden), wide),
            vmem((2, group, hidden), low), vmem((2, group, hidden), low), vmem((2, group, hidden), low),
            vmem((2, group, width), low), vmem((2, group, sides), low),
            dma((3,)), dma((3,)), dma((3, planes, 8)), dma((3, planes * 8)), dma((2,)), dma((2,)), dma((2, 5))],
        compiler_params=pltpu.CompilerParams(collective_id=collective_id, has_side_effects=True, vmem_limit_bytes=60 * 2**20),
    )(normal_h, side, all_cotangent, w_gate, w_up, w_down)


def entry_kernel(planes, entry_part, route_part, all_h, cot, active, grad_gate, grad_up, w_down,
                 entry_out, route_out, mixed_out, acc_gate, acc_up, acc_down, *scratch):
    buffers = [scratch[2 * i:2 * i + 2] for i in range(5)]
    semaphores = scratch[10:17]
    down_use, rows_h, rows_c, rows_x, mixed_stage, down_sem, load_sem, store_sem = scratch[17:]
    group = rows_h.shape[1]
    groups = all_h.shape[0] // group

    def loads(g):
        slot = g % 2
        at = pl.ds(pl.multiple_of(g * group, group), group)
        pairs = [(all_h, rows_h.at[slot]), (cot, rows_c.at[slot])] + [
            (source, rows_x.at[slot, i]) for i, source in enumerate((active, grad_gate, grad_up))]
        return [pltpu.make_async_copy(source.at[at], target, load_sem.at[slot, i]) for i, (source, target) in enumerate(pairs)]

    def store(g):
        at = pl.ds(pl.multiple_of(g * group, group), group)
        return pltpu.make_async_copy(mixed_stage, mixed_out.at[at], store_sem.at[0])

    def turned(left, right):
        return lax.dot_general(left, right, (((0,), (0,)), ((), ())), preferred_element_type=jnp.float32)

    down = pltpu.make_async_copy(w_down, down_use, down_sem.at[0])
    down.start()
    for load in loads(0):
        load.start()
    for acc in (acc_gate, acc_up, acc_down):
        @pl.loop(0, acc.shape[0] // 32)
        def _(t, acc=acc):
            acc[pl.ds(pl.multiple_of(t * 32, 32), 32), :] = jnp.zeros((32, acc.shape[1]), jnp.float32)
    down.wait()

    def one(g):
        @pl.when(g + 1 < groups)
        def _():
            for load in loads(g + 1):
                load.start()

        for load in loads(g):
            load.wait()
        slot = g % 2
        acc_gate[...] += turned(rows_h[slot], rows_x[slot, 1])
        acc_up[...] += turned(rows_h[slot], rows_x[slot, 2])
        acc_down[...] += turned(rows_x[slot, 0], rows_c[slot])

        @pl.when(g > 0)
        def _():
            store(g - 1).wait()

        mixed_stage[...] = jnp.dot(rows_x[slot, 0], down_use[...], preferred_element_type=jnp.float32).astype(jnp.bfloat16)
        store(g).start()

    steps = planes + 2
    per_step = -(-groups // (steps - 2))

    def filler(step):
        def body(i, _):
            @pl.when(step * per_step + i < groups)
            def _():
                one(step * per_step + i)
            return 0
        lax.fori_loop(0, per_step, body, 0)

    reduce_steps(planes, (entry_part, route_part), (entry_out, route_out), buffers, semaphores, filler)
    store(groups - 1).wait()


def entry_sums(entry_part, route_part, all_h, cot, active, grad_gate, grad_up, w_down, collective_id):
    planes = lax.axis_size("dp")
    partials = [entry_part, route_part]
    shapes, buffers, semaphores = reduce_scratch(partials, planes)
    (count, width), hidden, group = shapes[0][0], w_down.shape[0], 256
    low, wide, vmem, dma = jnp.bfloat16, jnp.float32, pltpu.VMEM, pltpu.SemaphoreType.DMA
    kept = pl.BlockSpec(memory_space=pltpu.VMEM)
    return pl.pallas_call(
        functools.partial(entry_kernel, planes),
        out_shape=[jax.ShapeDtypeStruct(shape, wide) for shape, _ in shapes] + [
            jax.ShapeDtypeStruct(entry_part.shape, low), jax.ShapeDtypeStruct((width, hidden), wide),
            jax.ShapeDtypeStruct((width, hidden), wide), jax.ShapeDtypeStruct((hidden, width), wide)],
        in_specs=[ANYSPEC] * 8, out_specs=[kept, kept, ANYSPEC, kept, kept, kept],
        scratch_shapes=buffers + semaphores + [
            vmem((hidden, width), low), vmem((2, group, width), low), vmem((2, group, width), low), vmem((2, 3, group, hidden), low),
            vmem((group, width), low), dma((1,)), dma((2, 5)), dma((1,))],
        compiler_params=pltpu.CompilerParams(collective_id=collective_id, has_side_effects=True, vmem_limit_bytes=60 * 2**20),
    )(entry_part, route_part, all_h, cot, active, grad_gate, grad_up, w_down)


HEAD_DIM = 128
SEQ_LEN = 1024
EPSILON = 1e-05
THETA = 10000.0
MASKED = -1e30
GROUP = ("row", "col")
EVERYONE = ("dp", "row", "col")


def on_links():
    return lax.axis_size("dp") == 4 and lax.axis_size("col") == 4 and lax.axis_size("row") == 2


def gather_tokens(arrays, everyone, collective_id, parts):
    if on_links():
        return gather(arrays, 4 if everyone else 1, collective_id, parts)
    axes = EVERYONE if everyone else GROUP
    return [lax.all_gather(a, axes, axis=0, tiled=True) for a in arrays]


def scatter_sums(arrays, everyone, collective_id):
    if on_links():
        return reduce_scatter(arrays, 4 if everyone else 1, collective_id)
    axes = EVERYONE if everyone else GROUP
    return [lax.psum_scatter(a, axes, scatter_dimension=0, tiled=True).astype(jnp.float32) for a in arrays]


def to_heads(w_query, w_key, w_value, w_out):
    if on_links():
        return exchange_weights(w_query, w_key, w_value, w_out, 1)
    pieces = [lax.all_to_all(w, "col", split_axis=1, concat_axis=0, tiled=True) for w in (w_query, w_key, w_value)]
    return jnp.concatenate(pieces, axis=1), lax.all_to_all(w_out, "col", split_axis=0, concat_axis=1, tiled=True)


def sum_over_heads(first_part, second_part, collective_id):
    if on_links():
        stacked = jnp.concatenate([first_part, second_part]).reshape(-1, 128)
        total = group_total(stacked, collective_id).reshape(2, -1)
        return total[0], total[1]
    return lax.psum((first_part, second_part), GROUP)


def inverse_rms(values):
    return lax.rsqrt(jnp.mean(values * values, axis=-1, keepdims=True) + EPSILON)


def norm_backward(values, inv_scale, gain_row, upstream):
    weighted = gain_row * upstream
    inner_sum = jnp.sum(weighted * values, axis=-1, keepdims=True)
    grad_values = inv_scale * weighted - values * inv_scale**3 * inner_sum / values.shape[-1]
    return (grad_values, jnp.sum(upstream * values * inv_scale, axis=0))


def contract(left, right):
    return jnp.dot(left, right, preferred_element_type=jnp.float32)


def contract_rows(left, right):
    return lax.dot_general(
        left, right, (((0,), (0,)), ((), ())), preferred_element_type=jnp.float32
    )


def contract_cols(left, right):
    return lax.dot_general(
        left, right, (((1,), (1,)), ((), ())), preferred_element_type=jnp.float32
    )


def turn_tables(total_rows, seq_length, head_width):
    positions = (jnp.arange(total_rows) % seq_length).astype(jnp.float32)
    inverse = THETA ** (-jnp.arange(0, head_width, 2, dtype=jnp.float32) / head_width)
    angles = positions[:, None] * inverse[None, :]
    angles = jnp.concatenate([angles, angles], axis=-1)
    return (jnp.cos(angles)[:, None, :], jnp.sin(angles)[:, None, :])


def rotate(values, cosine, sine_table):
    middle = values.shape[-1] // 2
    turned = jnp.concatenate([-values[..., middle:], values[..., :middle]], axis=-1)
    return values * cosine + turned * sine_table


def unrotate(upstream, cosine, sine_table):
    middle = upstream.shape[-1] // 2
    turned_part = upstream * sine_table
    return upstream * cosine + jnp.concatenate(
        [turned_part[..., middle:], -turned_part[..., :middle]], axis=-1
    )


def attend_forward(queries, key_rows, value_rows):
    length = queries.shape[0]
    block_rows = min(512, length)
    outputs = []
    sums_log = []
    for first_row in range(0, length, block_rows):
        finish = first_row + block_rows
        scores = jnp.einsum(
            "qhd,khd->hqk",
            queries[first_row:finish],
            key_rows[:finish],
            preferred_element_type=jnp.float32,
        )
        causal = (first_row + jnp.arange(block_rows))[:, None] >= jnp.arange(finish)[None, :]
        scores = jnp.where(causal[None], scores, MASKED)
        highest = jnp.max(scores, axis=-1, keepdims=True)
        weights = jnp.exp(scores - highest)
        totals = jnp.sum(weights, axis=-1, keepdims=True)
        weights = (weights / totals).astype(jnp.bfloat16)
        outputs.append(
            jnp.einsum(
                "hqk,khd->qhd", weights, value_rows[:finish], preferred_element_type=jnp.float32
            )
        )
        sums_log.append((highest + jnp.log(totals))[..., 0])
    return (jnp.concatenate(outputs, axis=0), jnp.concatenate(sums_log, axis=1))


def attend_backward(queries, key_rows, value_rows, grad_out, sums_log):
    length = queries.shape[0]
    block_rows = min(512, length)
    grad_queries = []
    grad_keys = jnp.zeros(key_rows.shape, jnp.float32)
    grad_values = jnp.zeros(value_rows.shape, jnp.float32)
    for first_row in range(0, length, block_rows):
        finish = first_row + block_rows
        scores = jnp.einsum(
            "qhd,khd->hqk",
            queries[first_row:finish],
            key_rows[:finish],
            preferred_element_type=jnp.float32,
        )
        causal = (first_row + jnp.arange(block_rows))[:, None] >= jnp.arange(finish)[None, :]
        scores = jnp.where(causal[None], scores, MASKED)
        weights = jnp.exp(scores - sums_log[:, first_row:finish, None])
        grad_weights = jnp.einsum(
            "qhd,khd->hqk",
            grad_out[first_row:finish],
            value_rows[:finish],
            preferred_element_type=jnp.float32,
        )
        centre = jnp.sum(weights * grad_weights, axis=-1, keepdims=True)
        grad_scores = (weights * (grad_weights - centre)).astype(jnp.bfloat16)
        grad_queries.append(
            jnp.einsum(
                "hqk,khd->qhd", grad_scores, key_rows[:finish], preferred_element_type=jnp.float32
            )
        )
        grad_keys = grad_keys.at[:finish].add(
            jnp.einsum(
                "hqk,qhd->khd",
                grad_scores,
                queries[first_row:finish],
                preferred_element_type=jnp.float32,
            )
        )
        grad_values = grad_values.at[:finish].add(
            jnp.einsum(
                "hqk,qhd->khd",
                weights.astype(jnp.bfloat16),
                grad_out[first_row:finish],
                preferred_element_type=jnp.float32,
            )
        )
    return (jnp.concatenate(grad_queries, axis=0), grad_keys, grad_values)


def by_sequence(step, pieces, sequences):
    if sequences == 1:
        return tuple(out[None] for out in step(*[p[0] for p in pieces]))
    return lax.map(lambda each: step(*each), tuple(pieces))


def expert_rows(normal_h, side, cotangent, gate_use, up_use, down_use, expert_count):
    all_cotangent = lax.all_gather(cotangent, EVERYONE, axis=0, tiled=True)
    if on_links():
        rows_h, _, entry_part, grad_side, active_share, grad_gate_rows, grad_up_rows = expert_rows_on_links(
            normal_h, side, all_cotangent, gate_use, up_use, down_use, expert_count, 6
        )
        entry_rows, grad_probs_all, out_part, *grads = entry_sums(
            entry_part, grad_side, rows_h, all_cotangent, active_share, grad_gate_rows, grad_up_rows, down_use, 7
        )
        (mixture,) = scatter_sums([out_part], True, 8)
        return (entry_rows, grad_probs_all, mixture, *grads)
    rows_h, rows_side = gather_tokens([normal_h, side], True, 6, 2)
    expert = lax.axis_index("dp") * lax.axis_size("col") + lax.axis_index("col")
    lane = jnp.arange(side.shape[1])
    own_share = jnp.sum(
        jnp.where((lane == expert) | (lane == expert + expert_count), rows_side.astype(jnp.float32), 0.0),
        axis=1,
        keepdims=True,
    )
    back_rows = contract_cols(all_cotangent, down_use)
    gate_rows = contract(rows_h, gate_use)
    up_rows = contract(rows_h, up_use)
    sigmoid_gate = jax.nn.sigmoid(gate_rows)
    silu_gate = gate_rows * sigmoid_gate
    active = silu_gate * up_rows
    route_grad = jnp.sum(active * back_rows, axis=1, keepdims=True)
    active_share = (own_share * active).astype(jnp.bfloat16)
    grad_active = own_share * back_rows
    grad_gate_rows = (
        grad_active * up_rows * sigmoid_gate * (1.0 + gate_rows * (1.0 - sigmoid_gate))
    ).astype(jnp.bfloat16)
    grad_up_rows = (grad_active * silu_gate).astype(jnp.bfloat16)
    entry_part = (contract_cols(grad_gate_rows, gate_use) + contract_cols(grad_up_rows, up_use)).astype(jnp.bfloat16)
    grad_side = jnp.where(jnp.arange(128 if expert_count <= 128 else expert_count)[None, :] == expert, route_grad, 0.0).astype(jnp.bfloat16)
    entry_rows, grad_probs_all = scatter_sums([entry_part, grad_side], True, 7)
    out_part = contract(active_share, down_use).astype(jnp.bfloat16)
    (mixture,) = scatter_sums([out_part], True, 8)
    grad_down_w = contract_rows(active_share, all_cotangent)
    grad_gate_w = contract_rows(rows_h, grad_gate_rows)
    grad_up_w = contract_rows(rows_h, grad_up_rows)
    return entry_rows, grad_probs_all, mixture, grad_gate_w, grad_up_w, grad_down_w


def per_device(
    hidden_in,
    cotangent,
    norm_attn,
    w_query,
    w_key,
    w_value,
    query_gain,
    key_gain,
    w_out,
    norm_moe,
    w_router,
    w_gate,
    w_up,
    w_down,
    routes,
):
    inputs = hidden_in.astype(jnp.float32)
    upstream = cotangent.astype(jnp.float32)
    token_count, top_count = routes.shape
    model_width = inputs.shape[1]
    expert_count = w_router.shape[1]

    inv_input = inverse_rms(inputs)
    normal_x = (inputs * inv_input * norm_attn).astype(jnp.bfloat16)
    w_proj, w_out_own = to_heads(w_query, w_key, w_value, w_out)
    (gathered_x,) = gather_tokens([normal_x], False, 2, 2)
    group_tokens = gathered_x.shape[0]
    raw = contract(gathered_x, w_proj)
    local_width = w_proj.shape[1] // 3
    query_raw = raw[:, :local_width]
    key_raw = raw[:, local_width : 2 * local_width]
    value_heads = raw[:, 2 * local_width :].astype(jnp.bfloat16)
    head_count = local_width // HEAD_DIM
    query_square, key_square = sum_over_heads(
        jnp.sum(query_raw * query_raw, axis=-1), jnp.sum(key_raw * key_raw, axis=-1), 4
    )
    inv_query = lax.rsqrt(query_square / model_width + EPSILON)[:, None]
    inv_key = lax.rsqrt(key_square / model_width + EPSILON)[:, None]
    offset = (lax.axis_index("row") * lax.axis_size("col") + lax.axis_index("col")) * local_width
    gain_query = lax.dynamic_slice_in_dim(query_gain, offset, local_width)
    gain_key = lax.dynamic_slice_in_dim(key_gain, offset, local_width)
    cosine, sine_table = turn_tables(group_tokens, SEQ_LEN, HEAD_DIM)
    head_shape = (group_tokens, head_count, HEAD_DIM)
    sequences = group_tokens // SEQ_LEN
    seq_shape = (sequences, SEQ_LEN, head_count, HEAD_DIM)
    query_heads = (
        rotate((query_raw * inv_query * gain_query).reshape(head_shape), cosine, sine_table)
        * HEAD_DIM ** (-0.5)
    ).astype(jnp.bfloat16)
    key_heads = rotate(
        (key_raw * inv_key * gain_key).reshape(head_shape), cosine, sine_table
    ).astype(jnp.bfloat16)
    query_seq = query_heads.reshape(seq_shape)
    key_seq = key_heads.reshape(seq_shape)
    value_seq = value_heads.reshape(seq_shape)
    mixed, sums_log = by_sequence(attend_forward, (query_seq, key_seq, value_seq), sequences)
    mixed_heads = mixed.reshape(group_tokens, local_width).astype(jnp.bfloat16)
    attn_part = contract(mixed_heads, w_out_own).astype(jnp.bfloat16)
    (attn_rows,) = scatter_sums([attn_part], False, 5)
    state_rows = inputs + attn_rows

    inv_state = inverse_rms(state_rows)
    normal_h = (state_rows * inv_state * norm_moe).astype(jnp.bfloat16)
    logits = contract(normal_h, w_router)
    shifted = jnp.exp(logits - jnp.max(logits, axis=-1, keepdims=True))
    probabilities = shifted / jnp.sum(shifted, axis=-1, keepdims=True)
    selected = jnp.sum(
        (routes[:, :, None] == jnp.arange(expert_count)[None, None, :]).astype(jnp.float32), axis=1
    )
    shares = probabilities * selected
    share_high = shares.astype(jnp.bfloat16)
    share_low = (shares - share_high.astype(jnp.float32)).astype(jnp.bfloat16)
    side_width = max(2 * expert_count, 128)
    side = jnp.concatenate(
        [
            share_high,
            share_low,
            jnp.zeros((token_count, side_width - 2 * expert_count), jnp.bfloat16),
        ],
        axis=1,
    )

    chunks = max(1, lax.axis_size(EVERYONE) // 32)
    if chunks == 1:
        entry_rows, grad_probs_all, mixture, *expert_grads = expert_rows(
            normal_h, side, cotangent, w_gate[0], w_up[0], w_down[0], expert_count
        )
    else:

        def piece_step(sums, piece):
            entry, probs, mixed_rows, *grads = expert_rows(*piece, w_gate[0], w_up[0], w_down[0], expert_count)
            return [s + g for s, g in zip(sums, grads)], (entry, probs, mixed_rows)

        cut = [a.reshape((chunks, token_count // chunks) + a.shape[1:]) for a in (normal_h, side, cotangent)]
        empty = [jnp.zeros(w.shape[1:], jnp.float32) for w in (w_gate, w_up, w_down)]
        expert_grads, rows = lax.scan(piece_step, empty, cut)
        entry_rows, grad_probs_all, mixture = [r.reshape((token_count,) + r.shape[2:]) for r in rows]
    grad_gate_w, grad_up_w, grad_down_w = expert_grads
    block_out = (state_rows + mixture).astype(jnp.bfloat16)

    grad_probs = selected * grad_probs_all[:, :expert_count]
    grad_logits = (
        probabilities * (grad_probs - jnp.sum(probabilities * grad_probs, axis=-1, keepdims=True))
    ).astype(jnp.bfloat16)
    grad_normal_h = entry_rows + contract_cols(grad_logits, w_router)
    grad_router_part = contract_rows(normal_h, grad_logits)
    grad_state_part, grad_moe_part = norm_backward(state_rows, inv_state, norm_moe, grad_normal_h)
    grad_state = upstream + grad_state_part
    grad_attn = grad_state.astype(jnp.bfloat16)
    (grad_gathered,) = gather_tokens([grad_attn], False, 9, 2)
    grad_out_own = contract_rows(mixed_heads, grad_gathered).astype(jnp.bfloat16)
    grad_mixed = contract_cols(grad_gathered, w_out_own).astype(jnp.bfloat16)
    grad_query_seq, grad_key_seq, grad_value_seq = by_sequence(
        attend_backward,
        (query_seq, key_seq, value_seq, grad_mixed.reshape(seq_shape), sums_log),
        sequences,
    )
    grad_normal_q = unrotate(
        grad_query_seq.reshape(head_shape) * HEAD_DIM ** (-0.5), cosine, sine_table
    ).reshape(group_tokens, local_width)
    grad_normal_k = unrotate(grad_key_seq.reshape(head_shape), cosine, sine_table).reshape(
        group_tokens, local_width
    )
    weighted_q = gain_query * grad_normal_q
    weighted_k = gain_key * grad_normal_k
    inner_q, inner_k = sum_over_heads(
        jnp.sum(weighted_q * query_raw, axis=-1), jnp.sum(weighted_k * key_raw, axis=-1), 10
    )
    grad_query_raw = (
        inv_query * weighted_q - query_raw * inv_query**3 * inner_q[:, None] / model_width
    )
    grad_key_raw = inv_key * weighted_k - key_raw * inv_key**3 * inner_k[:, None] / model_width
    grad_qgain_part = jnp.sum(grad_normal_q * query_raw * inv_query, axis=0)
    grad_kgain_part = jnp.sum(grad_normal_k * key_raw * inv_key, axis=0)
    grad_raw = jnp.concatenate(
        [grad_query_raw, grad_key_raw, grad_value_seq.reshape(group_tokens, local_width)], axis=1
    ).astype(jnp.bfloat16)
    grad_x_part = contract_cols(grad_raw, w_proj).astype(jnp.bfloat16)
    (grad_normal_x,) = scatter_sums([grad_x_part], False, 11)
    grad_proj_own = contract_rows(gathered_x, grad_raw).astype(jnp.bfloat16)
    grad_input_part, grad_attn_gain = norm_backward(inputs, inv_input, norm_attn, grad_normal_x)
    grad_input = grad_state + grad_input_part
    full_width = query_gain.shape[0]
    padded_qgain = lax.dynamic_update_slice_in_dim(
        jnp.zeros((full_width,), jnp.float32), grad_qgain_part, offset, 0
    )
    padded_kgain = lax.dynamic_update_slice_in_dim(
        jnp.zeros((full_width,), jnp.float32), grad_kgain_part, offset, 0
    )
    small = (grad_attn_gain, padded_qgain, padded_kgain, grad_moe_part, grad_router_part)
    grad_query, grad_key, grad_value, grad_out_proj, small = last_sums(grad_proj_own, grad_out_own, small)
    grad_norm_attn, grad_query_gain, grad_key_gain, grad_norm_moe, grad_router = small
    return (
        block_out,
        grad_input,
        grad_norm_attn,
        grad_query,
        grad_key,
        grad_value,
        grad_query_gain,
        grad_key_gain,
        grad_out_proj,
        grad_norm_moe,
        grad_router,
        grad_gate_w[None],
        grad_up_w[None],
        grad_down_w[None],
    )


def last_sums(grad_proj_own, grad_out_own, small):
    if on_links():
        flat = jnp.concatenate([part.reshape(-1) for part in small])
        proj, outp, total = finish(grad_proj_own, grad_out_own, flat.reshape(8, -1, 128), lax.axis_size("dp"), 12)
        total, sums, start = total.reshape(-1), [], 0
        for part in small:
            sums.append(total[start : start + part.size].reshape(part.shape))
            start += part.size
        return (*(proj[a].astype(jnp.float32) for a in range(3)), outp.astype(jnp.float32), sums)
    width = grad_proj_own.shape[1] // 3
    blocks = [
        lax.all_to_all(grad_proj_own[:, a * width : (a + 1) * width], "col", split_axis=0, concat_axis=1, tiled=True)
        for a in range(3)
    ]
    out_block = lax.all_to_all(grad_out_own, "col", split_axis=1, concat_axis=0, tiled=True)
    return (*(total.astype(jnp.float32) for total in lax.psum((*blocks, out_block), "dp")), lax.psum(small, EVERYONE))


def solution(mesh):
    placed = (
        P(("dp", "row", "col"), None),
        P(("dp", "row", "col"), None),
        P(),
        P("col", "row"),
        P("col", "row"),
        P("col", "row"),
        P(),
        P(),
        P("row", "col"),
        P(),
        P(),
        P(("dp", "col"), None, "row"),
        P(("dp", "col"), None, "row"),
        P(("dp", "col"), "row", None),
        P(("dp", "row", "col"), None),
    )
    return jax.shard_map(
        per_device,
        mesh=mesh,
        in_specs=placed,
        out_specs=(
            P(("dp", "row", "col"), None),
            P(("dp", "row", "col"), None),
            P(),
            P("col", "row"),
            P("col", "row"),
            P("col", "row"),
            P(),
            P(),
            P("row", "col"),
            P(),
            P(),
            P(("dp", "col"), None, "row"),
            P(("dp", "col"), None, "row"),
            P(("dp", "col"), "row", None),
        ),
        check_vma=False,
    )
```

```python
import functools

import jax
import jax.numpy as jnp
from jax import lax
from jax.experimental import pallas as pl
from jax.experimental.pallas import tpu as pltpu
from jax.sharding import PartitionSpec as P

MESH = pl.DeviceIdType.MESH
ANYSPEC = pl.BlockSpec(memory_space=pl.ANY)

def place():
    return lax.axis_index("dp"), lax.axis_index("row"), lax.axis_index("col")

def greet(peers):
    barrier = pltpu.get_barrier_semaphore()
    for peer in peers:
        pl.semaphore_signal(barrier, inc=1, device_id=peer, device_id_type=MESH)
    pl.semaphore_wait(barrier, len(peers))

def gather_kernel(planes, parts, count, *refs):
    ins, outs = refs[:count], refs[count:2 * count]
    own_sem, send_sem, recv_sem = refs[2 * count:]
    z, r, c = place()
    first, second, diag = c ^ (1 + r), c ^ (2 - r), c ^ 3
    partner = (z, 1 - r, c)
    to_first, to_second = (z, r, first), (z, r, second)
    greet([to_first, to_second, partner] + [(z ^ k, r, c) for k in range(1, planes)])
    pieces = []
    for a in range(count):
        cut = parts if a == 0 else 1
        pieces += [(a, p, ins[a].shape[0], ins[a].shape[0] // cut) for p in range(cut)]

    def number(zz, rr, cc):
        return ((zz if planes > 1 else 0) * 2 + rr) * 4 + cc

    def place_of(i, which):
        a, p, depth, cut = pieces[i]
        return outs[a].at[pl.ds(pl.multiple_of(which * depth + p * cut, cut), cut)]

    sent = [[] for _ in pieces]

    def send(i, which, target, own=False):
        a, p, depth, cut = pieces[i]
        spot = place_of(i, which)
        copy = pltpu.make_async_remote_copy(
            src_ref=ins[a].at[pl.ds(p * cut, cut)] if own else spot, dst_ref=spot,
            send_sem=send_sem.at[i, len(sent[i])], recv_sem=recv_sem.at[i, which],
            device_id=target, device_id_type=MESH)
        copy.start()
        sent[i].append(copy)

    def await_block(i, which):
        spot = place_of(i, which)
        pltpu.make_async_remote_copy(
            src_ref=spot, dst_ref=spot, send_sem=send_sem.at[i, 0], recv_sem=recv_sem.at[i, which],
            device_id=partner, device_id_type=MESH).wait_recv()

    mine = number(z, r, c)
    keeps = []
    every = range(len(pieces))
    for i in every:
        for target in [to_first, to_second] + [(z ^ k, r, c) for k in range(1, planes)] + [partner]:
            send(i, mine, target, True)
    for a in range(count):
        keep = pltpu.make_async_copy(ins[a], outs[a].at[pl.ds(pl.multiple_of(mine * ins[a].shape[0], ins[a].shape[0]), ins[a].shape[0])], own_sem.at[a])
        keep.start()
        keeps.append(keep)

    def forward(which, targets):
        for i in every:
            await_block(i, which)
            for target in targets:
                send(i, which, target)

    for step in range(planes + 2):
        if 0 < step < planes:
            forward(number(z ^ step, r, c), [to_first, to_second, partner])
        if 0 <= step - 1 < planes:
            forward(number(z ^ (step - 1), r, first), [to_second, partner])
            forward(number(z ^ (step - 1), r, second), [partner])
        if 0 <= step - 2 < planes:
            forward(number(z ^ (step - 2), r, diag), [partner])
    for k in range(planes):
        for j in range(4):
            for i in every:
                await_block(i, number(z ^ k, 1 - r, c ^ j))
    for keep in keeps:
        keep.wait()
    for copies in sent:
        for copy in copies:
            copy.wait_send()

def gather(arrays, planes, collective_id, parts=1):
    count = len(arrays)
    blocks = planes * 8
    sends = (3 + planes - 1) + (planes - 1) * 3 + planes * 4
    pieces = count - 1 + parts
    return pl.pallas_call(
        functools.partial(gather_kernel, planes, parts, count),
        out_shape=[jax.ShapeDtypeStruct((blocks * a.shape[0],) + a.shape[1:], a.dtype) for a in arrays],
        in_specs=[ANYSPEC] * count, out_specs=[ANYSPEC] * count,
        scratch_shapes=[pltpu.SemaphoreType.DMA((count,)), pltpu.SemaphoreType.DMA((pieces, sends)), pltpu.SemaphoreType.DMA((pieces, blocks))],
        compiler_params=pltpu.CompilerParams(collective_id=collective_id, has_side_effects=True),
    )(*arrays)

def reducer(planes, parts, outs, buffers, semaphores):
    held, fromp, relay, near, far = buffers
    load_sem, pair_send, pair_recv, send_sem, relay_recv, near_recv, far_recv = semaphores
    z, r, c = place()
    first, second, diag = c ^ (1 + r), c ^ (2 - r), c ^ 3
    partner = (z, 1 - r, c)
    to_first, to_second = (z, r, first), (z, r, second)
    depth = outs[0].shape[0]
    every = range(len(parts))

    def rows(a, k, rr, cc):
        which = (((z ^ k) if planes > 1 else 0) * 2 + rr) * 4 + cc
        return parts[a].at[pl.ds(pl.multiple_of(which * depth, depth), depth)]

    columns, partner_columns = [c, first, second, diag], [c, second, first, diag]

    def remote(source, target, send, recv, device):
        return pltpu.make_async_remote_copy(
            src_ref=source, dst_ref=target, send_sem=send, recv_sem=recv, device_id=device, device_id_type=MESH)

    def load(a, k, j):
        return pltpu.make_async_copy(rows(a, k, r, columns[j]), held[a].at[k, j], load_sem.at[a, k, j])

    def pair(a, k, j):
        return remote(rows(a, k, 1 - r, partner_columns[j]), fromp[a].at[k, j], pair_send.at[a, k, j], pair_recv.at[a, k, j], partner)

    def begin(i, _):
        k = planes - 1 - i
        for j in (3, 2, 1, 0):
            for a in every:
                load(a, k, j).start()
                pair(a, k, j).start()
        return 0

    step_rows = min(32, depth)

    def add(target, sources):
        def body(i, _):
            at = pl.ds(pl.multiple_of(i * step_rows, step_rows), step_rows)
            total = sources[0][at].astype(jnp.float32)
            for source in sources[1:]:
                total = total + source[at].astype(jnp.float32)
            target[at] = total.astype(target.dtype)
            return 0
        lax.fori_loop(0, depth // step_rows, body, 0)

    def ready(a, k, j):
        load(a, k, j).wait()
        pair(a, k, j).wait_recv()

    def to_diag(a, k):
        return remote(held[a].at[k, 3], relay[a].at[k], send_sem.at[a, k, 0], relay_recv.at[a, k], to_second)

    def to_near(a, k, which):
        source, device = (held[a].at[k, 2], to_second) if which else (held[a].at[k, 1], to_first)
        return remote(source, near[a].at[k, which], send_sem.at[a, k, 1 + which], near_recv.at[a, k, which], device)

    def to_far(a, k):
        slot = jnp.maximum(k - 1, 0)
        return remote(held[a].at[k, 0], far[a].at[slot], send_sem.at[a, k, 3], far_recv.at[a, slot], (z ^ k, r, c))

    def to_relay(k):
        for a in every:
            ready(a, k, 3)
            add(held[a].at[k, 3], [held[a].at[k, 3], fromp[a].at[k, 3]])
            to_diag(a, k).start()
        for a in every:
            ready(a, k, 2)
            add(held[a].at[k, 2], [held[a].at[k, 2], fromp[a].at[k, 2]])
            to_near(a, k, 1).start()

    def pass_on(k):
        for a in every:
            ready(a, k, 1)
            to_diag(a, k).wait_recv()
            add(held[a].at[k, 1], [held[a].at[k, 1], fromp[a].at[k, 1], relay[a].at[k]])
            to_near(a, k, 0).start()

    def collect(k):
        for a in every:
            ready(a, k, 0)
            to_near(a, k, 0).wait_recv()
            to_near(a, k, 1).wait_recv()
            terms = [held[a].at[k, 0], fromp[a].at[k, 0], near[a].at[k, 0], near[a].at[k, 1]]

            @pl.when(k > 0)
            def _():
                add(held[a].at[k, 0], terms)
                to_far(a, k).start()

            @pl.when(k == 0)
            def _():
                for i in range(1, planes):
                    to_far(a, i).wait_recv()
                add(outs[a], terms + [far[a].at[i] for i in range(planes - 1)])

    def drain(k, _):
        for a in every:
            for j in range(4):
                pair(a, k, j).wait_send()
            to_diag(a, k).wait_send()
            to_near(a, k, 0).wait_send()
            to_near(a, k, 1).wait_send()

            @pl.when(k > 0)
            def _():
                to_far(a, k).wait_send()
        return 0

    return begin, to_relay, pass_on, collect, drain


def reduce_steps(planes, parts, outs, buffers, semaphores, filler):
    z, r, c = place()
    greet([(z, r, c ^ 1), (z, r, c ^ 2), (z, 1 - r, c)] + [(z ^ k, r, c) for k in range(1, planes)])
    begin, to_relay, pass_on, collect, drain = reducer(planes, parts, outs, buffers, semaphores)
    lax.fori_loop(0, planes, begin, 0)

    def step_body(step, _):
        @pl.when(step < planes)
        def _():
            to_relay(planes - 1 - step)

        @pl.when(jnp.logical_and(step >= 1, step < planes + 1))
        def _():
            pass_on(planes - step)

        @pl.when(step >= 2)
        def _():
            collect(planes + 1 - step)
        if filler is not None:
            filler(step)
        return 0

    lax.fori_loop(0, planes + 2, step_body, 0)
    lax.fori_loop(0, planes, drain, 0)


def reduce_scratch(partials, planes):
    shapes = [((p.shape[0] // (planes * 8), p.shape[1]), p.dtype) for p in partials]
    count, far = len(partials), max(planes - 1, 1)
    dma = pltpu.SemaphoreType.DMA
    buffers = [pltpu.VMEM(lead + shape, kind) for lead in ((planes, 4), (planes, 4), (planes,), (planes, 2), (far,)) for shape, kind in shapes]
    return shapes, buffers, [
        dma((count, planes, 4)), dma((count, planes, 4)), dma((count, planes, 4)), dma((count, planes, 4)),
        dma((count, planes)), dma((count, planes, 2)), dma((count, far))]


def reduce_kernel(planes, count, *refs):
    buffers = [refs[(2 + i) * count:(3 + i) * count] for i in range(5)]
    reduce_steps(planes, refs[:count], refs[count:2 * count], buffers, refs[7 * count:], None)


def reduce_scatter(partials, planes, collective_id):
    count = len(partials)
    shapes, buffers, semaphores = reduce_scratch(partials, planes)
    return pl.pallas_call(
        functools.partial(reduce_kernel, planes, count),
        out_shape=[jax.ShapeDtypeStruct(shape, jnp.float32) for shape, _ in shapes],
        in_specs=[ANYSPEC] * count, out_specs=[pl.BlockSpec(memory_space=pltpu.VMEM)] * count,
        scratch_shapes=buffers + semaphores,
        compiler_params=pltpu.CompilerParams(collective_id=collective_id, has_side_effects=True, vmem_limit_bytes=48 * 2**20),
    )(*partials)


def exchange_kernel(wq_ref, wk_ref, wv_ref, wo_ref, proj_ref, out_ref, own_sem, send_sem, recv_sem):
    z, r, c = place()
    width = proj_ref.shape[1] // 3
    depth = wq_ref.shape[0]
    out_rows, out_width = out_ref.shape[0], wo_ref.shape[1]
    greet([(z, r, c ^ j) for j in range(1, 4)])

    def source(a, target):
        if a < 3:
            return (wq_ref, wk_ref, wv_ref)[a].at[:, pl.ds(pl.multiple_of(target * width, width), width)]
        return wo_ref.at[pl.ds(pl.multiple_of(target * out_rows, out_rows), out_rows), :]

    def spot(a, origin):
        if a < 3:
            return proj_ref.at[pl.ds(pl.multiple_of(origin * depth, depth), depth), pl.ds(a * width, width)]
        return out_ref.at[:, pl.ds(pl.multiple_of(origin * out_width, out_width), out_width)]

    waits = []
    for a in range(4):
        keep = pltpu.make_async_copy(source(a, c), spot(a, c), own_sem.at[a])
        keep.start()
        waits.append(keep.wait)
        for j in range(1, 4):
            copy = pltpu.make_async_remote_copy(
                src_ref=source(a, c ^ j), dst_ref=spot(a, c), send_sem=send_sem.at[a, j - 1],
                recv_sem=recv_sem.at[a, j - 1], device_id=(z, r, c ^ j), device_id_type=MESH)
            copy.start()
            waits.append(copy.wait_send)
    for a in range(4):
        for j in range(1, 4):
            arrived = spot(a, c ^ j)
            pltpu.make_async_remote_copy(
                src_ref=arrived, dst_ref=arrived, send_sem=send_sem.at[a, j - 1], recv_sem=recv_sem.at[a, j - 1],
                device_id=(z, r, c ^ j), device_id_type=MESH).wait_recv()
    for wait in waits:
        wait()


def exchange_weights(w_query, w_key, w_value, w_out, collective_id):
    depth, half = w_query.shape
    kind = w_query.dtype
    width, out_rows, out_width = half // 4, w_out.shape[0] // 4, w_out.shape[1] * 4
    return pl.pallas_call(
        exchange_kernel,
        out_shape=[jax.ShapeDtypeStruct((depth * 4, 3 * width), kind), jax.ShapeDtypeStruct((out_rows, out_width), kind)],
        in_specs=[ANYSPEC] * 4, out_specs=[ANYSPEC] * 2,
        scratch_shapes=[pltpu.SemaphoreType.DMA((4,)), pltpu.SemaphoreType.DMA((4, 3)), pltpu.SemaphoreType.DMA((4, 3))],
        compiler_params=pltpu.CompilerParams(collective_id=collective_id, has_side_effects=True),
    )(w_query, w_key, w_value, w_out)


def total_kernel(value_ref, out_ref, slots, send_sem, recv_sem):
    z, r, c = place()
    peers = [(z, r ^ (j >> 2), c ^ (j & 3)) for j in range(1, 8)]
    greet(peers)
    copies = []
    for j, peer in enumerate(peers):
        copy = pltpu.make_async_remote_copy(
            src_ref=value_ref, dst_ref=slots.at[j], send_sem=send_sem.at[j], recv_sem=recv_sem.at[j],
            device_id=peer, device_id_type=MESH)
        copy.start()
        copies.append(copy)
    for copy in copies:
        copy.wait()
    here = r * 4 + c
    total = jnp.zeros(value_ref.shape, jnp.float32)
    for who in range(8):
        which = here ^ who
        term = jnp.where(which == 0, value_ref[...], slots[jnp.maximum(which - 1, 0)])
        total = total + term
    out_ref[...] = total


def group_total(value, collective_id):
    return pl.pallas_call(
        total_kernel,
        out_shape=jax.ShapeDtypeStruct(value.shape, jnp.float32),
        in_specs=[pl.BlockSpec(memory_space=pltpu.VMEM)], out_specs=pl.BlockSpec(memory_space=pltpu.VMEM),
        scratch_shapes=[pltpu.VMEM((7,) + value.shape, jnp.float32), pltpu.SemaphoreType.DMA((7,)), pltpu.SemaphoreType.DMA((7,))],
        compiler_params=pltpu.CompilerParams(collective_id=collective_id, has_side_effects=True),
    )(value)


def finish_kernel(planes, proj_ref, outp_ref, small_ref, scaled_ref, mixed_part, entry_part,
                  proj_out, outp_out, small_out, mixed_out, entry_out, *scratch):
    (proj_own, outp_own, proj_in, outp_in, small_own, slices, far_slices, own_sem, swap_send, swap_recv, down_send, down_recv,
     up_send, up_recv, slice_send, slice_recv, far_send, far_recv, whole_send, whole_recv) = scratch[:20]
    wide = reducer(planes, (mixed_part,), (mixed_out,), [(ref,) for ref in scratch[20:25]], scratch[25:32])
    near = reducer(1, (entry_part,), (entry_out,), [(ref,) for ref in scratch[32:37]], scratch[37:44])
    z, r, c = place()
    here = r * 4 + c
    group = [(z, r ^ (j >> 2), c ^ (j & 3)) for j in range(1, 8)]
    greet(group + [(z ^ k, r, c) for k in range(1, planes)])
    width = proj_ref.shape[1] // 3
    depth, out_width = proj_ref.shape[0] // 4, outp_ref.shape[1] // 4
    out_rows, step = outp_ref.shape[0], proj_ref.shape[0] // 16
    chunks = 16

    def remote(source, target, send, recv, device):
        return pltpu.make_async_remote_copy(
            src_ref=source, dst_ref=target, send_sem=send, recv_sem=recv, device_id=device, device_id_type=MESH)

    def piece(i, target):
        if i < 12:
            a, m = i // 4, i % 4
            return proj_ref.at[pl.ds(pl.multiple_of(target * depth + m * step, step), step), pl.ds(a * width, width)]
        return outp_ref.at[:, pl.ds(pl.multiple_of(target * out_width, out_width), out_width)]

    def spot(i, origin):
        a, m = i // 4, i % 4
        return proj_own.at[a, pl.ds(m * step, step), pl.ds(pl.multiple_of(origin * width, width), width)]

    def rows(proj, outp, i):
        if i < 12:
            return proj.at[i // 4, pl.ds((i % 4) * step, step), :]
        return outp.at[pl.ds((i - 12) * out_rows, out_rows), :]

    small_copies = []

    def small_begin():
        lanes = small_ref.shape[2]
        small_own[...] = small_ref[...]
        for j in range(entry_out.shape[1] // lanes):
            at = pl.ds(j * lanes, lanes)
            part = jnp.sum(entry_out[:, at] * scaled_ref[:, at], axis=0, keepdims=True)
            small_own[j // small_ref.shape[1], pl.ds(j % small_ref.shape[1], 1), :] = part
        for j in range(1, 8):
            copy = remote(small_own.at[here ^ j], slices.at[here], slice_send.at[j], slice_recv.at[here], group[j - 1])
            copy.start()
            small_copies.append(copy)

    order = [0, 1, 2, 3, 12, 13, 4, 5, 6, 7, 14, 15, 8, 9, 10, 11]
    swaps = []

    def issue(i):
        if i < 12:
            keep = pltpu.make_async_copy(piece(i, c), spot(i, c), own_sem.at[i])
            keep.start()
            for j in range(1, 4):
                copy = remote(piece(i, c ^ j), spot(i, c), swap_send.at[i, j - 1], swap_recv.at[i, j - 1], (z, r, c ^ j))
                copy.start()
                swaps.append(copy)
        else:
            @pl.when(c == i - 12)
            def _():
                pltpu.make_async_copy(piece(i, c), rows(proj_own, outp_own, i), own_sem.at[i]).start()
                for j in range(1, 4):
                    remote(piece(i, c ^ j), rows(proj_own, outp_own, i), swap_send.at[i, j - 1], swap_recv.at[i, 0], (z, r, c ^ j)).start()

    ahead = 4
    for i in order[:ahead]:
        issue(i)
    near[0](0, 0)
    lax.fori_loop(0, planes, wide[0], 0)

    def local_ready(i):
        target = rows(proj_own, outp_own, i)
        if i < 12:
            pltpu.make_async_copy(piece(i, c), spot(i, c), own_sem.at[i]).wait()
            for j in range(1, 4):
                arrived = spot(i, c ^ j)
                remote(arrived, arrived, swap_send.at[i, j - 1], swap_recv.at[i, j - 1], (z, r, c ^ j)).wait_recv()
        else:
            @pl.when(c == i - 12)
            def _():
                pltpu.make_async_copy(piece(i, c), target, own_sem.at[i]).wait()

            @pl.when(c != i - 12)
            def _():
                remote(target, target, swap_send.at[i, 0], swap_recv.at[i, 0], (z, r, c ^ 1)).wait_recv()

    def combine(target, first, second, count):
        def body(s, _):
            at = pl.ds(pl.multiple_of(s * 32, 32), 32)
            total = first[at].astype(jnp.float32) + second[at].astype(jnp.float32)
            target[at] = total.astype(target.dtype)
            return 0
        lax.fori_loop(0, count // 32, body, 0)

    def seat(i):
        root_low = i % 2 == 0
        spot_from_root = z if root_low else planes - 1 - z
        up = (jnp.minimum(z + 1, planes - 1) if root_low else jnp.maximum(z - 1, 0), r, c)
        down = (jnp.maximum(z - 1, 0) if root_low else jnp.minimum(z + 1, planes - 1), r, c)
        return spot_from_root, up, down

    def count_of(i):
        return step if i < 12 else out_rows

    def to_root(i, p):
        _, up, down = seat(i)
        own, arriving, result = rows(proj_own, outp_own, i), rows(proj_in, outp_in, i), rows(proj_out, outp_out, i)
        local_ready(i)
        if p < planes - 1:
            remote(arriving, arriving, down_send.at[i], down_recv.at[i], up).wait_recv()
        if p == 0:
            combine(result, own, arriving, count_of(i))
            remote(result, result, up_send.at[i], up_recv.at[i], up).start()
        else:
            if p < planes - 1:
                combine(own, own, arriving, count_of(i))
            remote(own, arriving, down_send.at[i], down_recv.at[i], down).start()

    def from_root(i, p):
        _, up, down = seat(i)
        result = rows(proj_out, outp_out, i)
        remote(result, result, up_send.at[i], up_recv.at[i], down).wait_recv()
        if p < planes - 1:
            remote(result, result, up_send.at[i], up_recv.at[i], up).start()

    def small_group():
        for j in range(1, 8):
            arrived = slices.at[here ^ j]
            remote(arrived, arrived, slice_send.at[0], slice_recv.at[here ^ j], group[j - 1]).wait_recv()
        slices[here] = small_own[here]
        total = slices[0]
        for j in range(1, 8):
            total = total + slices[j]
        far_slices[z] = total
        for k in range(1, planes):
            copy = remote(far_slices.at[z], far_slices.at[z], far_send.at[k - 1], far_recv.at[z], (z ^ k, r, c))
            copy.start()
            small_copies.append(copy)

    def small_far():
        for k in range(1, planes):
            arrived = far_slices.at[z ^ k]
            remote(arrived, arrived, far_send.at[k - 1], far_recv.at[z ^ k], (z ^ k, r, c)).wait_recv()
        total = far_slices[0]
        for k in range(1, planes):
            total = total + far_slices[k]
        small_out[here] = total
        for j in range(1, 8):
            copy = remote(small_out.at[here], small_out.at[here], whole_send.at[j], whole_recv.at[here], group[j - 1])
            copy.start()
            small_copies.append(copy)

    lag = 2
    hops = 2 * planes - 1
    top = planes - 1
    actions = {0: [lambda: near[1](0)], 3: [lambda: near[2](0)], 6: [lambda: near[3](0), small_begin], 10: [small_group], 16: [small_far]}
    for turn in range(planes + 2):
        todo = []
        if turn < planes:
            todo.append(lambda k=top - turn: wide[1](k))
        if 0 <= turn - 1 < planes:
            todo.append(lambda k=top - turn + 1: wide[2](k))
        if 0 <= turn - 2 < planes:
            todo.append(lambda k=top - turn + 2: wide[3](k))
        for n, action in enumerate(todo):
            actions.setdefault(2 + 4 * turn + n, []).append(action)
    for s in range(chunks + (hops - 1) * lag):
        if s + ahead < chunks:
            issue(order[s + ahead])
        for h in range(hops):
            if 0 <= s - h * lag < chunks:
                i = order[s - h * lag]
                p = planes - 1 - h if h < planes else h - planes + 1

                @pl.when(seat(i)[0] == p)
                def _(i=i, p=p, h=h):
                    if h < planes:
                        to_root(i, p)
                    else:
                        from_root(i, p)
        for action in actions.get(s, ()):
            action()
    for j in range(1, 8):
        arrived = small_out.at[here ^ j]
        remote(arrived, arrived, whole_send.at[0], whole_recv.at[here ^ j], group[j - 1]).wait_recv()
    near[4](0, 0)
    lax.fori_loop(0, planes, wide[4], 0)
    for copy in small_copies + swaps:
        copy.wait_send()
    for i in range(12, 16):
        @pl.when(c == i - 12)
        def _():
            for j in range(1, 4):
                remote(piece(i, c ^ j), rows(proj_own, outp_own, i), swap_send.at[i, j - 1], swap_recv.at[i, 0], (z, r, c ^ j)).wait_send()
    for i in range(chunks):
        p, up, down = seat(i)
        own, arriving, result = rows(proj_own, outp_own, i), rows(proj_in, outp_in, i), rows(proj_out, outp_out, i)

        @pl.when(p > 0)
        def _():
            remote(own, arriving, down_send.at[i], down_recv.at[i], down).wait_send()

        @pl.when(p < planes - 1)
        def _():
            remote(result, result, up_send.at[i], up_recv.at[i], up).wait_send()


def finish(grad_proj_own, grad_out_own, small, scaled, mixed_part, entry_part, planes, collective_id):
    depth, width = grad_proj_own.shape[0] // 4, grad_proj_own.shape[1] // 3
    out_rows, out_width = grad_out_own.shape[0], grad_out_own.shape[1] // 4
    kind = grad_proj_own.dtype
    proj, outp = (3, depth, 4 * width), (4 * out_rows, out_width)
    vmem = pl.BlockSpec(memory_space=pltpu.VMEM)
    dma = pltpu.SemaphoreType.DMA
    [(mixed_shape, _)], mixed_buffers, mixed_semaphores = reduce_scratch([mixed_part], planes)
    [(entry_shape, _)], entry_buffers, entry_semaphores = reduce_scratch([entry_part], 1)
    return pl.pallas_call(
        functools.partial(finish_kernel, planes),
        out_shape=[jax.ShapeDtypeStruct(proj, kind), jax.ShapeDtypeStruct(outp, kind), jax.ShapeDtypeStruct(small.shape, small.dtype),
                   jax.ShapeDtypeStruct(mixed_shape, jnp.float32), jax.ShapeDtypeStruct(entry_shape, jnp.float32)],
        in_specs=[ANYSPEC, ANYSPEC, vmem, vmem, ANYSPEC, ANYSPEC], out_specs=[vmem] * 5,
        scratch_shapes=[
            pltpu.VMEM(proj, kind), pltpu.VMEM(outp, kind), pltpu.VMEM(proj, kind), pltpu.VMEM(outp, kind),
            pltpu.VMEM(small.shape, jnp.float32), pltpu.VMEM(small.shape, jnp.float32), pltpu.VMEM((planes,) + small.shape[1:], jnp.float32),
            dma((16,)), dma((16, 3)), dma((16, 3)), dma((16,)), dma((16,)), dma((16,)), dma((16,)),
            dma((8,)), dma((8,)), dma((planes,)), dma((planes,)), dma((8,)), dma((8,))]
        + mixed_buffers + mixed_semaphores + entry_buffers + entry_semaphores,
        compiler_params=pltpu.CompilerParams(collective_id=collective_id, has_side_effects=True, vmem_limit_bytes=58 * 2**20),
    )(grad_proj_own, grad_out_own, small, scaled, mixed_part, entry_part)


def expert_kernel(planes, experts, own_h, own_side, cot, w_gate, w_up, w_down,
                  all_h, all_side, entry_out, route_out, active_out, grad_gate_out, grad_up_out,
                  gate_use, up_use, down_use, rows_h, rows_c, rows_side, back_rows,
                  gate_rows, up_rows, active_rows, grad_gate, grad_up, entry_stage, route_stage,
                  weight_sem, own_sem, send_sem, recv_sem, cot_sem, load_sem, store_sem):
    z, r, c = place()
    first, second, diag = c ^ (1 + r), c ^ (2 - r), c ^ 3
    partner = (z, 1 - r, c)
    to_first, to_second = (z, r, first), (z, r, second)
    count = own_h.shape[0]
    group = 4 * count
    expert = z * 4 + c
    half = count // 2
    pieces = [(own_h, all_h, 0, half), (own_h, all_h, half, half), (own_side, all_side, 0, count)]

    weights = [(w_gate, gate_use), (w_up, up_use), (w_down, down_use)]
    for i, (source, target) in enumerate(weights):
        pltpu.make_async_copy(source, target, weight_sem.at[i]).start()

    def number(zz, rr, cc):
        return (zz * 2 + rr) * 4 + cc

    def spot(i, which):
        _, target, start, size = pieces[i]
        return target.at[pl.ds(pl.multiple_of(which * count + start, size), size)]

    def copy_of(i, source, which, k, slot, device):
        return pltpu.make_async_remote_copy(
            src_ref=source, dst_ref=spot(i, which), send_sem=send_sem.at[i, k, slot], recv_sem=recv_sem.at[i, which],
            device_id=device, device_id_type=MESH)

    def own_piece(i):
        source, _, start, size = pieces[i]
        return source.at[pl.ds(start, size)]

    def await_block(i, which):
        copy_of(i, spot(i, which), which, 0, 0, partner).wait_recv()

    def forward(which, k, targets):
        for i in range(3):
            await_block(i, which)
            for slot, device in targets:
                copy_of(i, spot(i, which), which, k, slot, device).start()

    greet([to_first, to_second, partner] + [(z ^ k, r, c) for k in range(1, planes)])
    mine = number(z, r, c)
    for i in range(3):
        for slot, device in ((0, to_first), (1, to_second)):
            copy_of(i, own_piece(i), mine, 0, slot, device).start()
        for k in range(1, planes):
            copy_of(i, own_piece(i), mine, k, 7, (z ^ k, r, c)).start()
        copy_of(i, own_piece(i), mine, 0, 2, partner).start()
    keeps = [pltpu.make_async_copy(own_piece(i), spot(i, mine), own_sem.at[i]) for i in range(3)]
    for keep in keeps:
        keep.start()

    def base_of(k, rr):
        return pl.multiple_of(number(z ^ k, rr, 0) * count, group)

    def dot(left, right):
        return jnp.dot(left, right, preferred_element_type=jnp.float32)

    def dot_turned(left, right):
        return lax.dot_general(left, right, (((1,), (1,)), ((), ())), preferred_element_type=jnp.float32)

    def cot_copy(g):
        rr = jnp.where(g % 2 == 0, r, 1 - r)
        return pltpu.make_async_copy(cot.at[pl.ds(base_of(g // 2, rr), group)], rows_c.at[g % 2], cot_sem.at[g % 2])

    cot_copy(0).start()
    for i, (source, target) in enumerate(weights):
        pltpu.make_async_copy(source, target, weight_sem.at[i]).wait()

    def back_body(g, _):
        @pl.when(g + 1 < 2 * planes)
        def _():
            cot_copy(g + 1).start()

        cot_copy(g).wait()
        back_rows[g] = dot_turned(rows_c[g % 2], down_use[...])
        return 0

    lax.fori_loop(0, 2 * planes, back_body, 0)
    for keep in keeps:
        keep.wait()

    def stores(k, rr, slot):
        at = pl.ds(base_of(k, rr), group)
        return [
            pltpu.make_async_copy(source.at[slot], target.at[at], store_sem.at[slot, i])
            for i, (source, target) in enumerate((
                (entry_stage, entry_out), (route_stage, route_out), (active_rows, active_out),
                (grad_gate, grad_gate_out), (grad_up, grad_up_out)))]

    def compute(k, rr, slot):
        at = pl.ds(base_of(k, rr), group)
        loads = [pltpu.make_async_copy(all_h.at[at], rows_h, load_sem.at[0]),
                 pltpu.make_async_copy(all_side.at[at], rows_side, load_sem.at[1])]
        for load in loads:
            load.start()
        for load in loads:
            load.wait()
        gate_rows[...] = dot(rows_h[...], gate_use[...])
        up_rows[...] = dot(rows_h[...], up_use[...])

        @pl.when(k > 0)
        def _():
            for store in stores(k, rr, slot):
                store.wait()

        part = 128
        lane = lax.broadcasted_iota(jnp.int32, (part, rows_side.shape[1]), 1)

        @pl.loop(0, group // part)
        def _(t):
            at = pl.ds(pl.multiple_of(t * part, part), part)
            mask = (lane == expert) | (lane == expert + experts)
            share = jnp.sum(jnp.where(mask, rows_side[at, :].astype(jnp.float32), 0.0), axis=1, keepdims=True)
            gate, up, back = gate_rows[at, :], up_rows[at, :], back_rows[2 * k + slot, at, :]
            squash = jax.nn.sigmoid(gate)
            silu = gate * squash
            active = silu * up
            route = jnp.sum(active * back, axis=1, keepdims=True)
            route_stage[slot, at, :] = jnp.where(lane == expert, route, 0.0).astype(jnp.bfloat16)
            active_rows[slot, at, :] = (share * active).astype(jnp.bfloat16)
            grad_active = share * back
            grad_gate[slot, at, :] = (grad_active * up * squash * (1.0 + gate * (1.0 - squash))).astype(jnp.bfloat16)
            grad_up[slot, at, :] = (grad_active * silu).astype(jnp.bfloat16)

    def finish_rows(k, rr, slot):
        entry = dot_turned(grad_gate[slot], gate_use[...]) + dot_turned(grad_up[slot], up_use[...])
        entry_stage[slot] = entry.astype(jnp.bfloat16)
        for store in stores(k, rr, slot):
            store.start()

    def step_body(step, _):
        @pl.when(jnp.logical_and(step > 0, step < planes))
        def _():
            forward(number(z ^ step, r, c), step, ((0, to_first), (1, to_second), (2, partner)))

        @pl.when(jnp.logical_and(step >= 3, step < planes + 3))
        def _():
            k = step - 3
            for j in range(4):
                for i in range(3):
                    await_block(i, number(z ^ k, 1 - r, c ^ j))
            compute(k, 1 - r, 1)

        @pl.when(jnp.logical_and(step >= 1, step < planes + 1))
        def _():
            k = step - 1
            forward(number(z ^ k, r, first), k, ((3, to_second), (4, partner)))
            forward(number(z ^ k, r, second), k, ((5, partner),))

        @pl.when(jnp.logical_and(step >= 3, step < planes + 3))
        def _():
            finish_rows(step - 3, 1 - r, 1)
            finish_rows(step - 3, r, 0)

        @pl.when(jnp.logical_and(step >= 2, step < planes + 2))
        def _():
            k = step - 2
            forward(number(z ^ k, r, diag), k, ((6, partner),))
            compute(k, r, 0)

        return 0

    lax.fori_loop(0, planes + 3, step_body, 0)
    for slot, rr in ((0, r), (1, 1 - r)):
        for store in stores(planes - 1, rr, slot):
            store.wait()

    def drain(k, _):
        for i in range(3):
            for slot in range(7):
                copy_of(i, spot(i, mine), mine, k, slot, partner).wait_send()

            @pl.when(k > 0)
            def _():
                copy_of(i, spot(i, mine), mine, k, 7, partner).wait_send()
        return 0

    lax.fori_loop(0, planes, drain, 0)


def expert_rows_on_links(normal_h, side, all_cotangent, w_gate, w_up, w_down, experts, collective_id):
    planes = lax.axis_size("dp")
    count, width = normal_h.shape
    hidden = w_gate.shape[1]
    total, group, low, wide = planes * 8 * count, 4 * count, jnp.bfloat16, jnp.float32
    sides = side.shape[1]
    vmem, dma = pltpu.VMEM, pltpu.SemaphoreType.DMA
    outs = [jax.ShapeDtypeStruct((total, n), low) for n in (width, sides, width, sides, hidden, hidden, hidden)]
    return pl.pallas_call(
        functools.partial(expert_kernel, planes, experts),
        out_shape=outs, in_specs=[ANYSPEC] * 6, out_specs=[ANYSPEC] * 7,
        scratch_shapes=[
            vmem((width, hidden), low), vmem((width, hidden), low), vmem((hidden, width), low),
            vmem((group, width), low), vmem((2, group, width), low), vmem((group, sides), low), vmem((2 * planes, group, hidden), wide),
            vmem((group, hidden), wide), vmem((group, hidden), wide),
            vmem((2, group, hidden), low), vmem((2, group, hidden), low), vmem((2, group, hidden), low),
            vmem((2, group, width), low), vmem((2, group, sides), low),
            dma((3,)), dma((3,)), dma((3, planes, 8)), dma((3, planes * 8)), dma((2,)), dma((2,)), dma((2, 5))],
        compiler_params=pltpu.CompilerParams(collective_id=collective_id, has_side_effects=True, vmem_limit_bytes=60 * 2**20),
    )(normal_h, side, all_cotangent, w_gate, w_up, w_down)


def entry_kernel(planes, entry_part, route_part, all_h, cot, active, grad_gate, grad_up, w_down,
                 entry_out, route_out, mixed_out, acc_gate, acc_up, acc_down, *scratch):
    buffers = [scratch[2 * i:2 * i + 2] for i in range(5)]
    semaphores = scratch[10:17]
    down_use, rows_h, rows_c, rows_x, mixed_stage, down_sem, load_sem, store_sem = scratch[17:]
    group = rows_h.shape[1]
    groups = all_h.shape[0] // group

    def loads(g):
        slot = g % 2
        at = pl.ds(pl.multiple_of(g * group, group), group)
        pairs = [(all_h, rows_h.at[slot]), (cot, rows_c.at[slot])] + [
            (source, rows_x.at[slot, i]) for i, source in enumerate((active, grad_gate, grad_up))]
        return [pltpu.make_async_copy(source.at[at], target, load_sem.at[slot, i]) for i, (source, target) in enumerate(pairs)]

    def store(g):
        at = pl.ds(pl.multiple_of(g * group, group), group)
        return pltpu.make_async_copy(mixed_stage, mixed_out.at[at], store_sem.at[0])

    def turned(left, right):
        return lax.dot_general(left, right, (((0,), (0,)), ((), ())), preferred_element_type=jnp.float32)

    down = pltpu.make_async_copy(w_down, down_use, down_sem.at[0])
    down.start()
    for load in loads(0):
        load.start()
    for acc in (acc_gate, acc_up, acc_down):
        @pl.loop(0, acc.shape[0] // 32)
        def _(t, acc=acc):
            acc[pl.ds(pl.multiple_of(t * 32, 32), 32), :] = jnp.zeros((32, acc.shape[1]), jnp.float32)
    down.wait()

    def one(g):
        @pl.when(g + 1 < groups)
        def _():
            for load in loads(g + 1):
                load.start()

        for load in loads(g):
            load.wait()
        slot = g % 2
        acc_gate[...] += turned(rows_h[slot], rows_x[slot, 1])
        acc_up[...] += turned(rows_h[slot], rows_x[slot, 2])
        acc_down[...] += turned(rows_x[slot, 0], rows_c[slot])

        @pl.when(g > 0)
        def _():
            store(g - 1).wait()

        mixed_stage[...] = jnp.dot(rows_x[slot, 0], down_use[...], preferred_element_type=jnp.float32).astype(jnp.bfloat16)
        store(g).start()

    steps = planes + 2
    per_step = -(-groups // (steps - 2))

    def filler(step):
        def body(i, _):
            @pl.when(step * per_step + i < groups)
            def _():
                one(step * per_step + i)
            return 0
        lax.fori_loop(0, per_step, body, 0)

    reduce_steps(planes, (entry_part, route_part), (entry_out, route_out), buffers, semaphores, filler)
    store(groups - 1).wait()


def entry_sums(entry_part, route_part, all_h, cot, active, grad_gate, grad_up, w_down, collective_id):
    planes = lax.axis_size("dp")
    partials = [entry_part, route_part]
    shapes, buffers, semaphores = reduce_scratch(partials, planes)
    (count, width), hidden, group = shapes[0][0], w_down.shape[0], 256
    low, wide, vmem, dma = jnp.bfloat16, jnp.float32, pltpu.VMEM, pltpu.SemaphoreType.DMA
    kept = pl.BlockSpec(memory_space=pltpu.VMEM)
    return pl.pallas_call(
        functools.partial(entry_kernel, planes),
        out_shape=[jax.ShapeDtypeStruct(shape, wide) for shape, _ in shapes] + [
            jax.ShapeDtypeStruct(entry_part.shape, low), jax.ShapeDtypeStruct((width, hidden), wide),
            jax.ShapeDtypeStruct((width, hidden), wide), jax.ShapeDtypeStruct((hidden, width), wide)],
        in_specs=[ANYSPEC] * 8, out_specs=[kept, kept, ANYSPEC, kept, kept, kept],
        scratch_shapes=buffers + semaphores + [
            vmem((hidden, width), low), vmem((2, group, width), low), vmem((2, group, width), low), vmem((2, 3, group, hidden), low),
            vmem((group, width), low), dma((1,)), dma((2, 5)), dma((1,))],
        compiler_params=pltpu.CompilerParams(collective_id=collective_id, has_side_effects=True, vmem_limit_bytes=60 * 2**20),
    )(entry_part, route_part, all_h, cot, active, grad_gate, grad_up, w_down)


def dot_plain(left, right):
    return jnp.dot(left, right, preferred_element_type=jnp.float32)


def dot_cols(left, right):
    return lax.dot_general(left, right, (((1,), (1,)), ((), ())), preferred_element_type=jnp.float32)


def dot_rows(left, right):
    return lax.dot_general(left, right, (((0,), (0,)), ((), ())), preferred_element_type=jnp.float32)


def group_peers():
    z, r, c = place()
    return r * 4 + c, [(z, r ^ (j >> 2), c ^ (j & 3)) for j in range(1, 8)]


def group_sums(own, slots, send_sem, recv_sem):
    here, peers = group_peers()
    copies = []
    for j, peer in enumerate(peers):
        copy = pltpu.make_async_remote_copy(
            src_ref=own, dst_ref=slots.at[j], send_sem=send_sem.at[j], recv_sem=recv_sem.at[j],
            device_id=peer, device_id_type=MESH)
        copy.start()
        copies.append(copy)
    for copy in copies:
        copy.wait()
    total = jnp.zeros(own.shape, jnp.float32)
    for who in range(8):
        which = here ^ who
        total = total + jnp.where(which == 0, own[...], slots[jnp.maximum(which - 1, 0)])
    return total


def row_of_tokens(values):
    folded = values[:, :128]
    for start in range(128, values.shape[1], 128):
        folded = folded + values[:, start:start + 128]
    return jnp.sum(folded.T, axis=0, keepdims=True)


def column_of(row):
    return jnp.broadcast_to(row, (128, row.shape[1])).T


BLOCK = 256


def block_weights(queries, keys, first, finish):
    scores = dot_cols(queries[first:finish], keys[:finish])
    at_query = lax.broadcasted_iota(jnp.int32, scores.shape, 0) + first
    at_key = lax.broadcasted_iota(jnp.int32, scores.shape, 1)
    scores = jnp.where(at_query >= at_key, scores, MASKED)
    weights = jnp.exp(scores - jnp.max(scores, axis=1, keepdims=True))
    return weights / jnp.sum(weights, axis=1, keepdims=True)


def forward_kernel(width, x_ref, proj_ref, gains, cosine, sine, w_out_ref,
                   part_out, query_out, key_out, value_out, raw_out, scale_out, mixed_out,
                   sums, slots, send_sem, recv_sem):
    greet(group_peers()[1])
    local = value_out.shape[1]
    raw = dot_plain(x_ref[...], proj_ref[...])
    raw_out[...] = raw[:, :2 * local]
    value_out[...] = raw[:, 2 * local:].astype(jnp.bfloat16)
    sums[...] = jnp.zeros(sums.shape, jnp.float32)
    for i in range(2):
        half = raw_out[:, pl.ds(i * local, local)]
        sums[pl.ds(i, 1), :] = row_of_tokens(half * half)
    total = group_sums(sums, slots, send_sem, recv_sem)
    for i, (target, factor) in enumerate(((query_out, 128 ** (-0.5)), (key_out, 1.0))):
        scale = lax.rsqrt(column_of(total[i:i + 1]) / width + EPSILON)
        scale_out[:, pl.ds(i * 128, 128)] = scale
        for start in range(0, local, 128):
            lanes = pl.ds(start, 128)
            normal = raw_out[:, pl.ds(i * local + start, 128)] * scale * gains[pl.ds(i, 1), lanes]
            turned = normal * cosine[...] + pltpu.roll(normal, 64, 1) * sine[...]
            target[:, lanes] = (turned * factor).astype(jnp.bfloat16)
    tokens = x_ref.shape[0]
    for start in range(0, local, 128):
        lanes = pl.ds(start, 128)
        queries, keys, values = query_out[:, lanes], key_out[:, lanes], value_out[:, lanes]
        for first in range(0, tokens, BLOCK):
            weights = block_weights(queries, keys, first, first + BLOCK).astype(jnp.bfloat16)
            mixed = dot_plain(weights, values[:first + BLOCK])
            mixed_out[pl.ds(first, BLOCK), lanes] = mixed.astype(jnp.bfloat16)
    part_out[...] = dot_plain(mixed_out[...], w_out_ref[...]).astype(jnp.bfloat16)


def attention_forward(gathered_x, w_proj, gains, cosine, sine, w_out_own, collective_id):
    tokens, width = gathered_x.shape
    local = w_proj.shape[1] // 3
    low, wide = jnp.bfloat16, jnp.float32
    shape, vmem = jax.ShapeDtypeStruct, pl.BlockSpec(memory_space=pltpu.VMEM)
    dma = pltpu.SemaphoreType.DMA
    return pl.pallas_call(
        functools.partial(forward_kernel, width),
        out_shape=[shape((tokens, width), low), shape((tokens, local), low), shape((tokens, local), low), shape((tokens, local), low),
                   shape((tokens, 2 * local), wide), shape((tokens, 256), wide), shape((tokens, local), low)],
        in_specs=[vmem] * 6, out_specs=[vmem] * 7,
        scratch_shapes=[pltpu.VMEM((8, tokens), wide), pltpu.VMEM((7, 8, tokens), wide), dma((7,)), dma((7,))],
        compiler_params=pltpu.CompilerParams(collective_id=collective_id, has_side_effects=True, vmem_limit_bytes=56 * 2**20),
    )(gathered_x, w_proj, gains, cosine, sine, w_out_own)


def backward_kernel(width, grad_ref, w_out_ref, x_hbm, proj_hbm, query_ref, key_ref, value_ref, raw_ref, scale_ref, mixed_ref,
                    gains, cosine, sine, grad_x_out, grad_proj_out, grad_out_out, gain_out,
                    x_ref, proj_ref, grad_query, grad_key, grad_value, grad_raw, sums, slots, load_sem, send_sem, recv_sem):
    greet(group_peers()[1])
    loads = [pltpu.make_async_copy(x_hbm, x_ref, load_sem.at[0]), pltpu.make_async_copy(proj_hbm, proj_ref, load_sem.at[1])]
    for load in loads:
        load.start()
    local, tokens = value_ref.shape[1], value_ref.shape[0]
    grad_mixed = dot_cols(grad_ref[...], w_out_ref[...]).astype(jnp.bfloat16)
    grad_raw[:, pl.ds(0, local)] = grad_mixed
    for start in range(0, local, 128):
        lanes = pl.ds(start, 128)
        queries, keys, values, upstream = query_ref[:, lanes], key_ref[:, lanes], value_ref[:, lanes], grad_raw[:, lanes]
        for first in reversed(range(0, tokens, BLOCK)):
            finish = first + BLOCK
            weights = block_weights(queries, keys, first, finish)
            grad_weights = dot_cols(upstream[first:finish], values[:finish])
            centre = jnp.sum(weights * grad_weights, axis=1, keepdims=True)
            grad_scores = (weights * (grad_weights - centre)).astype(jnp.bfloat16)
            grad_query[pl.ds(first, BLOCK), lanes] = dot_plain(grad_scores, keys[:finish])
            key_part = dot_rows(grad_scores, queries[first:finish])
            value_part = dot_rows(weights.astype(jnp.bfloat16), upstream[first:finish])
            if finish == tokens:
                grad_key[:, lanes] = key_part
                grad_value[:, lanes] = value_part
            else:
                grad_key[pl.ds(0, finish), lanes] += key_part
                grad_value[pl.ds(0, finish), lanes] += value_part
    sums[...] = jnp.zeros(sums.shape, jnp.float32)
    gain_out[...] = jnp.zeros(gain_out.shape, jnp.float32)
    for i, (grad, factor) in enumerate(((grad_query, 128 ** (-0.5)), (grad_key, 1.0))):
        scale = scale_ref[:, pl.ds(i * 128, 128)]
        inner = None
        for start in range(0, local, 128):
            lanes = pl.ds(start, 128)
            upstream = grad[:, lanes] * factor
            normal = upstream * cosine[...] - pltpu.roll(upstream, 64, 1) * sine[...]
            raw = raw_ref[:, pl.ds(i * local + start, 128)]
            gain_out[pl.ds(i, 1), lanes] = jnp.sum(normal * raw * scale, axis=0, keepdims=True)
            weighted = gains[pl.ds(i, 1), lanes] * normal
            grad[:, lanes] = weighted
            inner = weighted * raw if inner is None else inner + weighted * raw
        sums[pl.ds(i, 1), :] = row_of_tokens(inner)
    total = group_sums(sums, slots, send_sem, recv_sem)
    for i, grad in enumerate((grad_query, grad_key)):
        scale = scale_ref[:, pl.ds(i * 128, 128)]
        factor = scale * scale * scale * column_of(total[i:i + 1]) / width
        for start in range(0, local, 128):
            lanes = pl.ds(start, 128)
            raw = raw_ref[:, pl.ds(i * local + start, 128)]
            grad_raw[:, pl.ds(i * local + start, 128)] = (scale * grad[:, lanes] - raw * factor).astype(jnp.bfloat16)
    grad_raw[:, pl.ds(2 * local, local)] = grad_value[...].astype(jnp.bfloat16)
    for load in loads:
        load.wait()
    grad_x_out[...] = dot_cols(grad_raw[...], proj_ref[...]).astype(jnp.bfloat16)
    grad_proj_out[...] = dot_rows(x_ref[...], grad_raw[...]).astype(jnp.bfloat16)
    grad_out_out[...] = dot_rows(mixed_ref[...], grad_ref[...]).astype(jnp.bfloat16)


def attention_backward(grad_gathered, w_out_own, gathered_x, w_proj, kept, gains, cosine, sine, collective_id):
    tokens, width = gathered_x.shape
    local = w_proj.shape[1] // 3
    low, wide = jnp.bfloat16, jnp.float32
    shape, vmem = jax.ShapeDtypeStruct, pl.BlockSpec(memory_space=pltpu.VMEM)
    dma = pltpu.SemaphoreType.DMA
    return pl.pallas_call(
        functools.partial(backward_kernel, width),
        out_shape=[shape((tokens, width), low), shape(w_proj.shape, low), shape(w_out_own.shape, low), shape((8, local), wide)],
        in_specs=[vmem, vmem, ANYSPEC, ANYSPEC] + [vmem] * 9, out_specs=[vmem] * 4,
        scratch_shapes=[
            pltpu.VMEM(gathered_x.shape, low), pltpu.VMEM(w_proj.shape, low),
            pltpu.VMEM((tokens, local), wide), pltpu.VMEM((tokens, local), wide), pltpu.VMEM((tokens, local), wide),
            pltpu.VMEM((tokens, 3 * local), low), pltpu.VMEM((8, tokens), wide), pltpu.VMEM((7, 8, tokens), wide),
            dma((2,)), dma((7,)), dma((7,))],
        compiler_params=pltpu.CompilerParams(collective_id=collective_id, has_side_effects=True, vmem_limit_bytes=60 * 2**20),
    )(grad_gathered, w_out_own, gathered_x, w_proj, *kept, gains, cosine, sine)


HEAD_DIM = 128
SEQ_LEN = 1024
EPSILON = 1e-05
THETA = 10000.0
MASKED = -1e30
GROUP = ("row", "col")
EVERYONE = ("dp", "row", "col")


def on_links():
    return lax.axis_size("dp") == 4 and lax.axis_size("col") == 4 and lax.axis_size("row") == 2


def gather_tokens(arrays, everyone, collective_id, parts):
    if on_links():
        return gather(arrays, 4 if everyone else 1, collective_id, parts)
    axes = EVERYONE if everyone else GROUP
    return [lax.all_gather(a, axes, axis=0, tiled=True) for a in arrays]


def scatter_sums(arrays, everyone, collective_id):
    if on_links():
        return reduce_scatter(arrays, 4 if everyone else 1, collective_id)
    axes = EVERYONE if everyone else GROUP
    return [lax.psum_scatter(a, axes, scatter_dimension=0, tiled=True).astype(jnp.float32) for a in arrays]


def to_heads(w_query, w_key, w_value, w_out):
    if on_links():
        return exchange_weights(w_query, w_key, w_value, w_out, 1)
    pieces = [lax.all_to_all(w, "col", split_axis=1, concat_axis=0, tiled=True) for w in (w_query, w_key, w_value)]
    return jnp.concatenate(pieces, axis=1), lax.all_to_all(w_out, "col", split_axis=0, concat_axis=1, tiled=True)


def sum_over_heads(first_part, second_part, collective_id):
    if on_links():
        stacked = jnp.concatenate([first_part, second_part]).reshape(-1, 128)
        total = group_total(stacked, collective_id).reshape(2, -1)
        return total[0], total[1]
    return lax.psum((first_part, second_part), GROUP)


def inverse_rms(values):
    return lax.rsqrt(jnp.mean(values * values, axis=-1, keepdims=True) + EPSILON)


def norm_backward(values, inv_scale, gain_row, upstream):
    weighted = gain_row * upstream
    inner_sum = jnp.sum(weighted * values, axis=-1, keepdims=True)
    grad_values = inv_scale * weighted - values * inv_scale**3 * inner_sum / values.shape[-1]
    return (grad_values, jnp.sum(upstream * values * inv_scale, axis=0))


def contract(left, right):
    return jnp.dot(left, right, preferred_element_type=jnp.float32)


def contract_rows(left, right):
    return lax.dot_general(
        left, right, (((0,), (0,)), ((), ())), preferred_element_type=jnp.float32
    )


def contract_cols(left, right):
    return lax.dot_general(
        left, right, (((1,), (1,)), ((), ())), preferred_element_type=jnp.float32
    )


def turn_tables(total_rows, seq_length, head_width):
    positions = (jnp.arange(total_rows) % seq_length).astype(jnp.float32)
    inverse = THETA ** (-jnp.arange(0, head_width, 2, dtype=jnp.float32) / head_width)
    angles = positions[:, None] * inverse[None, :]
    angles = jnp.concatenate([angles, angles], axis=-1)
    return (jnp.cos(angles)[:, None, :], jnp.sin(angles)[:, None, :])


def rotate(values, cosine, sine_table):
    middle = values.shape[-1] // 2
    turned = jnp.concatenate([-values[..., middle:], values[..., :middle]], axis=-1)
    return values * cosine + turned * sine_table


def unrotate(upstream, cosine, sine_table):
    middle = upstream.shape[-1] // 2
    turned_part = upstream * sine_table
    return upstream * cosine + jnp.concatenate(
        [turned_part[..., middle:], -turned_part[..., :middle]], axis=-1
    )


def attend_forward(queries, key_rows, value_rows):
    length = queries.shape[0]
    block_rows = min(512, length)
    outputs = []
    sums_log = []
    for first_row in range(0, length, block_rows):
        finish = first_row + block_rows
        scores = jnp.einsum(
            "qhd,khd->hqk",
            queries[first_row:finish],
            key_rows[:finish],
            preferred_element_type=jnp.float32,
        )
        causal = (first_row + jnp.arange(block_rows))[:, None] >= jnp.arange(finish)[None, :]
        scores = jnp.where(causal[None], scores, MASKED)
        highest = jnp.max(scores, axis=-1, keepdims=True)
        weights = jnp.exp(scores - highest)
        totals = jnp.sum(weights, axis=-1, keepdims=True)
        weights = (weights / totals).astype(jnp.bfloat16)
        outputs.append(
            jnp.einsum(
                "hqk,khd->qhd", weights, value_rows[:finish], preferred_element_type=jnp.float32
            )
        )
        sums_log.append((highest + jnp.log(totals))[..., 0])
    return (jnp.concatenate(outputs, axis=0), jnp.concatenate(sums_log, axis=1))


def attend_backward(queries, key_rows, value_rows, grad_out, sums_log):
    length = queries.shape[0]
    block_rows = min(512, length)
    grad_queries = []
    grad_keys = jnp.zeros(key_rows.shape, jnp.float32)
    grad_values = jnp.zeros(value_rows.shape, jnp.float32)
    for first_row in range(0, length, block_rows):
        finish = first_row + block_rows
        scores = jnp.einsum(
            "qhd,khd->hqk",
            queries[first_row:finish],
            key_rows[:finish],
            preferred_element_type=jnp.float32,
        )
        causal = (first_row + jnp.arange(block_rows))[:, None] >= jnp.arange(finish)[None, :]
        scores = jnp.where(causal[None], scores, MASKED)
        weights = jnp.exp(scores - sums_log[:, first_row:finish, None])
        grad_weights = jnp.einsum(
            "qhd,khd->hqk",
            grad_out[first_row:finish],
            value_rows[:finish],
            preferred_element_type=jnp.float32,
        )
        centre = jnp.sum(weights * grad_weights, axis=-1, keepdims=True)
        grad_scores = (weights * (grad_weights - centre)).astype(jnp.bfloat16)
        grad_queries.append(
            jnp.einsum(
                "hqk,khd->qhd", grad_scores, key_rows[:finish], preferred_element_type=jnp.float32
            )
        )
        grad_keys = grad_keys.at[:finish].add(
            jnp.einsum(
                "hqk,qhd->khd",
                grad_scores,
                queries[first_row:finish],
                preferred_element_type=jnp.float32,
            )
        )
        grad_values = grad_values.at[:finish].add(
            jnp.einsum(
                "hqk,qhd->khd",
                weights.astype(jnp.bfloat16),
                grad_out[first_row:finish],
                preferred_element_type=jnp.float32,
            )
        )
    return (jnp.concatenate(grad_queries, axis=0), grad_keys, grad_values)


def by_sequence(step, pieces, sequences):
    if sequences == 1:
        return tuple(out[None] for out in step(*[p[0] for p in pieces]))
    return lax.map(lambda each: step(*each), tuple(pieces))


def expert_rows(normal_h, side, cotangent, gate_use, up_use, down_use, expert_count):
    all_cotangent = lax.all_gather(cotangent, EVERYONE, axis=0, tiled=True)
    if on_links():
        rows_h, _, entry_part, grad_side, active_share, grad_gate_rows, grad_up_rows = expert_rows_on_links(
            normal_h, side, all_cotangent, gate_use, up_use, down_use, expert_count, 6
        )
        entry_rows, grad_probs_all, out_part, *grads = entry_sums(
            entry_part, grad_side, rows_h, all_cotangent, active_share, grad_gate_rows, grad_up_rows, down_use, 7
        )
        return (entry_rows, grad_probs_all, out_part, *grads)
    rows_h, rows_side = gather_tokens([normal_h, side], True, 6, 2)
    expert = lax.axis_index("dp") * lax.axis_size("col") + lax.axis_index("col")
    lane = jnp.arange(side.shape[1])
    own_share = jnp.sum(
        jnp.where((lane == expert) | (lane == expert + expert_count), rows_side.astype(jnp.float32), 0.0),
        axis=1,
        keepdims=True,
    )
    back_rows = contract_cols(all_cotangent, down_use)
    gate_rows = contract(rows_h, gate_use)
    up_rows = contract(rows_h, up_use)
    sigmoid_gate = jax.nn.sigmoid(gate_rows)
    silu_gate = gate_rows * sigmoid_gate
    active = silu_gate * up_rows
    route_grad = jnp.sum(active * back_rows, axis=1, keepdims=True)
    active_share = (own_share * active).astype(jnp.bfloat16)
    grad_active = own_share * back_rows
    grad_gate_rows = (
        grad_active * up_rows * sigmoid_gate * (1.0 + gate_rows * (1.0 - sigmoid_gate))
    ).astype(jnp.bfloat16)
    grad_up_rows = (grad_active * silu_gate).astype(jnp.bfloat16)
    entry_part = (contract_cols(grad_gate_rows, gate_use) + contract_cols(grad_up_rows, up_use)).astype(jnp.bfloat16)
    grad_side = jnp.where(jnp.arange(128 if expert_count <= 128 else expert_count)[None, :] == expert, route_grad, 0.0).astype(jnp.bfloat16)
    entry_rows, grad_probs_all = scatter_sums([entry_part, grad_side], True, 7)
    out_part = contract(active_share, down_use).astype(jnp.bfloat16)
    (mixture,) = scatter_sums([out_part], True, 8)
    grad_down_w = contract_rows(active_share, all_cotangent)
    grad_gate_w = contract_rows(rows_h, grad_gate_rows)
    grad_up_w = contract_rows(rows_h, grad_up_rows)
    return entry_rows, grad_probs_all, mixture, grad_gate_w, grad_up_w, grad_down_w


def per_device(
    hidden_in,
    cotangent,
    norm_attn,
    w_query,
    w_key,
    w_value,
    query_gain,
    key_gain,
    w_out,
    norm_moe,
    w_router,
    w_gate,
    w_up,
    w_down,
    routes,
):
    inputs = hidden_in.astype(jnp.float32)
    upstream = cotangent.astype(jnp.float32)
    token_count, top_count = routes.shape
    model_width = inputs.shape[1]
    expert_count = w_router.shape[1]

    inv_input = inverse_rms(inputs)
    normal_x = (inputs * inv_input * norm_attn).astype(jnp.bfloat16)
    w_proj, w_out_own = to_heads(w_query, w_key, w_value, w_out)
    (gathered_x,) = gather_tokens([normal_x], False, 2, 2)
    group_tokens = gathered_x.shape[0]
    local_width = w_proj.shape[1] // 3
    head_count = local_width // HEAD_DIM
    offset = (lax.axis_index("row") * lax.axis_size("col") + lax.axis_index("col")) * local_width
    gain_query = lax.dynamic_slice_in_dim(query_gain, offset, local_width)
    gain_key = lax.dynamic_slice_in_dim(key_gain, offset, local_width)
    cosine, sine_table = turn_tables(group_tokens, SEQ_LEN, HEAD_DIM)
    head_shape = (group_tokens, head_count, HEAD_DIM)
    sequences = group_tokens // SEQ_LEN
    seq_shape = (sequences, SEQ_LEN, head_count, HEAD_DIM)
    in_kernels = on_links() and sequences == 1
    if in_kernels:
        gains = jnp.concatenate([gain_query[None], gain_key[None], jnp.zeros((6, local_width), jnp.float32)])
        sine_signed = jnp.where(jnp.arange(HEAD_DIM) < HEAD_DIM // 2, -sine_table[:, 0], sine_table[:, 0])
        tables = (gains, cosine[:, 0], sine_signed)
        attn_part, *kept = attention_forward(gathered_x, w_proj, *tables, w_out_own, 4)
    else:
        raw = contract(gathered_x, w_proj)
        query_raw = raw[:, :local_width]
        key_raw = raw[:, local_width : 2 * local_width]
        value_heads = raw[:, 2 * local_width :].astype(jnp.bfloat16)
        query_square, key_square = sum_over_heads(
            jnp.sum(query_raw * query_raw, axis=-1), jnp.sum(key_raw * key_raw, axis=-1), 4
        )
        inv_query = lax.rsqrt(query_square / model_width + EPSILON)[:, None]
        inv_key = lax.rsqrt(key_square / model_width + EPSILON)[:, None]
        query_heads = (
            rotate((query_raw * inv_query * gain_query).reshape(head_shape), cosine, sine_table)
            * HEAD_DIM ** (-0.5)
        ).astype(jnp.bfloat16)
        key_heads = rotate(
            (key_raw * inv_key * gain_key).reshape(head_shape), cosine, sine_table
        ).astype(jnp.bfloat16)
        query_seq = query_heads.reshape(seq_shape)
        key_seq = key_heads.reshape(seq_shape)
        value_seq = value_heads.reshape(seq_shape)
        mixed, sums_log = by_sequence(attend_forward, (query_seq, key_seq, value_seq), sequences)
        mixed_heads = mixed.reshape(group_tokens, local_width).astype(jnp.bfloat16)
        attn_part = contract(mixed_heads, w_out_own).astype(jnp.bfloat16)
    (attn_rows,) = scatter_sums([attn_part], False, 5)
    state_rows = inputs + attn_rows

    inv_state = inverse_rms(state_rows)
    normal_h = (state_rows * inv_state * norm_moe).astype(jnp.bfloat16)
    logits = contract(normal_h, w_router)
    shifted = jnp.exp(logits - jnp.max(logits, axis=-1, keepdims=True))
    probabilities = shifted / jnp.sum(shifted, axis=-1, keepdims=True)
    selected = jnp.sum(
        (routes[:, :, None] == jnp.arange(expert_count)[None, None, :]).astype(jnp.float32), axis=1
    )
    shares = probabilities * selected
    share_high = shares.astype(jnp.bfloat16)
    share_low = (shares - share_high.astype(jnp.float32)).astype(jnp.bfloat16)
    side_width = max(2 * expert_count, 128)
    side = jnp.concatenate(
        [
            share_high,
            share_low,
            jnp.zeros((token_count, side_width - 2 * expert_count), jnp.bfloat16),
        ],
        axis=1,
    )

    chunks = max(1, lax.axis_size(EVERYONE) // 32)
    if chunks == 1:
        entry_rows, grad_probs_all, mixture, *expert_grads = expert_rows(
            normal_h, side, cotangent, w_gate[0], w_up[0], w_down[0], expert_count
        )
    else:

        def piece_step(sums, piece):
            entry, probs, mixed_rows, *grads = expert_rows(*piece, w_gate[0], w_up[0], w_down[0], expert_count)
            return [s + g for s, g in zip(sums, grads)], (entry, probs, mixed_rows)

        cut = [a.reshape((chunks, token_count // chunks) + a.shape[1:]) for a in (normal_h, side, cotangent)]
        empty = [jnp.zeros(w.shape[1:], jnp.float32) for w in (w_gate, w_up, w_down)]
        expert_grads, rows = lax.scan(piece_step, empty, cut)
        entry_rows, grad_probs_all, mixture = [r.reshape((token_count,) + r.shape[2:]) for r in rows]
    grad_gate_w, grad_up_w, grad_down_w = expert_grads
    grad_probs = selected * grad_probs_all[:, :expert_count]
    grad_logits = (
        probabilities * (grad_probs - jnp.sum(probabilities * grad_probs, axis=-1, keepdims=True))
    ).astype(jnp.bfloat16)
    grad_normal_h = entry_rows + contract_cols(grad_logits, w_router)
    grad_router_part = contract_rows(normal_h, grad_logits)
    grad_state_part, grad_moe_part = norm_backward(state_rows, inv_state, norm_moe, grad_normal_h)
    grad_state = upstream + grad_state_part
    grad_attn = grad_state.astype(jnp.bfloat16)
    (grad_gathered,) = gather_tokens([grad_attn], False, 9, 2)
    if in_kernels:
        grad_x_part, grad_proj_own, grad_out_own, gain_parts = attention_backward(
            grad_gathered, w_out_own, gathered_x, w_proj, kept, *tables, 10
        )
        grad_qgain_part, grad_kgain_part = gain_parts[0], gain_parts[1]
    else:
        grad_out_own = contract_rows(mixed_heads, grad_gathered).astype(jnp.bfloat16)
        grad_mixed = contract_cols(grad_gathered, w_out_own).astype(jnp.bfloat16)
        grad_query_seq, grad_key_seq, grad_value_seq = by_sequence(
            attend_backward,
            (query_seq, key_seq, value_seq, grad_mixed.reshape(seq_shape), sums_log),
            sequences,
        )
        grad_normal_q = unrotate(
            grad_query_seq.reshape(head_shape) * HEAD_DIM ** (-0.5), cosine, sine_table
        ).reshape(group_tokens, local_width)
        grad_normal_k = unrotate(grad_key_seq.reshape(head_shape), cosine, sine_table).reshape(
            group_tokens, local_width
        )
        weighted_q = gain_query * grad_normal_q
        weighted_k = gain_key * grad_normal_k
        inner_q, inner_k = sum_over_heads(
            jnp.sum(weighted_q * query_raw, axis=-1), jnp.sum(weighted_k * key_raw, axis=-1), 10
        )
        grad_query_raw = (
            inv_query * weighted_q - query_raw * inv_query**3 * inner_q[:, None] / model_width
        )
        grad_key_raw = inv_key * weighted_k - key_raw * inv_key**3 * inner_k[:, None] / model_width
        grad_qgain_part = jnp.sum(grad_normal_q * query_raw * inv_query, axis=0)
        grad_kgain_part = jnp.sum(grad_normal_k * key_raw * inv_key, axis=0)
        grad_raw = jnp.concatenate(
            [grad_query_raw, grad_key_raw, grad_value_seq.reshape(group_tokens, local_width)], axis=1
        ).astype(jnp.bfloat16)
        grad_x_part = contract_cols(grad_raw, w_proj).astype(jnp.bfloat16)
        grad_proj_own = contract_rows(gathered_x, grad_raw).astype(jnp.bfloat16)
    full_width = query_gain.shape[0]
    padded_qgain = lax.dynamic_update_slice_in_dim(
        jnp.zeros((full_width,), jnp.float32), grad_qgain_part, offset, 0
    )
    padded_kgain = lax.dynamic_update_slice_in_dim(
        jnp.zeros((full_width,), jnp.float32), grad_kgain_part, offset, 0
    )
    small = (padded_qgain, padded_kgain, grad_moe_part, grad_router_part)
    grad_query, grad_key, grad_value, grad_out_proj, mixture, grad_normal_x, small = last_sums(
        grad_proj_own, grad_out_own, small, inputs * inv_input, mixture, grad_x_part
    )
    grad_norm_attn, grad_query_gain, grad_key_gain, grad_norm_moe, grad_router = small
    block_out = (state_rows + mixture).astype(jnp.bfloat16)
    grad_input = grad_state + norm_backward(inputs, inv_input, norm_attn, grad_normal_x)[0]
    return (
        block_out,
        grad_input,
        grad_norm_attn,
        grad_query,
        grad_key,
        grad_value,
        grad_query_gain,
        grad_key_gain,
        grad_out_proj,
        grad_norm_moe,
        grad_router,
        grad_gate_w[None],
        grad_up_w[None],
        grad_down_w[None],
    )


def last_sums(grad_proj_own, grad_out_own, small, scaled, mixed_part, entry_part):
    if on_links():
        parts = (jnp.zeros((scaled.shape[1],), jnp.float32), *small)
        flat = jnp.concatenate([part.reshape(-1) for part in parts])
        proj, outp, total, mixture, grad_normal_x = finish(
            grad_proj_own, grad_out_own, flat.reshape(8, -1, 128), scaled, mixed_part, entry_part, lax.axis_size("dp"), 12
        )
        total, sums, start = total.reshape(-1), [], 0
        for part in parts:
            sums.append(total[start : start + part.size].reshape(part.shape))
            start += part.size
        return (*(proj[a].astype(jnp.float32) for a in range(3)), outp.astype(jnp.float32), mixture, grad_normal_x, sums)
    (grad_normal_x,) = scatter_sums([entry_part], False, 11)
    small = (jnp.sum(grad_normal_x * scaled, axis=0), *small)
    width = grad_proj_own.shape[1] // 3
    blocks = [
        lax.all_to_all(grad_proj_own[:, a * width : (a + 1) * width], "col", split_axis=0, concat_axis=1, tiled=True)
        for a in range(3)
    ]
    out_block = lax.all_to_all(grad_out_own, "col", split_axis=1, concat_axis=0, tiled=True)
    weights = [total.astype(jnp.float32) for total in lax.psum((*blocks, out_block), "dp")]
    return (*weights, mixed_part, grad_normal_x, lax.psum(small, EVERYONE))


def solution(mesh):
    placed = (
        P(("dp", "row", "col"), None),
        P(("dp", "row", "col"), None),
        P(),
        P("col", "row"),
        P("col", "row"),
        P("col", "row"),
        P(),
        P(),
        P("row", "col"),
        P(),
        P(),
        P(("dp", "col"), None, "row"),
        P(("dp", "col"), None, "row"),
        P(("dp", "col"), "row", None),
        P(("dp", "row", "col"), None),
    )
    return jax.shard_map(
        per_device,
        mesh=mesh,
        in_specs=placed,
        out_specs=(
            P(("dp", "row", "col"), None),
            P(("dp", "row", "col"), None),
            P(),
            P("col", "row"),
            P("col", "row"),
            P("col", "row"),
            P(),
            P(),
            P("row", "col"),
            P(),
            P(),
            P(("dp", "col"), None, "row"),
            P(("dp", "col"), None, "row"),
            P(("dp", "col"), "row", None),
        ),
        check_vma=False,
    )
```

```python
import functools

import jax
import jax.numpy as jnp
from jax import lax
from jax.experimental import pallas as pl
from jax.experimental.pallas import tpu as pltpu
from jax.sharding import PartitionSpec as P

MESH = pl.DeviceIdType.MESH
ANYSPEC = pl.BlockSpec(memory_space=pl.ANY)

def place():
    return lax.axis_index("dp"), lax.axis_index("row"), lax.axis_index("col")

def greet(peers):
    barrier = pltpu.get_barrier_semaphore()
    for peer in peers:
        pl.semaphore_signal(barrier, inc=1, device_id=peer, device_id_type=MESH)
    pl.semaphore_wait(barrier, len(peers))

def gather_kernel(planes, parts, count, *refs):
    ins, outs = refs[:count], refs[count:2 * count]
    own_sem, send_sem, recv_sem = refs[2 * count:]
    z, r, c = place()
    first, second, diag = c ^ (1 + r), c ^ (2 - r), c ^ 3
    partner = (z, 1 - r, c)
    to_first, to_second = (z, r, first), (z, r, second)
    greet([to_first, to_second, partner] + [(z ^ k, r, c) for k in range(1, planes)])
    pieces = []
    for a in range(count):
        cut = parts if a == 0 else 1
        pieces += [(a, p, ins[a].shape[0], ins[a].shape[0] // cut) for p in range(cut)]

    def number(zz, rr, cc):
        return ((zz if planes > 1 else 0) * 2 + rr) * 4 + cc

    def place_of(i, which):
        a, p, depth, cut = pieces[i]
        return outs[a].at[pl.ds(pl.multiple_of(which * depth + p * cut, cut), cut)]

    sent = [[] for _ in pieces]

    def send(i, which, target, own=False):
        a, p, depth, cut = pieces[i]
        spot = place_of(i, which)
        copy = pltpu.make_async_remote_copy(
            src_ref=ins[a].at[pl.ds(p * cut, cut)] if own else spot, dst_ref=spot,
            send_sem=send_sem.at[i, len(sent[i])], recv_sem=recv_sem.at[i, which],
            device_id=target, device_id_type=MESH)
        copy.start()
        sent[i].append(copy)

    def await_block(i, which):
        spot = place_of(i, which)
        pltpu.make_async_remote_copy(
            src_ref=spot, dst_ref=spot, send_sem=send_sem.at[i, 0], recv_sem=recv_sem.at[i, which],
            device_id=partner, device_id_type=MESH).wait_recv()

    mine = number(z, r, c)
    keeps = []
    every = range(len(pieces))
    for i in every:
        for target in [to_first, to_second] + [(z ^ k, r, c) for k in range(1, planes)] + [partner]:
            send(i, mine, target, True)
    for a in range(count):
        keep = pltpu.make_async_copy(ins[a], outs[a].at[pl.ds(pl.multiple_of(mine * ins[a].shape[0], ins[a].shape[0]), ins[a].shape[0])], own_sem.at[a])
        keep.start()
        keeps.append(keep)

    def forward(which, targets):
        for i in every:
            await_block(i, which)
            for target in targets:
                send(i, which, target)

    for step in range(planes + 2):
        if 0 < step < planes:
            forward(number(z ^ step, r, c), [to_first, to_second, partner])
        if 0 <= step - 1 < planes:
            forward(number(z ^ (step - 1), r, first), [to_second, partner])
            forward(number(z ^ (step - 1), r, second), [partner])
        if 0 <= step - 2 < planes:
            forward(number(z ^ (step - 2), r, diag), [partner])
    for k in range(planes):
        for j in range(4):
            for i in every:
                await_block(i, number(z ^ k, 1 - r, c ^ j))
    for keep in keeps:
        keep.wait()
    for copies in sent:
        for copy in copies:
            copy.wait_send()

def gather(arrays, planes, collective_id, parts=1):
    count = len(arrays)
    blocks = planes * 8
    sends = (3 + planes - 1) + (planes - 1) * 3 + planes * 4
    pieces = count - 1 + parts
    return pl.pallas_call(
        functools.partial(gather_kernel, planes, parts, count),
        out_shape=[jax.ShapeDtypeStruct((blocks * a.shape[0],) + a.shape[1:], a.dtype) for a in arrays],
        in_specs=[ANYSPEC] * count, out_specs=[ANYSPEC] * count,
        scratch_shapes=[pltpu.SemaphoreType.DMA((count,)), pltpu.SemaphoreType.DMA((pieces, sends)), pltpu.SemaphoreType.DMA((pieces, blocks))],
        compiler_params=pltpu.CompilerParams(collective_id=collective_id, has_side_effects=True),
    )(*arrays)

def reducer(planes, parts, outs, buffers, semaphores):
    held, fromp, relay, near, far = buffers
    load_sem, pair_send, pair_recv, send_sem, relay_recv, near_recv, far_recv = semaphores
    z, r, c = place()
    first, second, diag = c ^ (1 + r), c ^ (2 - r), c ^ 3
    partner = (z, 1 - r, c)
    to_first, to_second = (z, r, first), (z, r, second)
    depth = outs[0].shape[0]
    every = range(len(parts))

    def rows(a, k, rr, cc):
        which = (((z ^ k) if planes > 1 else 0) * 2 + rr) * 4 + cc
        return parts[a].at[pl.ds(pl.multiple_of(which * depth, depth), depth)]

    columns, partner_columns = [c, first, second, diag], [c, second, first, diag]

    def remote(source, target, send, recv, device):
        return pltpu.make_async_remote_copy(
            src_ref=source, dst_ref=target, send_sem=send, recv_sem=recv, device_id=device, device_id_type=MESH)

    def load(a, k, j):
        return pltpu.make_async_copy(rows(a, k, r, columns[j]), held[a].at[k, j], load_sem.at[a, k, j])

    def pair(a, k, j):
        return remote(rows(a, k, 1 - r, partner_columns[j]), fromp[a].at[k, j], pair_send.at[a, k, j], pair_recv.at[a, k, j], partner)

    def begin(i, _):
        k = planes - 1 - i
        for j in (3, 2, 1, 0):
            for a in every:
                load(a, k, j).start()
                pair(a, k, j).start()
        return 0

    step_rows = min(32, depth)

    def add(target, sources):
        def body(i, _):
            at = pl.ds(pl.multiple_of(i * step_rows, step_rows), step_rows)
            total = sources[0][at].astype(jnp.float32)
            for source in sources[1:]:
                total = total + source[at].astype(jnp.float32)
            target[at] = total.astype(target.dtype)
            return 0
        lax.fori_loop(0, depth // step_rows, body, 0)

    def ready(a, k, j):
        load(a, k, j).wait()
        pair(a, k, j).wait_recv()

    def to_diag(a, k):
        return remote(held[a].at[k, 3], relay[a].at[k], send_sem.at[a, k, 0], relay_recv.at[a, k], to_second)

    def to_near(a, k, which):
        source, device = (held[a].at[k, 2], to_second) if which else (held[a].at[k, 1], to_first)
        return remote(source, near[a].at[k, which], send_sem.at[a, k, 1 + which], near_recv.at[a, k, which], device)

    def to_far(a, k):
        slot = jnp.maximum(k - 1, 0)
        return remote(held[a].at[k, 0], far[a].at[slot], send_sem.at[a, k, 3], far_recv.at[a, slot], (z ^ k, r, c))

    def to_relay(k):
        for a in every:
            ready(a, k, 3)
            add(held[a].at[k, 3], [held[a].at[k, 3], fromp[a].at[k, 3]])
            to_diag(a, k).start()
        for a in every:
            ready(a, k, 2)
            add(held[a].at[k, 2], [held[a].at[k, 2], fromp[a].at[k, 2]])
            to_near(a, k, 1).start()

    def pass_on(k):
        for a in every:
            ready(a, k, 1)
            to_diag(a, k).wait_recv()
            add(held[a].at[k, 1], [held[a].at[k, 1], fromp[a].at[k, 1], relay[a].at[k]])
            to_near(a, k, 0).start()

    def collect(k):
        for a in every:
            ready(a, k, 0)
            to_near(a, k, 0).wait_recv()
            to_near(a, k, 1).wait_recv()
            terms = [held[a].at[k, 0], fromp[a].at[k, 0], near[a].at[k, 0], near[a].at[k, 1]]

            @pl.when(k > 0)
            def _():
                add(held[a].at[k, 0], terms)
                to_far(a, k).start()

            @pl.when(k == 0)
            def _():
                for i in range(1, planes):
                    to_far(a, i).wait_recv()
                add(outs[a], terms + [far[a].at[i] for i in range(planes - 1)])

    def drain(k, _):
        for a in every:
            for j in range(4):
                pair(a, k, j).wait_send()
            to_diag(a, k).wait_send()
            to_near(a, k, 0).wait_send()
            to_near(a, k, 1).wait_send()

            @pl.when(k > 0)
            def _():
                to_far(a, k).wait_send()
        return 0

    return begin, to_relay, pass_on, collect, drain


def reduce_steps(planes, parts, outs, buffers, semaphores, filler):
    z, r, c = place()
    greet([(z, r, c ^ 1), (z, r, c ^ 2), (z, 1 - r, c)] + [(z ^ k, r, c) for k in range(1, planes)])
    begin, to_relay, pass_on, collect, drain = reducer(planes, parts, outs, buffers, semaphores)
    lax.fori_loop(0, planes, begin, 0)

    def step_body(step, _):
        @pl.when(step < planes)
        def _():
            to_relay(planes - 1 - step)

        @pl.when(jnp.logical_and(step >= 1, step < planes + 1))
        def _():
            pass_on(planes - step)

        @pl.when(step >= 2)
        def _():
            collect(planes + 1 - step)
        if filler is not None:
            filler(step)
        return 0

    lax.fori_loop(0, planes + 2, step_body, 0)
    lax.fori_loop(0, planes, drain, 0)


def reduce_scratch(partials, planes):
    shapes = [((p.shape[0] // (planes * 8), p.shape[1]), p.dtype) for p in partials]
    count, far = len(partials), max(planes - 1, 1)
    dma = pltpu.SemaphoreType.DMA
    buffers = [pltpu.VMEM(lead + shape, kind) for lead in ((planes, 4), (planes, 4), (planes,), (planes, 2), (far,)) for shape, kind in shapes]
    return shapes, buffers, [
        dma((count, planes, 4)), dma((count, planes, 4)), dma((count, planes, 4)), dma((count, planes, 4)),
        dma((count, planes)), dma((count, planes, 2)), dma((count, far))]


def reduce_kernel(planes, count, *refs):
    buffers = [refs[(2 + i) * count:(3 + i) * count] for i in range(5)]
    reduce_steps(planes, refs[:count], refs[count:2 * count], buffers, refs[7 * count:], None)


def reduce_scatter(partials, planes, collective_id):
    count = len(partials)
    shapes, buffers, semaphores = reduce_scratch(partials, planes)
    return pl.pallas_call(
        functools.partial(reduce_kernel, planes, count),
        out_shape=[jax.ShapeDtypeStruct(shape, jnp.float32) for shape, _ in shapes],
        in_specs=[ANYSPEC] * count, out_specs=[pl.BlockSpec(memory_space=pltpu.VMEM)] * count,
        scratch_shapes=buffers + semaphores,
        compiler_params=pltpu.CompilerParams(collective_id=collective_id, has_side_effects=True, vmem_limit_bytes=48 * 2**20),
    )(*partials)


def exchange_kernel(wq_ref, wk_ref, wv_ref, proj_ref, own_sem, send_sem, recv_sem):
    z, r, c = place()
    width = proj_ref.shape[1] // 3
    depth = wq_ref.shape[0]
    greet([(z, r, c ^ j) for j in range(1, 4)])

    def source(a, target):
        return (wq_ref, wk_ref, wv_ref)[a].at[:, pl.ds(pl.multiple_of(target * width, width), width)]

    def spot(a, origin):
        return proj_ref.at[pl.ds(pl.multiple_of(origin * depth, depth), depth), pl.ds(a * width, width)]

    waits = []
    for a in range(3):
        keep = pltpu.make_async_copy(source(a, c), spot(a, c), own_sem.at[a])
        keep.start()
        waits.append(keep.wait)
        for j in range(1, 4):
            copy = pltpu.make_async_remote_copy(
                src_ref=source(a, c ^ j), dst_ref=spot(a, c), send_sem=send_sem.at[a, j - 1],
                recv_sem=recv_sem.at[a, j - 1], device_id=(z, r, c ^ j), device_id_type=MESH)
            copy.start()
            waits.append(copy.wait_send)
    for a in range(3):
        for j in range(1, 4):
            arrived = spot(a, c ^ j)
            pltpu.make_async_remote_copy(
                src_ref=arrived, dst_ref=arrived, send_sem=send_sem.at[a, j - 1], recv_sem=recv_sem.at[a, j - 1],
                device_id=(z, r, c ^ j), device_id_type=MESH).wait_recv()
    for wait in waits:
        wait()


def exchange_weights(w_query, w_key, w_value, collective_id):
    depth, half = w_query.shape
    dma = pltpu.SemaphoreType.DMA
    return pl.pallas_call(
        exchange_kernel,
        out_shape=jax.ShapeDtypeStruct((depth * 4, 3 * (half // 4)), w_query.dtype),
        in_specs=[ANYSPEC] * 3, out_specs=ANYSPEC,
        scratch_shapes=[dma((3,)), dma((3, 3)), dma((3, 3))],
        compiler_params=pltpu.CompilerParams(collective_id=collective_id, has_side_effects=True),
    )(w_query, w_key, w_value)


NEAR, SMALL, WIDE, LAG, AHEAD = (8, 16, 24), (24, 30, 36), (2, 4, 4), 3, 8


def finish_kernel(planes, proj_ref, outp_ref, small_ref, scaled_ref, mixed_part, entry_part,
                  proj_out, outp_out, small_out, mixed_out, entry_out, *scratch):
    (proj_own, outp_own, proj_in, outp_in, proj_far, outp_far, small_own, slices, far_slices, own_sem, swap_send, swap_recv, down_send, down_recv,
     far_down, up_send, up_recv, slice_send, slice_recv, far_send, far_recv, whole_send, whole_recv) = scratch[:23]
    halves = 2
    share = mixed_out.shape[1] // halves
    wides = []
    for h in range(halves):
        cols = pl.ds(h * share, share)
        buffers = [(ref.at[:, :, :, cols],) if i in (0, 1, 3) else (ref.at[:, :, cols],) for i, ref in enumerate(scratch[23:28])]
        wides.append(reducer(planes, (mixed_part.at[:, cols],), (mixed_out.at[:, cols],), buffers, [ref.at[h:h + 1] for ref in scratch[28:35]]))
    near = reducer(1, (entry_part,), (entry_out,), [(ref,) for ref in scratch[35:40]], scratch[40:47])
    z, r, c = place()
    here = r * 4 + c
    group = [(z, r ^ (j >> 2), c ^ (j & 3)) for j in range(1, 8)]
    greet(group + [(z ^ k, r, c) for k in range(1, planes)])
    width = proj_ref.shape[1] // 3
    depth, out_width = proj_ref.shape[0] // 4, outp_ref.shape[1] // 4
    step, tall = depth // 8, outp_ref.shape[0] // 2
    chunks = 32

    def remote(source, target, send, recv, device):
        return pltpu.make_async_remote_copy(
            src_ref=source, dst_ref=target, send_sem=send, recv_sem=recv, device_id=device, device_id_type=MESH)

    def owner(i):
        return (i - 24) // 2

    def piece(i, target):
        if i < 24:
            a, m = i // 8, i % 8
            return proj_ref.at[pl.ds(pl.multiple_of(target * depth + m * step, step), step), pl.ds(a * width, width)]
        return outp_ref.at[pl.ds((i % 2) * tall, tall), pl.ds(pl.multiple_of(target * out_width, out_width), out_width)]

    def spot(i, origin):
        a, m = i // 8, i % 8
        return proj_own.at[a, pl.ds(m * step, step), pl.ds(pl.multiple_of(origin * width, width), width)]

    def rows(proj, outp, i):
        if i < 24:
            return proj.at[i // 8, pl.ds((i % 8) * step, step), :]
        return outp.at[pl.ds((i - 24) * tall, tall), :]

    small_copies = []

    def small_begin():
        lanes = small_ref.shape[2]
        small_own[...] = small_ref[...]
        for j in range(entry_out.shape[1] // lanes):
            at = pl.ds(j * lanes, lanes)
            part = jnp.sum(entry_out[:, at] * scaled_ref[:, at], axis=0, keepdims=True)
            small_own[j // small_ref.shape[1], pl.ds(j % small_ref.shape[1], 1), :] = part
        for j in range(1, 8):
            copy = remote(small_own.at[here ^ j], slices.at[here], slice_send.at[j], slice_recv.at[here], group[j - 1])
            copy.start()
            small_copies.append(copy)

    order = [24, 25, 0, 1, 26, 27, 2, 3, 28, 29, 4, 5, 30, 31] + list(range(6, 24))
    swaps = []

    def issue(i):
        if i < 24:
            keep = pltpu.make_async_copy(piece(i, c), spot(i, c), own_sem.at[i])
            keep.start()
            for j in range(1, 4):
                copy = remote(piece(i, c ^ j), spot(i, c), swap_send.at[i, j - 1], swap_recv.at[i, j - 1], (z, r, c ^ j))
                copy.start()
                swaps.append(copy)
        else:
            @pl.when(c == owner(i))
            def _():
                pltpu.make_async_copy(piece(i, c), rows(proj_own, outp_own, i), own_sem.at[i]).start()
                for j in range(1, 4):
                    remote(piece(i, c ^ j), rows(proj_own, outp_own, i), swap_send.at[i, j - 1], swap_recv.at[i, 0], (z, r, c ^ j)).start()

    ahead = AHEAD
    for i in order[:ahead]:
        issue(i)
    near[0](0, 0)
    for wide in wides:
        lax.fori_loop(0, planes, wide[0], 0)

    def local_ready(i):
        target = rows(proj_own, outp_own, i)
        if i < 24:
            pltpu.make_async_copy(piece(i, c), spot(i, c), own_sem.at[i]).wait()
            for j in range(1, 4):
                arrived = spot(i, c ^ j)
                remote(arrived, arrived, swap_send.at[i, j - 1], swap_recv.at[i, j - 1], (z, r, c ^ j)).wait_recv()
        else:
            @pl.when(c == owner(i))
            def _():
                pltpu.make_async_copy(piece(i, c), target, own_sem.at[i]).wait()

            @pl.when(c != owner(i))
            def _():
                remote(target, target, swap_send.at[i, 0], swap_recv.at[i, 0], (z, r, c ^ 1)).wait_recv()

    def combine(target, sources, count):
        def body(s, _):
            at = pl.ds(pl.multiple_of(s * 32, 32), 32)
            total = sources[0][at].astype(jnp.float32)
            for source in sources[1:]:
                total = total + source[at].astype(jnp.float32)
            target[at] = total.astype(target.dtype)
            return 0
        lax.fori_loop(0, count // 32, body, 0)

    def seat(i):
        return z if i % 2 == 0 else planes - 1 - z

    def at_seat(i, p):
        return (p if i % 2 == 0 else planes - 1 - p, r, c)

    def refs(i):
        return [rows(proj, outp, i) for proj, outp in ((proj_own, outp_own), (proj_in, outp_in), (proj_far, outp_far), (proj_out, outp_out))]

    def down_copy(i, p):
        own, near_in, far_in, _ = refs(i)
        if p == 0:
            return remote(own, near_in, down_send.at[i], down_recv.at[i], at_seat(i, 1))
        return remote(own, far_in, down_send.at[i], far_down.at[i], at_seat(i, p - 1))

    def up_copy(i, p, target):
        result = refs(i)[3]
        return remote(result, result, up_send.at[i, 0 if target == 0 else 1], up_recv.at[i], at_seat(i, target))

    def hop(i, h):
        own, near_in, far_in, result = refs(i)

        if h == 0:
            for p in (0, 3):
                @pl.when(seat(i) == p)
                def _(p=p):
                    local_ready(i)
                    down_copy(i, p).start()
        elif h == 1:
            @pl.when(seat(i) == 2)
            def _():
                local_ready(i)
                down_copy(i, 3).wait_recv()
                combine(own, [own, far_in], own.shape[0])
                down_copy(i, 2).start()
        elif h == 2:
            @pl.when(seat(i) == 1)
            def _():
                local_ready(i)
                down_copy(i, 0).wait_recv()
                down_copy(i, 2).wait_recv()
                combine(result, [own, near_in, far_in], own.shape[0])
                up_copy(i, 1, 0).start()
                up_copy(i, 1, 2).start()
        elif h == 3:
            @pl.when(seat(i) == 2)
            def _():
                up_copy(i, 1, 2).wait_recv()
                up_copy(i, 2, 3).start()
        else:
            for p in (0, 3):
                @pl.when(seat(i) == p)
                def _(p=p):
                    up_copy(i, 1, p).wait_recv()

    def small_group():
        for j in range(1, 8):
            arrived = slices.at[here ^ j]
            remote(arrived, arrived, slice_send.at[0], slice_recv.at[here ^ j], group[j - 1]).wait_recv()
        slices[here] = small_own[here]
        total = slices[0]
        for j in range(1, 8):
            total = total + slices[j]
        far_slices[z] = total
        for k in range(1, planes):
            copy = remote(far_slices.at[z], far_slices.at[z], far_send.at[k - 1], far_recv.at[z], (z ^ k, r, c))
            copy.start()
            small_copies.append(copy)

    def small_far():
        for k in range(1, planes):
            arrived = far_slices.at[z ^ k]
            remote(arrived, arrived, far_send.at[k - 1], far_recv.at[z ^ k], (z ^ k, r, c)).wait_recv()
        total = far_slices[0]
        for k in range(1, planes):
            total = total + far_slices[k]
        small_out[here] = total
        for j in range(1, 8):
            copy = remote(small_out.at[here], small_out.at[here], whole_send.at[j], whole_recv.at[here], group[j - 1])
            copy.start()
            small_copies.append(copy)

    lag = LAG
    hops = 5
    actions = {}

    def plan(slot, action):
        actions.setdefault(slot, []).append(action)

    for slot, kind in zip(NEAR, (1, 2, 3)):
        plan(slot, lambda kind=kind: near[kind](0))
    for slot, action in zip(SMALL, (small_begin, small_group, small_far)):
        plan(slot, action)
    turns = [(k, h) for k in reversed(range(planes)) for h in range(halves)]
    for n, (k, h) in enumerate(turns):
        for kind in (1, 2, 3):
            plan(int(WIDE[0] + n * WIDE[1] + (kind - 1) * WIDE[2]), lambda k=k, h=h, kind=kind: wides[h][kind](k))
    slots = chunks + (hops - 1) * lag
    for s in range(max(slots, max(actions) + 1)):
        if s + ahead < chunks:
            issue(order[s + ahead])
        for h in range(hops):
            if 0 <= s - h * lag < chunks:
                hop(order[s - h * lag], h)
        for action in actions.get(s, ()):
            action()
    for j in range(1, 8):
        arrived = small_out.at[here ^ j]
        remote(arrived, arrived, whole_send.at[0], whole_recv.at[here ^ j], group[j - 1]).wait_recv()
    near[4](0, 0)
    for wide in wides:
        lax.fori_loop(0, planes, wide[4], 0)
    for copy in small_copies + swaps:
        copy.wait_send()
    for i in range(24, 32):
        @pl.when(c == owner(i))
        def _():
            for j in range(1, 4):
                remote(piece(i, c ^ j), rows(proj_own, outp_own, i), swap_send.at[i, j - 1], swap_recv.at[i, 0], (z, r, c ^ j)).wait_send()
    for i in range(chunks):
        @pl.when(seat(i) != 1)
        def _(i=i):
            down_copy(i, 0).wait_send()

        @pl.when(seat(i) == 1)
        def _(i=i):
            up_copy(i, 1, 0).wait_send()

        @pl.when(jnp.logical_or(seat(i) == 1, seat(i) == 2))
        def _(i=i):
            up_copy(i, 1, 2).wait_send()


def finish(grad_proj_own, grad_out_own, small, scaled, mixed_part, entry_part, planes, collective_id):
    depth, width = grad_proj_own.shape[0] // 4, grad_proj_own.shape[1] // 3
    out_rows, out_width = grad_out_own.shape[0], grad_out_own.shape[1] // 4
    kind = grad_proj_own.dtype
    proj, outp = (3, depth, 4 * width), (4 * out_rows, out_width)
    vmem = pl.BlockSpec(memory_space=pltpu.VMEM)
    dma = pltpu.SemaphoreType.DMA
    [(mixed_shape, _)], mixed_buffers, _ = reduce_scratch([mixed_part], planes)
    mixed_semaphores = reduce_scratch([mixed_part] * 2, planes)[2]
    [(entry_shape, _)], entry_buffers, entry_semaphores = reduce_scratch([entry_part], 1)
    return pl.pallas_call(
        functools.partial(finish_kernel, planes),
        out_shape=[jax.ShapeDtypeStruct(proj, kind), jax.ShapeDtypeStruct(outp, kind), jax.ShapeDtypeStruct(small.shape, small.dtype),
                   jax.ShapeDtypeStruct(mixed_shape, jnp.float32), jax.ShapeDtypeStruct(entry_shape, jnp.float32)],
        in_specs=[ANYSPEC, ANYSPEC, vmem, vmem, ANYSPEC, ANYSPEC], out_specs=[vmem] * 5,
        scratch_shapes=[
            pltpu.VMEM(proj, kind), pltpu.VMEM(outp, kind), pltpu.VMEM(proj, kind), pltpu.VMEM(outp, kind), pltpu.VMEM(proj, kind), pltpu.VMEM(outp, kind),
            pltpu.VMEM(small.shape, jnp.float32), pltpu.VMEM(small.shape, jnp.float32), pltpu.VMEM((planes,) + small.shape[1:], jnp.float32),
            dma((32,)), dma((32, 3)), dma((32, 3)), dma((32,)), dma((32,)), dma((32,)), dma((32, 2)), dma((32,)),
            dma((8,)), dma((8,)), dma((planes,)), dma((planes,)), dma((8,)), dma((8,))]
        + mixed_buffers + mixed_semaphores + entry_buffers + entry_semaphores,
        compiler_params=pltpu.CompilerParams(collective_id=collective_id, has_side_effects=True, vmem_limit_bytes=58 * 2**20),
    )(grad_proj_own, grad_out_own, small, scaled, mixed_part, entry_part)


def expert_kernel(planes, experts, own_h, own_side, cot, w_gate, w_up, w_down,
                  all_h, all_side, entry_out, route_out, active_out, grad_gate_out, grad_up_out,
                  gate_use, up_use, down_use, rows_h, rows_c, rows_side, back_rows,
                  gate_rows, up_rows, active_rows, grad_gate, grad_up, entry_stage, route_stage,
                  weight_sem, own_sem, send_sem, recv_sem, cot_sem, load_sem, store_sem):
    z, r, c = place()
    first, second, diag = c ^ (1 + r), c ^ (2 - r), c ^ 3
    partner = (z, 1 - r, c)
    to_first, to_second = (z, r, first), (z, r, second)
    count = own_h.shape[0]
    group = 4 * count
    expert = z * 4 + c
    half = count // 2
    pieces = [(own_h, all_h, 0, half), (own_h, all_h, half, half), (own_side, all_side, 0, count)]

    weights = [(w_gate, gate_use), (w_up, up_use), (w_down, down_use)]
    for i, (source, target) in enumerate(weights):
        pltpu.make_async_copy(source, target, weight_sem.at[i]).start()

    def number(zz, rr, cc):
        return (zz * 2 + rr) * 4 + cc

    def spot(i, which):
        _, target, start, size = pieces[i]
        return target.at[pl.ds(pl.multiple_of(which * count + start, size), size)]

    def copy_of(i, source, which, k, slot, device):
        return pltpu.make_async_remote_copy(
            src_ref=source, dst_ref=spot(i, which), send_sem=send_sem.at[i, k, slot], recv_sem=recv_sem.at[i, which],
            device_id=device, device_id_type=MESH)

    def own_piece(i):
        source, _, start, size = pieces[i]
        return source.at[pl.ds(start, size)]

    def await_block(i, which):
        copy_of(i, spot(i, which), which, 0, 0, partner).wait_recv()

    def forward(which, k, targets):
        for i in range(3):
            await_block(i, which)
            for slot, device in targets:
                copy_of(i, spot(i, which), which, k, slot, device).start()

    greet([to_first, to_second, partner] + [(z ^ k, r, c) for k in range(1, planes)])
    mine = number(z, r, c)
    for i in range(3):
        for slot, device in ((0, to_first), (1, to_second)):
            copy_of(i, own_piece(i), mine, 0, slot, device).start()
        for k in range(1, planes):
            copy_of(i, own_piece(i), mine, k, 7, (z ^ k, r, c)).start()
        copy_of(i, own_piece(i), mine, 0, 2, partner).start()
    keeps = [pltpu.make_async_copy(own_piece(i), spot(i, mine), own_sem.at[i]) for i in range(3)]
    for keep in keeps:
        keep.start()

    def base_of(k, rr):
        return pl.multiple_of(number(z ^ k, rr, 0) * count, group)

    def dot(left, right):
        return jnp.dot(left, right, preferred_element_type=jnp.float32)

    def dot_turned(left, right):
        return lax.dot_general(left, right, (((1,), (1,)), ((), ())), preferred_element_type=jnp.float32)

    def cot_copy(g):
        rr = jnp.where(g % 2 == 0, r, 1 - r)
        return pltpu.make_async_copy(cot.at[pl.ds(base_of(g // 2, rr), group)], rows_c.at[g % 2], cot_sem.at[g % 2])

    cot_copy(0).start()
    for i, (source, target) in enumerate(weights):
        pltpu.make_async_copy(source, target, weight_sem.at[i]).wait()

    def back_body(g, _):
        @pl.when(g + 1 < 2 * planes)
        def _():
            cot_copy(g + 1).start()

        cot_copy(g).wait()
        back_rows[g] = dot_turned(rows_c[g % 2], down_use[...])
        return 0

    lax.fori_loop(0, 2 * planes, back_body, 0)
    for keep in keeps:
        keep.wait()

    def stores(k, rr, slot):
        at = pl.ds(base_of(k, rr), group)
        return [
            pltpu.make_async_copy(source.at[slot], target.at[at], store_sem.at[slot, i])
            for i, (source, target) in enumerate((
                (entry_stage, entry_out), (route_stage, route_out), (active_rows, active_out),
                (grad_gate, grad_gate_out), (grad_up, grad_up_out)))]

    def compute(k, rr, slot):
        at = pl.ds(base_of(k, rr), group)
        loads = [pltpu.make_async_copy(all_h.at[at], rows_h, load_sem.at[0]),
                 pltpu.make_async_copy(all_side.at[at], rows_side, load_sem.at[1])]
        for load in loads:
            load.start()
        for load in loads:
            load.wait()
        gate_rows[...] = dot(rows_h[...], gate_use[...])
        up_rows[...] = dot(rows_h[...], up_use[...])

        @pl.when(k > 0)
        def _():
            for store in stores(k, rr, slot):
                store.wait()

        part = 128
        lane = lax.broadcasted_iota(jnp.int32, (part, rows_side.shape[1]), 1)

        @pl.loop(0, group // part)
        def _(t):
            at = pl.ds(pl.multiple_of(t * part, part), part)
            mask = (lane == expert) | (lane == expert + experts)
            share = jnp.sum(jnp.where(mask, rows_side[at, :].astype(jnp.float32), 0.0), axis=1, keepdims=True)
            gate, up, back = gate_rows[at, :], up_rows[at, :], back_rows[2 * k + slot, at, :]
            squash = jax.nn.sigmoid(gate)
            silu = gate * squash
            active = silu * up
            route = jnp.sum(active * back, axis=1, keepdims=True)
            route_stage[slot, at, :] = jnp.where(lane == expert, route, 0.0).astype(jnp.bfloat16)
            active_rows[slot, at, :] = (share * active).astype(jnp.bfloat16)
            grad_active = share * back
            grad_gate[slot, at, :] = (grad_active * up * squash * (1.0 + gate * (1.0 - squash))).astype(jnp.bfloat16)
            grad_up[slot, at, :] = (grad_active * silu).astype(jnp.bfloat16)

    def finish_rows(k, rr, slot):
        entry = dot_turned(grad_gate[slot], gate_use[...]) + dot_turned(grad_up[slot], up_use[...])
        entry_stage[slot] = entry.astype(jnp.bfloat16)
        for store in stores(k, rr, slot):
            store.start()

    def step_body(step, _):
        @pl.when(jnp.logical_and(step > 0, step < planes))
        def _():
            forward(number(z ^ step, r, c), step, ((0, to_first), (1, to_second), (2, partner)))

        @pl.when(jnp.logical_and(step >= 3, step < planes + 3))
        def _():
            k = step - 3
            for j in range(4):
                for i in range(3):
                    await_block(i, number(z ^ k, 1 - r, c ^ j))
            compute(k, 1 - r, 1)

        @pl.when(jnp.logical_and(step >= 1, step < planes + 1))
        def _():
            k = step - 1
            forward(number(z ^ k, r, first), k, ((3, to_second), (4, partner)))
            forward(number(z ^ k, r, second), k, ((5, partner),))

        @pl.when(jnp.logical_and(step >= 3, step < planes + 3))
        def _():
            finish_rows(step - 3, 1 - r, 1)
            finish_rows(step - 3, r, 0)

        @pl.when(jnp.logical_and(step >= 2, step < planes + 2))
        def _():
            k = step - 2
            forward(number(z ^ k, r, diag), k, ((6, partner),))
            compute(k, r, 0)

        return 0

    lax.fori_loop(0, planes + 3, step_body, 0)
    for slot, rr in ((0, r), (1, 1 - r)):
        for store in stores(planes - 1, rr, slot):
            store.wait()

    def drain(k, _):
        for i in range(3):
            for slot in range(7):
                copy_of(i, spot(i, mine), mine, k, slot, partner).wait_send()

            @pl.when(k > 0)
            def _():
                copy_of(i, spot(i, mine), mine, k, 7, partner).wait_send()
        return 0

    lax.fori_loop(0, planes, drain, 0)


def expert_rows_on_links(normal_h, side, all_cotangent, w_gate, w_up, w_down, experts, collective_id):
    planes = lax.axis_size("dp")
    count, width = normal_h.shape
    hidden = w_gate.shape[1]
    total, group, low, wide = planes * 8 * count, 4 * count, jnp.bfloat16, jnp.float32
    sides = side.shape[1]
    vmem, dma = pltpu.VMEM, pltpu.SemaphoreType.DMA
    outs = [jax.ShapeDtypeStruct((total, n), low) for n in (width, sides, width, sides, hidden, hidden, hidden)]
    return pl.pallas_call(
        functools.partial(expert_kernel, planes, experts),
        out_shape=outs, in_specs=[ANYSPEC] * 6, out_specs=[ANYSPEC] * 7,
        scratch_shapes=[
            vmem((width, hidden), low), vmem((width, hidden), low), vmem((hidden, width), low),
            vmem((group, width), low), vmem((2, group, width), low), vmem((group, sides), low), vmem((2 * planes, group, hidden), wide),
            vmem((group, hidden), wide), vmem((group, hidden), wide),
            vmem((2, group, hidden), low), vmem((2, group, hidden), low), vmem((2, group, hidden), low),
            vmem((2, group, width), low), vmem((2, group, sides), low),
            dma((3,)), dma((3,)), dma((3, planes, 8)), dma((3, planes * 8)), dma((2,)), dma((2,)), dma((2, 5))],
        compiler_params=pltpu.CompilerParams(collective_id=collective_id, has_side_effects=True, vmem_limit_bytes=60 * 2**20),
    )(normal_h, side, all_cotangent, w_gate, w_up, w_down)


def entry_kernel(planes, entry_part, route_part, all_h, cot, active, grad_gate, grad_up, w_down,
                 entry_out, route_out, mixed_out, acc_gate, acc_up, acc_down, *scratch):
    buffers = [scratch[2 * i:2 * i + 2] for i in range(5)]
    semaphores = scratch[10:17]
    down_use, rows_h, rows_c, rows_x, mixed_stage, down_sem, load_sem, store_sem = scratch[17:]
    group = rows_h.shape[1]
    groups = all_h.shape[0] // group

    def loads(g):
        slot = g % 2
        at = pl.ds(pl.multiple_of(g * group, group), group)
        pairs = [(all_h.at[at], rows_h.at[slot]), (cot.at[at], rows_c.at[slot])] + [
            (source.at[at], rows_x.at[slot, i]) for i, source in enumerate((active, grad_gate, grad_up))]
        return [pltpu.make_async_copy(source, target, load_sem.at[slot, i]) for i, (source, target) in enumerate(pairs)]

    def store(g):
        at = pl.ds(pl.multiple_of(g * group, group), group)
        return pltpu.make_async_copy(mixed_stage, mixed_out.at[at], store_sem.at[0])

    def turned(left, right):
        return lax.dot_general(left, right, (((0,), (0,)), ((), ())), preferred_element_type=jnp.float32)

    down = pltpu.make_async_copy(w_down, down_use, down_sem.at[0])
    down.start()
    for load in loads(0):
        load.start()
    for acc in (acc_gate, acc_up, acc_down):
        @pl.loop(0, acc.shape[0] // 32)
        def _(t, acc=acc):
            acc[pl.ds(pl.multiple_of(t * 32, 32), 32), :] = jnp.zeros((32, acc.shape[1]), jnp.float32)
    down.wait()

    def one(g):
        @pl.when(g + 1 < groups)
        def _():
            for load in loads(g + 1):
                load.start()

        for load in loads(g):
            load.wait()
        slot = g % 2
        acc_gate[...] += turned(rows_h[slot], rows_x[slot, 1])
        acc_up[...] += turned(rows_h[slot], rows_x[slot, 2])
        acc_down[...] += turned(rows_x[slot, 0], rows_c[slot])

        @pl.when(g > 0)
        def _():
            store(g - 1).wait()

        mixed_stage[...] = jnp.dot(rows_x[slot, 0], down_use[...], preferred_element_type=jnp.float32).astype(jnp.bfloat16)
        store(g).start()

    steps = planes + 2
    per_step = -(-groups // (steps - 2))

    def filler(step):
        def body(i, _):
            @pl.when(step * per_step + i < groups)
            def _():
                one(step * per_step + i)
            return 0
        lax.fori_loop(0, per_step, body, 0)

    reduce_steps(planes, (entry_part, route_part), (entry_out, route_out), buffers, semaphores, filler)
    store(groups - 1).wait()


def entry_sums(entry_part, route_part, all_h, cot, active, grad_gate, grad_up, w_down, collective_id):
    planes = lax.axis_size("dp")
    partials = [entry_part, route_part]
    shapes, buffers, semaphores = reduce_scratch(partials, planes)
    (count, width), hidden, group = shapes[0][0], w_down.shape[0], 256
    low, wide, vmem, dma = jnp.bfloat16, jnp.float32, pltpu.VMEM, pltpu.SemaphoreType.DMA
    kept = pl.BlockSpec(memory_space=pltpu.VMEM)
    return pl.pallas_call(
        functools.partial(entry_kernel, planes),
        out_shape=[jax.ShapeDtypeStruct(shape, wide) for shape, _ in shapes] + [
            jax.ShapeDtypeStruct(entry_part.shape, low), jax.ShapeDtypeStruct((width, hidden), wide),
            jax.ShapeDtypeStruct((width, hidden), wide), jax.ShapeDtypeStruct((hidden, width), wide)],
        in_specs=[ANYSPEC] * 8, out_specs=[kept, kept, ANYSPEC, kept, kept, kept],
        scratch_shapes=buffers + semaphores + [
            vmem((hidden, width), low), vmem((2, group, width), low), vmem((2, group, width), low), vmem((2, 3, group, hidden), low),
            vmem((group, width), low), dma((1,)), dma((2, 5)), dma((1,))],
        compiler_params=pltpu.CompilerParams(collective_id=collective_id, has_side_effects=True, vmem_limit_bytes=60 * 2**20),
    )(entry_part, route_part, all_h, cot, active, grad_gate, grad_up, w_down)


def dot_plain(left, right):
    return jnp.dot(left, right, preferred_element_type=jnp.float32)


def dot_cols(left, right):
    return lax.dot_general(left, right, (((1,), (1,)), ((), ())), preferred_element_type=jnp.float32)


def dot_rows(left, right):
    return lax.dot_general(left, right, (((0,), (0,)), ((), ())), preferred_element_type=jnp.float32)


def group_peers():
    z, r, c = place()
    return r * 4 + c, [(z, r ^ (j >> 2), c ^ (j & 3)) for j in range(1, 8)]


def group_sums(own, slots, send_sem, recv_sem):
    here, peers = group_peers()
    copies = []
    for j, peer in enumerate(peers):
        copy = pltpu.make_async_remote_copy(
            src_ref=own, dst_ref=slots.at[j], send_sem=send_sem.at[j], recv_sem=recv_sem.at[j],
            device_id=peer, device_id_type=MESH)
        copy.start()
        copies.append(copy)
    for copy in copies:
        copy.wait()
    total = jnp.zeros(own.shape, jnp.float32)
    for who in range(8):
        which = here ^ who
        total = total + jnp.where(which == 0, own[...], slots[jnp.maximum(which - 1, 0)])
    return total


def row_of_tokens(values):
    folded = values[:, :128]
    for start in range(128, values.shape[1], 128):
        folded = folded + values[:, start:start + 128]
    return jnp.sum(folded.T, axis=0, keepdims=True)


def column_of(row):
    return jnp.broadcast_to(row, (128, row.shape[1])).T


BLOCK = 256


def block_weights(queries, keys, first, finish):
    scores = dot_cols(queries[first:finish], keys[:finish])
    at_query = lax.broadcasted_iota(jnp.int32, scores.shape, 0) + first
    at_key = lax.broadcasted_iota(jnp.int32, scores.shape, 1)
    scores = jnp.where(at_query >= at_key, scores, MASKED)
    weights = jnp.exp(scores - jnp.max(scores, axis=1, keepdims=True))
    return weights / jnp.sum(weights, axis=1, keepdims=True)


def forward_kernel(width, x_ref, proj_ref, gains, cosine, sine, w_out_ref,
                   part_out, query_out, key_out, value_out, raw_out, scale_out, mixed_out, w_out_own,
                   sums, slots, send_sem, recv_sem, keep_sem, swap_send, swap_recv):
    greet(group_peers()[1])
    z, r, c = place()
    rows, lanes_out = w_out_own.shape[0], w_out_ref.shape[1]

    def piece(target):
        return w_out_ref.at[pl.ds(pl.multiple_of(target * rows, rows), rows), :]

    def spot(origin):
        return w_out_own.at[:, pl.ds(pl.multiple_of(origin * lanes_out, lanes_out), lanes_out)]

    keep = pltpu.make_async_copy(piece(c), spot(c), keep_sem.at[0])
    keep.start()
    swaps = [pltpu.make_async_remote_copy(
        src_ref=piece(c ^ j), dst_ref=spot(c), send_sem=swap_send.at[j - 1], recv_sem=swap_recv.at[j - 1],
        device_id=(z, r, c ^ j), device_id_type=MESH) for j in range(1, 4)]
    local = value_out.shape[1]
    raw = dot_plain(x_ref[...], proj_ref[...])
    raw_out[...] = raw[:, :2 * local]
    value_out[...] = raw[:, 2 * local:].astype(jnp.bfloat16)
    sums[...] = jnp.zeros(sums.shape, jnp.float32)
    for i in range(2):
        half = raw_out[:, pl.ds(i * local, local)]
        sums[pl.ds(i, 1), :] = row_of_tokens(half * half)
    total = group_sums(sums, slots, send_sem, recv_sem)
    for swap in swaps:
        swap.start()
    for i, (target, factor) in enumerate(((query_out, 128 ** (-0.5)), (key_out, 1.0))):
        scale = lax.rsqrt(column_of(total[i:i + 1]) / width + EPSILON)
        scale_out[:, pl.ds(i * 128, 128)] = scale
        for start in range(0, local, 128):
            lanes = pl.ds(start, 128)
            normal = raw_out[:, pl.ds(i * local + start, 128)] * scale * gains[pl.ds(i, 1), lanes]
            turned = normal * cosine[...] + pltpu.roll(normal, 64, 1) * sine[...]
            target[:, lanes] = (turned * factor).astype(jnp.bfloat16)
    tokens = x_ref.shape[0]
    for start in range(0, local, 128):
        lanes = pl.ds(start, 128)
        queries, keys, values = query_out[:, lanes], key_out[:, lanes], value_out[:, lanes]
        for first in range(0, tokens, BLOCK):
            weights = block_weights(queries, keys, first, first + BLOCK).astype(jnp.bfloat16)
            mixed = dot_plain(weights, values[:first + BLOCK])
            mixed_out[pl.ds(first, BLOCK), lanes] = mixed.astype(jnp.bfloat16)
    keep.wait()
    for swap in swaps:
        swap.wait()
    part_out[...] = dot_plain(mixed_out[...], w_out_own[...]).astype(jnp.bfloat16)


def attention_forward(gathered_x, w_proj, gains, cosine, sine, w_out, collective_id):
    tokens, width = gathered_x.shape
    local = w_proj.shape[1] // 3
    low, wide = jnp.bfloat16, jnp.float32
    shape, vmem = jax.ShapeDtypeStruct, pl.BlockSpec(memory_space=pltpu.VMEM)
    dma = pltpu.SemaphoreType.DMA
    return pl.pallas_call(
        functools.partial(forward_kernel, width),
        out_shape=[shape((tokens, width), low), shape((tokens, local), low), shape((tokens, local), low), shape((tokens, local), low),
                   shape((tokens, 2 * local), wide), shape((tokens, 256), wide), shape((tokens, local), low),
                   shape((w_out.shape[0] // 4, 4 * w_out.shape[1]), low)],
        in_specs=[vmem] * 5 + [ANYSPEC], out_specs=[vmem] * 8,
        scratch_shapes=[pltpu.VMEM((8, tokens), wide), pltpu.VMEM((7, 8, tokens), wide), dma((7,)), dma((7,)), dma((1,)), dma((3,)), dma((3,))],
        compiler_params=pltpu.CompilerParams(collective_id=collective_id, has_side_effects=True, vmem_limit_bytes=56 * 2**20),
    )(gathered_x, w_proj, gains, cosine, sine, w_out)


def backward_kernel(width, grad_ref, w_out_ref, x_hbm, proj_hbm, query_ref, key_ref, value_ref, raw_ref, scale_ref, mixed_ref,
                    gains, cosine, sine, grad_x_out, grad_proj_out, grad_out_out, gain_out,
                    x_ref, proj_ref, grad_query, grad_key, grad_value, grad_raw, sums, slots, load_sem, send_sem, recv_sem):
    greet(group_peers()[1])
    loads = [pltpu.make_async_copy(x_hbm, x_ref, load_sem.at[0]), pltpu.make_async_copy(proj_hbm, proj_ref, load_sem.at[1])]
    for load in loads:
        load.start()
    local, tokens = value_ref.shape[1], value_ref.shape[0]
    grad_mixed = dot_cols(grad_ref[...], w_out_ref[...]).astype(jnp.bfloat16)
    grad_raw[:, pl.ds(0, local)] = grad_mixed
    for start in range(0, local, 128):
        lanes = pl.ds(start, 128)
        queries, keys, values, upstream = query_ref[:, lanes], key_ref[:, lanes], value_ref[:, lanes], grad_raw[:, lanes]
        for first in reversed(range(0, tokens, BLOCK)):
            finish = first + BLOCK
            weights = block_weights(queries, keys, first, finish)
            grad_weights = dot_cols(upstream[first:finish], values[:finish])
            centre = jnp.sum(weights * grad_weights, axis=1, keepdims=True)
            grad_scores = (weights * (grad_weights - centre)).astype(jnp.bfloat16)
            grad_query[pl.ds(first, BLOCK), lanes] = dot_plain(grad_scores, keys[:finish])
            key_part = dot_rows(grad_scores, queries[first:finish])
            value_part = dot_rows(weights.astype(jnp.bfloat16), upstream[first:finish])
            if finish == tokens:
                grad_key[:, lanes] = key_part
                grad_value[:, lanes] = value_part
            else:
                grad_key[pl.ds(0, finish), lanes] += key_part
                grad_value[pl.ds(0, finish), lanes] += value_part
    sums[...] = jnp.zeros(sums.shape, jnp.float32)
    gain_out[...] = jnp.zeros(gain_out.shape, jnp.float32)
    for i, (grad, factor) in enumerate(((grad_query, 128 ** (-0.5)), (grad_key, 1.0))):
        scale = scale_ref[:, pl.ds(i * 128, 128)]
        inner = None
        for start in range(0, local, 128):
            lanes = pl.ds(start, 128)
            upstream = grad[:, lanes] * factor
            normal = upstream * cosine[...] - pltpu.roll(upstream, 64, 1) * sine[...]
            raw = raw_ref[:, pl.ds(i * local + start, 128)]
            gain_out[pl.ds(i, 1), lanes] = jnp.sum(normal * raw * scale, axis=0, keepdims=True)
            weighted = gains[pl.ds(i, 1), lanes] * normal
            grad[:, lanes] = weighted
            inner = weighted * raw if inner is None else inner + weighted * raw
        sums[pl.ds(i, 1), :] = row_of_tokens(inner)
    total = group_sums(sums, slots, send_sem, recv_sem)
    for i, grad in enumerate((grad_query, grad_key)):
        scale = scale_ref[:, pl.ds(i * 128, 128)]
        factor = scale * scale * scale * column_of(total[i:i + 1]) / width
        for start in range(0, local, 128):
            lanes = pl.ds(start, 128)
            raw = raw_ref[:, pl.ds(i * local + start, 128)]
            grad_raw[:, pl.ds(i * local + start, 128)] = (scale * grad[:, lanes] - raw * factor).astype(jnp.bfloat16)
    grad_raw[:, pl.ds(2 * local, local)] = grad_value[...].astype(jnp.bfloat16)
    for load in loads:
        load.wait()
    grad_x_out[...] = dot_cols(grad_raw[...], proj_ref[...]).astype(jnp.bfloat16)
    grad_proj_out[...] = dot_rows(x_ref[...], grad_raw[...]).astype(jnp.bfloat16)
    grad_out_out[...] = dot_rows(mixed_ref[...], grad_ref[...]).astype(jnp.bfloat16)


def attention_backward(grad_gathered, w_out_own, gathered_x, w_proj, kept, gains, cosine, sine, collective_id):
    tokens, width = gathered_x.shape
    local = w_proj.shape[1] // 3
    low, wide = jnp.bfloat16, jnp.float32
    shape, vmem = jax.ShapeDtypeStruct, pl.BlockSpec(memory_space=pltpu.VMEM)
    dma = pltpu.SemaphoreType.DMA
    return pl.pallas_call(
        functools.partial(backward_kernel, width),
        out_shape=[shape((tokens, width), low), shape(w_proj.shape, low), shape(w_out_own.shape, low), shape((8, local), wide)],
        in_specs=[vmem, vmem, ANYSPEC, ANYSPEC] + [vmem] * 9, out_specs=[vmem] * 4,
        scratch_shapes=[
            pltpu.VMEM(gathered_x.shape, low), pltpu.VMEM(w_proj.shape, low),
            pltpu.VMEM((tokens, local), wide), pltpu.VMEM((tokens, local), wide), pltpu.VMEM((tokens, local), wide),
            pltpu.VMEM((tokens, 3 * local), low), pltpu.VMEM((8, tokens), wide), pltpu.VMEM((7, 8, tokens), wide),
            dma((2,)), dma((7,)), dma((7,))],
        compiler_params=pltpu.CompilerParams(collective_id=collective_id, has_side_effects=True, vmem_limit_bytes=60 * 2**20),
    )(grad_gathered, w_out_own, gathered_x, w_proj, *kept, gains, cosine, sine)


HEAD_DIM = 128
SEQ_LEN = 1024
EPSILON = 1e-05
THETA = 10000.0
MASKED = -1e30
GROUP = ("row", "col")
EVERYONE = ("dp", "row", "col")


def on_links():
    return lax.axis_size("dp") == 4 and lax.axis_size("col") == 4 and lax.axis_size("row") == 2


def gather_tokens(arrays, everyone, collective_id, parts):
    if on_links():
        return gather(arrays, 4 if everyone else 1, collective_id, parts)
    axes = EVERYONE if everyone else GROUP
    return [lax.all_gather(a, axes, axis=0, tiled=True) for a in arrays]


def scatter_sums(arrays, everyone, collective_id):
    if on_links():
        return reduce_scatter(arrays, 4 if everyone else 1, collective_id)
    axes = EVERYONE if everyone else GROUP
    return [lax.psum_scatter(a, axes, scatter_dimension=0, tiled=True).astype(jnp.float32) for a in arrays]


def to_heads(w_query, w_key, w_value):
    if on_links():
        return exchange_weights(w_query, w_key, w_value, 1)
    pieces = [lax.all_to_all(w, "col", split_axis=1, concat_axis=0, tiled=True) for w in (w_query, w_key, w_value)]
    return jnp.concatenate(pieces, axis=1)


def inverse_rms(values):
    return lax.rsqrt(jnp.mean(values * values, axis=-1, keepdims=True) + EPSILON)


def norm_backward(values, inv_scale, gain_row, upstream):
    weighted = gain_row * upstream
    inner_sum = jnp.sum(weighted * values, axis=-1, keepdims=True)
    grad_values = inv_scale * weighted - values * inv_scale**3 * inner_sum / values.shape[-1]
    return (grad_values, jnp.sum(upstream * values * inv_scale, axis=0))


def contract(left, right):
    return jnp.dot(left, right, preferred_element_type=jnp.float32)


def contract_rows(left, right):
    return lax.dot_general(
        left, right, (((0,), (0,)), ((), ())), preferred_element_type=jnp.float32
    )


def contract_cols(left, right):
    return lax.dot_general(
        left, right, (((1,), (1,)), ((), ())), preferred_element_type=jnp.float32
    )


def turn_tables(total_rows, seq_length, head_width):
    positions = (jnp.arange(total_rows) % seq_length).astype(jnp.float32)
    inverse = THETA ** (-jnp.arange(0, head_width, 2, dtype=jnp.float32) / head_width)
    angles = positions[:, None] * inverse[None, :]
    angles = jnp.concatenate([angles, angles], axis=-1)
    return (jnp.cos(angles)[:, None, :], jnp.sin(angles)[:, None, :])


def rotate(values, cosine, sine_table):
    middle = values.shape[-1] // 2
    turned = jnp.concatenate([-values[..., middle:], values[..., :middle]], axis=-1)
    return values * cosine + turned * sine_table


def unrotate(upstream, cosine, sine_table):
    middle = upstream.shape[-1] // 2
    turned_part = upstream * sine_table
    return upstream * cosine + jnp.concatenate(
        [turned_part[..., middle:], -turned_part[..., :middle]], axis=-1
    )


def attend_forward(queries, key_rows, value_rows):
    length = queries.shape[0]
    block_rows = min(512, length)
    outputs = []
    sums_log = []
    for first_row in range(0, length, block_rows):
        finish = first_row + block_rows
        scores = jnp.einsum(
            "qhd,khd->hqk",
            queries[first_row:finish],
            key_rows[:finish],
            preferred_element_type=jnp.float32,
        )
        causal = (first_row + jnp.arange(block_rows))[:, None] >= jnp.arange(finish)[None, :]
        scores = jnp.where(causal[None], scores, MASKED)
        highest = jnp.max(scores, axis=-1, keepdims=True)
        weights = jnp.exp(scores - highest)
        totals = jnp.sum(weights, axis=-1, keepdims=True)
        weights = (weights / totals).astype(jnp.bfloat16)
        outputs.append(
            jnp.einsum(
                "hqk,khd->qhd", weights, value_rows[:finish], preferred_element_type=jnp.float32
            )
        )
        sums_log.append((highest + jnp.log(totals))[..., 0])
    return (jnp.concatenate(outputs, axis=0), jnp.concatenate(sums_log, axis=1))


def attend_backward(queries, key_rows, value_rows, grad_out, sums_log):
    length = queries.shape[0]
    block_rows = min(512, length)
    grad_queries = []
    grad_keys = jnp.zeros(key_rows.shape, jnp.float32)
    grad_values = jnp.zeros(value_rows.shape, jnp.float32)
    for first_row in range(0, length, block_rows):
        finish = first_row + block_rows
        scores = jnp.einsum(
            "qhd,khd->hqk",
            queries[first_row:finish],
            key_rows[:finish],
            preferred_element_type=jnp.float32,
        )
        causal = (first_row + jnp.arange(block_rows))[:, None] >= jnp.arange(finish)[None, :]
        scores = jnp.where(causal[None], scores, MASKED)
        weights = jnp.exp(scores - sums_log[:, first_row:finish, None])
        grad_weights = jnp.einsum(
            "qhd,khd->hqk",
            grad_out[first_row:finish],
            value_rows[:finish],
            preferred_element_type=jnp.float32,
        )
        centre = jnp.sum(weights * grad_weights, axis=-1, keepdims=True)
        grad_scores = (weights * (grad_weights - centre)).astype(jnp.bfloat16)
        grad_queries.append(
            jnp.einsum(
                "hqk,khd->qhd", grad_scores, key_rows[:finish], preferred_element_type=jnp.float32
            )
        )
        grad_keys = grad_keys.at[:finish].add(
            jnp.einsum(
                "hqk,qhd->khd",
                grad_scores,
                queries[first_row:finish],
                preferred_element_type=jnp.float32,
            )
        )
        grad_values = grad_values.at[:finish].add(
            jnp.einsum(
                "hqk,qhd->khd",
                weights.astype(jnp.bfloat16),
                grad_out[first_row:finish],
                preferred_element_type=jnp.float32,
            )
        )
    return (jnp.concatenate(grad_queries, axis=0), grad_keys, grad_values)


def by_sequence(step, pieces, sequences):
    if sequences == 1:
        return tuple(out[None] for out in step(*[p[0] for p in pieces]))
    return lax.map(lambda each: step(*each), tuple(pieces))


def expert_rows(normal_h, side, cotangent, gate_use, up_use, down_use, expert_count):
    if on_links():
        all_cotangent = lax.all_gather(cotangent, EVERYONE, axis=0, tiled=True)
        rows_h, _, entry_part, grad_side, active_share, grad_gate_rows, grad_up_rows = expert_rows_on_links(
            normal_h, side, all_cotangent, gate_use, up_use, down_use, expert_count, 6
        )
        entry_rows, grad_probs_all, out_part, *grads = entry_sums(
            entry_part, grad_side, rows_h, all_cotangent, active_share, grad_gate_rows, grad_up_rows, down_use, 7
        )
        return (entry_rows, grad_probs_all, out_part, *grads)
    all_cotangent, rows_h, rows_side = gather_tokens([cotangent, normal_h, side], True, 6, 2)
    expert = lax.axis_index("dp") * lax.axis_size("col") + lax.axis_index("col")
    lane = jnp.arange(side.shape[1])
    own_share = jnp.sum(
        jnp.where((lane == expert) | (lane == expert + expert_count), rows_side.astype(jnp.float32), 0.0),
        axis=1,
        keepdims=True,
    )
    back_rows = contract_cols(all_cotangent, down_use)
    gate_rows = contract(rows_h, gate_use)
    up_rows = contract(rows_h, up_use)
    sigmoid_gate = jax.nn.sigmoid(gate_rows)
    silu_gate = gate_rows * sigmoid_gate
    active = silu_gate * up_rows
    route_grad = jnp.sum(active * back_rows, axis=1, keepdims=True)
    active_share = (own_share * active).astype(jnp.bfloat16)
    grad_active = own_share * back_rows
    grad_gate_rows = (
        grad_active * up_rows * sigmoid_gate * (1.0 + gate_rows * (1.0 - sigmoid_gate))
    ).astype(jnp.bfloat16)
    grad_up_rows = (grad_active * silu_gate).astype(jnp.bfloat16)
    entry_part = (contract_cols(grad_gate_rows, gate_use) + contract_cols(grad_up_rows, up_use)).astype(jnp.bfloat16)
    grad_side = jnp.where(jnp.arange(128 if expert_count <= 128 else expert_count)[None, :] == expert, route_grad, 0.0).astype(jnp.bfloat16)
    entry_rows, grad_probs_all = scatter_sums([entry_part, grad_side], True, 7)
    out_part = contract(active_share, down_use).astype(jnp.bfloat16)
    (mixture,) = scatter_sums([out_part], True, 8)
    grad_down_w = contract_rows(active_share, all_cotangent)
    grad_gate_w = contract_rows(rows_h, grad_gate_rows)
    grad_up_w = contract_rows(rows_h, grad_up_rows)
    return entry_rows, grad_probs_all, mixture, grad_gate_w, grad_up_w, grad_down_w


def per_device(
    hidden_in,
    cotangent,
    norm_attn,
    w_query,
    w_key,
    w_value,
    query_gain,
    key_gain,
    w_out,
    norm_moe,
    w_router,
    w_gate,
    w_up,
    w_down,
    routes,
):
    inputs = hidden_in.astype(jnp.float32)
    upstream = cotangent.astype(jnp.float32)
    token_count, top_count = routes.shape
    model_width = inputs.shape[1]
    expert_count = w_router.shape[1]

    inv_input = inverse_rms(inputs)
    normal_x = (inputs * inv_input * norm_attn).astype(jnp.bfloat16)
    w_proj = to_heads(w_query, w_key, w_value)
    (gathered_x,) = gather_tokens([normal_x], False, 2, 2)
    group_tokens = gathered_x.shape[0]
    local_width = w_proj.shape[1] // 3
    head_count = local_width // HEAD_DIM
    offset = (lax.axis_index("row") * lax.axis_size("col") + lax.axis_index("col")) * local_width
    gain_query = lax.dynamic_slice_in_dim(query_gain, offset, local_width)
    gain_key = lax.dynamic_slice_in_dim(key_gain, offset, local_width)
    cosine, sine_table = turn_tables(group_tokens, SEQ_LEN, HEAD_DIM)
    head_shape = (group_tokens, head_count, HEAD_DIM)
    sequences = group_tokens // SEQ_LEN
    seq_shape = (sequences, SEQ_LEN, head_count, HEAD_DIM)
    in_kernels = on_links() and sequences == 1
    if in_kernels:
        gains = jnp.concatenate([gain_query[None], gain_key[None], jnp.zeros((6, local_width), jnp.float32)])
        sine_signed = jnp.where(jnp.arange(HEAD_DIM) < HEAD_DIM // 2, -sine_table[:, 0], sine_table[:, 0])
        tables = (gains, cosine[:, 0], sine_signed)
        attn_part, *kept, w_out_own = attention_forward(gathered_x, w_proj, *tables, w_out, 4)
    else:
        w_out_own = lax.all_to_all(w_out, "col", split_axis=0, concat_axis=1, tiled=True)
        raw = contract(gathered_x, w_proj)
        query_raw = raw[:, :local_width]
        key_raw = raw[:, local_width : 2 * local_width]
        value_heads = raw[:, 2 * local_width :].astype(jnp.bfloat16)
        query_square, key_square = lax.psum(
            (jnp.sum(query_raw * query_raw, axis=-1), jnp.sum(key_raw * key_raw, axis=-1)), GROUP
        )
        inv_query = lax.rsqrt(query_square / model_width + EPSILON)[:, None]
        inv_key = lax.rsqrt(key_square / model_width + EPSILON)[:, None]
        query_heads = (
            rotate((query_raw * inv_query * gain_query).reshape(head_shape), cosine, sine_table)
            * HEAD_DIM ** (-0.5)
        ).astype(jnp.bfloat16)
        key_heads = rotate(
            (key_raw * inv_key * gain_key).reshape(head_shape), cosine, sine_table
        ).astype(jnp.bfloat16)
        query_seq = query_heads.reshape(seq_shape)
        key_seq = key_heads.reshape(seq_shape)
        value_seq = value_heads.reshape(seq_shape)
        mixed, sums_log = by_sequence(attend_forward, (query_seq, key_seq, value_seq), sequences)
        mixed_heads = mixed.reshape(group_tokens, local_width).astype(jnp.bfloat16)
        attn_part = contract(mixed_heads, w_out_own).astype(jnp.bfloat16)
    (attn_rows,) = scatter_sums([attn_part], False, 5)
    state_rows = inputs + attn_rows

    inv_state = inverse_rms(state_rows)
    normal_h = (state_rows * inv_state * norm_moe).astype(jnp.bfloat16)
    logits = contract(normal_h, w_router)
    shifted = jnp.exp(logits - jnp.max(logits, axis=-1, keepdims=True))
    probabilities = shifted / jnp.sum(shifted, axis=-1, keepdims=True)
    selected = jnp.sum(
        (routes[:, :, None] == jnp.arange(expert_count)[None, None, :]).astype(jnp.float32), axis=1
    )
    shares = probabilities * selected
    share_high = shares.astype(jnp.bfloat16)
    share_low = (shares - share_high.astype(jnp.float32)).astype(jnp.bfloat16)
    side_width = max(2 * expert_count, 128)
    side = jnp.concatenate(
        [
            share_high,
            share_low,
            jnp.zeros((token_count, side_width - 2 * expert_count), jnp.bfloat16),
        ],
        axis=1,
    )

    chunks = max(1, lax.axis_size(EVERYONE) // 32)
    if chunks == 1:
        entry_rows, grad_probs_all, mixture, *expert_grads = expert_rows(
            normal_h, side, cotangent, w_gate[0], w_up[0], w_down[0], expert_count
        )
    else:

        def piece_step(sums, piece):
            entry, probs, mixed_rows, *grads = expert_rows(*piece, w_gate[0], w_up[0], w_down[0], expert_count)
            return [s + g for s, g in zip(sums, grads)], (entry, probs, mixed_rows)

        cut = [a.reshape((chunks, token_count // chunks) + a.shape[1:]) for a in (normal_h, side, cotangent)]
        empty = [jnp.zeros(w.shape[1:], jnp.float32) for w in (w_gate, w_up, w_down)]
        expert_grads, rows = lax.scan(piece_step, empty, cut)
        entry_rows, grad_probs_all, mixture = [r.reshape((token_count,) + r.shape[2:]) for r in rows]
    grad_gate_w, grad_up_w, grad_down_w = expert_grads
    grad_probs = selected * grad_probs_all[:, :expert_count]
    grad_logits = (
        probabilities * (grad_probs - jnp.sum(probabilities * grad_probs, axis=-1, keepdims=True))
    ).astype(jnp.bfloat16)
    grad_normal_h = entry_rows + contract_cols(grad_logits, w_router)
    grad_router_part = contract_rows(normal_h, grad_logits)
    grad_state_part, grad_moe_part = norm_backward(state_rows, inv_state, norm_moe, grad_normal_h)
    grad_state = upstream + grad_state_part
    grad_attn = grad_state.astype(jnp.bfloat16)
    (grad_gathered,) = gather_tokens([grad_attn], False, 9, 2)
    if in_kernels:
        grad_x_part, grad_proj_own, grad_out_own, gain_parts = attention_backward(
            grad_gathered, w_out_own, gathered_x, w_proj, kept, *tables, 10
        )
        grad_qgain_part, grad_kgain_part = gain_parts[0], gain_parts[1]
    else:
        grad_out_own = contract_rows(mixed_heads, grad_gathered).astype(jnp.bfloat16)
        grad_mixed = contract_cols(grad_gathered, w_out_own).astype(jnp.bfloat16)
        grad_query_seq, grad_key_seq, grad_value_seq = by_sequence(
            attend_backward,
            (query_seq, key_seq, value_seq, grad_mixed.reshape(seq_shape), sums_log),
            sequences,
        )
        grad_normal_q = unrotate(
            grad_query_seq.reshape(head_shape) * HEAD_DIM ** (-0.5), cosine, sine_table
        ).reshape(group_tokens, local_width)
        grad_normal_k = unrotate(grad_key_seq.reshape(head_shape), cosine, sine_table).reshape(
            group_tokens, local_width
        )
        weighted_q = gain_query * grad_normal_q
        weighted_k = gain_key * grad_normal_k
        inner_q, inner_k = lax.psum(
            (jnp.sum(weighted_q * query_raw, axis=-1), jnp.sum(weighted_k * key_raw, axis=-1)), GROUP
        )
        grad_query_raw = (
            inv_query * weighted_q - query_raw * inv_query**3 * inner_q[:, None] / model_width
        )
        grad_key_raw = inv_key * weighted_k - key_raw * inv_key**3 * inner_k[:, None] / model_width
        grad_qgain_part = jnp.sum(grad_normal_q * query_raw * inv_query, axis=0)
        grad_kgain_part = jnp.sum(grad_normal_k * key_raw * inv_key, axis=0)
        grad_raw = jnp.concatenate(
            [grad_query_raw, grad_key_raw, grad_value_seq.reshape(group_tokens, local_width)], axis=1
        ).astype(jnp.bfloat16)
        grad_x_part = contract_cols(grad_raw, w_proj).astype(jnp.bfloat16)
        grad_proj_own = contract_rows(gathered_x, grad_raw).astype(jnp.bfloat16)
    full_width = query_gain.shape[0]
    padded_qgain = lax.dynamic_update_slice_in_dim(
        jnp.zeros((full_width,), jnp.float32), grad_qgain_part, offset, 0
    )
    padded_kgain = lax.dynamic_update_slice_in_dim(
        jnp.zeros((full_width,), jnp.float32), grad_kgain_part, offset, 0
    )
    small = (padded_qgain, padded_kgain, grad_moe_part, grad_router_part)
    grad_query, grad_key, grad_value, grad_out_proj, mixture, grad_normal_x, small = last_sums(
        grad_proj_own, grad_out_own, small, inputs * inv_input, mixture, grad_x_part
    )
    grad_norm_attn, grad_query_gain, grad_key_gain, grad_norm_moe, grad_router = small
    block_out = (state_rows + mixture).astype(jnp.bfloat16)
    grad_input = grad_state + norm_backward(inputs, inv_input, norm_attn, grad_normal_x)[0]
    return (
        block_out,
        grad_input,
        grad_norm_attn,
        grad_query,
        grad_key,
        grad_value,
        grad_query_gain,
        grad_key_gain,
        grad_out_proj,
        grad_norm_moe,
        grad_router,
        grad_gate_w[None],
        grad_up_w[None],
        grad_down_w[None],
    )


def last_sums(grad_proj_own, grad_out_own, small, scaled, mixed_part, entry_part):
    if on_links():
        parts = (jnp.zeros((scaled.shape[1],), jnp.float32), *small)
        flat = jnp.concatenate([part.reshape(-1) for part in parts])
        proj, outp, total, mixture, grad_normal_x = finish(
            grad_proj_own, grad_out_own, flat.reshape(8, -1, 128), scaled, mixed_part, entry_part, lax.axis_size("dp"), 12
        )
        total, sums, start = total.reshape(-1), [], 0
        for part in parts:
            sums.append(total[start : start + part.size].reshape(part.shape))
            start += part.size
        return (*(proj[a].astype(jnp.float32) for a in range(3)), outp.astype(jnp.float32), mixture, grad_normal_x, sums)
    (grad_normal_x,) = scatter_sums([entry_part], False, 11)
    small = (jnp.sum(grad_normal_x * scaled, axis=0), *small)
    width = grad_proj_own.shape[1] // 3
    blocks = [
        lax.all_to_all(grad_proj_own[:, a * width : (a + 1) * width], "col", split_axis=0, concat_axis=1, tiled=True)
        for a in range(3)
    ]
    out_block = lax.all_to_all(grad_out_own, "col", split_axis=1, concat_axis=0, tiled=True)
    weights = [total.astype(jnp.float32) for total in lax.psum((*blocks, out_block), "dp")]
    return (*weights, mixed_part, grad_normal_x, lax.psum(small, EVERYONE))


def solution(mesh):
    placed = (
        P(("dp", "row", "col"), None),
        P(("dp", "row", "col"), None),
        P(),
        P("col", "row"),
        P("col", "row"),
        P("col", "row"),
        P(),
        P(),
        P("row", "col"),
        P(),
        P(),
        P(("dp", "col"), None, "row"),
        P(("dp", "col"), None, "row"),
        P(("dp", "col"), "row", None),
        P(("dp", "row", "col"), None),
    )
    return jax.shard_map(
        per_device,
        mesh=mesh,
        in_specs=placed,
        out_specs=(
            P(("dp", "row", "col"), None),
            P(("dp", "row", "col"), None),
            P(),
            P("col", "row"),
            P("col", "row"),
            P("col", "row"),
            P(),
            P(),
            P("row", "col"),
            P(),
            P(),
            P(("dp", "col"), None, "row"),
            P(("dp", "col"), None, "row"),
            P(("dp", "col"), "row", None),
        ),
        check_vma=False,
    )
```

```python
import functools

import jax
import jax.numpy as jnp
from jax import lax
from jax.experimental import pallas as pl
from jax.experimental.pallas import tpu as pltpu
from jax.sharding import PartitionSpec as P

MESH = pl.DeviceIdType.MESH
ANYSPEC = pl.BlockSpec(memory_space=pl.ANY)
CUTS = 2

def place():
    return lax.axis_index("dp"), lax.axis_index("row"), lax.axis_index("col")

def greet(peers):
    barrier = pltpu.get_barrier_semaphore()
    for peer in peers:
        pl.semaphore_signal(barrier, inc=1, device_id=peer, device_id_type=MESH)
    pl.semaphore_wait(barrier, len(peers))

def gather_kernel(planes, parts, count, *refs):
    gather_steps(planes, parts, refs[:count], refs[count:2 * count], *refs[2 * count:])


def gather_steps(planes, parts, ins, outs, own_sem, send_sem, recv_sem, more_peers=(), beside=None):
    count = len(ins)
    z, r, c = place()
    first, second, diag = c ^ (1 + r), c ^ (2 - r), c ^ 3
    partner = (z, 1 - r, c)
    to_first, to_second = (z, r, first), (z, r, second)
    greet([to_first, to_second, partner] + [(z ^ k, r, c) for k in range(1, planes)] + list(more_peers))
    pieces = []
    for a in range(count):
        cut = parts if a == 0 else 1
        pieces += [(a, p, ins[a].shape[0], ins[a].shape[0] // cut) for p in range(cut)]

    def number(zz, rr, cc):
        return ((zz if planes > 1 else 0) * 2 + rr) * 4 + cc

    def place_of(i, which):
        a, p, depth, cut = pieces[i]
        return outs[a].at[pl.ds(pl.multiple_of(which * depth + p * cut, cut), cut)]

    sent = [[] for _ in pieces]

    def send(i, which, target, own=False):
        a, p, depth, cut = pieces[i]
        spot = place_of(i, which)
        copy = pltpu.make_async_remote_copy(
            src_ref=ins[a].at[pl.ds(p * cut, cut)] if own else spot, dst_ref=spot,
            send_sem=send_sem.at[i, len(sent[i])], recv_sem=recv_sem.at[i, which],
            device_id=target, device_id_type=MESH)
        copy.start()
        sent[i].append(copy)

    def await_block(i, which):
        spot = place_of(i, which)
        pltpu.make_async_remote_copy(
            src_ref=spot, dst_ref=spot, send_sem=send_sem.at[i, 0], recv_sem=recv_sem.at[i, which],
            device_id=partner, device_id_type=MESH).wait_recv()

    mine = number(z, r, c)
    keeps = []
    every = range(len(pieces))
    for i in every:
        for target in [to_first, to_second] + [(z ^ k, r, c) for k in range(1, planes)] + [partner]:
            send(i, mine, target, True)
    if beside is not None:
        beside()
    for a in range(count):
        keep = pltpu.make_async_copy(ins[a], outs[a].at[pl.ds(pl.multiple_of(mine * ins[a].shape[0], ins[a].shape[0]), ins[a].shape[0])], own_sem.at[a])
        keep.start()
        keeps.append(keep)

    def forward(which, targets):
        for i in every:
            await_block(i, which)
            for target in targets:
                send(i, which, target)

    for step in range(planes + 2):
        if 0 < step < planes:
            forward(number(z ^ step, r, c), [to_first, to_second, partner])
        if 0 <= step - 1 < planes:
            forward(number(z ^ (step - 1), r, first), [to_second, partner])
            forward(number(z ^ (step - 1), r, second), [partner])
        if 0 <= step - 2 < planes:
            forward(number(z ^ (step - 2), r, diag), [partner])
    for k in range(planes):
        for j in range(4):
            for i in every:
                await_block(i, number(z ^ k, 1 - r, c ^ j))
    for keep in keeps:
        keep.wait()
    for copies in sent:
        for copy in copies:
            copy.wait_send()

def gather(arrays, planes, collective_id, parts=1):
    count = len(arrays)
    blocks = planes * 8
    sends = (3 + planes - 1) + (planes - 1) * 3 + planes * 4
    pieces = count - 1 + parts
    return pl.pallas_call(
        functools.partial(gather_kernel, planes, parts, count),
        out_shape=[jax.ShapeDtypeStruct((blocks * a.shape[0],) + a.shape[1:], a.dtype) for a in arrays],
        in_specs=[ANYSPEC] * count, out_specs=[ANYSPEC] * count,
        scratch_shapes=[pltpu.SemaphoreType.DMA((count,)), pltpu.SemaphoreType.DMA((pieces, sends)), pltpu.SemaphoreType.DMA((pieces, blocks))],
        compiler_params=pltpu.CompilerParams(collective_id=collective_id, has_side_effects=True),
    )(*arrays)

def reducer(planes, cuts, parts, outs, buffers, semaphores):
    held, fromp, relay, near, far = buffers
    load_sem, pair_send, pair_recv, send_sem, relay_recv, near_recv, far_recv = semaphores
    z, r, c = place()
    first, second, diag = c ^ (1 + r), c ^ (2 - r), c ^ 3
    partner = (z, 1 - r, c)
    to_first, to_second = (z, r, first), (z, r, second)
    full = outs[0].shape[0]
    depth = full // cuts
    every = range(len(parts))

    def cut(ref, v):
        return ref.at[pl.ds(pl.multiple_of((v % cuts) * depth, depth), depth)]

    def rows(a, v, rr, cc):
        which = (((z ^ (v // cuts)) if planes > 1 else 0) * 2 + rr) * 4 + cc
        return parts[a].at[pl.ds(pl.multiple_of(which * full + (v % cuts) * depth, depth), depth)]

    columns, partner_columns = [c, first, second, diag], [c, second, first, diag]

    def remote(source, target, send, recv, device):
        return pltpu.make_async_remote_copy(
            src_ref=source, dst_ref=target, send_sem=send, recv_sem=recv, device_id=device, device_id_type=MESH)

    def mine(a, v, j):
        return cut(held[a].at[v // cuts, j], v)

    def paired(a, v, j):
        return cut(fromp[a].at[v // cuts, j], v)

    def nearby(a, v, which):
        return cut(near[a].at[v // cuts, which], v)

    def load(a, v, j):
        return pltpu.make_async_copy(rows(a, v, r, columns[j]), mine(a, v, j), load_sem.at[a, v, j])

    def pair(a, v, j):
        return remote(rows(a, v, 1 - r, partner_columns[j]), paired(a, v, j), pair_send.at[a, v, j], pair_recv.at[a, v, j], partner)

    def begin(i, _):
        v = planes * cuts - 1 - i
        for j in (3, 2, 1, 0):
            for a in every:
                load(a, v, j).start()
                pair(a, v, j).start()
        return 0

    step_rows = min(32, depth)

    def add(target, sources):
        def body(i, _):
            at = pl.ds(pl.multiple_of(i * step_rows, step_rows), step_rows)
            total = sources[0][at].astype(jnp.float32)
            for source in sources[1:]:
                total = total + source[at].astype(jnp.float32)
            target[at] = total.astype(target.dtype)
            return 0
        lax.fori_loop(0, depth // step_rows, body, 0)

    def ready(a, v, j):
        load(a, v, j).wait()
        pair(a, v, j).wait_recv()

    def to_diag(a, v):
        return remote(mine(a, v, 3), cut(relay[a].at[v // cuts], v), send_sem.at[a, v, 0], relay_recv.at[a, v], to_second)

    def to_near(a, v, which):
        source, device = (mine(a, v, 2), to_second) if which else (mine(a, v, 1), to_first)
        return remote(source, nearby(a, v, which), send_sem.at[a, v, 1 + which], near_recv.at[a, v, which], device)

    def to_far(a, v):
        slot = jnp.maximum(v - cuts, 0)
        return remote(mine(a, v, 0), cut(far[a].at[slot // cuts], v), send_sem.at[a, v, 3], far_recv.at[a, slot], (z ^ (v // cuts), r, c))

    def to_relay(v):
        for a in every:
            ready(a, v, 3)
            add(mine(a, v, 3), [mine(a, v, 3), paired(a, v, 3)])
            to_diag(a, v).start()
        for a in every:
            ready(a, v, 2)
            add(mine(a, v, 2), [mine(a, v, 2), paired(a, v, 2)])
            to_near(a, v, 1).start()

    def pass_on(v):
        for a in every:
            ready(a, v, 1)
            to_diag(a, v).wait_recv()
            add(mine(a, v, 1), [mine(a, v, 1), paired(a, v, 1), cut(relay[a].at[v // cuts], v)])
            to_near(a, v, 0).start()

    def collect(v):
        for a in every:
            ready(a, v, 0)
            to_near(a, v, 0).wait_recv()
            to_near(a, v, 1).wait_recv()
            terms = [mine(a, v, 0), paired(a, v, 0), nearby(a, v, 0), nearby(a, v, 1)]

            @pl.when(v >= cuts)
            def _():
                add(mine(a, v, 0), terms)
                to_far(a, v).start()

            @pl.when(v < cuts)
            def _():
                for i in range(1, planes):
                    to_far(a, v + i * cuts).wait_recv()
                add(cut(outs[a], v), terms + [cut(far[a].at[i], v) for i in range(planes - 1)])

    def drain(v, _):
        for a in every:
            for j in range(4):
                pair(a, v, j).wait_send()
            to_diag(a, v).wait_send()
            to_near(a, v, 0).wait_send()
            to_near(a, v, 1).wait_send()

            @pl.when(v >= cuts)
            def _():
                to_far(a, v).wait_send()
        return 0

    return begin, to_relay, pass_on, collect, drain


def reduce_steps(planes, cuts, parts, outs, buffers, semaphores, filler):
    z, r, c = place()
    greet([(z, r, c ^ 1), (z, r, c ^ 2), (z, 1 - r, c)] + [(z ^ k, r, c) for k in range(1, planes)])
    begin, to_relay, pass_on, collect, drain = reducer(planes, cuts, parts, outs, buffers, semaphores)
    units = planes * cuts
    lax.fori_loop(0, units, begin, 0)
    lag = 1

    def step_body(step, _):
        @pl.when(step < units)
        def _():
            to_relay(units - 1 - step)

        @pl.when(jnp.logical_and(step >= lag, step < units + lag))
        def _():
            pass_on(units - 1 - step + lag)

        @pl.when(step >= 2 * lag)
        def _():
            collect(units - 1 - step + 2 * lag)
        if filler is not None:
            filler(step)
        return 0

    lax.fori_loop(0, units + 2 * lag, step_body, 0)
    lax.fori_loop(0, units, drain, 0)


def reduce_scratch(partials, planes, cuts):
    shapes = [((p.shape[0] // (planes * 8), p.shape[1]), p.dtype) for p in partials]
    count, far, units = len(partials), max(planes - 1, 1), planes * cuts
    dma = pltpu.SemaphoreType.DMA
    buffers = [pltpu.VMEM(lead + shape, kind) for lead in ((planes, 4), (planes, 4), (planes,), (planes, 2), (far,)) for shape, kind in shapes]
    return shapes, buffers, [
        dma((count, units, 4)), dma((count, units, 4)), dma((count, units, 4)), dma((count, units, 4)),
        dma((count, units)), dma((count, units, 2)), dma((count, far * cuts))]


def reduce_kernel(planes, count, *refs):
    buffers = [refs[(2 + i) * count:(3 + i) * count] for i in range(5)]
    reduce_steps(planes, CUTS, refs[:count], refs[count:2 * count], buffers, refs[7 * count:], None)


def reduce_scatter(partials, planes, collective_id):
    count = len(partials)
    shapes, buffers, semaphores = reduce_scratch(partials, planes, CUTS)
    return pl.pallas_call(
        functools.partial(reduce_kernel, planes, count),
        out_shape=[jax.ShapeDtypeStruct(shape, jnp.float32) for shape, _ in shapes],
        in_specs=[ANYSPEC] * count, out_specs=[pl.BlockSpec(memory_space=pltpu.VMEM)] * count,
        scratch_shapes=buffers + semaphores,
        compiler_params=pltpu.CompilerParams(collective_id=collective_id, has_side_effects=True, vmem_limit_bytes=48 * 2**20),
    )(*partials)


def opening_kernel(x_ref, wq_ref, wk_ref, wv_ref, all_x, proj_ref, own_sem, send_sem, recv_sem, keep_sem, swap_send, swap_recv):
    z, r, c = place()
    width = proj_ref.shape[1] // 3
    depth = wq_ref.shape[0]

    def source(a, target):
        return (wq_ref, wk_ref, wv_ref)[a].at[:, pl.ds(pl.multiple_of(target * width, width), width)]

    def spot(a, origin):
        return proj_ref.at[pl.ds(pl.multiple_of(origin * depth, depth), depth), pl.ds(a * width, width)]

    keeps = [pltpu.make_async_copy(source(a, c), spot(a, c), keep_sem.at[a]) for a in range(3)]
    swaps = [pltpu.make_async_remote_copy(
        src_ref=source(a, c ^ j), dst_ref=spot(a, c), send_sem=swap_send.at[a, j - 1], recv_sem=swap_recv.at[a, j - 1],
        device_id=(z, r, c ^ j), device_id_type=MESH) for a in range(3) for j in range(1, 4)]

    def beside():
        for copy in keeps + swaps:
            copy.start()

    gather_steps(1, 2, (x_ref,), (all_x,), own_sem, send_sem, recv_sem, [(z, r, c ^ 3)], beside)
    for a in range(3):
        keeps[a].wait()
        for j in range(1, 4):
            arrived = spot(a, c ^ j)
            pltpu.make_async_remote_copy(
                src_ref=arrived, dst_ref=arrived, send_sem=swap_send.at[a, j - 1], recv_sem=swap_recv.at[a, j - 1],
                device_id=(z, r, c ^ j), device_id_type=MESH).wait_recv()
    for swap in swaps:
        swap.wait_send()


def opening(normal_x, w_query, w_key, w_value, collective_id):
    depth, half = w_query.shape
    dma = pltpu.SemaphoreType.DMA
    shape = jax.ShapeDtypeStruct
    return pl.pallas_call(
        opening_kernel,
        out_shape=[shape((8 * normal_x.shape[0], normal_x.shape[1]), normal_x.dtype), shape((depth * 4, 3 * (half // 4)), w_query.dtype)],
        in_specs=[ANYSPEC] * 4, out_specs=[ANYSPEC] * 2,
        scratch_shapes=[dma((1,)), dma((2, 7)), dma((2, 8)), dma((3,)), dma((3, 3)), dma((3, 3))],
        compiler_params=pltpu.CompilerParams(collective_id=collective_id, has_side_effects=True),
    )(normal_x, w_query, w_key, w_value)


NEAR, SMALL, WIDE, LAG, AHEAD = (8, 16, 24), (24, 30, 36), (2, 4, 4), 3, 8


def finish_kernel(planes, proj_ref, outp_ref, small_ref, scaled_ref, mixed_part, entry_part,
                  proj_out, outp_out, small_out, mixed_out, entry_out, *scratch):
    (proj_own, outp_own, proj_in, outp_in, proj_far, outp_far, small_own, slices, far_slices, own_sem, swap_send, swap_recv, down_send, down_recv,
     far_down, up_send, up_recv, slice_send, slice_recv, far_send, far_recv, whole_send, whole_recv) = scratch[:23]
    wide = reducer(planes, CUTS, (mixed_part,), (mixed_out,), [(ref,) for ref in scratch[23:28]], scratch[28:35])
    near = reducer(1, 1, (entry_part,), (entry_out,), [(ref,) for ref in scratch[35:40]], scratch[40:47])
    z, r, c = place()
    here = r * 4 + c
    group = [(z, r ^ (j >> 2), c ^ (j & 3)) for j in range(1, 8)]
    greet(group + [(z ^ k, r, c) for k in range(1, planes)])
    width = proj_ref.shape[1] // 3
    depth, out_width = proj_ref.shape[0] // 4, outp_ref.shape[1] // 4
    step, tall = depth // 8, outp_ref.shape[0] // 2
    chunks = 32

    def remote(source, target, send, recv, device):
        return pltpu.make_async_remote_copy(
            src_ref=source, dst_ref=target, send_sem=send, recv_sem=recv, device_id=device, device_id_type=MESH)

    def owner(i):
        return (i - 24) // 2

    def piece(i, target):
        if i < 24:
            a, m = i // 8, i % 8
            return proj_ref.at[pl.ds(pl.multiple_of(target * depth + m * step, step), step), pl.ds(a * width, width)]
        return outp_ref.at[pl.ds((i % 2) * tall, tall), pl.ds(pl.multiple_of(target * out_width, out_width), out_width)]

    def spot(i, origin):
        a, m = i // 8, i % 8
        return proj_own.at[a, pl.ds(m * step, step), pl.ds(pl.multiple_of(origin * width, width), width)]

    def rows(proj, outp, i):
        if i < 24:
            return proj.at[i // 8, pl.ds((i % 8) * step, step), :]
        return outp.at[pl.ds((i - 24) * tall, tall), :]

    small_copies = []

    def small_begin():
        lanes = small_ref.shape[2]
        small_own[...] = small_ref[...]
        for j in range(entry_out.shape[1] // lanes):
            at = pl.ds(j * lanes, lanes)
            part = jnp.sum(entry_out[:, at] * scaled_ref[:, at], axis=0, keepdims=True)
            small_own[j // small_ref.shape[1], pl.ds(j % small_ref.shape[1], 1), :] = part
        for j in range(1, 8):
            copy = remote(small_own.at[here ^ j], slices.at[here], slice_send.at[j], slice_recv.at[here], group[j - 1])
            copy.start()
            small_copies.append(copy)

    order = [24, 25, 0, 1, 26, 27, 2, 3, 28, 29, 4, 5, 30, 31] + list(range(6, 24))
    swaps = []

    def issue(i):
        if i < 24:
            keep = pltpu.make_async_copy(piece(i, c), spot(i, c), own_sem.at[i])
            keep.start()
            for j in range(1, 4):
                copy = remote(piece(i, c ^ j), spot(i, c), swap_send.at[i, j - 1], swap_recv.at[i, j - 1], (z, r, c ^ j))
                copy.start()
                swaps.append(copy)
        else:
            @pl.when(c == owner(i))
            def _():
                pltpu.make_async_copy(piece(i, c), rows(proj_own, outp_own, i), own_sem.at[i]).start()
                for j in range(1, 4):
                    remote(piece(i, c ^ j), rows(proj_own, outp_own, i), swap_send.at[i, j - 1], swap_recv.at[i, 0], (z, r, c ^ j)).start()

    ahead = AHEAD
    for i in order[:ahead]:
        issue(i)
    near[0](0, 0)
    lax.fori_loop(0, planes * CUTS, wide[0], 0)

    def local_ready(i):
        target = rows(proj_own, outp_own, i)
        if i < 24:
            pltpu.make_async_copy(piece(i, c), spot(i, c), own_sem.at[i]).wait()
            for j in range(1, 4):
                arrived = spot(i, c ^ j)
                remote(arrived, arrived, swap_send.at[i, j - 1], swap_recv.at[i, j - 1], (z, r, c ^ j)).wait_recv()
        else:
            @pl.when(c == owner(i))
            def _():
                pltpu.make_async_copy(piece(i, c), target, own_sem.at[i]).wait()

            @pl.when(c != owner(i))
            def _():
                remote(target, target, swap_send.at[i, 0], swap_recv.at[i, 0], (z, r, c ^ 1)).wait_recv()

    def combine(target, sources, count):
        def body(s, _):
            at = pl.ds(pl.multiple_of(s * 32, 32), 32)
            total = sources[0][at].astype(jnp.float32)
            for source in sources[1:]:
                total = total + source[at].astype(jnp.float32)
            target[at] = total.astype(target.dtype)
            return 0
        lax.fori_loop(0, count // 32, body, 0)

    def seat(i):
        return z if i % 2 == 0 else planes - 1 - z

    def at_seat(i, p):
        return (p if i % 2 == 0 else planes - 1 - p, r, c)

    def refs(i):
        return [rows(proj, outp, i) for proj, outp in ((proj_own, outp_own), (proj_in, outp_in), (proj_far, outp_far), (proj_out, outp_out))]

    def down_copy(i, p):
        own, near_in, far_in, _ = refs(i)
        if p == 0:
            return remote(own, near_in, down_send.at[i], down_recv.at[i], at_seat(i, 1))
        return remote(own, far_in, down_send.at[i], far_down.at[i], at_seat(i, p - 1))

    def up_copy(i, p, target):
        result = refs(i)[3]
        return remote(result, result, up_send.at[i, 0 if target == 0 else 1], up_recv.at[i], at_seat(i, target))

    def hop(i, h):
        own, near_in, far_in, result = refs(i)

        if h == 0:
            for p in (0, 3):
                @pl.when(seat(i) == p)
                def _(p=p):
                    local_ready(i)
                    down_copy(i, p).start()
        elif h == 1:
            @pl.when(seat(i) == 2)
            def _():
                local_ready(i)
                down_copy(i, 3).wait_recv()
                combine(own, [own, far_in], own.shape[0])
                down_copy(i, 2).start()
        elif h == 2:
            @pl.when(seat(i) == 1)
            def _():
                local_ready(i)
                down_copy(i, 0).wait_recv()
                down_copy(i, 2).wait_recv()
                combine(result, [own, near_in, far_in], own.shape[0])
                up_copy(i, 1, 0).start()
                up_copy(i, 1, 2).start()
        elif h == 3:
            @pl.when(seat(i) == 2)
            def _():
                up_copy(i, 1, 2).wait_recv()
                up_copy(i, 2, 3).start()
        else:
            for p in (0, 3):
                @pl.when(seat(i) == p)
                def _(p=p):
                    up_copy(i, 1, p).wait_recv()

    def small_group():
        for j in range(1, 8):
            arrived = slices.at[here ^ j]
            remote(arrived, arrived, slice_send.at[0], slice_recv.at[here ^ j], group[j - 1]).wait_recv()
        slices[here] = small_own[here]
        total = slices[0]
        for j in range(1, 8):
            total = total + slices[j]
        far_slices[z] = total
        for k in range(1, planes):
            copy = remote(far_slices.at[z], far_slices.at[z], far_send.at[k - 1], far_recv.at[z], (z ^ k, r, c))
            copy.start()
            small_copies.append(copy)

    def small_far():
        for k in range(1, planes):
            arrived = far_slices.at[z ^ k]
            remote(arrived, arrived, far_send.at[k - 1], far_recv.at[z ^ k], (z ^ k, r, c)).wait_recv()
        total = far_slices[0]
        for k in range(1, planes):
            total = total + far_slices[k]
        small_out[here] = total
        for j in range(1, 8):
            copy = remote(small_out.at[here], small_out.at[here], whole_send.at[j], whole_recv.at[here], group[j - 1])
            copy.start()
            small_copies.append(copy)

    lag = LAG
    hops = 5
    actions = {}

    def plan(slot, action):
        actions.setdefault(slot, []).append(action)

    for slot, kind in zip(NEAR, (1, 2, 3)):
        plan(slot, lambda kind=kind: near[kind](0))
    for slot, action in zip(SMALL, (small_begin, small_group, small_far)):
        plan(slot, action)
    for n in range(planes * CUTS):
        for kind in (1, 2, 3):
            plan(int(WIDE[0] + n * WIDE[1] + (kind - 1) * WIDE[2]), lambda v=planes * CUTS - 1 - n, kind=kind: wide[kind](v))
    slots = chunks + (hops - 1) * lag
    for s in range(max(slots, max(actions) + 1)):
        if s + ahead < chunks:
            issue(order[s + ahead])
        for h in range(hops):
            if 0 <= s - h * lag < chunks:
                hop(order[s - h * lag], h)
        for action in actions.get(s, ()):
            action()
    for j in range(1, 8):
        arrived = small_out.at[here ^ j]
        remote(arrived, arrived, whole_send.at[0], whole_recv.at[here ^ j], group[j - 1]).wait_recv()
    near[4](0, 0)
    lax.fori_loop(0, planes * CUTS, wide[4], 0)
    for copy in small_copies + swaps:
        copy.wait_send()
    for i in range(24, 32):
        @pl.when(c == owner(i))
        def _():
            for j in range(1, 4):
                remote(piece(i, c ^ j), rows(proj_own, outp_own, i), swap_send.at[i, j - 1], swap_recv.at[i, 0], (z, r, c ^ j)).wait_send()
    for i in range(chunks):
        @pl.when(seat(i) != 1)
        def _(i=i):
            down_copy(i, 0).wait_send()

        @pl.when(seat(i) == 1)
        def _(i=i):
            up_copy(i, 1, 0).wait_send()

        @pl.when(jnp.logical_or(seat(i) == 1, seat(i) == 2))
        def _(i=i):
            up_copy(i, 1, 2).wait_send()


def finish(grad_proj_own, grad_out_own, small, scaled, mixed_part, entry_part, planes, collective_id):
    depth, width = grad_proj_own.shape[0] // 4, grad_proj_own.shape[1] // 3
    out_rows, out_width = grad_out_own.shape[0], grad_out_own.shape[1] // 4
    kind = grad_proj_own.dtype
    proj, outp = (3, depth, 4 * width), (4 * out_rows, out_width)
    vmem = pl.BlockSpec(memory_space=pltpu.VMEM)
    dma = pltpu.SemaphoreType.DMA
    [(mixed_shape, _)], mixed_buffers, mixed_semaphores = reduce_scratch([mixed_part], planes, CUTS)
    [(entry_shape, _)], entry_buffers, entry_semaphores = reduce_scratch([entry_part], 1, 1)
    return pl.pallas_call(
        functools.partial(finish_kernel, planes),
        out_shape=[jax.ShapeDtypeStruct(proj, kind), jax.ShapeDtypeStruct(outp, kind), jax.ShapeDtypeStruct(small.shape, small.dtype),
                   jax.ShapeDtypeStruct(mixed_shape, jnp.float32), jax.ShapeDtypeStruct(entry_shape, jnp.float32)],
        in_specs=[ANYSPEC, ANYSPEC, vmem, vmem, ANYSPEC, ANYSPEC], out_specs=[vmem] * 5,
        scratch_shapes=[
            pltpu.VMEM(proj, kind), pltpu.VMEM(outp, kind), pltpu.VMEM(proj, kind), pltpu.VMEM(outp, kind), pltpu.VMEM(proj, kind), pltpu.VMEM(outp, kind),
            pltpu.VMEM(small.shape, jnp.float32), pltpu.VMEM(small.shape, jnp.float32), pltpu.VMEM((planes,) + small.shape[1:], jnp.float32),
            dma((32,)), dma((32, 3)), dma((32, 3)), dma((32,)), dma((32,)), dma((32,)), dma((32, 2)), dma((32,)),
            dma((8,)), dma((8,)), dma((planes,)), dma((planes,)), dma((8,)), dma((8,))]
        + mixed_buffers + mixed_semaphores + entry_buffers + entry_semaphores,
        compiler_params=pltpu.CompilerParams(collective_id=collective_id, has_side_effects=True, vmem_limit_bytes=58 * 2**20),
    )(grad_proj_own, grad_out_own, small, scaled, mixed_part, entry_part)


def expert_kernel(planes, experts, own_h, own_side, cot, w_gate, w_up, w_down,
                  all_h, all_side, entry_out, route_out, active_out, grad_gate_out, grad_up_out,
                  gate_use, up_use, down_use, rows_h, rows_c, rows_side, back_rows,
                  gate_rows, up_rows, active_rows, grad_gate, grad_up, entry_stage, route_stage,
                  weight_sem, own_sem, send_sem, recv_sem, cot_sem, load_sem, store_sem):
    z, r, c = place()
    first, second, diag = c ^ (1 + r), c ^ (2 - r), c ^ 3
    partner = (z, 1 - r, c)
    to_first, to_second = (z, r, first), (z, r, second)
    count = own_h.shape[0]
    group = 4 * count
    expert = z * 4 + c
    half = count // 2
    pieces = [(own_h, all_h, 0, half), (own_h, all_h, half, half), (own_side, all_side, 0, count)]

    weights = [(w_gate, gate_use), (w_up, up_use), (w_down, down_use)]
    for i, (source, target) in enumerate(weights):
        pltpu.make_async_copy(source, target, weight_sem.at[i]).start()

    def number(zz, rr, cc):
        return (zz * 2 + rr) * 4 + cc

    def spot(i, which):
        _, target, start, size = pieces[i]
        return target.at[pl.ds(pl.multiple_of(which * count + start, size), size)]

    def copy_of(i, source, which, k, slot, device):
        return pltpu.make_async_remote_copy(
            src_ref=source, dst_ref=spot(i, which), send_sem=send_sem.at[i, k, slot], recv_sem=recv_sem.at[i, which],
            device_id=device, device_id_type=MESH)

    def own_piece(i):
        source, _, start, size = pieces[i]
        return source.at[pl.ds(start, size)]

    def await_block(i, which):
        copy_of(i, spot(i, which), which, 0, 0, partner).wait_recv()

    def forward(which, k, targets):
        for i in range(3):
            await_block(i, which)
            for slot, device in targets:
                copy_of(i, spot(i, which), which, k, slot, device).start()

    greet([to_first, to_second, partner] + [(z ^ k, r, c) for k in range(1, planes)])
    mine = number(z, r, c)
    for i in range(3):
        for slot, device in ((0, to_first), (1, to_second)):
            copy_of(i, own_piece(i), mine, 0, slot, device).start()
        for k in range(1, planes):
            copy_of(i, own_piece(i), mine, k, 7, (z ^ k, r, c)).start()
        copy_of(i, own_piece(i), mine, 0, 2, partner).start()
    keeps = [pltpu.make_async_copy(own_piece(i), spot(i, mine), own_sem.at[i]) for i in range(3)]
    for keep in keeps:
        keep.start()

    def base_of(k, rr):
        return pl.multiple_of(number(z ^ k, rr, 0) * count, group)

    def dot(left, right):
        return jnp.dot(left, right, preferred_element_type=jnp.float32)

    def dot_turned(left, right):
        return lax.dot_general(left, right, (((1,), (1,)), ((), ())), preferred_element_type=jnp.float32)

    def cot_copy(g):
        rr = jnp.where(g % 2 == 0, r, 1 - r)
        return pltpu.make_async_copy(cot.at[pl.ds(base_of(g // 2, rr), group)], rows_c.at[g % 2], cot_sem.at[g % 2])

    cot_copy(0).start()
    for i, (source, target) in enumerate(weights):
        pltpu.make_async_copy(source, target, weight_sem.at[i]).wait()

    def back_body(g, _):
        @pl.when(g + 1 < 2 * planes)
        def _():
            cot_copy(g + 1).start()

        cot_copy(g).wait()
        back_rows[g] = dot_turned(rows_c[g % 2], down_use[...])
        return 0

    lax.fori_loop(0, 2 * planes, back_body, 0)
    for keep in keeps:
        keep.wait()

    def stores(k, rr, slot):
        at = pl.ds(base_of(k, rr), group)
        return [
            pltpu.make_async_copy(source.at[slot], target.at[at], store_sem.at[slot, i])
            for i, (source, target) in enumerate((
                (entry_stage, entry_out), (route_stage, route_out), (active_rows, active_out),
                (grad_gate, grad_gate_out), (grad_up, grad_up_out)))]

    def compute(k, rr, slot):
        at = pl.ds(base_of(k, rr), group)
        loads = [pltpu.make_async_copy(all_h.at[at], rows_h, load_sem.at[0]),
                 pltpu.make_async_copy(all_side.at[at], rows_side, load_sem.at[1])]
        for load in loads:
            load.start()
        for load in loads:
            load.wait()
        gate_rows[...] = dot(rows_h[...], gate_use[...])
        up_rows[...] = dot(rows_h[...], up_use[...])

        @pl.when(k > 0)
        def _():
            for store in stores(k, rr, slot):
                store.wait()

        part = 128
        lane = lax.broadcasted_iota(jnp.int32, (part, rows_side.shape[1]), 1)

        @pl.loop(0, group // part)
        def _(t):
            at = pl.ds(pl.multiple_of(t * part, part), part)
            mask = (lane == expert) | (lane == expert + experts)
            share = jnp.sum(jnp.where(mask, rows_side[at, :].astype(jnp.float32), 0.0), axis=1, keepdims=True)
            gate, up, back = gate_rows[at, :], up_rows[at, :], back_rows[2 * k + slot, at, :]
            squash = jax.nn.sigmoid(gate)
            silu = gate * squash
            active = silu * up
            route = jnp.sum(active * back, axis=1, keepdims=True)
            route_stage[slot, at, :] = jnp.where(lane == expert, route, 0.0).astype(jnp.bfloat16)
            active_rows[slot, at, :] = (share * active).astype(jnp.bfloat16)
            grad_active = share * back
            grad_gate[slot, at, :] = (grad_active * up * squash * (1.0 + gate * (1.0 - squash))).astype(jnp.bfloat16)
            grad_up[slot, at, :] = (grad_active * silu).astype(jnp.bfloat16)

    def finish_rows(k, rr, slot):
        entry = dot_turned(grad_gate[slot], gate_use[...]) + dot_turned(grad_up[slot], up_use[...])
        entry_stage[slot] = entry.astype(jnp.bfloat16)
        for store in stores(k, rr, slot):
            store.start()

    def step_body(step, _):
        @pl.when(jnp.logical_and(step > 0, step < planes))
        def _():
            forward(number(z ^ step, r, c), step, ((0, to_first), (1, to_second), (2, partner)))

        @pl.when(jnp.logical_and(step >= 3, step < planes + 3))
        def _():
            k = step - 3
            for j in range(4):
                for i in range(3):
                    await_block(i, number(z ^ k, 1 - r, c ^ j))
            compute(k, 1 - r, 1)

        @pl.when(jnp.logical_and(step >= 1, step < planes + 1))
        def _():
            k = step - 1
            forward(number(z ^ k, r, first), k, ((3, to_second), (4, partner)))
            forward(number(z ^ k, r, second), k, ((5, partner),))

        @pl.when(jnp.logical_and(step >= 3, step < planes + 3))
        def _():
            finish_rows(step - 3, 1 - r, 1)
            finish_rows(step - 3, r, 0)

        @pl.when(jnp.logical_and(step >= 2, step < planes + 2))
        def _():
            k = step - 2
            forward(number(z ^ k, r, diag), k, ((6, partner),))
            compute(k, r, 0)

        return 0

    lax.fori_loop(0, planes + 3, step_body, 0)
    for slot, rr in ((0, r), (1, 1 - r)):
        for store in stores(planes - 1, rr, slot):
            store.wait()

    def drain(k, _):
        for i in range(3):
            for slot in range(7):
                copy_of(i, spot(i, mine), mine, k, slot, partner).wait_send()

            @pl.when(k > 0)
            def _():
                copy_of(i, spot(i, mine), mine, k, 7, partner).wait_send()
        return 0

    lax.fori_loop(0, planes, drain, 0)


def expert_rows_on_links(normal_h, side, all_cotangent, w_gate, w_up, w_down, experts, collective_id):
    planes = lax.axis_size("dp")
    count, width = normal_h.shape
    hidden = w_gate.shape[1]
    total, group, low, wide = planes * 8 * count, 4 * count, jnp.bfloat16, jnp.float32
    sides = side.shape[1]
    vmem, dma = pltpu.VMEM, pltpu.SemaphoreType.DMA
    outs = [jax.ShapeDtypeStruct((total, n), low) for n in (width, sides, width, sides, hidden, hidden, hidden)]
    return pl.pallas_call(
        functools.partial(expert_kernel, planes, experts),
        out_shape=outs, in_specs=[ANYSPEC] * 6, out_specs=[ANYSPEC] * 7,
        scratch_shapes=[
            vmem((width, hidden), low), vmem((width, hidden), low), vmem((hidden, width), low),
            vmem((group, width), low), vmem((2, group, width), low), vmem((group, sides), low), vmem((2 * planes, group, hidden), wide),
            vmem((group, hidden), wide), vmem((group, hidden), wide),
            vmem((2, group, hidden), low), vmem((2, group, hidden), low), vmem((2, group, hidden), low),
            vmem((2, group, width), low), vmem((2, group, sides), low),
            dma((3,)), dma((3,)), dma((3, planes, 8)), dma((3, planes * 8)), dma((2,)), dma((2,)), dma((2, 5))],
        compiler_params=pltpu.CompilerParams(collective_id=collective_id, has_side_effects=True, vmem_limit_bytes=60 * 2**20),
    )(normal_h, side, all_cotangent, w_gate, w_up, w_down)


def entry_kernel(planes, entry_part, route_part, all_h, cot, active, grad_gate, grad_up, w_down,
                 entry_out, route_out, mixed_out, acc_gate, acc_up, acc_down, *scratch):
    buffers = [scratch[2 * i:2 * i + 2] for i in range(5)]
    semaphores = scratch[10:17]
    down_use, rows_h, rows_c, rows_x, mixed_stage, down_sem, load_sem, store_sem = scratch[17:]
    group = rows_h.shape[1]
    groups = all_h.shape[0] // group

    def loads(g):
        slot = g % 2
        at = pl.ds(pl.multiple_of(g * group, group), group)
        pairs = [(all_h.at[at], rows_h.at[slot]), (cot.at[at], rows_c.at[slot])] + [
            (source.at[at], rows_x.at[slot, i]) for i, source in enumerate((active, grad_gate, grad_up))]
        return [pltpu.make_async_copy(source, target, load_sem.at[slot, i]) for i, (source, target) in enumerate(pairs)]

    def store(g):
        at = pl.ds(pl.multiple_of(g * group, group), group)
        return pltpu.make_async_copy(mixed_stage, mixed_out.at[at], store_sem.at[0])

    def turned(left, right):
        return lax.dot_general(left, right, (((0,), (0,)), ((), ())), preferred_element_type=jnp.float32)

    down = pltpu.make_async_copy(w_down, down_use, down_sem.at[0])
    down.start()
    for load in loads(0):
        load.start()
    for acc in (acc_gate, acc_up, acc_down):
        @pl.loop(0, acc.shape[0] // 32)
        def _(t, acc=acc):
            acc[pl.ds(pl.multiple_of(t * 32, 32), 32), :] = jnp.zeros((32, acc.shape[1]), jnp.float32)
    down.wait()

    def one(g):
        @pl.when(g + 1 < groups)
        def _():
            for load in loads(g + 1):
                load.start()

        for load in loads(g):
            load.wait()
        slot = g % 2
        acc_gate[...] += turned(rows_h[slot], rows_x[slot, 1])
        acc_up[...] += turned(rows_h[slot], rows_x[slot, 2])
        acc_down[...] += turned(rows_x[slot, 0], rows_c[slot])

        @pl.when(g > 0)
        def _():
            store(g - 1).wait()

        mixed_stage[...] = jnp.dot(rows_x[slot, 0], down_use[...], preferred_element_type=jnp.float32).astype(jnp.bfloat16)
        store(g).start()

    per_step = -(-groups // (planes * CUTS))

    def filler(step):
        def body(i, _):
            @pl.when(step * per_step + i < groups)
            def _():
                one(step * per_step + i)
            return 0
        lax.fori_loop(0, per_step, body, 0)

    reduce_steps(planes, CUTS, (entry_part, route_part), (entry_out, route_out), buffers, semaphores, filler)
    store(groups - 1).wait()


def entry_sums(entry_part, route_part, all_h, cot, active, grad_gate, grad_up, w_down, collective_id):
    planes = lax.axis_size("dp")
    partials = [entry_part, route_part]
    shapes, buffers, semaphores = reduce_scratch(partials, planes, CUTS)
    (count, width), hidden, group = shapes[0][0], w_down.shape[0], 256
    low, wide, vmem, dma = jnp.bfloat16, jnp.float32, pltpu.VMEM, pltpu.SemaphoreType.DMA
    kept = pl.BlockSpec(memory_space=pltpu.VMEM)
    return pl.pallas_call(
        functools.partial(entry_kernel, planes),
        out_shape=[jax.ShapeDtypeStruct(shape, wide) for shape, _ in shapes] + [
            jax.ShapeDtypeStruct(entry_part.shape, low), jax.ShapeDtypeStruct((width, hidden), wide),
            jax.ShapeDtypeStruct((width, hidden), wide), jax.ShapeDtypeStruct((hidden, width), wide)],
        in_specs=[ANYSPEC] * 8, out_specs=[kept, kept, ANYSPEC, kept, kept, kept],
        scratch_shapes=buffers + semaphores + [
            vmem((hidden, width), low), vmem((2, group, width), low), vmem((2, group, width), low), vmem((2, 3, group, hidden), low),
            vmem((group, width), low), dma((1,)), dma((2, 5)), dma((1,))],
        compiler_params=pltpu.CompilerParams(collective_id=collective_id, has_side_effects=True, vmem_limit_bytes=60 * 2**20),
    )(entry_part, route_part, all_h, cot, active, grad_gate, grad_up, w_down)


def dot_plain(left, right):
    return jnp.dot(left, right, preferred_element_type=jnp.float32)


def dot_cols(left, right):
    return lax.dot_general(left, right, (((1,), (1,)), ((), ())), preferred_element_type=jnp.float32)


def dot_rows(left, right):
    return lax.dot_general(left, right, (((0,), (0,)), ((), ())), preferred_element_type=jnp.float32)


def group_peers():
    z, r, c = place()
    return r * 4 + c, [(z, r ^ (j >> 2), c ^ (j & 3)) for j in range(1, 8)]


def group_sums(own, slots, send_sem, recv_sem):
    here, peers = group_peers()
    copies = []
    for j, peer in enumerate(peers):
        copy = pltpu.make_async_remote_copy(
            src_ref=own, dst_ref=slots.at[j], send_sem=send_sem.at[j], recv_sem=recv_sem.at[j],
            device_id=peer, device_id_type=MESH)
        copy.start()
        copies.append(copy)
    for copy in copies:
        copy.wait()
    total = jnp.zeros(own.shape, jnp.float32)
    for who in range(8):
        which = here ^ who
        total = total + jnp.where(which == 0, own[...], slots[jnp.maximum(which - 1, 0)])
    return total


def row_of_tokens(values):
    folded = values[:, :128]
    for start in range(128, values.shape[1], 128):
        folded = folded + values[:, start:start + 128]
    return jnp.sum(folded.T, axis=0, keepdims=True)


def column_of(row):
    return jnp.broadcast_to(row, (128, row.shape[1])).T


BLOCK = 256


def block_weights(queries, keys, first, finish):
    scores = dot_cols(queries[first:finish], keys[:finish])
    at_query = lax.broadcasted_iota(jnp.int32, scores.shape, 0) + first
    at_key = lax.broadcasted_iota(jnp.int32, scores.shape, 1)
    scores = jnp.where(at_query >= at_key, scores, MASKED)
    weights = jnp.exp(scores - jnp.max(scores, axis=1, keepdims=True))
    return weights / jnp.sum(weights, axis=1, keepdims=True)


def forward_kernel(width, x_ref, proj_ref, gains, cosine, sine, w_out_ref,
                   part_out, query_out, key_out, value_out, raw_out, scale_out, mixed_out, w_out_own,
                   sums, slots, send_sem, recv_sem, keep_sem, swap_send, swap_recv):
    greet(group_peers()[1])
    z, r, c = place()
    rows, lanes_out = w_out_own.shape[0], w_out_ref.shape[1]

    def piece(target):
        return w_out_ref.at[pl.ds(pl.multiple_of(target * rows, rows), rows), :]

    def spot(origin):
        return w_out_own.at[:, pl.ds(pl.multiple_of(origin * lanes_out, lanes_out), lanes_out)]

    keep = pltpu.make_async_copy(piece(c), spot(c), keep_sem.at[0])
    keep.start()
    swaps = [pltpu.make_async_remote_copy(
        src_ref=piece(c ^ j), dst_ref=spot(c), send_sem=swap_send.at[j - 1], recv_sem=swap_recv.at[j - 1],
        device_id=(z, r, c ^ j), device_id_type=MESH) for j in range(1, 4)]
    local = value_out.shape[1]
    raw = dot_plain(x_ref[...], proj_ref[...])
    raw_out[...] = raw[:, :2 * local]
    value_out[...] = raw[:, 2 * local:].astype(jnp.bfloat16)
    sums[...] = jnp.zeros(sums.shape, jnp.float32)
    for i in range(2):
        half = raw_out[:, pl.ds(i * local, local)]
        sums[pl.ds(i, 1), :] = row_of_tokens(half * half)
    total = group_sums(sums, slots, send_sem, recv_sem)
    for swap in swaps:
        swap.start()
    for i, (target, factor) in enumerate(((query_out, 128 ** (-0.5)), (key_out, 1.0))):
        scale = lax.rsqrt(column_of(total[i:i + 1]) / width + EPSILON)
        scale_out[:, pl.ds(i * 128, 128)] = scale
        for start in range(0, local, 128):
            lanes = pl.ds(start, 128)
            normal = raw_out[:, pl.ds(i * local + start, 128)] * scale * gains[pl.ds(i, 1), lanes]
            turned = normal * cosine[...] + pltpu.roll(normal, 64, 1) * sine[...]
            target[:, lanes] = (turned * factor).astype(jnp.bfloat16)
    tokens = x_ref.shape[0]
    for start in range(0, local, 128):
        lanes = pl.ds(start, 128)
        queries, keys, values = query_out[:, lanes], key_out[:, lanes], value_out[:, lanes]
        for first in range(0, tokens, BLOCK):
            weights = block_weights(queries, keys, first, first + BLOCK).astype(jnp.bfloat16)
            mixed = dot_plain(weights, values[:first + BLOCK])
            mixed_out[pl.ds(first, BLOCK), lanes] = mixed.astype(jnp.bfloat16)
    keep.wait()
    for swap in swaps:
        swap.wait()
    part_out[...] = dot_plain(mixed_out[...], w_out_own[...]).astype(jnp.bfloat16)


def attention_forward(gathered_x, w_proj, gains, cosine, sine, w_out, collective_id):
    tokens, width = gathered_x.shape
    local = w_proj.shape[1] // 3
    low, wide = jnp.bfloat16, jnp.float32
    shape, vmem = jax.ShapeDtypeStruct, pl.BlockSpec(memory_space=pltpu.VMEM)
    dma = pltpu.SemaphoreType.DMA
    return pl.pallas_call(
        functools.partial(forward_kernel, width),
        out_shape=[shape((tokens, width), low), shape((tokens, local), low), shape((tokens, local), low), shape((tokens, local), low),
                   shape((tokens, 2 * local), wide), shape((tokens, 256), wide), shape((tokens, local), low),
                   shape((w_out.shape[0] // 4, 4 * w_out.shape[1]), low)],
        in_specs=[vmem] * 5 + [ANYSPEC], out_specs=[vmem] * 8,
        scratch_shapes=[pltpu.VMEM((8, tokens), wide), pltpu.VMEM((7, 8, tokens), wide), dma((7,)), dma((7,)), dma((1,)), dma((3,)), dma((3,))],
        compiler_params=pltpu.CompilerParams(collective_id=collective_id, has_side_effects=True, vmem_limit_bytes=56 * 2**20),
    )(gathered_x, w_proj, gains, cosine, sine, w_out)


def backward_kernel(width, grad_ref, w_out_ref, x_hbm, proj_hbm, query_ref, key_ref, value_ref, raw_ref, scale_ref, mixed_ref,
                    gains, cosine, sine, grad_x_out, grad_proj_out, grad_out_out, gain_out,
                    x_ref, proj_ref, grad_query, grad_key, grad_value, grad_raw, sums, slots, load_sem, send_sem, recv_sem):
    greet(group_peers()[1])
    loads = [pltpu.make_async_copy(x_hbm, x_ref, load_sem.at[0]), pltpu.make_async_copy(proj_hbm, proj_ref, load_sem.at[1])]
    for load in loads:
        load.start()
    local, tokens = value_ref.shape[1], value_ref.shape[0]
    grad_mixed = dot_cols(grad_ref[...], w_out_ref[...]).astype(jnp.bfloat16)
    grad_raw[:, pl.ds(0, local)] = grad_mixed
    for start in range(0, local, 128):
        lanes = pl.ds(start, 128)
        queries, keys, values, upstream = query_ref[:, lanes], key_ref[:, lanes], value_ref[:, lanes], grad_raw[:, lanes]
        for first in reversed(range(0, tokens, BLOCK)):
            finish = first + BLOCK
            weights = block_weights(queries, keys, first, finish)
            grad_weights = dot_cols(upstream[first:finish], values[:finish])
            centre = jnp.sum(weights * grad_weights, axis=1, keepdims=True)
            grad_scores = (weights * (grad_weights - centre)).astype(jnp.bfloat16)
            grad_query[pl.ds(first, BLOCK), lanes] = dot_plain(grad_scores, keys[:finish])
            key_part = dot_rows(grad_scores, queries[first:finish])
            value_part = dot_rows(weights.astype(jnp.bfloat16), upstream[first:finish])
            if finish == tokens:
                grad_key[:, lanes] = key_part
                grad_value[:, lanes] = value_part
            else:
                grad_key[pl.ds(0, finish), lanes] += key_part
                grad_value[pl.ds(0, finish), lanes] += value_part
    sums[...] = jnp.zeros(sums.shape, jnp.float32)
    gain_out[...] = jnp.zeros(gain_out.shape, jnp.float32)
    for i, (grad, factor) in enumerate(((grad_query, 128 ** (-0.5)), (grad_key, 1.0))):
        scale = scale_ref[:, pl.ds(i * 128, 128)]
        inner = None
        for start in range(0, local, 128):
            lanes = pl.ds(start, 128)
            upstream = grad[:, lanes] * factor
            normal = upstream * cosine[...] - pltpu.roll(upstream, 64, 1) * sine[...]
            raw = raw_ref[:, pl.ds(i * local + start, 128)]
            gain_out[pl.ds(i, 1), lanes] = jnp.sum(normal * raw * scale, axis=0, keepdims=True)
            weighted = gains[pl.ds(i, 1), lanes] * normal
            grad[:, lanes] = weighted
            inner = weighted * raw if inner is None else inner + weighted * raw
        sums[pl.ds(i, 1), :] = row_of_tokens(inner)
    total = group_sums(sums, slots, send_sem, recv_sem)
    for i, grad in enumerate((grad_query, grad_key)):
        scale = scale_ref[:, pl.ds(i * 128, 128)]
        factor = scale * scale * scale * column_of(total[i:i + 1]) / width
        for start in range(0, local, 128):
            lanes = pl.ds(start, 128)
            raw = raw_ref[:, pl.ds(i * local + start, 128)]
            grad_raw[:, pl.ds(i * local + start, 128)] = (scale * grad[:, lanes] - raw * factor).astype(jnp.bfloat16)
    grad_raw[:, pl.ds(2 * local, local)] = grad_value[...].astype(jnp.bfloat16)
    for load in loads:
        load.wait()
    grad_x_out[...] = dot_cols(grad_raw[...], proj_ref[...]).astype(jnp.bfloat16)
    grad_proj_out[...] = dot_rows(x_ref[...], grad_raw[...]).astype(jnp.bfloat16)
    grad_out_out[...] = dot_rows(mixed_ref[...], grad_ref[...]).astype(jnp.bfloat16)


def attention_backward(grad_gathered, w_out_own, gathered_x, w_proj, kept, gains, cosine, sine, collective_id):
    tokens, width = gathered_x.shape
    local = w_proj.shape[1] // 3
    low, wide = jnp.bfloat16, jnp.float32
    shape, vmem = jax.ShapeDtypeStruct, pl.BlockSpec(memory_space=pltpu.VMEM)
    dma = pltpu.SemaphoreType.DMA
    return pl.pallas_call(
        functools.partial(backward_kernel, width),
        out_shape=[shape((tokens, width), low), shape(w_proj.shape, low), shape(w_out_own.shape, low), shape((8, local), wide)],
        in_specs=[vmem, vmem, ANYSPEC, ANYSPEC] + [vmem] * 9, out_specs=[vmem] * 4,
        scratch_shapes=[
            pltpu.VMEM(gathered_x.shape, low), pltpu.VMEM(w_proj.shape, low),
            pltpu.VMEM((tokens, local), wide), pltpu.VMEM((tokens, local), wide), pltpu.VMEM((tokens, local), wide),
            pltpu.VMEM((tokens, 3 * local), low), pltpu.VMEM((8, tokens), wide), pltpu.VMEM((7, 8, tokens), wide),
            dma((2,)), dma((7,)), dma((7,))],
        compiler_params=pltpu.CompilerParams(collective_id=collective_id, has_side_effects=True, vmem_limit_bytes=60 * 2**20),
    )(grad_gathered, w_out_own, gathered_x, w_proj, *kept, gains, cosine, sine)


HEAD_DIM = 128
SEQ_LEN = 1024
EPSILON = 1e-05
THETA = 10000.0
MASKED = -1e30
GROUP = ("row", "col")
EVERYONE = ("dp", "row", "col")


def on_links():
    return lax.axis_size("dp") == 4 and lax.axis_size("col") == 4 and lax.axis_size("row") == 2


def gather_tokens(arrays, everyone, collective_id, parts):
    if on_links():
        return gather(arrays, 4 if everyone else 1, collective_id, parts)
    axes = EVERYONE if everyone else GROUP
    return [lax.all_gather(a, axes, axis=0, tiled=True) for a in arrays]


def scatter_sums(arrays, everyone, collective_id):
    if on_links():
        return reduce_scatter(arrays, 4 if everyone else 1, collective_id)
    axes = EVERYONE if everyone else GROUP
    return [lax.psum_scatter(a, axes, scatter_dimension=0, tiled=True).astype(jnp.float32) for a in arrays]


def open_attention(normal_x, w_query, w_key, w_value):
    if on_links():
        return opening(normal_x, w_query, w_key, w_value, 1)
    pieces = [lax.all_to_all(w, "col", split_axis=1, concat_axis=0, tiled=True) for w in (w_query, w_key, w_value)]
    (gathered_x,) = gather_tokens([normal_x], False, 2, 2)
    return gathered_x, jnp.concatenate(pieces, axis=1)


def inverse_rms(values):
    return lax.rsqrt(jnp.mean(values * values, axis=-1, keepdims=True) + EPSILON)


def norm_backward(values, inv_scale, gain_row, upstream):
    weighted = gain_row * upstream
    inner_sum = jnp.sum(weighted * values, axis=-1, keepdims=True)
    grad_values = inv_scale * weighted - values * inv_scale**3 * inner_sum / values.shape[-1]
    return (grad_values, jnp.sum(upstream * values * inv_scale, axis=0))


def contract(left, right):
    return jnp.dot(left, right, preferred_element_type=jnp.float32)


def contract_rows(left, right):
    return lax.dot_general(
        left, right, (((0,), (0,)), ((), ())), preferred_element_type=jnp.float32
    )


def contract_cols(left, right):
    return lax.dot_general(
        left, right, (((1,), (1,)), ((), ())), preferred_element_type=jnp.float32
    )


def turn_tables(total_rows, seq_length, head_width):
    positions = (jnp.arange(total_rows) % seq_length).astype(jnp.float32)
    inverse = THETA ** (-jnp.arange(0, head_width, 2, dtype=jnp.float32) / head_width)
    angles = positions[:, None] * inverse[None, :]
    angles = jnp.concatenate([angles, angles], axis=-1)
    return (jnp.cos(angles)[:, None, :], jnp.sin(angles)[:, None, :])


def rotate(values, cosine, sine_table):
    middle = values.shape[-1] // 2
    turned = jnp.concatenate([-values[..., middle:], values[..., :middle]], axis=-1)
    return values * cosine + turned * sine_table


def unrotate(upstream, cosine, sine_table):
    middle = upstream.shape[-1] // 2
    turned_part = upstream * sine_table
    return upstream * cosine + jnp.concatenate(
        [turned_part[..., middle:], -turned_part[..., :middle]], axis=-1
    )


def attend_forward(queries, key_rows, value_rows):
    length = queries.shape[0]
    block_rows = min(512, length)
    outputs = []
    sums_log = []
    for first_row in range(0, length, block_rows):
        finish = first_row + block_rows
        scores = jnp.einsum(
            "qhd,khd->hqk",
            queries[first_row:finish],
            key_rows[:finish],
            preferred_element_type=jnp.float32,
        )
        causal = (first_row + jnp.arange(block_rows))[:, None] >= jnp.arange(finish)[None, :]
        scores = jnp.where(causal[None], scores, MASKED)
        highest = jnp.max(scores, axis=-1, keepdims=True)
        weights = jnp.exp(scores - highest)
        totals = jnp.sum(weights, axis=-1, keepdims=True)
        weights = (weights / totals).astype(jnp.bfloat16)
        outputs.append(
            jnp.einsum(
                "hqk,khd->qhd", weights, value_rows[:finish], preferred_element_type=jnp.float32
            )
        )
        sums_log.append((highest + jnp.log(totals))[..., 0])
    return (jnp.concatenate(outputs, axis=0), jnp.concatenate(sums_log, axis=1))


def attend_backward(queries, key_rows, value_rows, grad_out, sums_log):
    length = queries.shape[0]
    block_rows = min(512, length)
    grad_queries = []
    grad_keys = jnp.zeros(key_rows.shape, jnp.float32)
    grad_values = jnp.zeros(value_rows.shape, jnp.float32)
    for first_row in range(0, length, block_rows):
        finish = first_row + block_rows
        scores = jnp.einsum(
            "qhd,khd->hqk",
            queries[first_row:finish],
            key_rows[:finish],
            preferred_element_type=jnp.float32,
        )
        causal = (first_row + jnp.arange(block_rows))[:, None] >= jnp.arange(finish)[None, :]
        scores = jnp.where(causal[None], scores, MASKED)
        weights = jnp.exp(scores - sums_log[:, first_row:finish, None])
        grad_weights = jnp.einsum(
            "qhd,khd->hqk",
            grad_out[first_row:finish],
            value_rows[:finish],
            preferred_element_type=jnp.float32,
        )
        centre = jnp.sum(weights * grad_weights, axis=-1, keepdims=True)
        grad_scores = (weights * (grad_weights - centre)).astype(jnp.bfloat16)
        grad_queries.append(
            jnp.einsum(
                "hqk,khd->qhd", grad_scores, key_rows[:finish], preferred_element_type=jnp.float32
            )
        )
        grad_keys = grad_keys.at[:finish].add(
            jnp.einsum(
                "hqk,qhd->khd",
                grad_scores,
                queries[first_row:finish],
                preferred_element_type=jnp.float32,
            )
        )
        grad_values = grad_values.at[:finish].add(
            jnp.einsum(
                "hqk,qhd->khd",
                weights.astype(jnp.bfloat16),
                grad_out[first_row:finish],
                preferred_element_type=jnp.float32,
            )
        )
    return (jnp.concatenate(grad_queries, axis=0), grad_keys, grad_values)


def by_sequence(step, pieces, sequences):
    if sequences == 1:
        return tuple(out[None] for out in step(*[p[0] for p in pieces]))
    return lax.map(lambda each: step(*each), tuple(pieces))


def expert_rows(normal_h, side, cotangent, gate_use, up_use, down_use, expert_count):
    if on_links():
        all_cotangent = lax.all_gather(cotangent, EVERYONE, axis=0, tiled=True)
        rows_h, _, entry_part, grad_side, active_share, grad_gate_rows, grad_up_rows = expert_rows_on_links(
            normal_h, side, all_cotangent, gate_use, up_use, down_use, expert_count, 6
        )
        entry_rows, grad_probs_all, out_part, *grads = entry_sums(
            entry_part, grad_side, rows_h, all_cotangent, active_share, grad_gate_rows, grad_up_rows, down_use, 7
        )
        return (entry_rows, grad_probs_all, out_part, *grads)
    all_cotangent, rows_h, rows_side = gather_tokens([cotangent, normal_h, side], True, 6, 2)
    expert = lax.axis_index("dp") * lax.axis_size("col") + lax.axis_index("col")
    lane = jnp.arange(side.shape[1])
    own_share = jnp.sum(
        jnp.where((lane == expert) | (lane == expert + expert_count), rows_side.astype(jnp.float32), 0.0),
        axis=1,
        keepdims=True,
    )
    back_rows = contract_cols(all_cotangent, down_use)
    gate_rows = contract(rows_h, gate_use)
    up_rows = contract(rows_h, up_use)
    sigmoid_gate = jax.nn.sigmoid(gate_rows)
    silu_gate = gate_rows * sigmoid_gate
    active = silu_gate * up_rows
    route_grad = jnp.sum(active * back_rows, axis=1, keepdims=True)
    active_share = (own_share * active).astype(jnp.bfloat16)
    grad_active = own_share * back_rows
    grad_gate_rows = (
        grad_active * up_rows * sigmoid_gate * (1.0 + gate_rows * (1.0 - sigmoid_gate))
    ).astype(jnp.bfloat16)
    grad_up_rows = (grad_active * silu_gate).astype(jnp.bfloat16)
    entry_part = (contract_cols(grad_gate_rows, gate_use) + contract_cols(grad_up_rows, up_use)).astype(jnp.bfloat16)
    grad_side = jnp.where(jnp.arange(128 if expert_count <= 128 else expert_count)[None, :] == expert, route_grad, 0.0).astype(jnp.bfloat16)
    entry_rows, grad_probs_all = scatter_sums([entry_part, grad_side], True, 7)
    out_part = contract(active_share, down_use).astype(jnp.bfloat16)
    (mixture,) = scatter_sums([out_part], True, 8)
    grad_down_w = contract_rows(active_share, all_cotangent)
    grad_gate_w = contract_rows(rows_h, grad_gate_rows)
    grad_up_w = contract_rows(rows_h, grad_up_rows)
    return entry_rows, grad_probs_all, mixture, grad_gate_w, grad_up_w, grad_down_w


def per_device(
    hidden_in,
    cotangent,
    norm_attn,
    w_query,
    w_key,
    w_value,
    query_gain,
    key_gain,
    w_out,
    norm_moe,
    w_router,
    w_gate,
    w_up,
    w_down,
    routes,
):
    inputs = hidden_in.astype(jnp.float32)
    upstream = cotangent.astype(jnp.float32)
    token_count, top_count = routes.shape
    model_width = inputs.shape[1]
    expert_count = w_router.shape[1]

    inv_input = inverse_rms(inputs)
    normal_x = (inputs * inv_input * norm_attn).astype(jnp.bfloat16)
    gathered_x, w_proj = open_attention(normal_x, w_query, w_key, w_value)
    group_tokens = gathered_x.shape[0]
    local_width = w_proj.shape[1] // 3
    head_count = local_width // HEAD_DIM
    offset = (lax.axis_index("row") * lax.axis_size("col") + lax.axis_index("col")) * local_width
    gain_query = lax.dynamic_slice_in_dim(query_gain, offset, local_width)
    gain_key = lax.dynamic_slice_in_dim(key_gain, offset, local_width)
    cosine, sine_table = turn_tables(group_tokens, SEQ_LEN, HEAD_DIM)
    head_shape = (group_tokens, head_count, HEAD_DIM)
    sequences = group_tokens // SEQ_LEN
    seq_shape = (sequences, SEQ_LEN, head_count, HEAD_DIM)
    in_kernels = on_links() and sequences == 1
    if in_kernels:
        gains = jnp.concatenate([gain_query[None], gain_key[None], jnp.zeros((6, local_width), jnp.float32)])
        sine_signed = jnp.where(jnp.arange(HEAD_DIM) < HEAD_DIM // 2, -sine_table[:, 0], sine_table[:, 0])
        tables = (gains, cosine[:, 0], sine_signed)
        attn_part, *kept, w_out_own = attention_forward(gathered_x, w_proj, *tables, w_out, 4)
    else:
        w_out_own = lax.all_to_all(w_out, "col", split_axis=0, concat_axis=1, tiled=True)
        raw = contract(gathered_x, w_proj)
        query_raw = raw[:, :local_width]
        key_raw = raw[:, local_width : 2 * local_width]
        value_heads = raw[:, 2 * local_width :].astype(jnp.bfloat16)
        query_square, key_square = lax.psum(
            (jnp.sum(query_raw * query_raw, axis=-1), jnp.sum(key_raw * key_raw, axis=-1)), GROUP
        )
        inv_query = lax.rsqrt(query_square / model_width + EPSILON)[:, None]
        inv_key = lax.rsqrt(key_square / model_width + EPSILON)[:, None]
        query_heads = (
            rotate((query_raw * inv_query * gain_query).reshape(head_shape), cosine, sine_table)
            * HEAD_DIM ** (-0.5)
        ).astype(jnp.bfloat16)
        key_heads = rotate(
            (key_raw * inv_key * gain_key).reshape(head_shape), cosine, sine_table
        ).astype(jnp.bfloat16)
        query_seq = query_heads.reshape(seq_shape)
        key_seq = key_heads.reshape(seq_shape)
        value_seq = value_heads.reshape(seq_shape)
        mixed, sums_log = by_sequence(attend_forward, (query_seq, key_seq, value_seq), sequences)
        mixed_heads = mixed.reshape(group_tokens, local_width).astype(jnp.bfloat16)
        attn_part = contract(mixed_heads, w_out_own).astype(jnp.bfloat16)
    (attn_rows,) = scatter_sums([attn_part], False, 5)
    state_rows = inputs + attn_rows

    inv_state = inverse_rms(state_rows)
    normal_h = (state_rows * inv_state * norm_moe).astype(jnp.bfloat16)
    logits = contract(normal_h, w_router)
    shifted = jnp.exp(logits - jnp.max(logits, axis=-1, keepdims=True))
    probabilities = shifted / jnp.sum(shifted, axis=-1, keepdims=True)
    selected = jnp.sum(
        (routes[:, :, None] == jnp.arange(expert_count)[None, None, :]).astype(jnp.float32), axis=1
    )
    shares = probabilities * selected
    share_high = shares.astype(jnp.bfloat16)
    share_low = (shares - share_high.astype(jnp.float32)).astype(jnp.bfloat16)
    side_width = max(2 * expert_count, 128)
    side = jnp.concatenate(
        [
            share_high,
            share_low,
            jnp.zeros((token_count, side_width - 2 * expert_count), jnp.bfloat16),
        ],
        axis=1,
    )

    chunks = max(1, lax.axis_size(EVERYONE) // 32)
    if chunks == 1:
        entry_rows, grad_probs_all, mixture, *expert_grads = expert_rows(
            normal_h, side, cotangent, w_gate[0], w_up[0], w_down[0], expert_count
        )
    else:

        def piece_step(sums, piece):
            entry, probs, mixed_rows, *grads = expert_rows(*piece, w_gate[0], w_up[0], w_down[0], expert_count)
            return [s + g for s, g in zip(sums, grads)], (entry, probs, mixed_rows)

        cut = [a.reshape((chunks, token_count // chunks) + a.shape[1:]) for a in (normal_h, side, cotangent)]
        empty = [jnp.zeros(w.shape[1:], jnp.float32) for w in (w_gate, w_up, w_down)]
        expert_grads, rows = lax.scan(piece_step, empty, cut)
        entry_rows, grad_probs_all, mixture = [r.reshape((token_count,) + r.shape[2:]) for r in rows]
    grad_gate_w, grad_up_w, grad_down_w = expert_grads
    grad_probs = selected * grad_probs_all[:, :expert_count]
    grad_logits = (
        probabilities * (grad_probs - jnp.sum(probabilities * grad_probs, axis=-1, keepdims=True))
    ).astype(jnp.bfloat16)
    grad_normal_h = entry_rows + contract_cols(grad_logits, w_router)
    grad_router_part = contract_rows(grad_logits, normal_h)
    grad_state_part, grad_moe_part = norm_backward(state_rows, inv_state, norm_moe, grad_normal_h)
    grad_state = upstream + grad_state_part
    grad_attn = grad_state.astype(jnp.bfloat16)
    (grad_gathered,) = gather_tokens([grad_attn], False, 9, 2)
    if in_kernels:
        grad_x_part, grad_proj_own, grad_out_own, gain_parts = attention_backward(
            grad_gathered, w_out_own, gathered_x, w_proj, kept, *tables, 10
        )
        grad_qgain_part, grad_kgain_part = gain_parts[0], gain_parts[1]
    else:
        grad_out_own = contract_rows(mixed_heads, grad_gathered).astype(jnp.bfloat16)
        grad_mixed = contract_cols(grad_gathered, w_out_own).astype(jnp.bfloat16)
        grad_query_seq, grad_key_seq, grad_value_seq = by_sequence(
            attend_backward,
            (query_seq, key_seq, value_seq, grad_mixed.reshape(seq_shape), sums_log),
            sequences,
        )
        grad_normal_q = unrotate(
            grad_query_seq.reshape(head_shape) * HEAD_DIM ** (-0.5), cosine, sine_table
        ).reshape(group_tokens, local_width)
        grad_normal_k = unrotate(grad_key_seq.reshape(head_shape), cosine, sine_table).reshape(
            group_tokens, local_width
        )
        weighted_q = gain_query * grad_normal_q
        weighted_k = gain_key * grad_normal_k
        inner_q, inner_k = lax.psum(
            (jnp.sum(weighted_q * query_raw, axis=-1), jnp.sum(weighted_k * key_raw, axis=-1)), GROUP
        )
        grad_query_raw = (
            inv_query * weighted_q - query_raw * inv_query**3 * inner_q[:, None] / model_width
        )
        grad_key_raw = inv_key * weighted_k - key_raw * inv_key**3 * inner_k[:, None] / model_width
        grad_qgain_part = jnp.sum(grad_normal_q * query_raw * inv_query, axis=0)
        grad_kgain_part = jnp.sum(grad_normal_k * key_raw * inv_key, axis=0)
        grad_raw = jnp.concatenate(
            [grad_query_raw, grad_key_raw, grad_value_seq.reshape(group_tokens, local_width)], axis=1
        ).astype(jnp.bfloat16)
        grad_x_part = contract_cols(grad_raw, w_proj).astype(jnp.bfloat16)
        grad_proj_own = contract_rows(gathered_x, grad_raw).astype(jnp.bfloat16)
    full_width = query_gain.shape[0]
    padded_qgain = lax.dynamic_update_slice_in_dim(
        jnp.zeros((full_width,), jnp.float32), grad_qgain_part, offset, 0
    )
    padded_kgain = lax.dynamic_update_slice_in_dim(
        jnp.zeros((full_width,), jnp.float32), grad_kgain_part, offset, 0
    )
    small = (padded_qgain, padded_kgain, grad_moe_part, grad_router_part)
    grad_query, grad_key, grad_value, grad_out_proj, mixture, grad_normal_x, small = last_sums(
        grad_proj_own, grad_out_own, small, inputs * inv_input, mixture, grad_x_part
    )
    grad_norm_attn, grad_query_gain, grad_key_gain, grad_norm_moe, grad_router = small
    grad_router = grad_router.T
    block_out = (state_rows + mixture).astype(jnp.bfloat16)
    grad_input = grad_state + norm_backward(inputs, inv_input, norm_attn, grad_normal_x)[0]
    return (
        block_out,
        grad_input,
        grad_norm_attn,
        grad_query,
        grad_key,
        grad_value,
        grad_query_gain,
        grad_key_gain,
        grad_out_proj,
        grad_norm_moe,
        grad_router,
        grad_gate_w[None],
        grad_up_w[None],
        grad_down_w[None],
    )


def last_sums(grad_proj_own, grad_out_own, small, scaled, mixed_part, entry_part):
    if on_links():
        parts = (jnp.zeros((scaled.shape[1],), jnp.float32), *small)
        flat = jnp.concatenate([part.reshape(-1) for part in parts])
        proj, outp, total, mixture, grad_normal_x = finish(
            grad_proj_own, grad_out_own, flat.reshape(8, -1, 128), scaled, mixed_part, entry_part, lax.axis_size("dp"), 12
        )
        total, sums, start = total.reshape(-1), [], 0
        for part in parts:
            sums.append(total[start : start + part.size].reshape(part.shape))
            start += part.size
        return (*(proj[a].astype(jnp.float32) for a in range(3)), outp.astype(jnp.float32), mixture, grad_normal_x, sums)
    (grad_normal_x,) = scatter_sums([entry_part], False, 11)
    small = (jnp.sum(grad_normal_x * scaled, axis=0), *small)
    width = grad_proj_own.shape[1] // 3
    blocks = [
        lax.all_to_all(grad_proj_own[:, a * width : (a + 1) * width], "col", split_axis=0, concat_axis=1, tiled=True)
        for a in range(3)
    ]
    out_block = lax.all_to_all(grad_out_own, "col", split_axis=1, concat_axis=0, tiled=True)
    weights = [total.astype(jnp.float32) for total in lax.psum((*blocks, out_block), "dp")]
    return (*weights, mixed_part, grad_normal_x, lax.psum(small, EVERYONE))


def solution(mesh):
    placed = (
        P(("dp", "row", "col"), None),
        P(("dp", "row", "col"), None),
        P(),
        P("col", "row"),
        P("col", "row"),
        P("col", "row"),
        P(),
        P(),
        P("row", "col"),
        P(),
        P(),
        P(("dp", "col"), None, "row"),
        P(("dp", "col"), None, "row"),
        P(("dp", "col"), "row", None),
        P(("dp", "row", "col"), None),
    )
    return jax.shard_map(
        per_device,
        mesh=mesh,
        in_specs=placed,
        out_specs=(
            P(("dp", "row", "col"), None),
            P(("dp", "row", "col"), None),
            P(),
            P("col", "row"),
            P("col", "row"),
            P("col", "row"),
            P(),
            P(),
            P("row", "col"),
            P(),
            P(),
            P(("dp", "col"), None, "row"),
            P(("dp", "col"), None, "row"),
            P(("dp", "col"), "row", None),
        ),
        check_vma=False,
    )
```

```python
import functools

import jax
import jax.numpy as jnp
import numpy as np
from jax import lax
from jax.experimental import pallas as pl
from jax.experimental.pallas import tpu as pltpu
from jax.sharding import PartitionSpec as P

MESH = pl.DeviceIdType.MESH
ANYSPEC = pl.BlockSpec(memory_space=pl.ANY)
CUTS = 2

def place():
    return lax.axis_index("dp"), lax.axis_index("row"), lax.axis_index("col")

def greet(peers):
    barrier = pltpu.get_barrier_semaphore()
    for peer in peers:
        pl.semaphore_signal(barrier, inc=1, device_id=peer, device_id_type=MESH)
    pl.semaphore_wait(barrier, len(peers))

def gather_kernel(planes, parts, count, *refs):
    gather_steps(planes, parts, refs[:count], refs[count:2 * count], *refs[2 * count:])


def gather_steps(planes, parts, ins, outs, own_sem, send_sem, recv_sem, more_peers=(), beside=None):
    count = len(ins)
    z, r, c = place()
    first, second, diag = c ^ (1 + r), c ^ (2 - r), c ^ 3
    partner = (z, 1 - r, c)
    to_first, to_second = (z, r, first), (z, r, second)
    greet([to_first, to_second, partner] + [(z ^ k, r, c) for k in range(1, planes)] + list(more_peers))
    if beside is not None:
        beside()
    pieces = []
    for a in range(count):
        cut = parts if a == 0 else 1
        pieces += [(a, p, ins[a].shape[0], ins[a].shape[0] // cut) for p in range(cut)]

    def number(zz, rr, cc):
        return ((zz if planes > 1 else 0) * 2 + rr) * 4 + cc

    def place_of(i, which):
        a, p, depth, cut = pieces[i]
        return outs[a].at[pl.ds(pl.multiple_of(which * depth + p * cut, cut), cut)]

    sent = [[] for _ in pieces]

    def send(i, which, target, own=False):
        a, p, depth, cut = pieces[i]
        spot = place_of(i, which)
        copy = pltpu.make_async_remote_copy(
            src_ref=ins[a].at[pl.ds(p * cut, cut)] if own else spot, dst_ref=spot,
            send_sem=send_sem.at[i, len(sent[i])], recv_sem=recv_sem.at[i, which],
            device_id=target, device_id_type=MESH)
        copy.start()
        sent[i].append(copy)

    def await_block(i, which):
        spot = place_of(i, which)
        pltpu.make_async_remote_copy(
            src_ref=spot, dst_ref=spot, send_sem=send_sem.at[i, 0], recv_sem=recv_sem.at[i, which],
            device_id=partner, device_id_type=MESH).wait_recv()

    mine = number(z, r, c)
    keeps = []
    every = range(len(pieces))
    for i in every:
        for target in [to_first, to_second] + [(z ^ k, r, c) for k in range(1, planes)] + [partner]:
            send(i, mine, target, True)
    for a in range(count):
        keep = pltpu.make_async_copy(ins[a], outs[a].at[pl.ds(pl.multiple_of(mine * ins[a].shape[0], ins[a].shape[0]), ins[a].shape[0])], own_sem.at[a])
        keep.start()
        keeps.append(keep)

    def forward(which, targets):
        for i in every:
            await_block(i, which)
            for target in targets:
                send(i, which, target)

    for step in range(planes + 2):
        if 0 < step < planes:
            forward(number(z ^ step, r, c), [to_first, to_second, partner])
        if 0 <= step - 1 < planes:
            forward(number(z ^ (step - 1), r, first), [to_second, partner])
            forward(number(z ^ (step - 1), r, second), [partner])
        if 0 <= step - 2 < planes:
            forward(number(z ^ (step - 2), r, diag), [partner])
    for k in range(planes):
        for j in range(4):
            for i in every:
                await_block(i, number(z ^ k, 1 - r, c ^ j))
    for keep in keeps:
        keep.wait()
    for copies in sent:
        for copy in copies:
            copy.wait_send()

def gather(arrays, planes, collective_id, parts=1):
    count = len(arrays)
    blocks = planes * 8
    sends = (3 + planes - 1) + (planes - 1) * 3 + planes * 4
    pieces = count - 1 + parts
    return pl.pallas_call(
        functools.partial(gather_kernel, planes, parts, count),
        out_shape=[jax.ShapeDtypeStruct((blocks * a.shape[0],) + a.shape[1:], a.dtype) for a in arrays],
        in_specs=[ANYSPEC] * count, out_specs=[ANYSPEC] * count,
        scratch_shapes=[pltpu.SemaphoreType.DMA((count,)), pltpu.SemaphoreType.DMA((pieces, sends)), pltpu.SemaphoreType.DMA((pieces, blocks))],
        compiler_params=pltpu.CompilerParams(collective_id=collective_id, has_side_effects=True),
    )(*arrays)

def reducer(planes, cuts, parts, outs, buffers, semaphores):
    held, fromp, relay, near, far = buffers
    load_sem, pair_send, pair_recv, send_sem, relay_recv, near_recv, far_recv = semaphores
    z, r, c = place()
    first, second, diag = c ^ (1 + r), c ^ (2 - r), c ^ 3
    partner = (z, 1 - r, c)
    to_first, to_second = (z, r, first), (z, r, second)
    full = outs[0].shape[0]
    depth = full // cuts
    every = range(len(parts))

    def cut(ref, v):
        return ref.at[pl.ds(pl.multiple_of((v % cuts) * depth, depth), depth)]

    def rows(a, v, rr, cc):
        which = (((z ^ (v // cuts)) if planes > 1 else 0) * 2 + rr) * 4 + cc
        return parts[a].at[pl.ds(pl.multiple_of(which * full + (v % cuts) * depth, depth), depth)]

    columns, partner_columns = [c, first, second, diag], [c, second, first, diag]

    def remote(source, target, send, recv, device):
        return pltpu.make_async_remote_copy(
            src_ref=source, dst_ref=target, send_sem=send, recv_sem=recv, device_id=device, device_id_type=MESH)

    def mine(a, v, j):
        return cut(held[a].at[v // cuts, j], v)

    def paired(a, v, j):
        return cut(fromp[a].at[v // cuts, j], v)

    def nearby(a, v, which):
        return cut(near[a].at[v // cuts, which], v)

    def load(a, v, j):
        return pltpu.make_async_copy(rows(a, v, r, columns[j]), mine(a, v, j), load_sem.at[a, v, j])

    def pair(a, v, j):
        return remote(rows(a, v, 1 - r, partner_columns[j]), paired(a, v, j), pair_send.at[a, v, j], pair_recv.at[a, v, j], partner)

    def begin(i, _):
        v = planes * cuts - 1 - i
        for j in (3, 2, 1, 0):
            for a in every:
                load(a, v, j).start()
                pair(a, v, j).start()
        return 0

    step_rows = min(32, depth)

    def add(target, sources):
        def body(i, _):
            at = pl.ds(pl.multiple_of(i * step_rows, step_rows), step_rows)
            total = sources[0][at].astype(jnp.float32)
            for source in sources[1:]:
                total = total + source[at].astype(jnp.float32)
            target[at] = total.astype(target.dtype)
            return 0
        lax.fori_loop(0, depth // step_rows, body, 0)

    def ready(a, v, j):
        load(a, v, j).wait()
        pair(a, v, j).wait_recv()

    def to_diag(a, v):
        return remote(mine(a, v, 3), cut(relay[a].at[v // cuts], v), send_sem.at[a, v, 0], relay_recv.at[a, v], to_second)

    def to_near(a, v, which):
        source, device = (mine(a, v, 2), to_second) if which else (mine(a, v, 1), to_first)
        return remote(source, nearby(a, v, which), send_sem.at[a, v, 1 + which], near_recv.at[a, v, which], device)

    def to_far(a, v):
        slot = jnp.maximum(v - cuts, 0)
        return remote(mine(a, v, 0), cut(far[a].at[slot // cuts], v), send_sem.at[a, v, 3], far_recv.at[a, slot], (z ^ (v // cuts), r, c))

    def to_relay(v):
        for a in every:
            ready(a, v, 3)
            add(mine(a, v, 3), [mine(a, v, 3), paired(a, v, 3)])
            to_diag(a, v).start()
        for a in every:
            ready(a, v, 2)
            add(mine(a, v, 2), [mine(a, v, 2), paired(a, v, 2)])
            to_near(a, v, 1).start()

    def pass_on(v):
        for a in every:
            ready(a, v, 1)
            to_diag(a, v).wait_recv()
            add(mine(a, v, 1), [mine(a, v, 1), paired(a, v, 1), cut(relay[a].at[v // cuts], v)])
            to_near(a, v, 0).start()

    def collect(v):
        for a in every:
            ready(a, v, 0)
            to_near(a, v, 0).wait_recv()
            to_near(a, v, 1).wait_recv()
            terms = [mine(a, v, 0), paired(a, v, 0), nearby(a, v, 0), nearby(a, v, 1)]

            @pl.when(v >= cuts)
            def _():
                add(mine(a, v, 0), terms)
                to_far(a, v).start()

            @pl.when(v < cuts)
            def _():
                for i in range(1, planes):
                    to_far(a, v + i * cuts).wait_recv()
                add(cut(outs[a], v), terms + [cut(far[a].at[i], v) for i in range(planes - 1)])

    def drain(v, _):
        for a in every:
            for j in range(4):
                pair(a, v, j).wait_send()
            to_diag(a, v).wait_send()
            to_near(a, v, 0).wait_send()
            to_near(a, v, 1).wait_send()

            @pl.when(v >= cuts)
            def _():
                to_far(a, v).wait_send()
        return 0

    return begin, to_relay, pass_on, collect, drain


def reduce_steps(planes, cuts, parts, outs, buffers, semaphores, filler):
    z, r, c = place()
    greet([(z, r, c ^ 1), (z, r, c ^ 2), (z, 1 - r, c)] + [(z ^ k, r, c) for k in range(1, planes)])
    begin, to_relay, pass_on, collect, drain = reducer(planes, cuts, parts, outs, buffers, semaphores)
    units = planes * cuts
    lax.fori_loop(0, units, begin, 0)
    lag = 1

    def step_body(step, _):
        @pl.when(step < units)
        def _():
            to_relay(units - 1 - step)

        @pl.when(jnp.logical_and(step >= lag, step < units + lag))
        def _():
            pass_on(units - 1 - step + lag)

        @pl.when(step >= 2 * lag)
        def _():
            collect(units - 1 - step + 2 * lag)
        if filler is not None:
            filler(step)
        return 0

    lax.fori_loop(0, units + 2 * lag, step_body, 0)
    lax.fori_loop(0, units, drain, 0)


def reduce_scratch(partials, planes, cuts):
    shapes = [((p.shape[0] // (planes * 8), p.shape[1]), p.dtype) for p in partials]
    count, far, units = len(partials), max(planes - 1, 1), planes * cuts
    dma = pltpu.SemaphoreType.DMA
    buffers = [pltpu.VMEM(lead + shape, kind) for lead in ((planes, 4), (planes, 4), (planes,), (planes, 2), (far,)) for shape, kind in shapes]
    return shapes, buffers, [
        dma((count, units, 4)), dma((count, units, 4)), dma((count, units, 4)), dma((count, units, 4)),
        dma((count, units)), dma((count, units, 2)), dma((count, far * cuts))]


def reduce_kernel(planes, count, *refs):
    buffers = [refs[(2 + i) * count:(3 + i) * count] for i in range(5)]
    reduce_steps(planes, CUTS, refs[:count], refs[count:2 * count], buffers, refs[7 * count:], None)


def reduce_scatter(partials, planes, collective_id):
    count = len(partials)
    shapes, buffers, semaphores = reduce_scratch(partials, planes, CUTS)
    return pl.pallas_call(
        functools.partial(reduce_kernel, planes, count),
        out_shape=[jax.ShapeDtypeStruct(shape, jnp.float32) for shape, _ in shapes],
        in_specs=[ANYSPEC] * count, out_specs=[pl.BlockSpec(memory_space=pltpu.VMEM)] * count,
        scratch_shapes=buffers + semaphores,
        compiler_params=pltpu.CompilerParams(collective_id=collective_id, has_side_effects=True, vmem_limit_bytes=48 * 2**20),
    )(*partials)


def opening_kernel(x_ref, gain_ref, wq_ref, wk_ref, wv_ref, all_x, proj_ref, normal, own_sem, send_sem, recv_sem, keep_sem, swap_send, swap_recv):
    z, r, c = place()
    width = proj_ref.shape[1] // 3
    depth = wq_ref.shape[0]

    def source(a, target):
        return (wq_ref, wk_ref, wv_ref)[a].at[:, pl.ds(pl.multiple_of(target * width, width), width)]

    def spot(a, origin):
        return proj_ref.at[pl.ds(pl.multiple_of(origin * depth, depth), depth), pl.ds(a * width, width)]

    keeps = [pltpu.make_async_copy(source(a, c), spot(a, c), keep_sem.at[a]) for a in range(3)]
    swaps = [pltpu.make_async_remote_copy(
        src_ref=source(a, c ^ j), dst_ref=spot(a, c), send_sem=swap_send.at[a, j - 1], recv_sem=swap_recv.at[a, j - 1],
        device_id=(z, r, c ^ j), device_id_type=MESH) for a in range(3) for j in range(1, 4)]

    def beside():
        for copy in keeps + swaps:
            copy.start()
        rows = x_ref[...].astype(jnp.float32)
        scale = lax.rsqrt(jnp.mean(rows * rows, axis=1, keepdims=True) + EPSILON)
        normal[...] = (rows * scale * gain_ref[...]).astype(jnp.bfloat16)

    gather_steps(1, 2, (normal,), (all_x,), own_sem, send_sem, recv_sem, [(z, r, c ^ 3)], beside)
    for a in range(3):
        keeps[a].wait()
        for j in range(1, 4):
            arrived = spot(a, c ^ j)
            pltpu.make_async_remote_copy(
                src_ref=arrived, dst_ref=arrived, send_sem=swap_send.at[a, j - 1], recv_sem=swap_recv.at[a, j - 1],
                device_id=(z, r, c ^ j), device_id_type=MESH).wait_recv()
    for swap in swaps:
        swap.wait_send()


def opening(hidden, gain, w_query, w_key, w_value, collective_id):
    depth, half = w_query.shape
    dma = pltpu.SemaphoreType.DMA
    shape = jax.ShapeDtypeStruct
    return pl.pallas_call(
        opening_kernel,
        out_shape=[shape((8 * hidden.shape[0], hidden.shape[1]), jnp.bfloat16), shape((depth * 4, 3 * (half // 4)), w_query.dtype)],
        in_specs=[pl.BlockSpec(memory_space=pltpu.VMEM)] * 2 + [ANYSPEC] * 3, out_specs=[ANYSPEC] * 2,
        scratch_shapes=[pltpu.VMEM(hidden.shape, jnp.bfloat16), dma((1,)), dma((2, 7)), dma((2, 8)), dma((3,)), dma((3, 3)), dma((3, 3))],
        compiler_params=pltpu.CompilerParams(collective_id=collective_id, has_side_effects=True),
    )(hidden, gain, w_query, w_key, w_value)


NEAR, SMALL, WIDE, LAG, AHEAD = (8, 16, 24), (24, 30, 36), (2, 4, 4), 3, 8


def finish_kernel(planes, proj_ref, outp_ref, small_ref, scaled_ref, mixed_part, entry_part,
                  proj_out, outp_out, small_out, mixed_out, entry_out, *scratch):
    (proj_own, outp_own, proj_in, outp_in, proj_far, outp_far, small_own, slices, far_slices, own_sem, swap_send, swap_recv, down_send, down_recv,
     far_down, up_send, up_recv, slice_send, slice_recv, far_send, far_recv, whole_send, whole_recv) = scratch[:23]
    wide = reducer(planes, CUTS, (mixed_part,), (mixed_out,), [(ref,) for ref in scratch[23:28]], scratch[28:35])
    near = reducer(1, 1, (entry_part,), (entry_out,), [(ref,) for ref in scratch[35:40]], scratch[40:47])
    z, r, c = place()
    here = r * 4 + c
    group = [(z, r ^ (j >> 2), c ^ (j & 3)) for j in range(1, 8)]
    greet(group + [(z ^ k, r, c) for k in range(1, planes)])
    width = proj_ref.shape[1] // 3
    depth, out_width = proj_ref.shape[0] // 4, outp_ref.shape[1] // 4
    step, tall = depth // 8, outp_ref.shape[0] // 2
    chunks = 32

    def remote(source, target, send, recv, device):
        return pltpu.make_async_remote_copy(
            src_ref=source, dst_ref=target, send_sem=send, recv_sem=recv, device_id=device, device_id_type=MESH)

    def owner(i):
        return (i - 24) // 2

    def piece(i, target):
        if i < 24:
            a, m = i // 8, i % 8
            return proj_ref.at[pl.ds(pl.multiple_of(target * depth + m * step, step), step), pl.ds(a * width, width)]
        return outp_ref.at[pl.ds((i % 2) * tall, tall), pl.ds(pl.multiple_of(target * out_width, out_width), out_width)]

    def spot(i, origin):
        a, m = i // 8, i % 8
        return proj_own.at[a, pl.ds(m * step, step), pl.ds(pl.multiple_of(origin * width, width), width)]

    def rows(proj, outp, i):
        if i < 24:
            return proj.at[i // 8, pl.ds((i % 8) * step, step), :]
        return outp.at[pl.ds((i - 24) * tall, tall), :]

    small_copies = []

    def small_begin():
        lanes = small_ref.shape[2]
        small_own[...] = small_ref[...]
        for j in range(entry_out.shape[1] // lanes):
            at = pl.ds(j * lanes, lanes)
            part = jnp.sum(entry_out[:, at] * scaled_ref[:, at], axis=0, keepdims=True)
            small_own[j // small_ref.shape[1], pl.ds(j % small_ref.shape[1], 1), :] = part
        for j in range(1, 8):
            copy = remote(small_own.at[here ^ j], slices.at[here], slice_send.at[j], slice_recv.at[here], group[j - 1])
            copy.start()
            small_copies.append(copy)

    order = [24, 25, 0, 1, 26, 27, 2, 3, 28, 29, 4, 5, 30, 31] + list(range(6, 24))
    swaps = []

    def issue(i):
        if i < 24:
            keep = pltpu.make_async_copy(piece(i, c), spot(i, c), own_sem.at[i])
            keep.start()
            for j in range(1, 4):
                copy = remote(piece(i, c ^ j), spot(i, c), swap_send.at[i, j - 1], swap_recv.at[i, j - 1], (z, r, c ^ j))
                copy.start()
                swaps.append(copy)
        else:
            @pl.when(c == owner(i))
            def _():
                pltpu.make_async_copy(piece(i, c), rows(proj_own, outp_own, i), own_sem.at[i]).start()
                for j in range(1, 4):
                    remote(piece(i, c ^ j), rows(proj_own, outp_own, i), swap_send.at[i, j - 1], swap_recv.at[i, 0], (z, r, c ^ j)).start()

    ahead = AHEAD
    for i in order[:ahead]:
        issue(i)
    near[0](0, 0)
    lax.fori_loop(0, planes * CUTS, wide[0], 0)

    def local_ready(i):
        target = rows(proj_own, outp_own, i)
        if i < 24:
            pltpu.make_async_copy(piece(i, c), spot(i, c), own_sem.at[i]).wait()
            for j in range(1, 4):
                arrived = spot(i, c ^ j)
                remote(arrived, arrived, swap_send.at[i, j - 1], swap_recv.at[i, j - 1], (z, r, c ^ j)).wait_recv()
        else:
            @pl.when(c == owner(i))
            def _():
                pltpu.make_async_copy(piece(i, c), target, own_sem.at[i]).wait()

            @pl.when(c != owner(i))
            def _():
                remote(target, target, swap_send.at[i, 0], swap_recv.at[i, 0], (z, r, c ^ 1)).wait_recv()

    def combine(target, sources, count):
        def body(s, _):
            at = pl.ds(pl.multiple_of(s * 32, 32), 32)
            total = sources[0][at].astype(jnp.float32)
            for source in sources[1:]:
                total = total + source[at].astype(jnp.float32)
            target[at] = total.astype(target.dtype)
            return 0
        lax.fori_loop(0, count // 32, body, 0)

    def seat(i):
        return z if i % 2 == 0 else planes - 1 - z

    def at_seat(i, p):
        return (p if i % 2 == 0 else planes - 1 - p, r, c)

    def refs(i):
        return [rows(proj, outp, i) for proj, outp in ((proj_own, outp_own), (proj_in, outp_in), (proj_far, outp_far), (proj_out, outp_out))]

    def down_copy(i, p):
        own, near_in, far_in, _ = refs(i)
        if p == 0:
            return remote(own, near_in, down_send.at[i], down_recv.at[i], at_seat(i, 1))
        return remote(own, far_in, down_send.at[i], far_down.at[i], at_seat(i, p - 1))

    def up_copy(i, p, target):
        result = refs(i)[3]
        return remote(result, result, up_send.at[i, 0 if target == 0 else 1], up_recv.at[i], at_seat(i, target))

    def hop(i, h):
        own, near_in, far_in, result = refs(i)

        if h == 0:
            for p in (0, 3):
                @pl.when(seat(i) == p)
                def _(p=p):
                    local_ready(i)
                    down_copy(i, p).start()
        elif h == 1:
            @pl.when(seat(i) == 2)
            def _():
                local_ready(i)
                down_copy(i, 3).wait_recv()
                combine(own, [own, far_in], own.shape[0])
                down_copy(i, 2).start()
        elif h == 2:
            @pl.when(seat(i) == 1)
            def _():
                local_ready(i)
                down_copy(i, 0).wait_recv()
                down_copy(i, 2).wait_recv()
                combine(result, [own, near_in, far_in], own.shape[0])
                up_copy(i, 1, 0).start()
                up_copy(i, 1, 2).start()
        elif h == 3:
            @pl.when(seat(i) == 2)
            def _():
                up_copy(i, 1, 2).wait_recv()
                up_copy(i, 2, 3).start()
        else:
            for p in (0, 3):
                @pl.when(seat(i) == p)
                def _(p=p):
                    up_copy(i, 1, p).wait_recv()

    def small_group():
        for j in range(1, 8):
            arrived = slices.at[here ^ j]
            remote(arrived, arrived, slice_send.at[0], slice_recv.at[here ^ j], group[j - 1]).wait_recv()
        slices[here] = small_own[here]
        total = slices[0]
        for j in range(1, 8):
            total = total + slices[j]
        far_slices[z] = total
        for k in range(1, planes):
            copy = remote(far_slices.at[z], far_slices.at[z], far_send.at[k - 1], far_recv.at[z], (z ^ k, r, c))
            copy.start()
            small_copies.append(copy)

    def small_far():
        for k in range(1, planes):
            arrived = far_slices.at[z ^ k]
            remote(arrived, arrived, far_send.at[k - 1], far_recv.at[z ^ k], (z ^ k, r, c)).wait_recv()
        total = far_slices[0]
        for k in range(1, planes):
            total = total + far_slices[k]
        small_out[here] = total
        for j in range(1, 8):
            copy = remote(small_out.at[here], small_out.at[here], whole_send.at[j], whole_recv.at[here], group[j - 1])
            copy.start()
            small_copies.append(copy)

    lag = LAG
    hops = 5
    actions = {}

    def plan(slot, action):
        actions.setdefault(slot, []).append(action)

    for slot, kind in zip(NEAR, (1, 2, 3)):
        plan(slot, lambda kind=kind: near[kind](0))
    for slot, action in zip(SMALL, (small_begin, small_group, small_far)):
        plan(slot, action)
    for n in range(planes * CUTS):
        for kind in (1, 2, 3):
            plan(int(WIDE[0] + n * WIDE[1] + (kind - 1) * WIDE[2]), lambda v=planes * CUTS - 1 - n, kind=kind: wide[kind](v))
    slots = chunks + (hops - 1) * lag
    for s in range(max(slots, max(actions) + 1)):
        if s + ahead < chunks:
            issue(order[s + ahead])
        for h in range(hops):
            if 0 <= s - h * lag < chunks:
                hop(order[s - h * lag], h)
        for action in actions.get(s, ()):
            action()
    for j in range(1, 8):
        arrived = small_out.at[here ^ j]
        remote(arrived, arrived, whole_send.at[0], whole_recv.at[here ^ j], group[j - 1]).wait_recv()
    near[4](0, 0)
    lax.fori_loop(0, planes * CUTS, wide[4], 0)
    for copy in small_copies + swaps:
        copy.wait_send()
    for i in range(24, 32):
        @pl.when(c == owner(i))
        def _():
            for j in range(1, 4):
                remote(piece(i, c ^ j), rows(proj_own, outp_own, i), swap_send.at[i, j - 1], swap_recv.at[i, 0], (z, r, c ^ j)).wait_send()
    for i in range(chunks):
        @pl.when(seat(i) != 1)
        def _(i=i):
            down_copy(i, 0).wait_send()

        @pl.when(seat(i) == 1)
        def _(i=i):
            up_copy(i, 1, 0).wait_send()

        @pl.when(jnp.logical_or(seat(i) == 1, seat(i) == 2))
        def _(i=i):
            up_copy(i, 1, 2).wait_send()


def finish(grad_proj_own, grad_out_own, small, scaled, mixed_part, entry_part, planes, collective_id):
    depth, width = grad_proj_own.shape[0] // 4, grad_proj_own.shape[1] // 3
    out_rows, out_width = grad_out_own.shape[0], grad_out_own.shape[1] // 4
    kind = grad_proj_own.dtype
    proj, outp = (3, depth, 4 * width), (4 * out_rows, out_width)
    vmem = pl.BlockSpec(memory_space=pltpu.VMEM)
    dma = pltpu.SemaphoreType.DMA
    [(mixed_shape, _)], mixed_buffers, mixed_semaphores = reduce_scratch([mixed_part], planes, CUTS)
    [(entry_shape, _)], entry_buffers, entry_semaphores = reduce_scratch([entry_part], 1, 1)
    return pl.pallas_call(
        functools.partial(finish_kernel, planes),
        out_shape=[jax.ShapeDtypeStruct(proj, kind), jax.ShapeDtypeStruct(outp, kind), jax.ShapeDtypeStruct(small.shape, small.dtype),
                   jax.ShapeDtypeStruct(mixed_shape, jnp.float32), jax.ShapeDtypeStruct(entry_shape, jnp.float32)],
        in_specs=[ANYSPEC, ANYSPEC, vmem, vmem, ANYSPEC, ANYSPEC], out_specs=[vmem] * 5,
        scratch_shapes=[
            pltpu.VMEM(proj, kind), pltpu.VMEM(outp, kind), pltpu.VMEM(proj, kind), pltpu.VMEM(outp, kind), pltpu.VMEM(proj, kind), pltpu.VMEM(outp, kind),
            pltpu.VMEM(small.shape, jnp.float32), pltpu.VMEM(small.shape, jnp.float32), pltpu.VMEM((planes,) + small.shape[1:], jnp.float32),
            dma((32,)), dma((32, 3)), dma((32, 3)), dma((32,)), dma((32,)), dma((32,)), dma((32, 2)), dma((32,)),
            dma((8,)), dma((8,)), dma((planes,)), dma((planes,)), dma((8,)), dma((8,))]
        + mixed_buffers + mixed_semaphores + entry_buffers + entry_semaphores,
        compiler_params=pltpu.CompilerParams(collective_id=collective_id, has_side_effects=True, vmem_limit_bytes=58 * 2**20),
    )(grad_proj_own, grad_out_own, small, scaled, mixed_part, entry_part)


def expert_kernel(planes, experts, own_h, own_side, cot, w_gate, w_up, w_down,
                  all_h, all_side, entry_out, route_out, active_out, grad_gate_out, grad_up_out,
                  gate_use, up_use, down_use, rows_h, rows_c, rows_side, back_rows,
                  gate_rows, up_rows, active_rows, grad_gate, grad_up, entry_stage, route_stage,
                  weight_sem, own_sem, send_sem, recv_sem, cot_sem, load_sem, store_sem):
    z, r, c = place()
    first, second, diag = c ^ (1 + r), c ^ (2 - r), c ^ 3
    partner = (z, 1 - r, c)
    to_first, to_second = (z, r, first), (z, r, second)
    count = own_h.shape[0]
    group = 4 * count
    expert = z * 4 + c
    half = count // 2
    pieces = [(own_h, all_h, 0, half), (own_h, all_h, half, half), (own_side, all_side, 0, count)]

    weights = [(w_gate, gate_use), (w_up, up_use), (w_down, down_use)]
    for i, (source, target) in enumerate(weights):
        pltpu.make_async_copy(source, target, weight_sem.at[i]).start()

    def number(zz, rr, cc):
        return (zz * 2 + rr) * 4 + cc

    def spot(i, which):
        _, target, start, size = pieces[i]
        return target.at[pl.ds(pl.multiple_of(which * count + start, size), size)]

    def copy_of(i, source, which, k, slot, device):
        return pltpu.make_async_remote_copy(
            src_ref=source, dst_ref=spot(i, which), send_sem=send_sem.at[i, k, slot], recv_sem=recv_sem.at[i, which],
            device_id=device, device_id_type=MESH)

    def own_piece(i):
        source, _, start, size = pieces[i]
        return source.at[pl.ds(start, size)]

    def await_block(i, which):
        copy_of(i, spot(i, which), which, 0, 0, partner).wait_recv()

    def forward(which, k, targets):
        for i in range(3):
            await_block(i, which)
            for slot, device in targets:
                copy_of(i, spot(i, which), which, k, slot, device).start()

    greet([to_first, to_second, partner] + [(z ^ k, r, c) for k in range(1, planes)])
    mine = number(z, r, c)
    for i in range(3):
        for slot, device in ((0, to_first), (1, to_second)):
            copy_of(i, own_piece(i), mine, 0, slot, device).start()
        for k in range(1, planes):
            copy_of(i, own_piece(i), mine, k, 7, (z ^ k, r, c)).start()
        copy_of(i, own_piece(i), mine, 0, 2, partner).start()
    keeps = [pltpu.make_async_copy(own_piece(i), spot(i, mine), own_sem.at[i]) for i in range(3)]
    for keep in keeps:
        keep.start()

    def base_of(k, rr):
        return pl.multiple_of(number(z ^ k, rr, 0) * count, group)

    def dot(left, right):
        return jnp.dot(left, right, preferred_element_type=jnp.float32)

    def dot_turned(left, right):
        return lax.dot_general(left, right, (((1,), (1,)), ((), ())), preferred_element_type=jnp.float32)

    def cot_copy(g):
        rr = jnp.where(g % 2 == 0, r, 1 - r)
        return pltpu.make_async_copy(cot.at[pl.ds(base_of(g // 2, rr), group)], rows_c.at[g % 2], cot_sem.at[g % 2])

    cot_copy(0).start()
    for i, (source, target) in enumerate(weights):
        pltpu.make_async_copy(source, target, weight_sem.at[i]).wait()

    def back_body(g, _):
        @pl.when(g + 1 < 2 * planes)
        def _():
            cot_copy(g + 1).start()

        cot_copy(g).wait()
        back_rows[g] = dot_turned(rows_c[g % 2], down_use[...])
        return 0

    lax.fori_loop(0, 2 * planes, back_body, 0)
    for keep in keeps:
        keep.wait()

    def stores(k, rr, slot):
        at = pl.ds(base_of(k, rr), group)
        return [
            pltpu.make_async_copy(source.at[slot], target.at[at], store_sem.at[slot, i])
            for i, (source, target) in enumerate((
                (entry_stage, entry_out), (route_stage, route_out), (active_rows, active_out),
                (grad_gate, grad_gate_out), (grad_up, grad_up_out)))]

    def compute(k, rr, slot):
        at = pl.ds(base_of(k, rr), group)
        loads = [pltpu.make_async_copy(all_h.at[at], rows_h, load_sem.at[0]),
                 pltpu.make_async_copy(all_side.at[at], rows_side, load_sem.at[1])]
        for load in loads:
            load.start()
        for load in loads:
            load.wait()
        gate_rows[...] = dot(rows_h[...], gate_use[...])
        up_rows[...] = dot(rows_h[...], up_use[...])

        @pl.when(k > 0)
        def _():
            for store in stores(k, rr, slot):
                store.wait()

        part = 128
        lane = lax.broadcasted_iota(jnp.int32, (part, rows_side.shape[1]), 1)

        @pl.loop(0, group // part)
        def _(t):
            at = pl.ds(pl.multiple_of(t * part, part), part)
            mask = (lane == expert) | (lane == expert + experts)
            share = jnp.sum(jnp.where(mask, rows_side[at, :].astype(jnp.float32), 0.0), axis=1, keepdims=True)
            gate, up, back = gate_rows[at, :], up_rows[at, :], back_rows[2 * k + slot, at, :]
            squash = jax.nn.sigmoid(gate)
            silu = gate * squash
            active = silu * up
            route = jnp.sum(active * back, axis=1, keepdims=True)
            route_stage[slot, at, :] = jnp.where(lane == expert, route, 0.0).astype(jnp.bfloat16)
            active_rows[slot, at, :] = (share * active).astype(jnp.bfloat16)
            grad_active = share * back
            grad_gate[slot, at, :] = (grad_active * up * squash * (1.0 + gate * (1.0 - squash))).astype(jnp.bfloat16)
            grad_up[slot, at, :] = (grad_active * silu).astype(jnp.bfloat16)

    def finish_rows(k, rr, slot):
        entry = dot_turned(grad_gate[slot], gate_use[...]) + dot_turned(grad_up[slot], up_use[...])
        entry_stage[slot] = entry.astype(jnp.bfloat16)
        for store in stores(k, rr, slot):
            store.start()

    def step_body(step, _):
        @pl.when(jnp.logical_and(step > 0, step < planes))
        def _():
            forward(number(z ^ step, r, c), step, ((0, to_first), (1, to_second), (2, partner)))

        @pl.when(jnp.logical_and(step >= 3, step < planes + 3))
        def _():
            k = step - 3
            for j in range(4):
                for i in range(3):
                    await_block(i, number(z ^ k, 1 - r, c ^ j))
            compute(k, 1 - r, 1)

        @pl.when(jnp.logical_and(step >= 1, step < planes + 1))
        def _():
            k = step - 1
            forward(number(z ^ k, r, first), k, ((3, to_second), (4, partner)))
            forward(number(z ^ k, r, second), k, ((5, partner),))

        @pl.when(jnp.logical_and(step >= 3, step < planes + 3))
        def _():
            finish_rows(step - 3, 1 - r, 1)
            finish_rows(step - 3, r, 0)

        @pl.when(jnp.logical_and(step >= 2, step < planes + 2))
        def _():
            k = step - 2
            forward(number(z ^ k, r, diag), k, ((6, partner),))
            compute(k, r, 0)

        return 0

    lax.fori_loop(0, planes + 3, step_body, 0)
    for slot, rr in ((0, r), (1, 1 - r)):
        for store in stores(planes - 1, rr, slot):
            store.wait()

    def drain(k, _):
        for i in range(3):
            for slot in range(7):
                copy_of(i, spot(i, mine), mine, k, slot, partner).wait_send()

            @pl.when(k > 0)
            def _():
                copy_of(i, spot(i, mine), mine, k, 7, partner).wait_send()
        return 0

    lax.fori_loop(0, planes, drain, 0)


def expert_rows_on_links(normal_h, side, all_cotangent, w_gate, w_up, w_down, experts, collective_id):
    planes = lax.axis_size("dp")
    count, width = normal_h.shape
    hidden = w_gate.shape[1]
    total, group, low, wide = planes * 8 * count, 4 * count, jnp.bfloat16, jnp.float32
    sides = side.shape[1]
    vmem, dma = pltpu.VMEM, pltpu.SemaphoreType.DMA
    outs = [jax.ShapeDtypeStruct((total, n), low) for n in (width, sides, width, sides, hidden, hidden, hidden)]
    return pl.pallas_call(
        functools.partial(expert_kernel, planes, experts),
        out_shape=outs, in_specs=[ANYSPEC] * 6, out_specs=[ANYSPEC] * 7,
        scratch_shapes=[
            vmem((width, hidden), low), vmem((width, hidden), low), vmem((hidden, width), low),
            vmem((group, width), low), vmem((2, group, width), low), vmem((group, sides), low), vmem((2 * planes, group, hidden), wide),
            vmem((group, hidden), wide), vmem((group, hidden), wide),
            vmem((2, group, hidden), low), vmem((2, group, hidden), low), vmem((2, group, hidden), low),
            vmem((2, group, width), low), vmem((2, group, sides), low),
            dma((3,)), dma((3,)), dma((3, planes, 8)), dma((3, planes * 8)), dma((2,)), dma((2,)), dma((2, 5))],
        compiler_params=pltpu.CompilerParams(collective_id=collective_id, has_side_effects=True, vmem_limit_bytes=60 * 2**20),
    )(normal_h, side, all_cotangent, w_gate, w_up, w_down)


def entry_kernel(planes, entry_part, route_part, all_h, cot, active, grad_gate, grad_up, w_down,
                 entry_out, route_out, mixed_out, acc_gate, acc_up, acc_down, *scratch):
    buffers = [scratch[2 * i:2 * i + 2] for i in range(5)]
    semaphores = scratch[10:17]
    down_use, rows_h, rows_c, rows_x, mixed_stage, down_sem, load_sem, store_sem = scratch[17:]
    group = rows_h.shape[1]
    groups = all_h.shape[0] // group

    def loads(g):
        slot = g % 2
        at = pl.ds(pl.multiple_of(g * group, group), group)
        pairs = [(all_h.at[at], rows_h.at[slot]), (cot.at[at], rows_c.at[slot])] + [
            (source.at[at], rows_x.at[slot, i]) for i, source in enumerate((active, grad_gate, grad_up))]
        return [pltpu.make_async_copy(source, target, load_sem.at[slot, i]) for i, (source, target) in enumerate(pairs)]

    def store(g):
        at = pl.ds(pl.multiple_of(g * group, group), group)
        return pltpu.make_async_copy(mixed_stage, mixed_out.at[at], store_sem.at[0])

    def turned(left, right):
        return lax.dot_general(left, right, (((0,), (0,)), ((), ())), preferred_element_type=jnp.float32)

    down = pltpu.make_async_copy(w_down, down_use, down_sem.at[0])
    down.start()
    for load in loads(0):
        load.start()
    for acc in (acc_gate, acc_up, acc_down):
        @pl.loop(0, acc.shape[0] // 32)
        def _(t, acc=acc):
            acc[pl.ds(pl.multiple_of(t * 32, 32), 32), :] = jnp.zeros((32, acc.shape[1]), jnp.float32)
    down.wait()

    def one(g):
        @pl.when(g + 1 < groups)
        def _():
            for load in loads(g + 1):
                load.start()

        for load in loads(g):
            load.wait()
        slot = g % 2
        acc_gate[...] += turned(rows_h[slot], rows_x[slot, 1])
        acc_up[...] += turned(rows_h[slot], rows_x[slot, 2])
        acc_down[...] += turned(rows_x[slot, 0], rows_c[slot])

        @pl.when(g > 0)
        def _():
            store(g - 1).wait()

        mixed_stage[...] = jnp.dot(rows_x[slot, 0], down_use[...], preferred_element_type=jnp.float32).astype(jnp.bfloat16)
        store(g).start()

    per_step = -(-groups // (planes * CUTS))

    def filler(step):
        def body(i, _):
            @pl.when(step * per_step + i < groups)
            def _():
                one(step * per_step + i)
            return 0
        lax.fori_loop(0, per_step, body, 0)

    reduce_steps(planes, CUTS, (entry_part, route_part), (entry_out, route_out), buffers, semaphores, filler)
    store(groups - 1).wait()


def entry_sums(entry_part, route_part, all_h, cot, active, grad_gate, grad_up, w_down, collective_id):
    planes = lax.axis_size("dp")
    partials = [entry_part, route_part]
    shapes, buffers, semaphores = reduce_scratch(partials, planes, CUTS)
    (count, width), hidden, group = shapes[0][0], w_down.shape[0], 256
    low, wide, vmem, dma = jnp.bfloat16, jnp.float32, pltpu.VMEM, pltpu.SemaphoreType.DMA
    kept = pl.BlockSpec(memory_space=pltpu.VMEM)
    return pl.pallas_call(
        functools.partial(entry_kernel, planes),
        out_shape=[jax.ShapeDtypeStruct(shape, wide) for shape, _ in shapes] + [
            jax.ShapeDtypeStruct(entry_part.shape, low), jax.ShapeDtypeStruct((width, hidden), wide),
            jax.ShapeDtypeStruct((width, hidden), wide), jax.ShapeDtypeStruct((hidden, width), wide)],
        in_specs=[ANYSPEC] * 8, out_specs=[kept, kept, ANYSPEC, kept, kept, kept],
        scratch_shapes=buffers + semaphores + [
            vmem((hidden, width), low), vmem((2, group, width), low), vmem((2, group, width), low), vmem((2, 3, group, hidden), low),
            vmem((group, width), low), dma((1,)), dma((2, 5)), dma((1,))],
        compiler_params=pltpu.CompilerParams(collective_id=collective_id, has_side_effects=True, vmem_limit_bytes=60 * 2**20),
    )(entry_part, route_part, all_h, cot, active, grad_gate, grad_up, w_down)


def dot_plain(left, right):
    return jnp.dot(left, right, preferred_element_type=jnp.float32)


def dot_cols(left, right):
    return lax.dot_general(left, right, (((1,), (1,)), ((), ())), preferred_element_type=jnp.float32)


def dot_rows(left, right):
    return lax.dot_general(left, right, (((0,), (0,)), ((), ())), preferred_element_type=jnp.float32)


def group_peers():
    z, r, c = place()
    return r * 4 + c, [(z, r ^ (j >> 2), c ^ (j & 3)) for j in range(1, 8)]


def group_sums(own, slots, send_sem, recv_sem):
    here, peers = group_peers()
    copies = []
    for j, peer in enumerate(peers):
        copy = pltpu.make_async_remote_copy(
            src_ref=own, dst_ref=slots.at[j], send_sem=send_sem.at[j], recv_sem=recv_sem.at[j],
            device_id=peer, device_id_type=MESH)
        copy.start()
        copies.append(copy)
    for copy in copies:
        copy.wait()
    total = jnp.zeros(own.shape, jnp.float32)
    for who in range(8):
        which = here ^ who
        total = total + jnp.where(which == 0, own[...], slots[jnp.maximum(which - 1, 0)])
    return total


def row_of_tokens(values):
    folded = values[:, :128]
    for start in range(128, values.shape[1], 128):
        folded = folded + values[:, start:start + 128]
    return jnp.sum(folded.T, axis=0, keepdims=True)


def column_of(row):
    return jnp.broadcast_to(row, (128, row.shape[1])).T


BLOCK = 256


def block_weights(queries, keys, first, finish):
    scores = dot_cols(queries[first:finish], keys[:finish])
    at_query = lax.broadcasted_iota(jnp.int32, scores.shape, 0) + first
    at_key = lax.broadcasted_iota(jnp.int32, scores.shape, 1)
    scores = jnp.where(at_query >= at_key, scores, MASKED)
    weights = jnp.exp(scores - jnp.max(scores, axis=1, keepdims=True))
    return weights / jnp.sum(weights, axis=1, keepdims=True)


def forward_kernel(width, x_ref, proj_ref, gains, cosine, sine, w_out_ref,
                   part_out, query_out, key_out, value_out, raw_out, scale_out, mixed_out, w_out_own,
                   sums, slots, send_sem, recv_sem, keep_sem, swap_send, swap_recv):
    greet(group_peers()[1])
    z, r, c = place()
    rows, lanes_out = w_out_own.shape[0], w_out_ref.shape[1]

    def piece(target):
        return w_out_ref.at[pl.ds(pl.multiple_of(target * rows, rows), rows), :]

    def spot(origin):
        return w_out_own.at[:, pl.ds(pl.multiple_of(origin * lanes_out, lanes_out), lanes_out)]

    keep = pltpu.make_async_copy(piece(c), spot(c), keep_sem.at[0])
    keep.start()
    swaps = [pltpu.make_async_remote_copy(
        src_ref=piece(c ^ j), dst_ref=spot(c), send_sem=swap_send.at[j - 1], recv_sem=swap_recv.at[j - 1],
        device_id=(z, r, c ^ j), device_id_type=MESH) for j in range(1, 4)]
    local = value_out.shape[1]
    raw = dot_plain(x_ref[...], proj_ref[...])
    raw_out[...] = raw[:, :2 * local]
    value_out[...] = raw[:, 2 * local:].astype(jnp.bfloat16)
    sums[...] = jnp.zeros(sums.shape, jnp.float32)
    for i in range(2):
        half = raw_out[:, pl.ds(i * local, local)]
        sums[pl.ds(i, 1), :] = row_of_tokens(half * half)
    total = group_sums(sums, slots, send_sem, recv_sem)
    for swap in swaps:
        swap.start()
    for i, (target, factor) in enumerate(((query_out, 128 ** (-0.5)), (key_out, 1.0))):
        scale = lax.rsqrt(column_of(total[i:i + 1]) / width + EPSILON)
        scale_out[:, pl.ds(i * 128, 128)] = scale
        for start in range(0, local, 128):
            lanes = pl.ds(start, 128)
            normal = raw_out[:, pl.ds(i * local + start, 128)] * scale * gains[pl.ds(i, 1), lanes]
            turned = normal * cosine[...] + pltpu.roll(normal, 64, 1) * sine[...]
            target[:, lanes] = (turned * factor).astype(jnp.bfloat16)
    tokens = x_ref.shape[0]
    for start in range(0, local, 128):
        lanes = pl.ds(start, 128)
        queries, keys, values = query_out[:, lanes], key_out[:, lanes], value_out[:, lanes]
        for first in range(0, tokens, BLOCK):
            weights = block_weights(queries, keys, first, first + BLOCK).astype(jnp.bfloat16)
            mixed = dot_plain(weights, values[:first + BLOCK])
            mixed_out[pl.ds(first, BLOCK), lanes] = mixed.astype(jnp.bfloat16)
    keep.wait()
    for swap in swaps:
        swap.wait()
    part_out[...] = dot_plain(mixed_out[...], w_out_own[...]).astype(jnp.bfloat16)


def attention_forward(gathered_x, w_proj, gains, cosine, sine, w_out, collective_id):
    tokens, width = gathered_x.shape
    local = w_proj.shape[1] // 3
    low, wide = jnp.bfloat16, jnp.float32
    shape, vmem = jax.ShapeDtypeStruct, pl.BlockSpec(memory_space=pltpu.VMEM)
    dma = pltpu.SemaphoreType.DMA
    return pl.pallas_call(
        functools.partial(forward_kernel, width),
        out_shape=[shape((tokens, width), low), shape((tokens, local), low), shape((tokens, local), low), shape((tokens, local), low),
                   shape((tokens, 2 * local), wide), shape((tokens, 256), wide), shape((tokens, local), low),
                   shape((w_out.shape[0] // 4, 4 * w_out.shape[1]), low)],
        in_specs=[vmem] * 5 + [ANYSPEC], out_specs=[vmem] * 8,
        scratch_shapes=[pltpu.VMEM((8, tokens), wide), pltpu.VMEM((7, 8, tokens), wide), dma((7,)), dma((7,)), dma((1,)), dma((3,)), dma((3,))],
        compiler_params=pltpu.CompilerParams(collective_id=collective_id, has_side_effects=True, vmem_limit_bytes=56 * 2**20),
    )(gathered_x, w_proj, gains, cosine, sine, w_out)


def backward_kernel(width, grad_ref, w_out_ref, x_hbm, proj_hbm, query_ref, key_ref, value_ref, raw_ref, scale_ref, mixed_ref,
                    gains, cosine, sine, grad_x_out, grad_proj_out, grad_out_out, gain_out,
                    x_ref, proj_ref, grad_query, grad_key, grad_value, grad_raw, sums, slots, load_sem, send_sem, recv_sem):
    greet(group_peers()[1])
    loads = [pltpu.make_async_copy(x_hbm, x_ref, load_sem.at[0]), pltpu.make_async_copy(proj_hbm, proj_ref, load_sem.at[1])]
    for load in loads:
        load.start()
    local, tokens = value_ref.shape[1], value_ref.shape[0]
    grad_mixed = dot_cols(grad_ref[...], w_out_ref[...]).astype(jnp.bfloat16)
    grad_raw[:, pl.ds(0, local)] = grad_mixed
    for start in range(0, local, 128):
        lanes = pl.ds(start, 128)
        queries, keys, values, upstream = query_ref[:, lanes], key_ref[:, lanes], value_ref[:, lanes], grad_raw[:, lanes]
        for first in reversed(range(0, tokens, BLOCK)):
            finish = first + BLOCK
            weights = block_weights(queries, keys, first, finish)
            grad_weights = dot_cols(upstream[first:finish], values[:finish])
            centre = jnp.sum(weights * grad_weights, axis=1, keepdims=True)
            grad_scores = (weights * (grad_weights - centre)).astype(jnp.bfloat16)
            grad_query[pl.ds(first, BLOCK), lanes] = dot_plain(grad_scores, keys[:finish])
            key_part = dot_rows(grad_scores, queries[first:finish])
            value_part = dot_rows(weights.astype(jnp.bfloat16), upstream[first:finish])
            if finish == tokens:
                grad_key[:, lanes] = key_part
                grad_value[:, lanes] = value_part
            else:
                grad_key[pl.ds(0, finish), lanes] += key_part
                grad_value[pl.ds(0, finish), lanes] += value_part
    sums[...] = jnp.zeros(sums.shape, jnp.float32)
    gain_out[...] = jnp.zeros(gain_out.shape, jnp.float32)
    for i, (grad, factor) in enumerate(((grad_query, 128 ** (-0.5)), (grad_key, 1.0))):
        scale = scale_ref[:, pl.ds(i * 128, 128)]
        inner = None
        for start in range(0, local, 128):
            lanes = pl.ds(start, 128)
            upstream = grad[:, lanes] * factor
            normal = upstream * cosine[...] - pltpu.roll(upstream, 64, 1) * sine[...]
            raw = raw_ref[:, pl.ds(i * local + start, 128)]
            gain_out[pl.ds(i, 1), lanes] = jnp.sum(normal * raw * scale, axis=0, keepdims=True)
            weighted = gains[pl.ds(i, 1), lanes] * normal
            grad[:, lanes] = weighted
            inner = weighted * raw if inner is None else inner + weighted * raw
        sums[pl.ds(i, 1), :] = row_of_tokens(inner)
    total = group_sums(sums, slots, send_sem, recv_sem)
    for i, grad in enumerate((grad_query, grad_key)):
        scale = scale_ref[:, pl.ds(i * 128, 128)]
        factor = scale * scale * scale * column_of(total[i:i + 1]) / width
        for start in range(0, local, 128):
            lanes = pl.ds(start, 128)
            raw = raw_ref[:, pl.ds(i * local + start, 128)]
            grad_raw[:, pl.ds(i * local + start, 128)] = (scale * grad[:, lanes] - raw * factor).astype(jnp.bfloat16)
    grad_raw[:, pl.ds(2 * local, local)] = grad_value[...].astype(jnp.bfloat16)
    for load in loads:
        load.wait()
    grad_x_out[...] = dot_cols(grad_raw[...], proj_ref[...]).astype(jnp.bfloat16)
    grad_proj_out[...] = dot_rows(x_ref[...], grad_raw[...]).astype(jnp.bfloat16)
    grad_out_out[...] = dot_rows(mixed_ref[...], grad_ref[...]).astype(jnp.bfloat16)


def attention_backward(grad_gathered, w_out_own, gathered_x, w_proj, kept, gains, cosine, sine, collective_id):
    tokens, width = gathered_x.shape
    local = w_proj.shape[1] // 3
    low, wide = jnp.bfloat16, jnp.float32
    shape, vmem = jax.ShapeDtypeStruct, pl.BlockSpec(memory_space=pltpu.VMEM)
    dma = pltpu.SemaphoreType.DMA
    return pl.pallas_call(
        functools.partial(backward_kernel, width),
        out_shape=[shape((tokens, width), low), shape(w_proj.shape, low), shape(w_out_own.shape, low), shape((8, local), wide)],
        in_specs=[vmem, vmem, ANYSPEC, ANYSPEC] + [vmem] * 9, out_specs=[vmem] * 4,
        scratch_shapes=[
            pltpu.VMEM(gathered_x.shape, low), pltpu.VMEM(w_proj.shape, low),
            pltpu.VMEM((tokens, local), wide), pltpu.VMEM((tokens, local), wide), pltpu.VMEM((tokens, local), wide),
            pltpu.VMEM((tokens, 3 * local), low), pltpu.VMEM((8, tokens), wide), pltpu.VMEM((7, 8, tokens), wide),
            dma((2,)), dma((7,)), dma((7,))],
        compiler_params=pltpu.CompilerParams(collective_id=collective_id, has_side_effects=True, vmem_limit_bytes=60 * 2**20),
    )(grad_gathered, w_out_own, gathered_x, w_proj, *kept, gains, cosine, sine)


HEAD_DIM = 128
SEQ_LEN = 1024
EPSILON = 1e-05
THETA = 10000.0
MASKED = -1e30
GROUP = ("row", "col")
EVERYONE = ("dp", "row", "col")


def on_links():
    return lax.axis_size("dp") == 4 and lax.axis_size("col") == 4 and lax.axis_size("row") == 2


def gather_tokens(arrays, everyone, collective_id, parts):
    if on_links():
        return gather(arrays, 4 if everyone else 1, collective_id, parts)
    axes = EVERYONE if everyone else GROUP
    return [lax.all_gather(a, axes, axis=0, tiled=True) for a in arrays]


def scatter_sums(arrays, everyone, collective_id):
    if on_links():
        return reduce_scatter(arrays, 4 if everyone else 1, collective_id)
    axes = EVERYONE if everyone else GROUP
    return [lax.psum_scatter(a, axes, scatter_dimension=0, tiled=True).astype(jnp.float32) for a in arrays]


def open_attention(hidden_in, norm_attn, normal_x, w_query, w_key, w_value):
    if on_links():
        return opening(hidden_in, norm_attn[None], w_query, w_key, w_value, 1)
    pieces = [lax.all_to_all(w, "col", split_axis=1, concat_axis=0, tiled=True) for w in (w_query, w_key, w_value)]
    (gathered_x,) = gather_tokens([normal_x], False, 2, 2)
    return gathered_x, jnp.concatenate(pieces, axis=1)


def inverse_rms(values):
    return lax.rsqrt(jnp.mean(values * values, axis=-1, keepdims=True) + EPSILON)


def norm_backward(values, inv_scale, gain_row, upstream):
    weighted = gain_row * upstream
    inner_sum = jnp.sum(weighted * values, axis=-1, keepdims=True)
    grad_values = inv_scale * weighted - values * inv_scale**3 * inner_sum / values.shape[-1]
    return (grad_values, jnp.sum(upstream * values * inv_scale, axis=0))


def contract(left, right):
    return jnp.dot(left, right, preferred_element_type=jnp.float32)


def contract_rows(left, right):
    return lax.dot_general(
        left, right, (((0,), (0,)), ((), ())), preferred_element_type=jnp.float32
    )


def contract_cols(left, right):
    return lax.dot_general(
        left, right, (((1,), (1,)), ((), ())), preferred_element_type=jnp.float32
    )


def turn_tables(total_rows, seq_length, head_width):
    positions = (np.arange(total_rows) % seq_length).astype(np.float32)
    inverse = np.float32(THETA) ** (-np.arange(0, head_width, 2, dtype=np.float32) / np.float32(head_width))
    angles = positions[:, None] * inverse.astype(np.float32)[None, :]
    angles = np.concatenate([angles, angles], axis=-1).astype(np.float64)
    return (np.cos(angles)[:, None, :].astype(np.float32), np.sin(angles)[:, None, :].astype(np.float32))


def rotate(values, cosine, sine_table):
    middle = values.shape[-1] // 2
    turned = jnp.concatenate([-values[..., middle:], values[..., :middle]], axis=-1)
    return values * cosine + turned * sine_table


def unrotate(upstream, cosine, sine_table):
    middle = upstream.shape[-1] // 2
    turned_part = upstream * sine_table
    return upstream * cosine + jnp.concatenate(
        [turned_part[..., middle:], -turned_part[..., :middle]], axis=-1
    )


def attend_forward(queries, key_rows, value_rows):
    length = queries.shape[0]
    block_rows = min(512, length)
    outputs = []
    sums_log = []
    for first_row in range(0, length, block_rows):
        finish = first_row + block_rows
        scores = jnp.einsum(
            "qhd,khd->hqk",
            queries[first_row:finish],
            key_rows[:finish],
            preferred_element_type=jnp.float32,
        )
        causal = (first_row + jnp.arange(block_rows))[:, None] >= jnp.arange(finish)[None, :]
        scores = jnp.where(causal[None], scores, MASKED)
        highest = jnp.max(scores, axis=-1, keepdims=True)
        weights = jnp.exp(scores - highest)
        totals = jnp.sum(weights, axis=-1, keepdims=True)
        weights = (weights / totals).astype(jnp.bfloat16)
        outputs.append(
            jnp.einsum(
                "hqk,khd->qhd", weights, value_rows[:finish], preferred_element_type=jnp.float32
            )
        )
        sums_log.append((highest + jnp.log(totals))[..., 0])
    return (jnp.concatenate(outputs, axis=0), jnp.concatenate(sums_log, axis=1))


def attend_backward(queries, key_rows, value_rows, grad_out, sums_log):
    length = queries.shape[0]
    block_rows = min(512, length)
    grad_queries = []
    grad_keys = jnp.zeros(key_rows.shape, jnp.float32)
    grad_values = jnp.zeros(value_rows.shape, jnp.float32)
    for first_row in range(0, length, block_rows):
        finish = first_row + block_rows
        scores = jnp.einsum(
            "qhd,khd->hqk",
            queries[first_row:finish],
            key_rows[:finish],
            preferred_element_type=jnp.float32,
        )
        causal = (first_row + jnp.arange(block_rows))[:, None] >= jnp.arange(finish)[None, :]
        scores = jnp.where(causal[None], scores, MASKED)
        weights = jnp.exp(scores - sums_log[:, first_row:finish, None])
        grad_weights = jnp.einsum(
            "qhd,khd->hqk",
            grad_out[first_row:finish],
            value_rows[:finish],
            preferred_element_type=jnp.float32,
        )
        centre = jnp.sum(weights * grad_weights, axis=-1, keepdims=True)
        grad_scores = (weights * (grad_weights - centre)).astype(jnp.bfloat16)
        grad_queries.append(
            jnp.einsum(
                "hqk,khd->qhd", grad_scores, key_rows[:finish], preferred_element_type=jnp.float32
            )
        )
        grad_keys = grad_keys.at[:finish].add(
            jnp.einsum(
                "hqk,qhd->khd",
                grad_scores,
                queries[first_row:finish],
                preferred_element_type=jnp.float32,
            )
        )
        grad_values = grad_values.at[:finish].add(
            jnp.einsum(
                "hqk,qhd->khd",
                weights.astype(jnp.bfloat16),
                grad_out[first_row:finish],
                preferred_element_type=jnp.float32,
            )
        )
    return (jnp.concatenate(grad_queries, axis=0), grad_keys, grad_values)


def by_sequence(step, pieces, sequences):
    if sequences == 1:
        return tuple(out[None] for out in step(*[p[0] for p in pieces]))
    return lax.map(lambda each: step(*each), tuple(pieces))


def expert_rows(normal_h, side, cotangent, gate_use, up_use, down_use, expert_count):
    if on_links():
        all_cotangent = lax.all_gather(cotangent, EVERYONE, axis=0, tiled=True)
        rows_h, _, entry_part, grad_side, active_share, grad_gate_rows, grad_up_rows = expert_rows_on_links(
            normal_h, side, all_cotangent, gate_use, up_use, down_use, expert_count, 6
        )
        entry_rows, grad_probs_all, out_part, *grads = entry_sums(
            entry_part, grad_side, rows_h, all_cotangent, active_share, grad_gate_rows, grad_up_rows, down_use, 7
        )
        return (entry_rows, grad_probs_all, out_part, *grads)
    all_cotangent, rows_h, rows_side = gather_tokens([cotangent, normal_h, side], True, 6, 2)
    expert = lax.axis_index("dp") * lax.axis_size("col") + lax.axis_index("col")
    lane = jnp.arange(side.shape[1])
    own_share = jnp.sum(
        jnp.where((lane == expert) | (lane == expert + expert_count), rows_side.astype(jnp.float32), 0.0),
        axis=1,
        keepdims=True,
    )
    back_rows = contract_cols(all_cotangent, down_use)
    gate_rows = contract(rows_h, gate_use)
    up_rows = contract(rows_h, up_use)
    sigmoid_gate = jax.nn.sigmoid(gate_rows)
    silu_gate = gate_rows * sigmoid_gate
    active = silu_gate * up_rows
    route_grad = jnp.sum(active * back_rows, axis=1, keepdims=True)
    active_share = (own_share * active).astype(jnp.bfloat16)
    grad_active = own_share * back_rows
    grad_gate_rows = (
        grad_active * up_rows * sigmoid_gate * (1.0 + gate_rows * (1.0 - sigmoid_gate))
    ).astype(jnp.bfloat16)
    grad_up_rows = (grad_active * silu_gate).astype(jnp.bfloat16)
    entry_part = (contract_cols(grad_gate_rows, gate_use) + contract_cols(grad_up_rows, up_use)).astype(jnp.bfloat16)
    grad_side = jnp.where(jnp.arange(128 if expert_count <= 128 else expert_count)[None, :] == expert, route_grad, 0.0).astype(jnp.bfloat16)
    entry_rows, grad_probs_all = scatter_sums([entry_part, grad_side], True, 7)
    out_part = contract(active_share, down_use).astype(jnp.bfloat16)
    (mixture,) = scatter_sums([out_part], True, 8)
    grad_down_w = contract_rows(active_share, all_cotangent)
    grad_gate_w = contract_rows(rows_h, grad_gate_rows)
    grad_up_w = contract_rows(rows_h, grad_up_rows)
    return entry_rows, grad_probs_all, mixture, grad_gate_w, grad_up_w, grad_down_w


def per_device(
    hidden_in,
    cotangent,
    norm_attn,
    w_query,
    w_key,
    w_value,
    query_gain,
    key_gain,
    w_out,
    norm_moe,
    w_router,
    w_gate,
    w_up,
    w_down,
    routes,
):
    inputs = hidden_in.astype(jnp.float32)
    upstream = cotangent.astype(jnp.float32)
    token_count, top_count = routes.shape
    model_width = inputs.shape[1]
    expert_count = w_router.shape[1]

    inv_input = inverse_rms(inputs)
    normal_x = (inputs * inv_input * norm_attn).astype(jnp.bfloat16)
    gathered_x, w_proj = open_attention(hidden_in, norm_attn, normal_x, w_query, w_key, w_value)
    group_tokens = gathered_x.shape[0]
    local_width = w_proj.shape[1] // 3
    head_count = local_width // HEAD_DIM
    offset = (lax.axis_index("row") * lax.axis_size("col") + lax.axis_index("col")) * local_width
    gain_query = lax.dynamic_slice_in_dim(query_gain, offset, local_width)
    gain_key = lax.dynamic_slice_in_dim(key_gain, offset, local_width)
    cosine, sine_table = turn_tables(group_tokens, SEQ_LEN, HEAD_DIM)
    head_shape = (group_tokens, head_count, HEAD_DIM)
    sequences = group_tokens // SEQ_LEN
    seq_shape = (sequences, SEQ_LEN, head_count, HEAD_DIM)
    in_kernels = on_links() and sequences == 1
    if in_kernels:
        gains = jnp.concatenate([gain_query[None], gain_key[None], jnp.zeros((6, local_width), jnp.float32)])
        sine_signed = np.where(np.arange(HEAD_DIM) < HEAD_DIM // 2, -sine_table[:, 0], sine_table[:, 0])
        tables = (gains, jnp.asarray(cosine[:, 0]), jnp.asarray(sine_signed))
        attn_part, *kept, w_out_own = attention_forward(gathered_x, w_proj, *tables, w_out, 4)
    else:
        w_out_own = lax.all_to_all(w_out, "col", split_axis=0, concat_axis=1, tiled=True)
        raw = contract(gathered_x, w_proj)
        query_raw = raw[:, :local_width]
        key_raw = raw[:, local_width : 2 * local_width]
        value_heads = raw[:, 2 * local_width :].astype(jnp.bfloat16)
        query_square, key_square = lax.psum(
            (jnp.sum(query_raw * query_raw, axis=-1), jnp.sum(key_raw * key_raw, axis=-1)), GROUP
        )
        inv_query = lax.rsqrt(query_square / model_width + EPSILON)[:, None]
        inv_key = lax.rsqrt(key_square / model_width + EPSILON)[:, None]
        query_heads = (
            rotate((query_raw * inv_query * gain_query).reshape(head_shape), cosine, sine_table)
            * HEAD_DIM ** (-0.5)
        ).astype(jnp.bfloat16)
        key_heads = rotate(
            (key_raw * inv_key * gain_key).reshape(head_shape), cosine, sine_table
        ).astype(jnp.bfloat16)
        query_seq = query_heads.reshape(seq_shape)
        key_seq = key_heads.reshape(seq_shape)
        value_seq = value_heads.reshape(seq_shape)
        mixed, sums_log = by_sequence(attend_forward, (query_seq, key_seq, value_seq), sequences)
        mixed_heads = mixed.reshape(group_tokens, local_width).astype(jnp.bfloat16)
        attn_part = contract(mixed_heads, w_out_own).astype(jnp.bfloat16)
    (attn_rows,) = scatter_sums([attn_part], False, 5)
    state_rows = inputs + attn_rows

    inv_state = inverse_rms(state_rows)
    normal_h = (state_rows * inv_state * norm_moe).astype(jnp.bfloat16)
    logits = contract(normal_h, w_router)
    shifted = jnp.exp(logits - jnp.max(logits, axis=-1, keepdims=True))
    probabilities = shifted / jnp.sum(shifted, axis=-1, keepdims=True)
    selected = jnp.sum(
        (routes[:, :, None] == jnp.arange(expert_count)[None, None, :]).astype(jnp.float32), axis=1
    )
    shares = probabilities * selected
    share_high = shares.astype(jnp.bfloat16)
    share_low = (shares - share_high.astype(jnp.float32)).astype(jnp.bfloat16)
    side_width = max(2 * expert_count, 128)
    side = jnp.concatenate(
        [
            share_high,
            share_low,
            jnp.zeros((token_count, side_width - 2 * expert_count), jnp.bfloat16),
        ],
        axis=1,
    )

    chunks = max(1, lax.axis_size(EVERYONE) // 32)
    if chunks == 1:
        entry_rows, grad_probs_all, mixture, *expert_grads = expert_rows(
            normal_h, side, cotangent, w_gate[0], w_up[0], w_down[0], expert_count
        )
    else:

        def piece_step(sums, piece):
            entry, probs, mixed_rows, *grads = expert_rows(*piece, w_gate[0], w_up[0], w_down[0], expert_count)
            return [s + g for s, g in zip(sums, grads)], (entry, probs, mixed_rows)

        cut = [a.reshape((chunks, token_count // chunks) + a.shape[1:]) for a in (normal_h, side, cotangent)]
        empty = [jnp.zeros(w.shape[1:], jnp.float32) for w in (w_gate, w_up, w_down)]
        expert_grads, rows = lax.scan(piece_step, empty, cut)
        entry_rows, grad_probs_all, mixture = [r.reshape((token_count,) + r.shape[2:]) for r in rows]
    grad_gate_w, grad_up_w, grad_down_w = expert_grads
    grad_probs = selected * grad_probs_all[:, :expert_count]
    grad_logits = (
        probabilities * (grad_probs - jnp.sum(probabilities * grad_probs, axis=-1, keepdims=True))
    ).astype(jnp.bfloat16)
    grad_normal_h = entry_rows + contract_cols(grad_logits, w_router)
    grad_router_part = contract_rows(grad_logits, normal_h)
    grad_state_part, grad_moe_part = norm_backward(state_rows, inv_state, norm_moe, grad_normal_h)
    grad_state = upstream + grad_state_part
    grad_attn = grad_state.astype(jnp.bfloat16)
    (grad_gathered,) = gather_tokens([grad_attn], False, 9, 2)
    if in_kernels:
        grad_x_part, grad_proj_own, grad_out_own, gain_parts = attention_backward(
            grad_gathered, w_out_own, gathered_x, w_proj, kept, *tables, 10
        )
        grad_qgain_part, grad_kgain_part = gain_parts[0], gain_parts[1]
    else:
        grad_out_own = contract_rows(mixed_heads, grad_gathered).astype(jnp.bfloat16)
        grad_mixed = contract_cols(grad_gathered, w_out_own).astype(jnp.bfloat16)
        grad_query_seq, grad_key_seq, grad_value_seq = by_sequence(
            attend_backward,
            (query_seq, key_seq, value_seq, grad_mixed.reshape(seq_shape), sums_log),
            sequences,
        )
        grad_normal_q = unrotate(
            grad_query_seq.reshape(head_shape) * HEAD_DIM ** (-0.5), cosine, sine_table
        ).reshape(group_tokens, local_width)
        grad_normal_k = unrotate(grad_key_seq.reshape(head_shape), cosine, sine_table).reshape(
            group_tokens, local_width
        )
        weighted_q = gain_query * grad_normal_q
        weighted_k = gain_key * grad_normal_k
        inner_q, inner_k = lax.psum(
            (jnp.sum(weighted_q * query_raw, axis=-1), jnp.sum(weighted_k * key_raw, axis=-1)), GROUP
        )
        grad_query_raw = (
            inv_query * weighted_q - query_raw * inv_query**3 * inner_q[:, None] / model_width
        )
        grad_key_raw = inv_key * weighted_k - key_raw * inv_key**3 * inner_k[:, None] / model_width
        grad_qgain_part = jnp.sum(grad_normal_q * query_raw * inv_query, axis=0)
        grad_kgain_part = jnp.sum(grad_normal_k * key_raw * inv_key, axis=0)
        grad_raw = jnp.concatenate(
            [grad_query_raw, grad_key_raw, grad_value_seq.reshape(group_tokens, local_width)], axis=1
        ).astype(jnp.bfloat16)
        grad_x_part = contract_cols(grad_raw, w_proj).astype(jnp.bfloat16)
        grad_proj_own = contract_rows(gathered_x, grad_raw).astype(jnp.bfloat16)
    full_width = query_gain.shape[0]
    padded_qgain = lax.dynamic_update_slice_in_dim(
        jnp.zeros((full_width,), jnp.float32), grad_qgain_part, offset, 0
    )
    padded_kgain = lax.dynamic_update_slice_in_dim(
        jnp.zeros((full_width,), jnp.float32), grad_kgain_part, offset, 0
    )
    small = (padded_qgain, padded_kgain, grad_moe_part, grad_router_part)
    grad_query, grad_key, grad_value, grad_out_proj, mixture, grad_normal_x, small = last_sums(
        grad_proj_own, grad_out_own, small, inputs * inv_input, mixture, grad_x_part
    )
    grad_norm_attn, grad_query_gain, grad_key_gain, grad_norm_moe, grad_router = small
    grad_router = grad_router.T
    block_out = (state_rows + mixture).astype(jnp.bfloat16)
    grad_input = grad_state + norm_backward(inputs, inv_input, norm_attn, grad_normal_x)[0]
    return (
        block_out,
        grad_input,
        grad_norm_attn,
        grad_query,
        grad_key,
        grad_value,
        grad_query_gain,
        grad_key_gain,
        grad_out_proj,
        grad_norm_moe,
        grad_router,
        grad_gate_w[None],
        grad_up_w[None],
        grad_down_w[None],
    )


def last_sums(grad_proj_own, grad_out_own, small, scaled, mixed_part, entry_part):
    if on_links():
        parts = (jnp.zeros((scaled.shape[1],), jnp.float32), *small)
        flat = jnp.concatenate([part.reshape(-1) for part in parts])
        proj, outp, total, mixture, grad_normal_x = finish(
            grad_proj_own, grad_out_own, flat.reshape(8, -1, 128), scaled, mixed_part, entry_part, lax.axis_size("dp"), 12
        )
        total, sums, start = total.reshape(-1), [], 0
        for part in parts:
            sums.append(total[start : start + part.size].reshape(part.shape))
            start += part.size
        return (*(proj[a].astype(jnp.float32) for a in range(3)), outp.astype(jnp.float32), mixture, grad_normal_x, sums)
    (grad_normal_x,) = scatter_sums([entry_part], False, 11)
    small = (jnp.sum(grad_normal_x * scaled, axis=0), *small)
    width = grad_proj_own.shape[1] // 3
    blocks = [
        lax.all_to_all(grad_proj_own[:, a * width : (a + 1) * width], "col", split_axis=0, concat_axis=1, tiled=True)
        for a in range(3)
    ]
    out_block = lax.all_to_all(grad_out_own, "col", split_axis=1, concat_axis=0, tiled=True)
    weights = [total.astype(jnp.float32) for total in lax.psum((*blocks, out_block), "dp")]
    return (*weights, mixed_part, grad_normal_x, lax.psum(small, EVERYONE))


def solution(mesh):
    placed = (
        P(("dp", "row", "col"), None),
        P(("dp", "row", "col"), None),
        P(),
        P("col", "row"),
        P("col", "row"),
        P("col", "row"),
        P(),
        P(),
        P("row", "col"),
        P(),
        P(),
        P(("dp", "col"), None, "row"),
        P(("dp", "col"), None, "row"),
        P(("dp", "col"), "row", None),
        P(("dp", "row", "col"), None),
    )
    return jax.shard_map(
        per_device,
        mesh=mesh,
        in_specs=placed,
        out_specs=(
            P(("dp", "row", "col"), None),
            P(("dp", "row", "col"), None),
            P(),
            P("col", "row"),
            P("col", "row"),
            P("col", "row"),
            P(),
            P(),
            P("row", "col"),
            P(),
            P(),
            P(("dp", "col"), None, "row"),
            P(("dp", "col"), None, "row"),
            P(("dp", "col"), "row", None),
        ),
        check_vma=False,
    )
```

```python
import functools

import jax
import jax.numpy as jnp
import numpy as np
from jax import lax
from jax.experimental import pallas as pl
from jax.experimental.pallas import tpu as pltpu
from jax.sharding import PartitionSpec as P

MESH = pl.DeviceIdType.MESH
ANYSPEC = pl.BlockSpec(memory_space=pl.ANY)
CUTS = 2

def place():
    return lax.axis_index("dp"), lax.axis_index("row"), lax.axis_index("col")

def greet(peers):
    barrier = pltpu.get_barrier_semaphore()
    for peer in peers:
        pl.semaphore_signal(barrier, inc=1, device_id=peer, device_id_type=MESH)
    pl.semaphore_wait(barrier, len(peers))

def gather_kernel(planes, parts, count, *refs):
    gather_steps(planes, parts, refs[:count], refs[count:2 * count], *refs[2 * count:])


def gather_steps(planes, parts, ins, outs, own_sem, send_sem, recv_sem, more_peers=(), beside=None):
    count = len(ins)
    z, r, c = place()
    first, second, diag = c ^ (1 + r), c ^ (2 - r), c ^ 3
    partner = (z, 1 - r, c)
    to_first, to_second = (z, r, first), (z, r, second)
    greet([to_first, to_second, partner] + [(z ^ k, r, c) for k in range(1, planes)] + list(more_peers))
    if beside is not None:
        beside()
    pieces = []
    for a in range(count):
        cut = parts if a == 0 else 1
        pieces += [(a, p, ins[a].shape[0], ins[a].shape[0] // cut) for p in range(cut)]

    def number(zz, rr, cc):
        return ((zz if planes > 1 else 0) * 2 + rr) * 4 + cc

    def place_of(i, which):
        a, p, depth, cut = pieces[i]
        return outs[a].at[pl.ds(pl.multiple_of(which * depth + p * cut, cut), cut)]

    sent = [[] for _ in pieces]

    def send(i, which, target, own=False):
        a, p, depth, cut = pieces[i]
        spot = place_of(i, which)
        copy = pltpu.make_async_remote_copy(
            src_ref=ins[a].at[pl.ds(p * cut, cut)] if own else spot, dst_ref=spot,
            send_sem=send_sem.at[i, len(sent[i])], recv_sem=recv_sem.at[i, which],
            device_id=target, device_id_type=MESH)
        copy.start()
        sent[i].append(copy)

    def await_block(i, which):
        spot = place_of(i, which)
        pltpu.make_async_remote_copy(
            src_ref=spot, dst_ref=spot, send_sem=send_sem.at[i, 0], recv_sem=recv_sem.at[i, which],
            device_id=partner, device_id_type=MESH).wait_recv()

    mine = number(z, r, c)
    keeps = []
    every = range(len(pieces))
    for i in every:
        for target in [to_first, to_second] + [(z ^ k, r, c) for k in range(1, planes)] + [partner]:
            send(i, mine, target, True)
    for a in range(count):
        keep = pltpu.make_async_copy(ins[a], outs[a].at[pl.ds(pl.multiple_of(mine * ins[a].shape[0], ins[a].shape[0]), ins[a].shape[0])], own_sem.at[a])
        keep.start()
        keeps.append(keep)

    def forward(which, targets):
        for i in every:
            await_block(i, which)
            for target in targets:
                send(i, which, target)

    for step in range(planes + 2):
        if 0 < step < planes:
            forward(number(z ^ step, r, c), [to_first, to_second, partner])
        if 0 <= step - 1 < planes:
            forward(number(z ^ (step - 1), r, first), [to_second, partner])
            forward(number(z ^ (step - 1), r, second), [partner])
        if 0 <= step - 2 < planes:
            forward(number(z ^ (step - 2), r, diag), [partner])
    for k in range(planes):
        for j in range(4):
            for i in every:
                await_block(i, number(z ^ k, 1 - r, c ^ j))
    for keep in keeps:
        keep.wait()
    for copies in sent:
        for copy in copies:
            copy.wait_send()

def gather(arrays, planes, collective_id, parts=1):
    count = len(arrays)
    blocks = planes * 8
    sends = (3 + planes - 1) + (planes - 1) * 3 + planes * 4
    pieces = count - 1 + parts
    return pl.pallas_call(
        functools.partial(gather_kernel, planes, parts, count),
        out_shape=[jax.ShapeDtypeStruct((blocks * a.shape[0],) + a.shape[1:], a.dtype) for a in arrays],
        in_specs=[ANYSPEC] * count, out_specs=[ANYSPEC] * count,
        scratch_shapes=[pltpu.SemaphoreType.DMA((count,)), pltpu.SemaphoreType.DMA((pieces, sends)), pltpu.SemaphoreType.DMA((pieces, blocks))],
        compiler_params=pltpu.CompilerParams(collective_id=collective_id, has_side_effects=True),
    )(*arrays)

def reducer(planes, cuts, parts, outs, buffers, semaphores):
    held, fromp, relay, near, far = buffers
    load_sem, pair_send, pair_recv, send_sem, relay_recv, near_recv, far_recv = semaphores
    z, r, c = place()
    first, second, diag = c ^ (1 + r), c ^ (2 - r), c ^ 3
    partner = (z, 1 - r, c)
    to_first, to_second = (z, r, first), (z, r, second)
    full = outs[0].shape[0]
    depth = full // cuts
    every = range(len(parts))

    def cut(ref, v):
        return ref.at[pl.ds(pl.multiple_of((v % cuts) * depth, depth), depth)]

    def rows(a, v, rr, cc):
        which = (((z ^ (v // cuts)) if planes > 1 else 0) * 2 + rr) * 4 + cc
        return parts[a].at[pl.ds(pl.multiple_of(which * full + (v % cuts) * depth, depth), depth)]

    columns, partner_columns = [c, first, second, diag], [c, second, first, diag]

    def remote(source, target, send, recv, device):
        return pltpu.make_async_remote_copy(
            src_ref=source, dst_ref=target, send_sem=send, recv_sem=recv, device_id=device, device_id_type=MESH)

    def mine(a, v, j):
        return cut(held[a].at[v // cuts, j], v)

    def paired(a, v, j):
        return cut(fromp[a].at[v // cuts, j], v)

    def nearby(a, v, which):
        return cut(near[a].at[v // cuts, which], v)

    def load(a, v, j):
        return pltpu.make_async_copy(rows(a, v, r, columns[j]), mine(a, v, j), load_sem.at[a, v, j])

    def pair(a, v, j):
        return remote(rows(a, v, 1 - r, partner_columns[j]), paired(a, v, j), pair_send.at[a, v, j], pair_recv.at[a, v, j], partner)

    def begin(i, _):
        v = planes * cuts - 1 - i
        for j in (3, 2, 1, 0):
            for a in every:
                load(a, v, j).start()
                pair(a, v, j).start()
        return 0

    step_rows = min(32, depth)

    def add(target, sources):
        def body(i, _):
            at = pl.ds(pl.multiple_of(i * step_rows, step_rows), step_rows)
            total = sources[0][at].astype(jnp.float32)
            for source in sources[1:]:
                total = total + source[at].astype(jnp.float32)
            target[at] = total.astype(target.dtype)
            return 0
        lax.fori_loop(0, depth // step_rows, body, 0)

    def ready(a, v, j):
        load(a, v, j).wait()
        pair(a, v, j).wait_recv()

    def to_diag(a, v):
        return remote(mine(a, v, 3), cut(relay[a].at[v // cuts], v), send_sem.at[a, v, 0], relay_recv.at[a, v], to_second)

    def to_near(a, v, which):
        source, device = (mine(a, v, 2), to_second) if which else (mine(a, v, 1), to_first)
        return remote(source, nearby(a, v, which), send_sem.at[a, v, 1 + which], near_recv.at[a, v, which], device)

    def to_far(a, v):
        slot = jnp.maximum(v - cuts, 0)
        return remote(mine(a, v, 0), cut(far[a].at[slot // cuts], v), send_sem.at[a, v, 3], far_recv.at[a, slot], (z ^ (v // cuts), r, c))

    def to_relay(v):
        for a in every:
            ready(a, v, 3)
            add(mine(a, v, 3), [mine(a, v, 3), paired(a, v, 3)])
            to_diag(a, v).start()
        for a in every:
            ready(a, v, 2)
            add(mine(a, v, 2), [mine(a, v, 2), paired(a, v, 2)])
            to_near(a, v, 1).start()

    def pass_on(v):
        for a in every:
            ready(a, v, 1)
            to_diag(a, v).wait_recv()
            add(mine(a, v, 1), [mine(a, v, 1), paired(a, v, 1), cut(relay[a].at[v // cuts], v)])
            to_near(a, v, 0).start()

    def collect(v):
        for a in every:
            ready(a, v, 0)
            to_near(a, v, 0).wait_recv()
            to_near(a, v, 1).wait_recv()
            terms = [mine(a, v, 0), paired(a, v, 0), nearby(a, v, 0), nearby(a, v, 1)]

            @pl.when(v >= cuts)
            def _():
                add(mine(a, v, 0), terms)
                to_far(a, v).start()

            @pl.when(v < cuts)
            def _():
                for i in range(1, planes):
                    to_far(a, v + i * cuts).wait_recv()
                add(cut(outs[a], v), terms + [cut(far[a].at[i], v) for i in range(planes - 1)])

    def drain(v, _):
        for a in every:
            for j in range(4):
                pair(a, v, j).wait_send()
            to_diag(a, v).wait_send()
            to_near(a, v, 0).wait_send()
            to_near(a, v, 1).wait_send()

            @pl.when(v >= cuts)
            def _():
                to_far(a, v).wait_send()
        return 0

    return begin, to_relay, pass_on, collect, drain


def reduce_steps(planes, cuts, parts, outs, buffers, semaphores, filler):
    z, r, c = place()
    greet([(z, r, c ^ 1), (z, r, c ^ 2), (z, 1 - r, c)] + [(z ^ k, r, c) for k in range(1, planes)])
    begin, to_relay, pass_on, collect, drain = reducer(planes, cuts, parts, outs, buffers, semaphores)
    units = planes * cuts
    lax.fori_loop(0, units, begin, 0)
    lag = 1

    def step_body(step, _):
        @pl.when(step < units)
        def _():
            to_relay(units - 1 - step)

        @pl.when(jnp.logical_and(step >= lag, step < units + lag))
        def _():
            pass_on(units - 1 - step + lag)

        @pl.when(step >= 2 * lag)
        def _():
            collect(units - 1 - step + 2 * lag)
        if filler is not None:
            filler(step)
        return 0

    lax.fori_loop(0, units + 2 * lag, step_body, 0)
    lax.fori_loop(0, units, drain, 0)


def reduce_scratch(partials, planes, cuts):
    shapes = [((p.shape[0] // (planes * 8), p.shape[1]), p.dtype) for p in partials]
    count, far, units = len(partials), max(planes - 1, 1), planes * cuts
    dma = pltpu.SemaphoreType.DMA
    buffers = [pltpu.VMEM(lead + shape, kind) for lead in ((planes, 4), (planes, 4), (planes,), (planes, 2), (far,)) for shape, kind in shapes]
    return shapes, buffers, [
        dma((count, units, 4)), dma((count, units, 4)), dma((count, units, 4)), dma((count, units, 4)),
        dma((count, units)), dma((count, units, 2)), dma((count, far * cuts))]


def reduce_kernel(planes, count, *refs):
    buffers = [refs[(2 + i) * count:(3 + i) * count] for i in range(5)]
    reduce_steps(planes, CUTS, refs[:count], refs[count:2 * count], buffers, refs[7 * count:], None)


def reduce_scatter(partials, planes, collective_id):
    count = len(partials)
    shapes, buffers, semaphores = reduce_scratch(partials, planes, CUTS)
    return pl.pallas_call(
        functools.partial(reduce_kernel, planes, count),
        out_shape=[jax.ShapeDtypeStruct(shape, jnp.float32) for shape, _ in shapes],
        in_specs=[ANYSPEC] * count, out_specs=[pl.BlockSpec(memory_space=pltpu.VMEM)] * count,
        scratch_shapes=buffers + semaphores,
        compiler_params=pltpu.CompilerParams(collective_id=collective_id, has_side_effects=True, vmem_limit_bytes=48 * 2**20),
    )(*partials)


def opening_kernel(x_ref, gain_ref, wq_ref, wk_ref, wv_ref, all_x, proj_ref, normal, own_sem, send_sem, recv_sem, keep_sem, swap_send, swap_recv):
    z, r, c = place()
    width = proj_ref.shape[1] // 3
    depth = wq_ref.shape[0]

    def source(a, target):
        return (wq_ref, wk_ref, wv_ref)[a].at[:, pl.ds(pl.multiple_of(target * width, width), width)]

    def spot(a, origin):
        return proj_ref.at[pl.ds(pl.multiple_of(origin * depth, depth), depth), pl.ds(a * width, width)]

    keeps = [pltpu.make_async_copy(source(a, c), spot(a, c), keep_sem.at[a]) for a in range(3)]
    swaps = [pltpu.make_async_remote_copy(
        src_ref=source(a, c ^ j), dst_ref=spot(a, c), send_sem=swap_send.at[a, j - 1], recv_sem=swap_recv.at[a, j - 1],
        device_id=(z, r, c ^ j), device_id_type=MESH) for a in range(3) for j in range(1, 4)]

    def beside():
        for copy in keeps + swaps:
            copy.start()
        rows = x_ref[...].astype(jnp.float32)
        scale = lax.rsqrt(jnp.mean(rows * rows, axis=1, keepdims=True) + EPSILON)
        normal[...] = (rows * scale * gain_ref[...]).astype(jnp.bfloat16)

    gather_steps(1, 2, (normal,), (all_x,), own_sem, send_sem, recv_sem, [(z, r, c ^ 3)], beside)
    for a in range(3):
        keeps[a].wait()
        for j in range(1, 4):
            arrived = spot(a, c ^ j)
            pltpu.make_async_remote_copy(
                src_ref=arrived, dst_ref=arrived, send_sem=swap_send.at[a, j - 1], recv_sem=swap_recv.at[a, j - 1],
                device_id=(z, r, c ^ j), device_id_type=MESH).wait_recv()
    for swap in swaps:
        swap.wait_send()


def opening(hidden, gain, w_query, w_key, w_value, collective_id):
    depth, half = w_query.shape
    dma = pltpu.SemaphoreType.DMA
    shape = jax.ShapeDtypeStruct
    return pl.pallas_call(
        opening_kernel,
        out_shape=[shape((8 * hidden.shape[0], hidden.shape[1]), jnp.bfloat16), shape((depth * 4, 3 * (half // 4)), w_query.dtype)],
        in_specs=[pl.BlockSpec(memory_space=pltpu.VMEM)] * 2 + [ANYSPEC] * 3, out_specs=[ANYSPEC] * 2,
        scratch_shapes=[pltpu.VMEM(hidden.shape, jnp.bfloat16), dma((1,)), dma((2, 7)), dma((2, 8)), dma((3,)), dma((3, 3)), dma((3, 3))],
        compiler_params=pltpu.CompilerParams(collective_id=collective_id, has_side_effects=True),
    )(hidden, gain, w_query, w_key, w_value)


NEAR, SMALL, WIDE, LAG, AHEAD = (8, 16, 24), (24, 30, 36), (2, 4, 4), 3, 8


def finish_kernel(planes, proj_ref, outp_ref, small_ref, scaled_ref, mixed_part, entry_part,
                  proj_out, outp_out, small_out, mixed_out, entry_out, *scratch):
    (proj_own, outp_own, proj_in, outp_in, proj_far, outp_far, small_own, slices, far_slices, own_sem, swap_send, swap_recv, down_send, down_recv,
     far_down, up_send, up_recv, slice_send, slice_recv, far_send, far_recv, whole_send, whole_recv) = scratch[:23]
    wide = reducer(planes, CUTS, (mixed_part,), (mixed_out,), [(ref,) for ref in scratch[23:28]], scratch[28:35])
    near = reducer(1, 1, (entry_part,), (entry_out,), [(ref,) for ref in scratch[35:40]], scratch[40:47])
    z, r, c = place()
    here = r * 4 + c
    group = [(z, r ^ (j >> 2), c ^ (j & 3)) for j in range(1, 8)]
    greet(group + [(z ^ k, r, c) for k in range(1, planes)])
    width = proj_ref.shape[1] // 3
    depth, out_width = proj_ref.shape[0] // 4, outp_ref.shape[1] // 4
    step, tall = depth // 8, outp_ref.shape[0] // 2
    chunks = 32

    def remote(source, target, send, recv, device):
        return pltpu.make_async_remote_copy(
            src_ref=source, dst_ref=target, send_sem=send, recv_sem=recv, device_id=device, device_id_type=MESH)

    def owner(i):
        return (i - 24) // 2

    def piece(i, target):
        if i < 24:
            a, m = i // 8, i % 8
            return proj_ref.at[pl.ds(pl.multiple_of(target * depth + m * step, step), step), pl.ds(a * width, width)]
        return outp_ref.at[pl.ds((i % 2) * tall, tall), pl.ds(pl.multiple_of(target * out_width, out_width), out_width)]

    def spot(i, origin):
        a, m = i // 8, i % 8
        return proj_own.at[a, pl.ds(m * step, step), pl.ds(pl.multiple_of(origin * width, width), width)]

    def rows(proj, outp, i):
        if i < 24:
            return proj.at[i // 8, pl.ds((i % 8) * step, step), :]
        return outp.at[pl.ds((i - 24) * tall, tall), :]

    small_copies = []

    def small_begin():
        lanes = small_ref.shape[2]
        small_own[...] = small_ref[...]
        for j in range(entry_out.shape[1] // lanes):
            at = pl.ds(j * lanes, lanes)
            part = jnp.sum(entry_out[:, at] * scaled_ref[:, at], axis=0, keepdims=True)
            small_own[j // small_ref.shape[1], pl.ds(j % small_ref.shape[1], 1), :] = part
        for j in range(1, 8):
            copy = remote(small_own.at[here ^ j], slices.at[here], slice_send.at[j], slice_recv.at[here], group[j - 1])
            copy.start()
            small_copies.append(copy)

    order = [24, 25, 0, 1, 26, 27, 2, 3, 28, 29, 4, 5, 30, 31] + list(range(6, 24))
    swaps = []

    def issue(i):
        if i < 24:
            keep = pltpu.make_async_copy(piece(i, c), spot(i, c), own_sem.at[i])
            keep.start()
            for j in range(1, 4):
                copy = remote(piece(i, c ^ j), spot(i, c), swap_send.at[i, j - 1], swap_recv.at[i, j - 1], (z, r, c ^ j))
                copy.start()
                swaps.append(copy)
        else:
            @pl.when(c == owner(i))
            def _():
                pltpu.make_async_copy(piece(i, c), rows(proj_own, outp_own, i), own_sem.at[i]).start()
                for j in range(1, 4):
                    remote(piece(i, c ^ j), rows(proj_own, outp_own, i), swap_send.at[i, j - 1], swap_recv.at[i, 0], (z, r, c ^ j)).start()

    ahead = AHEAD
    for i in order[:ahead]:
        issue(i)
    near[0](0, 0)
    lax.fori_loop(0, planes * CUTS, wide[0], 0)

    def local_ready(i):
        target = rows(proj_own, outp_own, i)
        if i < 24:
            pltpu.make_async_copy(piece(i, c), spot(i, c), own_sem.at[i]).wait()
            for j in range(1, 4):
                arrived = spot(i, c ^ j)
                remote(arrived, arrived, swap_send.at[i, j - 1], swap_recv.at[i, j - 1], (z, r, c ^ j)).wait_recv()
        else:
            @pl.when(c == owner(i))
            def _():
                pltpu.make_async_copy(piece(i, c), target, own_sem.at[i]).wait()

            @pl.when(c != owner(i))
            def _():
                remote(target, target, swap_send.at[i, 0], swap_recv.at[i, 0], (z, r, c ^ 1)).wait_recv()

    def combine(target, sources, count):
        def body(s, _):
            at = pl.ds(pl.multiple_of(s * 32, 32), 32)
            total = sources[0][at].astype(jnp.float32)
            for source in sources[1:]:
                total = total + source[at].astype(jnp.float32)
            target[at] = total.astype(target.dtype)
            return 0
        lax.fori_loop(0, count // 32, body, 0)

    def seat(i):
        return z if i % 2 == 0 else planes - 1 - z

    def at_seat(i, p):
        return (p if i % 2 == 0 else planes - 1 - p, r, c)

    def refs(i):
        return [rows(proj, outp, i) for proj, outp in ((proj_own, outp_own), (proj_in, outp_in), (proj_far, outp_far), (proj_out, outp_out))]

    def down_copy(i, p):
        own, near_in, far_in, _ = refs(i)
        if p == 0:
            return remote(own, near_in, down_send.at[i], down_recv.at[i], at_seat(i, 1))
        return remote(own, far_in, down_send.at[i], far_down.at[i], at_seat(i, p - 1))

    def up_copy(i, p, target):
        result = refs(i)[3]
        return remote(result, result, up_send.at[i, 0 if target == 0 else 1], up_recv.at[i], at_seat(i, target))

    def hop(i, h):
        own, near_in, far_in, result = refs(i)

        if h == 0:
            for p in (0, 3):
                @pl.when(seat(i) == p)
                def _(p=p):
                    local_ready(i)
                    down_copy(i, p).start()
        elif h == 1:
            @pl.when(seat(i) == 2)
            def _():
                local_ready(i)
                down_copy(i, 3).wait_recv()
                combine(own, [own, far_in], own.shape[0])
                down_copy(i, 2).start()
        elif h == 2:
            @pl.when(seat(i) == 1)
            def _():
                local_ready(i)
                down_copy(i, 0).wait_recv()
                down_copy(i, 2).wait_recv()
                combine(result, [own, near_in, far_in], own.shape[0])
                up_copy(i, 1, 0).start()
                up_copy(i, 1, 2).start()
        elif h == 3:
            @pl.when(seat(i) == 2)
            def _():
                up_copy(i, 1, 2).wait_recv()
                up_copy(i, 2, 3).start()
        else:
            for p in (0, 3):
                @pl.when(seat(i) == p)
                def _(p=p):
                    up_copy(i, 1, p).wait_recv()

    def small_group():
        for j in range(1, 8):
            arrived = slices.at[here ^ j]
            remote(arrived, arrived, slice_send.at[0], slice_recv.at[here ^ j], group[j - 1]).wait_recv()
        slices[here] = small_own[here]
        total = slices[0]
        for j in range(1, 8):
            total = total + slices[j]
        far_slices[z] = total
        for k in range(1, planes):
            copy = remote(far_slices.at[z], far_slices.at[z], far_send.at[k - 1], far_recv.at[z], (z ^ k, r, c))
            copy.start()
            small_copies.append(copy)

    def small_far():
        for k in range(1, planes):
            arrived = far_slices.at[z ^ k]
            remote(arrived, arrived, far_send.at[k - 1], far_recv.at[z ^ k], (z ^ k, r, c)).wait_recv()
        total = far_slices[0]
        for k in range(1, planes):
            total = total + far_slices[k]
        small_out[here] = total
        for j in range(1, 8):
            copy = remote(small_out.at[here], small_out.at[here], whole_send.at[j], whole_recv.at[here], group[j - 1])
            copy.start()
            small_copies.append(copy)

    lag = LAG
    hops = 5
    actions = {}

    def plan(slot, action):
        actions.setdefault(slot, []).append(action)

    for slot, kind in zip(NEAR, (1, 2, 3)):
        plan(slot, lambda kind=kind: near[kind](0))
    for slot, action in zip(SMALL, (small_begin, small_group, small_far)):
        plan(slot, action)
    for n in range(planes * CUTS):
        for kind in (1, 2, 3):
            plan(int(WIDE[0] + n * WIDE[1] + (kind - 1) * WIDE[2]), lambda v=planes * CUTS - 1 - n, kind=kind: wide[kind](v))
    slots = chunks + (hops - 1) * lag
    for s in range(max(slots, max(actions) + 1)):
        if s + ahead < chunks:
            issue(order[s + ahead])
        for h in range(hops):
            if 0 <= s - h * lag < chunks:
                hop(order[s - h * lag], h)
        for action in actions.get(s, ()):
            action()
    for j in range(1, 8):
        arrived = small_out.at[here ^ j]
        remote(arrived, arrived, whole_send.at[0], whole_recv.at[here ^ j], group[j - 1]).wait_recv()
    near[4](0, 0)
    lax.fori_loop(0, planes * CUTS, wide[4], 0)
    for copy in small_copies + swaps:
        copy.wait_send()
    for i in range(24, 32):
        @pl.when(c == owner(i))
        def _():
            for j in range(1, 4):
                remote(piece(i, c ^ j), rows(proj_own, outp_own, i), swap_send.at[i, j - 1], swap_recv.at[i, 0], (z, r, c ^ j)).wait_send()
    for i in range(chunks):
        @pl.when(seat(i) != 1)
        def _(i=i):
            down_copy(i, 0).wait_send()

        @pl.when(seat(i) == 1)
        def _(i=i):
            up_copy(i, 1, 0).wait_send()

        @pl.when(jnp.logical_or(seat(i) == 1, seat(i) == 2))
        def _(i=i):
            up_copy(i, 1, 2).wait_send()


def finish(grad_proj_own, grad_out_own, small, scaled, mixed_part, entry_part, planes, collective_id):
    depth, width = grad_proj_own.shape[0] // 4, grad_proj_own.shape[1] // 3
    out_rows, out_width = grad_out_own.shape[0], grad_out_own.shape[1] // 4
    kind = grad_proj_own.dtype
    proj, outp = (3, depth, 4 * width), (4 * out_rows, out_width)
    vmem = pl.BlockSpec(memory_space=pltpu.VMEM)
    dma = pltpu.SemaphoreType.DMA
    [(mixed_shape, _)], mixed_buffers, mixed_semaphores = reduce_scratch([mixed_part], planes, CUTS)
    [(entry_shape, _)], entry_buffers, entry_semaphores = reduce_scratch([entry_part], 1, 1)
    return pl.pallas_call(
        functools.partial(finish_kernel, planes),
        out_shape=[jax.ShapeDtypeStruct(proj, kind), jax.ShapeDtypeStruct(outp, kind), jax.ShapeDtypeStruct(small.shape, small.dtype),
                   jax.ShapeDtypeStruct(mixed_shape, jnp.float32), jax.ShapeDtypeStruct(entry_shape, jnp.float32)],
        in_specs=[ANYSPEC, ANYSPEC, vmem, vmem, ANYSPEC, ANYSPEC], out_specs=[vmem] * 5,
        scratch_shapes=[
            pltpu.VMEM(proj, kind), pltpu.VMEM(outp, kind), pltpu.VMEM(proj, kind), pltpu.VMEM(outp, kind), pltpu.VMEM(proj, kind), pltpu.VMEM(outp, kind),
            pltpu.VMEM(small.shape, jnp.float32), pltpu.VMEM(small.shape, jnp.float32), pltpu.VMEM((planes,) + small.shape[1:], jnp.float32),
            dma((32,)), dma((32, 3)), dma((32, 3)), dma((32,)), dma((32,)), dma((32,)), dma((32, 2)), dma((32,)),
            dma((8,)), dma((8,)), dma((planes,)), dma((planes,)), dma((8,)), dma((8,))]
        + mixed_buffers + mixed_semaphores + entry_buffers + entry_semaphores,
        compiler_params=pltpu.CompilerParams(collective_id=collective_id, has_side_effects=True, vmem_limit_bytes=58 * 2**20),
    )(grad_proj_own, grad_out_own, small, scaled, mixed_part, entry_part)


def expert_kernel(planes, experts, own_h, own_side, cot, w_gate, w_up, w_down,
                  all_h, all_side, entry_out, route_out, active_out, grad_gate_out, grad_up_out,
                  gate_use, up_use, down_use, rows_h, rows_c, rows_side, back_rows,
                  gate_rows, up_rows, active_rows, grad_gate, grad_up, entry_stage, route_stage,
                  weight_sem, own_sem, send_sem, recv_sem, cot_sem, load_sem, store_sem):
    z, r, c = place()
    first, second, diag = c ^ (1 + r), c ^ (2 - r), c ^ 3
    partner = (z, 1 - r, c)
    to_first, to_second = (z, r, first), (z, r, second)
    count = own_h.shape[0]
    group = 4 * count
    expert = z * 4 + c
    half = count // 2
    pieces = [(own_h, all_h, 0, half), (own_h, all_h, half, half), (own_side, all_side, 0, count)]

    weights = [(w_gate, gate_use), (w_up, up_use), (w_down, down_use)]
    for i, (source, target) in enumerate(weights):
        pltpu.make_async_copy(source, target, weight_sem.at[i]).start()

    def number(zz, rr, cc):
        return (zz * 2 + rr) * 4 + cc

    def spot(i, which):
        _, target, start, size = pieces[i]
        return target.at[pl.ds(pl.multiple_of(which * count + start, size), size)]

    def copy_of(i, source, which, k, slot, device):
        return pltpu.make_async_remote_copy(
            src_ref=source, dst_ref=spot(i, which), send_sem=send_sem.at[i, k, slot], recv_sem=recv_sem.at[i, which],
            device_id=device, device_id_type=MESH)

    def own_piece(i):
        source, _, start, size = pieces[i]
        return source.at[pl.ds(start, size)]

    def await_block(i, which):
        copy_of(i, spot(i, which), which, 0, 0, partner).wait_recv()

    def forward(which, k, targets):
        for i in range(3):
            await_block(i, which)
            for slot, device in targets:
                copy_of(i, spot(i, which), which, k, slot, device).start()

    greet([to_first, to_second, partner] + [(z ^ k, r, c) for k in range(1, planes)])
    mine = number(z, r, c)
    for i in range(3):
        for slot, device in ((0, to_first), (1, to_second)):
            copy_of(i, own_piece(i), mine, 0, slot, device).start()
        for k in range(1, planes):
            copy_of(i, own_piece(i), mine, k, 7, (z ^ k, r, c)).start()
        copy_of(i, own_piece(i), mine, 0, 2, partner).start()
    keeps = [pltpu.make_async_copy(own_piece(i), spot(i, mine), own_sem.at[i]) for i in range(3)]
    for keep in keeps:
        keep.start()

    def base_of(k, rr):
        return pl.multiple_of(number(z ^ k, rr, 0) * count, group)

    def dot(left, right):
        return jnp.dot(left, right, preferred_element_type=jnp.float32)

    def dot_turned(left, right):
        return lax.dot_general(left, right, (((1,), (1,)), ((), ())), preferred_element_type=jnp.float32)

    def cot_copy(g):
        rr = jnp.where(g % 2 == 0, r, 1 - r)
        return pltpu.make_async_copy(cot.at[pl.ds(base_of(g // 2, rr), group)], rows_c.at[g % 2], cot_sem.at[g % 2])

    cot_copy(0).start()
    for i, (source, target) in enumerate(weights):
        pltpu.make_async_copy(source, target, weight_sem.at[i]).wait()

    def back_body(g, _):
        @pl.when(g + 1 < 2 * planes)
        def _():
            cot_copy(g + 1).start()

        cot_copy(g).wait()
        back_rows[g] = dot_turned(rows_c[g % 2], down_use[...])
        return 0

    lax.fori_loop(0, 2 * planes, back_body, 0)
    for keep in keeps:
        keep.wait()

    def stores(k, rr, slot):
        at = pl.ds(base_of(k, rr), group)
        return [
            pltpu.make_async_copy(source.at[slot], target.at[at], store_sem.at[slot, i])
            for i, (source, target) in enumerate((
                (entry_stage, entry_out), (route_stage, route_out), (active_rows, active_out),
                (grad_gate, grad_gate_out), (grad_up, grad_up_out)))]

    def compute(k, rr, slot):
        at = pl.ds(base_of(k, rr), group)
        loads = [pltpu.make_async_copy(all_h.at[at], rows_h, load_sem.at[0]),
                 pltpu.make_async_copy(all_side.at[at], rows_side, load_sem.at[1])]
        for load in loads:
            load.start()
        for load in loads:
            load.wait()
        gate_rows[...] = dot(rows_h[...], gate_use[...])
        up_rows[...] = dot(rows_h[...], up_use[...])

        @pl.when(k > 0)
        def _():
            for store in stores(k, rr, slot):
                store.wait()

        part = 128
        lane = lax.broadcasted_iota(jnp.int32, (part, rows_side.shape[1]), 1)

        @pl.loop(0, group // part)
        def _(t):
            at = pl.ds(pl.multiple_of(t * part, part), part)
            mask = (lane == expert) | (lane == expert + experts)
            share = jnp.sum(jnp.where(mask, rows_side[at, :].astype(jnp.float32), 0.0), axis=1, keepdims=True)
            gate, up, back = gate_rows[at, :], up_rows[at, :], back_rows[2 * k + slot, at, :]
            squash = jax.nn.sigmoid(gate)
            silu = gate * squash
            active = silu * up
            route = jnp.sum(active * back, axis=1, keepdims=True)
            route_stage[slot, at, :] = jnp.where(lane == expert, route, 0.0).astype(jnp.bfloat16)
            active_rows[slot, at, :] = (share * active).astype(jnp.bfloat16)
            grad_active = share * back
            grad_gate[slot, at, :] = (grad_active * up * squash * (1.0 + gate * (1.0 - squash))).astype(jnp.bfloat16)
            grad_up[slot, at, :] = (grad_active * silu).astype(jnp.bfloat16)

    def finish_rows(k, rr, slot):
        entry = dot_turned(grad_gate[slot], gate_use[...]) + dot_turned(grad_up[slot], up_use[...])
        entry_stage[slot] = entry.astype(jnp.bfloat16)
        for store in stores(k, rr, slot):
            store.start()

    def step_body(step, _):
        @pl.when(jnp.logical_and(step > 0, step < planes))
        def _():
            forward(number(z ^ step, r, c), step, ((0, to_first), (1, to_second), (2, partner)))

        @pl.when(jnp.logical_and(step >= 3, step < planes + 3))
        def _():
            k = step - 3
            for j in range(4):
                for i in range(3):
                    await_block(i, number(z ^ k, 1 - r, c ^ j))
            compute(k, 1 - r, 1)

        @pl.when(jnp.logical_and(step >= 1, step < planes + 1))
        def _():
            k = step - 1
            forward(number(z ^ k, r, first), k, ((3, to_second), (4, partner)))
            forward(number(z ^ k, r, second), k, ((5, partner),))

        @pl.when(jnp.logical_and(step >= 3, step < planes + 3))
        def _():
            finish_rows(step - 3, 1 - r, 1)
            finish_rows(step - 3, r, 0)

        @pl.when(jnp.logical_and(step >= 2, step < planes + 2))
        def _():
            k = step - 2
            forward(number(z ^ k, r, diag), k, ((6, partner),))
            compute(k, r, 0)

        return 0

    lax.fori_loop(0, planes + 3, step_body, 0)
    for slot, rr in ((0, r), (1, 1 - r)):
        for store in stores(planes - 1, rr, slot):
            store.wait()

    def drain(k, _):
        for i in range(3):
            for slot in range(7):
                copy_of(i, spot(i, mine), mine, k, slot, partner).wait_send()

            @pl.when(k > 0)
            def _():
                copy_of(i, spot(i, mine), mine, k, 7, partner).wait_send()
        return 0

    lax.fori_loop(0, planes, drain, 0)


def expert_rows_on_links(normal_h, side, all_cotangent, w_gate, w_up, w_down, experts, collective_id):
    planes = lax.axis_size("dp")
    count, width = normal_h.shape
    hidden = w_gate.shape[1]
    total, group, low, wide = planes * 8 * count, 4 * count, jnp.bfloat16, jnp.float32
    sides = side.shape[1]
    vmem, dma = pltpu.VMEM, pltpu.SemaphoreType.DMA
    outs = [jax.ShapeDtypeStruct((total, n), low) for n in (width, sides, width, sides, hidden, hidden, hidden)]
    return pl.pallas_call(
        functools.partial(expert_kernel, planes, experts),
        out_shape=outs, in_specs=[ANYSPEC] * 6, out_specs=[ANYSPEC] * 7,
        scratch_shapes=[
            vmem((width, hidden), low), vmem((width, hidden), low), vmem((hidden, width), low),
            vmem((group, width), low), vmem((2, group, width), low), vmem((group, sides), low), vmem((2 * planes, group, hidden), wide),
            vmem((group, hidden), wide), vmem((group, hidden), wide),
            vmem((2, group, hidden), low), vmem((2, group, hidden), low), vmem((2, group, hidden), low),
            vmem((2, group, width), low), vmem((2, group, sides), low),
            dma((3,)), dma((3,)), dma((3, planes, 8)), dma((3, planes * 8)), dma((2,)), dma((2,)), dma((2, 5))],
        compiler_params=pltpu.CompilerParams(collective_id=collective_id, has_side_effects=True, vmem_limit_bytes=60 * 2**20),
    )(normal_h, side, all_cotangent, w_gate, w_up, w_down)


def entry_kernel(planes, entry_part, route_part, all_h, cot, active, grad_gate, grad_up, w_down,
                 entry_out, route_out, mixed_out, gate_grad, up_grad, down_grad, *scratch):
    buffers = [scratch[2 * i:2 * i + 2] for i in range(5)]
    semaphores = scratch[10:17]
    down_use, rows_h, rows_c, rows_x, mixed_stage, acc_gate, acc_up, acc_down, down_sem, load_sem, store_sem, grad_sem = scratch[17:]
    leaves = [pltpu.make_async_copy(source, target, grad_sem.at[i]) for i, (source, target) in enumerate((
        (acc_gate, gate_grad), (acc_up, up_grad), (acc_down, down_grad)))]
    group = rows_h.shape[1]
    groups = all_h.shape[0] // group

    def loads(g):
        slot = g % 2
        at = pl.ds(pl.multiple_of(g * group, group), group)
        pairs = [(all_h.at[at], rows_h.at[slot]), (cot.at[at], rows_c.at[slot])] + [
            (source.at[at], rows_x.at[slot, i]) for i, source in enumerate((active, grad_gate, grad_up))]
        return [pltpu.make_async_copy(source, target, load_sem.at[slot, i]) for i, (source, target) in enumerate(pairs)]

    def store(g):
        at = pl.ds(pl.multiple_of(g * group, group), group)
        return pltpu.make_async_copy(mixed_stage, mixed_out.at[at], store_sem.at[0])

    def turned(left, right):
        return lax.dot_general(left, right, (((0,), (0,)), ((), ())), preferred_element_type=jnp.float32)

    down = pltpu.make_async_copy(w_down, down_use, down_sem.at[0])
    down.start()
    for load in loads(0):
        load.start()
    for acc in (acc_gate, acc_up, acc_down):
        @pl.loop(0, acc.shape[0] // 32)
        def _(t, acc=acc):
            acc[pl.ds(pl.multiple_of(t * 32, 32), 32), :] = jnp.zeros((32, acc.shape[1]), jnp.float32)
    down.wait()

    def one(g):
        @pl.when(g + 1 < groups)
        def _():
            for load in loads(g + 1):
                load.start()

        for load in loads(g):
            load.wait()
        slot = g % 2
        acc_gate[...] += turned(rows_h[slot], rows_x[slot, 1])
        acc_up[...] += turned(rows_h[slot], rows_x[slot, 2])
        acc_down[...] += turned(rows_x[slot, 0], rows_c[slot])

        @pl.when(g > 0)
        def _():
            store(g - 1).wait()

        mixed_stage[...] = jnp.dot(rows_x[slot, 0], down_use[...], preferred_element_type=jnp.float32).astype(jnp.bfloat16)
        store(g).start()

        @pl.when(g == groups - 1)
        def _():
            for leave in leaves:
                leave.start()

    per_step = -(-groups // (planes * CUTS))

    def filler(step):
        def body(i, _):
            @pl.when(step * per_step + i < groups)
            def _():
                one(step * per_step + i)
            return 0
        lax.fori_loop(0, per_step, body, 0)

    reduce_steps(planes, CUTS, (entry_part, route_part), (entry_out, route_out), buffers, semaphores, filler)
    store(groups - 1).wait()
    for leave in leaves:
        leave.wait()


def entry_sums(entry_part, route_part, all_h, cot, active, grad_gate, grad_up, w_down, collective_id):
    planes = lax.axis_size("dp")
    partials = [entry_part, route_part]
    shapes, buffers, semaphores = reduce_scratch(partials, planes, CUTS)
    (count, width), hidden, group = shapes[0][0], w_down.shape[0], 256
    low, wide, vmem, dma = jnp.bfloat16, jnp.float32, pltpu.VMEM, pltpu.SemaphoreType.DMA
    kept = pl.BlockSpec(memory_space=pltpu.VMEM)
    return pl.pallas_call(
        functools.partial(entry_kernel, planes),
        out_shape=[jax.ShapeDtypeStruct(shape, wide) for shape, _ in shapes] + [
            jax.ShapeDtypeStruct(entry_part.shape, low), jax.ShapeDtypeStruct((width, hidden), wide),
            jax.ShapeDtypeStruct((width, hidden), wide), jax.ShapeDtypeStruct((hidden, width), wide)],
        in_specs=[ANYSPEC] * 8, out_specs=[kept, kept] + [ANYSPEC] * 4,
        scratch_shapes=buffers + semaphores + [
            vmem((hidden, width), low), vmem((2, group, width), low), vmem((2, group, width), low), vmem((2, 3, group, hidden), low),
            vmem((group, width), low), vmem((width, hidden), wide), vmem((width, hidden), wide), vmem((hidden, width), wide),
            dma((1,)), dma((2, 5)), dma((1,)), dma((3,))],
        compiler_params=pltpu.CompilerParams(collective_id=collective_id, has_side_effects=True, vmem_limit_bytes=60 * 2**20),
    )(entry_part, route_part, all_h, cot, active, grad_gate, grad_up, w_down)


def dot_plain(left, right):
    return jnp.dot(left, right, preferred_element_type=jnp.float32)


def dot_cols(left, right):
    return lax.dot_general(left, right, (((1,), (1,)), ((), ())), preferred_element_type=jnp.float32)


def dot_rows(left, right):
    return lax.dot_general(left, right, (((0,), (0,)), ((), ())), preferred_element_type=jnp.float32)


def group_peers():
    z, r, c = place()
    return r * 4 + c, [(z, r ^ (j >> 2), c ^ (j & 3)) for j in range(1, 8)]


def group_sums(own, slots, send_sem, recv_sem):
    here, peers = group_peers()
    copies = []
    for j, peer in enumerate(peers):
        copy = pltpu.make_async_remote_copy(
            src_ref=own, dst_ref=slots.at[j], send_sem=send_sem.at[j], recv_sem=recv_sem.at[j],
            device_id=peer, device_id_type=MESH)
        copy.start()
        copies.append(copy)
    for copy in copies:
        copy.wait()
    total = jnp.zeros(own.shape, jnp.float32)
    for who in range(8):
        which = here ^ who
        total = total + jnp.where(which == 0, own[...], slots[jnp.maximum(which - 1, 0)])
    return total


def row_of_tokens(values):
    folded = values[:, :128]
    for start in range(128, values.shape[1], 128):
        folded = folded + values[:, start:start + 128]
    return jnp.sum(folded.T, axis=0, keepdims=True)


def column_of(row):
    return jnp.broadcast_to(row, (128, row.shape[1])).T


BLOCK = 256


def block_weights(queries, keys, first, finish):
    scores = dot_cols(queries[first:finish], keys[:finish])
    at_query = lax.broadcasted_iota(jnp.int32, scores.shape, 0) + first
    at_key = lax.broadcasted_iota(jnp.int32, scores.shape, 1)
    scores = jnp.where(at_query >= at_key, scores, MASKED)
    weights = jnp.exp(scores - jnp.max(scores, axis=1, keepdims=True))
    return weights / jnp.sum(weights, axis=1, keepdims=True)


def forward_kernel(width, x_ref, proj_ref, gains, cosine, sine, w_out_ref,
                   part_out, query_out, key_out, value_out, raw_out, scale_out, mixed_out, w_out_own,
                   sums, slots, send_sem, recv_sem, keep_sem, swap_send, swap_recv):
    greet(group_peers()[1])
    z, r, c = place()
    rows, lanes_out = w_out_own.shape[0], w_out_ref.shape[1]

    def piece(target):
        return w_out_ref.at[pl.ds(pl.multiple_of(target * rows, rows), rows), :]

    def spot(origin):
        return w_out_own.at[:, pl.ds(pl.multiple_of(origin * lanes_out, lanes_out), lanes_out)]

    keep = pltpu.make_async_copy(piece(c), spot(c), keep_sem.at[0])
    keep.start()
    swaps = [pltpu.make_async_remote_copy(
        src_ref=piece(c ^ j), dst_ref=spot(c), send_sem=swap_send.at[j - 1], recv_sem=swap_recv.at[j - 1],
        device_id=(z, r, c ^ j), device_id_type=MESH) for j in range(1, 4)]
    local = value_out.shape[1]
    raw = dot_plain(x_ref[...], proj_ref[...])
    raw_out[...] = raw[:, :2 * local]
    value_out[...] = raw[:, 2 * local:].astype(jnp.bfloat16)
    sums[...] = jnp.zeros(sums.shape, jnp.float32)
    for i in range(2):
        half = raw_out[:, pl.ds(i * local, local)]
        sums[pl.ds(i, 1), :] = row_of_tokens(half * half)
    total = group_sums(sums, slots, send_sem, recv_sem)
    for swap in swaps:
        swap.start()
    for i, (target, factor) in enumerate(((query_out, 128 ** (-0.5)), (key_out, 1.0))):
        scale = lax.rsqrt(column_of(total[i:i + 1]) / width + EPSILON)
        scale_out[:, pl.ds(i * 128, 128)] = scale
        for start in range(0, local, 128):
            lanes = pl.ds(start, 128)
            normal = raw_out[:, pl.ds(i * local + start, 128)] * scale * gains[pl.ds(i, 1), lanes]
            turned = normal * cosine[...] + pltpu.roll(normal, 64, 1) * sine[...]
            target[:, lanes] = (turned * factor).astype(jnp.bfloat16)
    tokens = x_ref.shape[0]
    for start in range(0, local, 128):
        lanes = pl.ds(start, 128)
        queries, keys, values = query_out[:, lanes], key_out[:, lanes], value_out[:, lanes]
        for first in range(0, tokens, BLOCK):
            weights = block_weights(queries, keys, first, first + BLOCK).astype(jnp.bfloat16)
            mixed = dot_plain(weights, values[:first + BLOCK])
            mixed_out[pl.ds(first, BLOCK), lanes] = mixed.astype(jnp.bfloat16)
    keep.wait()
    for swap in swaps:
        swap.wait()
    part_out[...] = dot_plain(mixed_out[...], w_out_own[...]).astype(jnp.bfloat16)


def attention_forward(gathered_x, w_proj, gains, cosine, sine, w_out, collective_id):
    tokens, width = gathered_x.shape
    local = w_proj.shape[1] // 3
    low, wide = jnp.bfloat16, jnp.float32
    shape, vmem = jax.ShapeDtypeStruct, pl.BlockSpec(memory_space=pltpu.VMEM)
    dma = pltpu.SemaphoreType.DMA
    return pl.pallas_call(
        functools.partial(forward_kernel, width),
        out_shape=[shape((tokens, width), low), shape((tokens, local), low), shape((tokens, local), low), shape((tokens, local), low),
                   shape((tokens, 2 * local), wide), shape((tokens, 256), wide), shape((tokens, local), low),
                   shape((w_out.shape[0] // 4, 4 * w_out.shape[1]), low)],
        in_specs=[vmem] * 5 + [ANYSPEC], out_specs=[vmem] * 8,
        scratch_shapes=[pltpu.VMEM((8, tokens), wide), pltpu.VMEM((7, 8, tokens), wide), dma((7,)), dma((7,)), dma((1,)), dma((3,)), dma((3,))],
        compiler_params=pltpu.CompilerParams(collective_id=collective_id, has_side_effects=True, vmem_limit_bytes=56 * 2**20),
    )(gathered_x, w_proj, gains, cosine, sine, w_out)


def backward_kernel(width, grad_ref, w_out_ref, x_hbm, proj_hbm, query_ref, key_ref, value_ref, raw_ref, scale_ref, mixed_ref,
                    gains, cosine, sine, grad_x_hbm, grad_proj_hbm, grad_out_out, gain_out,
                    grad_x_out, grad_proj_out, leave_sem, x_ref, proj_ref, grad_query, grad_key, grad_value, grad_raw, sums, slots, load_sem, send_sem, recv_sem):
    greet(group_peers()[1])
    loads = [pltpu.make_async_copy(x_hbm, x_ref, load_sem.at[0]), pltpu.make_async_copy(proj_hbm, proj_ref, load_sem.at[1])]
    for load in loads:
        load.start()
    local, tokens = value_ref.shape[1], value_ref.shape[0]
    grad_mixed = dot_cols(grad_ref[...], w_out_ref[...]).astype(jnp.bfloat16)
    grad_raw[:, pl.ds(0, local)] = grad_mixed
    for start in range(0, local, 128):
        lanes = pl.ds(start, 128)
        queries, keys, values, upstream = query_ref[:, lanes], key_ref[:, lanes], value_ref[:, lanes], grad_raw[:, lanes]
        for first in reversed(range(0, tokens, BLOCK)):
            finish = first + BLOCK
            weights = block_weights(queries, keys, first, finish)
            grad_weights = dot_cols(upstream[first:finish], values[:finish])
            centre = jnp.sum(weights * grad_weights, axis=1, keepdims=True)
            grad_scores = (weights * (grad_weights - centre)).astype(jnp.bfloat16)
            grad_query[pl.ds(first, BLOCK), lanes] = dot_plain(grad_scores, keys[:finish])
            key_part = dot_rows(grad_scores, queries[first:finish])
            value_part = dot_rows(weights.astype(jnp.bfloat16), upstream[first:finish])
            if finish == tokens:
                grad_key[:, lanes] = key_part
                grad_value[:, lanes] = value_part
            else:
                grad_key[pl.ds(0, finish), lanes] += key_part
                grad_value[pl.ds(0, finish), lanes] += value_part
    sums[...] = jnp.zeros(sums.shape, jnp.float32)
    gain_out[...] = jnp.zeros(gain_out.shape, jnp.float32)
    for i, (grad, factor) in enumerate(((grad_query, 128 ** (-0.5)), (grad_key, 1.0))):
        scale = scale_ref[:, pl.ds(i * 128, 128)]
        inner = None
        for start in range(0, local, 128):
            lanes = pl.ds(start, 128)
            upstream = grad[:, lanes] * factor
            normal = upstream * cosine[...] - pltpu.roll(upstream, 64, 1) * sine[...]
            raw = raw_ref[:, pl.ds(i * local + start, 128)]
            gain_out[pl.ds(i, 1), lanes] = jnp.sum(normal * raw * scale, axis=0, keepdims=True)
            weighted = gains[pl.ds(i, 1), lanes] * normal
            grad[:, lanes] = weighted
            inner = weighted * raw if inner is None else inner + weighted * raw
        sums[pl.ds(i, 1), :] = row_of_tokens(inner)
    total = group_sums(sums, slots, send_sem, recv_sem)
    for i, grad in enumerate((grad_query, grad_key)):
        scale = scale_ref[:, pl.ds(i * 128, 128)]
        factor = scale * scale * scale * column_of(total[i:i + 1]) / width
        for start in range(0, local, 128):
            lanes = pl.ds(start, 128)
            raw = raw_ref[:, pl.ds(i * local + start, 128)]
            grad_raw[:, pl.ds(i * local + start, 128)] = (scale * grad[:, lanes] - raw * factor).astype(jnp.bfloat16)
    grad_raw[:, pl.ds(2 * local, local)] = grad_value[...].astype(jnp.bfloat16)
    for load in loads:
        load.wait()
    leaves = [pltpu.make_async_copy(grad_x_out, grad_x_hbm, leave_sem.at[0]), pltpu.make_async_copy(grad_proj_out, grad_proj_hbm, leave_sem.at[1])]
    grad_x_out[...] = dot_cols(grad_raw[...], proj_ref[...]).astype(jnp.bfloat16)
    leaves[0].start()
    grad_proj_out[...] = dot_rows(x_ref[...], grad_raw[...]).astype(jnp.bfloat16)
    leaves[1].start()
    grad_out_out[...] = dot_rows(mixed_ref[...], grad_ref[...]).astype(jnp.bfloat16)
    for leave in leaves:
        leave.wait()


def attention_backward(grad_gathered, w_out_own, gathered_x, w_proj, kept, gains, cosine, sine, collective_id):
    tokens, width = gathered_x.shape
    local = w_proj.shape[1] // 3
    low, wide = jnp.bfloat16, jnp.float32
    shape, vmem = jax.ShapeDtypeStruct, pl.BlockSpec(memory_space=pltpu.VMEM)
    dma = pltpu.SemaphoreType.DMA
    return pl.pallas_call(
        functools.partial(backward_kernel, width),
        out_shape=[shape((tokens, width), low), shape(w_proj.shape, low), shape(w_out_own.shape, low), shape((8, local), wide)],
        in_specs=[vmem, vmem, ANYSPEC, ANYSPEC] + [vmem] * 9, out_specs=[ANYSPEC, ANYSPEC, vmem, vmem],
        scratch_shapes=[
            pltpu.VMEM((tokens, width), low), pltpu.VMEM(w_proj.shape, low), dma((2,)),
            pltpu.VMEM(gathered_x.shape, low), pltpu.VMEM(w_proj.shape, low),
            pltpu.VMEM((tokens, local), wide), pltpu.VMEM((tokens, local), wide), pltpu.VMEM((tokens, local), wide),
            pltpu.VMEM((tokens, 3 * local), low), pltpu.VMEM((8, tokens), wide), pltpu.VMEM((7, 8, tokens), wide),
            dma((2,)), dma((7,)), dma((7,))],
        compiler_params=pltpu.CompilerParams(collective_id=collective_id, has_side_effects=True, vmem_limit_bytes=60 * 2**20),
    )(grad_gathered, w_out_own, gathered_x, w_proj, *kept, gains, cosine, sine)


HEAD_DIM = 128
SEQ_LEN = 1024
EPSILON = 1e-05
THETA = 10000.0
MASKED = -1e30
GROUP = ("row", "col")
EVERYONE = ("dp", "row", "col")


def on_links():
    return lax.axis_size("dp") == 4 and lax.axis_size("col") == 4 and lax.axis_size("row") == 2


def gather_tokens(arrays, everyone, collective_id, parts):
    if on_links():
        return gather(arrays, 4 if everyone else 1, collective_id, parts)
    axes = EVERYONE if everyone else GROUP
    return [lax.all_gather(a, axes, axis=0, tiled=True) for a in arrays]


def scatter_sums(arrays, everyone, collective_id):
    if on_links():
        return reduce_scatter(arrays, 4 if everyone else 1, collective_id)
    axes = EVERYONE if everyone else GROUP
    return [lax.psum_scatter(a, axes, scatter_dimension=0, tiled=True).astype(jnp.float32) for a in arrays]


def open_attention(hidden_in, norm_attn, normal_x, w_query, w_key, w_value):
    if on_links():
        return opening(hidden_in, norm_attn[None], w_query, w_key, w_value, 1)
    pieces = [lax.all_to_all(w, "col", split_axis=1, concat_axis=0, tiled=True) for w in (w_query, w_key, w_value)]
    (gathered_x,) = gather_tokens([normal_x], False, 2, 2)
    return gathered_x, jnp.concatenate(pieces, axis=1)


def inverse_rms(values):
    return lax.rsqrt(jnp.mean(values * values, axis=-1, keepdims=True) + EPSILON)


def norm_backward(values, inv_scale, gain_row, upstream):
    weighted = gain_row * upstream
    inner_sum = jnp.sum(weighted * values, axis=-1, keepdims=True)
    grad_values = inv_scale * weighted - values * inv_scale**3 * inner_sum / values.shape[-1]
    return (grad_values, jnp.sum(upstream * values * inv_scale, axis=0))


def contract(left, right):
    return jnp.dot(left, right, preferred_element_type=jnp.float32)


def contract_rows(left, right):
    return lax.dot_general(
        left, right, (((0,), (0,)), ((), ())), preferred_element_type=jnp.float32
    )


def contract_cols(left, right):
    return lax.dot_general(
        left, right, (((1,), (1,)), ((), ())), preferred_element_type=jnp.float32
    )


def turn_tables(total_rows, seq_length, head_width):
    positions = (np.arange(total_rows) % seq_length).astype(np.float32)
    inverse = np.float32(THETA) ** (-np.arange(0, head_width, 2, dtype=np.float32) / np.float32(head_width))
    angles = positions[:, None] * inverse.astype(np.float32)[None, :]
    angles = np.concatenate([angles, angles], axis=-1).astype(np.float64)
    return (np.cos(angles)[:, None, :].astype(np.float32), np.sin(angles)[:, None, :].astype(np.float32))


def rotate(values, cosine, sine_table):
    middle = values.shape[-1] // 2
    turned = jnp.concatenate([-values[..., middle:], values[..., :middle]], axis=-1)
    return values * cosine + turned * sine_table


def unrotate(upstream, cosine, sine_table):
    middle = upstream.shape[-1] // 2
    turned_part = upstream * sine_table
    return upstream * cosine + jnp.concatenate(
        [turned_part[..., middle:], -turned_part[..., :middle]], axis=-1
    )


def attend_forward(queries, key_rows, value_rows):
    length = queries.shape[0]
    block_rows = min(512, length)
    outputs = []
    sums_log = []
    for first_row in range(0, length, block_rows):
        finish = first_row + block_rows
        scores = jnp.einsum(
            "qhd,khd->hqk",
            queries[first_row:finish],
            key_rows[:finish],
            preferred_element_type=jnp.float32,
        )
        causal = (first_row + jnp.arange(block_rows))[:, None] >= jnp.arange(finish)[None, :]
        scores = jnp.where(causal[None], scores, MASKED)
        highest = jnp.max(scores, axis=-1, keepdims=True)
        weights = jnp.exp(scores - highest)
        totals = jnp.sum(weights, axis=-1, keepdims=True)
        weights = (weights / totals).astype(jnp.bfloat16)
        outputs.append(
            jnp.einsum(
                "hqk,khd->qhd", weights, value_rows[:finish], preferred_element_type=jnp.float32
            )
        )
        sums_log.append((highest + jnp.log(totals))[..., 0])
    return (jnp.concatenate(outputs, axis=0), jnp.concatenate(sums_log, axis=1))


def attend_backward(queries, key_rows, value_rows, grad_out, sums_log):
    length = queries.shape[0]
    block_rows = min(512, length)
    grad_queries = []
    grad_keys = jnp.zeros(key_rows.shape, jnp.float32)
    grad_values = jnp.zeros(value_rows.shape, jnp.float32)
    for first_row in range(0, length, block_rows):
        finish = first_row + block_rows
        scores = jnp.einsum(
            "qhd,khd->hqk",
            queries[first_row:finish],
            key_rows[:finish],
            preferred_element_type=jnp.float32,
        )
        causal = (first_row + jnp.arange(block_rows))[:, None] >= jnp.arange(finish)[None, :]
        scores = jnp.where(causal[None], scores, MASKED)
        weights = jnp.exp(scores - sums_log[:, first_row:finish, None])
        grad_weights = jnp.einsum(
            "qhd,khd->hqk",
            grad_out[first_row:finish],
            value_rows[:finish],
            preferred_element_type=jnp.float32,
        )
        centre = jnp.sum(weights * grad_weights, axis=-1, keepdims=True)
        grad_scores = (weights * (grad_weights - centre)).astype(jnp.bfloat16)
        grad_queries.append(
            jnp.einsum(
                "hqk,khd->qhd", grad_scores, key_rows[:finish], preferred_element_type=jnp.float32
            )
        )
        grad_keys = grad_keys.at[:finish].add(
            jnp.einsum(
                "hqk,qhd->khd",
                grad_scores,
                queries[first_row:finish],
                preferred_element_type=jnp.float32,
            )
        )
        grad_values = grad_values.at[:finish].add(
            jnp.einsum(
                "hqk,qhd->khd",
                weights.astype(jnp.bfloat16),
                grad_out[first_row:finish],
                preferred_element_type=jnp.float32,
            )
        )
    return (jnp.concatenate(grad_queries, axis=0), grad_keys, grad_values)


def by_sequence(step, pieces, sequences):
    if sequences == 1:
        return tuple(out[None] for out in step(*[p[0] for p in pieces]))
    return lax.map(lambda each: step(*each), tuple(pieces))


def expert_rows(normal_h, side, cotangent, gate_use, up_use, down_use, expert_count):
    if on_links():
        all_cotangent = lax.all_gather(cotangent, EVERYONE, axis=0, tiled=True)
        rows_h, _, entry_part, grad_side, active_share, grad_gate_rows, grad_up_rows = expert_rows_on_links(
            normal_h, side, all_cotangent, gate_use, up_use, down_use, expert_count, 6
        )
        entry_rows, grad_probs_all, out_part, *grads = entry_sums(
            entry_part, grad_side, rows_h, all_cotangent, active_share, grad_gate_rows, grad_up_rows, down_use, 7
        )
        return (entry_rows, grad_probs_all, out_part, *grads)
    all_cotangent, rows_h, rows_side = gather_tokens([cotangent, normal_h, side], True, 6, 2)
    expert = lax.axis_index("dp") * lax.axis_size("col") + lax.axis_index("col")
    lane = jnp.arange(side.shape[1])
    own_share = jnp.sum(
        jnp.where((lane == expert) | (lane == expert + expert_count), rows_side.astype(jnp.float32), 0.0),
        axis=1,
        keepdims=True,
    )
    back_rows = contract_cols(all_cotangent, down_use)
    gate_rows = contract(rows_h, gate_use)
    up_rows = contract(rows_h, up_use)
    sigmoid_gate = jax.nn.sigmoid(gate_rows)
    silu_gate = gate_rows * sigmoid_gate
    active = silu_gate * up_rows
    route_grad = jnp.sum(active * back_rows, axis=1, keepdims=True)
    active_share = (own_share * active).astype(jnp.bfloat16)
    grad_active = own_share * back_rows
    grad_gate_rows = (
        grad_active * up_rows * sigmoid_gate * (1.0 + gate_rows * (1.0 - sigmoid_gate))
    ).astype(jnp.bfloat16)
    grad_up_rows = (grad_active * silu_gate).astype(jnp.bfloat16)
    entry_part = (contract_cols(grad_gate_rows, gate_use) + contract_cols(grad_up_rows, up_use)).astype(jnp.bfloat16)
    grad_side = jnp.where(jnp.arange(128 if expert_count <= 128 else expert_count)[None, :] == expert, route_grad, 0.0).astype(jnp.bfloat16)
    entry_rows, grad_probs_all = scatter_sums([entry_part, grad_side], True, 7)
    out_part = contract(active_share, down_use).astype(jnp.bfloat16)
    (mixture,) = scatter_sums([out_part], True, 8)
    grad_down_w = contract_rows(active_share, all_cotangent)
    grad_gate_w = contract_rows(rows_h, grad_gate_rows)
    grad_up_w = contract_rows(rows_h, grad_up_rows)
    return entry_rows, grad_probs_all, mixture, grad_gate_w, grad_up_w, grad_down_w


def per_device(
    hidden_in,
    cotangent,
    norm_attn,
    w_query,
    w_key,
    w_value,
    query_gain,
    key_gain,
    w_out,
    norm_moe,
    w_router,
    w_gate,
    w_up,
    w_down,
    routes,
):
    inputs = hidden_in.astype(jnp.float32)
    upstream = cotangent.astype(jnp.float32)
    token_count, top_count = routes.shape
    model_width = inputs.shape[1]
    expert_count = w_router.shape[1]

    inv_input = inverse_rms(inputs)
    normal_x = (inputs * inv_input * norm_attn).astype(jnp.bfloat16)
    gathered_x, w_proj = open_attention(hidden_in, norm_attn, normal_x, w_query, w_key, w_value)
    group_tokens = gathered_x.shape[0]
    local_width = w_proj.shape[1] // 3
    head_count = local_width // HEAD_DIM
    offset = (lax.axis_index("row") * lax.axis_size("col") + lax.axis_index("col")) * local_width
    gain_query = lax.dynamic_slice_in_dim(query_gain, offset, local_width)
    gain_key = lax.dynamic_slice_in_dim(key_gain, offset, local_width)
    cosine, sine_table = turn_tables(group_tokens, SEQ_LEN, HEAD_DIM)
    head_shape = (group_tokens, head_count, HEAD_DIM)
    sequences = group_tokens // SEQ_LEN
    seq_shape = (sequences, SEQ_LEN, head_count, HEAD_DIM)
    in_kernels = on_links() and sequences == 1
    if in_kernels:
        gains = jnp.concatenate([gain_query[None], gain_key[None], jnp.zeros((6, local_width), jnp.float32)])
        sine_signed = np.where(np.arange(HEAD_DIM) < HEAD_DIM // 2, -sine_table[:, 0], sine_table[:, 0])
        tables = (gains, jnp.asarray(cosine[:, 0]), jnp.asarray(sine_signed))
        attn_part, *kept, w_out_own = attention_forward(gathered_x, w_proj, *tables, w_out, 4)
    else:
        w_out_own = lax.all_to_all(w_out, "col", split_axis=0, concat_axis=1, tiled=True)
        raw = contract(gathered_x, w_proj)
        query_raw = raw[:, :local_width]
        key_raw = raw[:, local_width : 2 * local_width]
        value_heads = raw[:, 2 * local_width :].astype(jnp.bfloat16)
        query_square, key_square = lax.psum(
            (jnp.sum(query_raw * query_raw, axis=-1), jnp.sum(key_raw * key_raw, axis=-1)), GROUP
        )
        inv_query = lax.rsqrt(query_square / model_width + EPSILON)[:, None]
        inv_key = lax.rsqrt(key_square / model_width + EPSILON)[:, None]
        query_heads = (
            rotate((query_raw * inv_query * gain_query).reshape(head_shape), cosine, sine_table)
            * HEAD_DIM ** (-0.5)
        ).astype(jnp.bfloat16)
        key_heads = rotate(
            (key_raw * inv_key * gain_key).reshape(head_shape), cosine, sine_table
        ).astype(jnp.bfloat16)
        query_seq = query_heads.reshape(seq_shape)
        key_seq = key_heads.reshape(seq_shape)
        value_seq = value_heads.reshape(seq_shape)
        mixed, sums_log = by_sequence(attend_forward, (query_seq, key_seq, value_seq), sequences)
        mixed_heads = mixed.reshape(group_tokens, local_width).astype(jnp.bfloat16)
        attn_part = contract(mixed_heads, w_out_own).astype(jnp.bfloat16)
    (attn_rows,) = scatter_sums([attn_part], False, 5)
    state_rows = inputs + attn_rows

    inv_state = inverse_rms(state_rows)
    normal_h = (state_rows * inv_state * norm_moe).astype(jnp.bfloat16)
    logits = contract(normal_h, w_router)
    shifted = jnp.exp(logits - jnp.max(logits, axis=-1, keepdims=True))
    probabilities = shifted / jnp.sum(shifted, axis=-1, keepdims=True)
    selected = jnp.sum(
        (routes[:, :, None] == jnp.arange(expert_count)[None, None, :]).astype(jnp.float32), axis=1
    )
    shares = probabilities * selected
    share_high = shares.astype(jnp.bfloat16)
    share_low = (shares - share_high.astype(jnp.float32)).astype(jnp.bfloat16)
    side_width = max(2 * expert_count, 128)
    side = jnp.concatenate(
        [
            share_high,
            share_low,
            jnp.zeros((token_count, side_width - 2 * expert_count), jnp.bfloat16),
        ],
        axis=1,
    )

    chunks = max(1, lax.axis_size(EVERYONE) // 32)
    if chunks == 1:
        entry_rows, grad_probs_all, mixture, *expert_grads = expert_rows(
            normal_h, side, cotangent, w_gate[0], w_up[0], w_down[0], expert_count
        )
    else:

        def piece_step(sums, piece):
            entry, probs, mixed_rows, *grads = expert_rows(*piece, w_gate[0], w_up[0], w_down[0], expert_count)
            return [s + g for s, g in zip(sums, grads)], (entry, probs, mixed_rows)

        cut = [a.reshape((chunks, token_count // chunks) + a.shape[1:]) for a in (normal_h, side, cotangent)]
        empty = [jnp.zeros(w.shape[1:], jnp.float32) for w in (w_gate, w_up, w_down)]
        expert_grads, rows = lax.scan(piece_step, empty, cut)
        entry_rows, grad_probs_all, mixture = [r.reshape((token_count,) + r.shape[2:]) for r in rows]
    grad_gate_w, grad_up_w, grad_down_w = expert_grads
    grad_probs = selected * grad_probs_all[:, :expert_count]
    grad_logits = (
        probabilities * (grad_probs - jnp.sum(probabilities * grad_probs, axis=-1, keepdims=True))
    ).astype(jnp.bfloat16)
    grad_normal_h = entry_rows + contract_cols(grad_logits, w_router)
    grad_router_part = contract_rows(grad_logits, normal_h)
    grad_state_part, grad_moe_part = norm_backward(state_rows, inv_state, norm_moe, grad_normal_h)
    grad_state = upstream + grad_state_part
    grad_attn = grad_state.astype(jnp.bfloat16)
    (grad_gathered,) = gather_tokens([grad_attn], False, 9, 2)
    if in_kernels:
        grad_x_part, grad_proj_own, grad_out_own, gain_parts = attention_backward(
            grad_gathered, w_out_own, gathered_x, w_proj, kept, *tables, 10
        )
        grad_qgain_part, grad_kgain_part = gain_parts[0], gain_parts[1]
    else:
        grad_out_own = contract_rows(mixed_heads, grad_gathered).astype(jnp.bfloat16)
        grad_mixed = contract_cols(grad_gathered, w_out_own).astype(jnp.bfloat16)
        grad_query_seq, grad_key_seq, grad_value_seq = by_sequence(
            attend_backward,
            (query_seq, key_seq, value_seq, grad_mixed.reshape(seq_shape), sums_log),
            sequences,
        )
        grad_normal_q = unrotate(
            grad_query_seq.reshape(head_shape) * HEAD_DIM ** (-0.5), cosine, sine_table
        ).reshape(group_tokens, local_width)
        grad_normal_k = unrotate(grad_key_seq.reshape(head_shape), cosine, sine_table).reshape(
            group_tokens, local_width
        )
        weighted_q = gain_query * grad_normal_q
        weighted_k = gain_key * grad_normal_k
        inner_q, inner_k = lax.psum(
            (jnp.sum(weighted_q * query_raw, axis=-1), jnp.sum(weighted_k * key_raw, axis=-1)), GROUP
        )
        grad_query_raw = (
            inv_query * weighted_q - query_raw * inv_query**3 * inner_q[:, None] / model_width
        )
        grad_key_raw = inv_key * weighted_k - key_raw * inv_key**3 * inner_k[:, None] / model_width
        grad_qgain_part = jnp.sum(grad_normal_q * query_raw * inv_query, axis=0)
        grad_kgain_part = jnp.sum(grad_normal_k * key_raw * inv_key, axis=0)
        grad_raw = jnp.concatenate(
            [grad_query_raw, grad_key_raw, grad_value_seq.reshape(group_tokens, local_width)], axis=1
        ).astype(jnp.bfloat16)
        grad_x_part = contract_cols(grad_raw, w_proj).astype(jnp.bfloat16)
        grad_proj_own = contract_rows(gathered_x, grad_raw).astype(jnp.bfloat16)
    full_width = query_gain.shape[0]
    padded_qgain = lax.dynamic_update_slice_in_dim(
        jnp.zeros((full_width,), jnp.float32), grad_qgain_part, offset, 0
    )
    padded_kgain = lax.dynamic_update_slice_in_dim(
        jnp.zeros((full_width,), jnp.float32), grad_kgain_part, offset, 0
    )
    small = (padded_qgain, padded_kgain, grad_moe_part, grad_router_part)
    grad_query, grad_key, grad_value, grad_out_proj, mixture, grad_normal_x, small = last_sums(
        grad_proj_own, grad_out_own, small, inputs * inv_input, mixture, grad_x_part
    )
    grad_norm_attn, grad_query_gain, grad_key_gain, grad_norm_moe, grad_router = small
    grad_router = grad_router.T
    block_out = (state_rows + mixture).astype(jnp.bfloat16)
    grad_input = grad_state + norm_backward(inputs, inv_input, norm_attn, grad_normal_x)[0]
    return (
        block_out,
        grad_input,
        grad_norm_attn,
        grad_query,
        grad_key,
        grad_value,
        grad_query_gain,
        grad_key_gain,
        grad_out_proj,
        grad_norm_moe,
        grad_router,
        grad_gate_w[None],
        grad_up_w[None],
        grad_down_w[None],
    )


def last_sums(grad_proj_own, grad_out_own, small, scaled, mixed_part, entry_part):
    if on_links():
        parts = (jnp.zeros((scaled.shape[1],), jnp.float32), *small)
        flat = jnp.concatenate([part.reshape(-1) for part in parts])
        proj, outp, total, mixture, grad_normal_x = finish(
            grad_proj_own, grad_out_own, flat.reshape(8, -1, 128), scaled, mixed_part, entry_part, lax.axis_size("dp"), 12
        )
        total, sums, start = total.reshape(-1), [], 0
        for part in parts:
            sums.append(total[start : start + part.size].reshape(part.shape))
            start += part.size
        return (*(proj[a].astype(jnp.float32) for a in range(3)), outp.astype(jnp.float32), mixture, grad_normal_x, sums)
    (grad_normal_x,) = scatter_sums([entry_part], False, 11)
    small = (jnp.sum(grad_normal_x * scaled, axis=0), *small)
    width = grad_proj_own.shape[1] // 3
    blocks = [
        lax.all_to_all(grad_proj_own[:, a * width : (a + 1) * width], "col", split_axis=0, concat_axis=1, tiled=True)
        for a in range(3)
    ]
    out_block = lax.all_to_all(grad_out_own, "col", split_axis=1, concat_axis=0, tiled=True)
    weights = [total.astype(jnp.float32) for total in lax.psum((*blocks, out_block), "dp")]
    return (*weights, mixed_part, grad_normal_x, lax.psum(small, EVERYONE))


def solution(mesh):
    placed = (
        P(("dp", "row", "col"), None),
        P(("dp", "row", "col"), None),
        P(),
        P("col", "row"),
        P("col", "row"),
        P("col", "row"),
        P(),
        P(),
        P("row", "col"),
        P(),
        P(),
        P(("dp", "col"), None, "row"),
        P(("dp", "col"), None, "row"),
        P(("dp", "col"), "row", None),
        P(("dp", "row", "col"), None),
    )
    return jax.shard_map(
        per_device,
        mesh=mesh,
        in_specs=placed,
        out_specs=(
            P(("dp", "row", "col"), None),
            P(("dp", "row", "col"), None),
            P(),
            P("col", "row"),
            P("col", "row"),
            P("col", "row"),
            P(),
            P(),
            P("row", "col"),
            P(),
            P(),
            P(("dp", "col"), None, "row"),
            P(("dp", "col"), None, "row"),
            P(("dp", "col"), "row", None),
        ),
        check_vma=False,
    )
```
